32 devices in a mesh: wide: 8 (over z, x), narrow: 4 (over y, core).
Axes of the slice: x: 2, y: 2, z: 4, core: 2. Of those that a mesh axis runs over, the one named last changes fastest.
Arguments:
- block_input: bfloat16 [12288, 768], P('wide')
- cotangent: bfloat16 [12288, 768], P('wide'), may hold values from -6 to 6
- lengths: int32 [16, 12], P('wide'), may hold values from 0 to 384, as said below
- project_weight: float32 [3, 768, 768], P(None, 'wide', 'narrow'), may hold values from -0.125 to 0.125
- output_weight: float32 [768, 768], P('narrow', 'wide'), may hold values from -1.25 to 1.25
- expand_weight: float32 [2, 768, 2048], P(None, 'wide', 'narrow'), may hold values from -0.21875 to 0.21875
- shrink_weight: float32 [2048, 768], P('narrow', 'wide'), may hold values from -0.1875 to 0.1875
- bucket_bias: float32 [32, 12], replicated, may hold values from -3 to 3
- norm_gains: float32 [2, 768], P(None, 'wide'), may hold values from 0.5 to 1.5
- project_first: float32 [3, 768, 768], P(None, 'wide', 'narrow'), may hold values from -0.00061035156 to 0.00061035156
- output_first: float32 [768, 768], P('narrow', 'wide'), may hold values from -7.6293945e-05 to 7.6293945e-05
- expand_first: float32 [2, 768, 2048], P(None, 'wide', 'narrow'), may hold values from -0.00015258789 to 0.00015258789
- shrink_first: float32 [2048, 768], P('narrow', 'wide'), may hold values from -0.00015258789 to 0.00015258789
- bucket_first: float32 [32, 12], replicated, may hold values from -0.00010681152 to 0.00010681152
- gains_first: float32 [2, 768], P(None, 'wide'), may hold values from -0.00048828125 to 0.00048828125
- project_second: float32 [3, 768, 768], P(None, 'wide', 'narrow'), may hold values from 4.3798376e-10 to 7.064254e-09
- output_second: float32 [768, 768], P('narrow', 'wide'), may hold values from 6.3578288e-12 to 1.0172526e-10
- expand_second: float32 [2, 768, 2048], P(None, 'wide', 'narrow'), may hold values from 2.5431315e-11 to 4.0972675e-10
- shrink_second: float32 [2048, 768], P('narrow', 'wide'), may hold values from 2.5431315e-11 to 4.0972675e-10
- bucket_second: float32 [32, 12], replicated, may hold values from 1.1302807e-11 to 1.8084491e-10
- gains_second: float32 [2, 768], P(None, 'wide'), may hold values from 2.8257016e-10 to 4.5211226e-09
Outputs:
- block_output: bfloat16 [12288, 768], P('wide')
- input_gradient: bfloat16 [12288, 768], P('wide')
- global_norm: float32 [], replicated
- new_project: float32 [3, 768, 768], P(None, 'wide', 'narrow')
- new_output: float32 [768, 768], P('narrow', 'wide')
- new_expand: float32 [2, 768, 2048], P(None, 'wide', 'narrow')
- new_shrink: float32 [2048, 768], P('narrow', 'wide')
- new_bucket: float32 [32, 12], replicated
- new_gains: float32 [2, 768], P(None, 'wide')
- project_first_new: float32 [3, 768, 768], P(None, 'wide', 'narrow')
- output_first_new: float32 [768, 768], P('narrow', 'wide')
- expand_first_new: float32 [2, 768, 2048], P(None, 'wide', 'narrow')
- shrink_first_new: float32 [2048, 768], P('narrow', 'wide')
- bucket_first_new: float32 [32, 12], replicated
- gains_first_new: float32 [2, 768], P(None, 'wide')
- project_second_new: float32 [3, 768, 768], P(None, 'wide', 'narrow')
- output_second_new: float32 [768, 768], P('narrow', 'wide')
- expand_second_new: float32 [2, 768, 2048], P(None, 'wide', 'narrow')
- shrink_second_new: float32 [2048, 768], P('narrow', 'wide')
- bucket_second_new: float32 [32, 12], replicated
- gains_second_new: float32 [2, 768], P(None, 'wide')
The draws below stay inside these ranges and needn't reach their ends.
Inputs may be any that keep to these rules, and one draw needn't show every extreme that they name: Each row lists one buffer's passage lengths in packing order, each from 64 to 384, followed by zeros; a row sums to at most 768, and every row holds one passage of exactly 384 tokens.
All inputs are finite; a program needn't handle non-finite values.
Results may differ from the reference program's by a relative error of at most 0.013.
The reference program's roundings to bfloat16 on the way count: a program that leaves them out, or rounds other values in their place, can miss the bound.
Values may be sent and summed in bfloat16 or wider, within the bound.
A program may use at most 128 MiB of HBM per device.

```python
import math
import jax
import jax.numpy as jnp
from jax import lax

D = 768
H = 12
DH = 64
FF = 2048
NB = 32
BUF_LEN = 768
MAX_LEN = 384
MIN_LEN = 64
STEP = 10
SEGS = 12
BUFS = 16
TOKENS = 12288


def draw_block_input(key, part):
    noise_key, column_key = jax.random.split(key)
    columns = jnp.arange(D, dtype=jnp.float32) / max(D - 1, 1)
    jitter = jax.random.uniform(column_key, (D,), jnp.float32, 0.7, 1.3)
    sample = jax.random.normal(noise_key, (TOKENS, D), jnp.float32)
    spread = 3.0 ** columns
    return (sample * spread * jitter).astype(jnp.bfloat16)


def draw_lengths(key, part):
    raw_key, slot_key = jax.random.split(key)
    raw_lengths = jax.random.randint(raw_key, (BUFS, SEGS), MIN_LEN, MAX_LEN + 1, dtype=jnp.int32)
    longest_slot = jax.random.randint(slot_key, (BUFS, 1), 0, 2, dtype=jnp.int32)
    slots = jnp.arange(SEGS, dtype=jnp.int32)[None, :]
    raw_lengths = jnp.where(slots == longest_slot, MAX_LEN, raw_lengths)
    running = jnp.cumsum(raw_lengths, axis=1)
    return jnp.where(running <= BUF_LEN, raw_lengths, 0).astype(jnp.int32)


def steps_of(key, extent, shards, least, top_value):
    level = 1.0
    for axis_at, blocks in shards:
        steps = jax.random.uniform(jax.random.fold_in(jax.random.fold_in(key, 6), axis_at), (blocks,), jnp.float32, least / len(shards), top_value / len(shards))
        level = level * jnp.repeat(jnp.exp(steps), extent[axis_at] // blocks).reshape((-1,) + (1,) * (len(extent) - 1 - axis_at))
    return level


def centred(stream_key, dims, deviation, bound, shards=(), kind=jnp.bfloat16):
    result = deviation * jax.random.normal(stream_key, dims, jnp.float32)
    if shards:
        result = result * steps_of(stream_key, dims, shards, -0.22, 0.18)
    return jnp.clip(result, -bound, bound).astype(kind)


def setup_inputs(seed: int = 0) -> dict:
    keys = jax.random.split(jax.random.key(seed), 22)
    block_input = draw_block_input(jax.random.fold_in(keys[21], 71), 0)
    cotangent = centred(keys[1], (TOKENS, D), 1.0, 6.0, ((0, 8),))
    lengths = draw_lengths(jax.random.fold_in(keys[21], 71), 0)
    project_weight = centred(keys[3], (3, D, H * DH), (3 * D) ** -0.5, 0.125, ((1, 8), (2, 4)), jnp.float32)
    output_weight = centred(keys[4], (H * DH, D), (H * DH // 32) ** -0.5, 1.25, ((0, 4), (1, 8)), jnp.float32)
    expand_weight = centred(keys[5], (2, D, FF), D ** -0.5, 0.21875, ((1, 8), (2, 4)), jnp.float32)
    shrink_weight = centred(keys[6], (FF, D), (FF // 2) ** -0.5, 0.1875, ((0, 4), (1, 8)), jnp.float32)
    bucket_bias = centred(keys[7], (NB, H), 0.5, 3.0, (), jnp.float32)
    norm_gains = jnp.clip(1.0 + 0.1 * jax.random.normal(keys[8], (2, D), jnp.float32), 0.5, 1.5)
    project_first = centred(keys[9], (3, D, H * DH), (0.275 / (4 * D * H * DH + 3 * D * FF) ** 0.5), 0.00061035156, ((1, 8), (2, 4)), jnp.float32)
    output_first = centred(keys[10], (H * DH, D), (0.033 / (4 * D * H * DH + 3 * D * FF) ** 0.5), 7.62939453125e-05, ((0, 4), (1, 8)), jnp.float32)
    expand_first = centred(keys[11], (2, D, FF), (0.066 / (4 * D * H * DH + 3 * D * FF) ** 0.5), 0.00015258789, ((1, 8), (2, 4)), jnp.float32)
    shrink_first = centred(keys[12], (FF, D), (0.066 / (4 * D * H * DH + 3 * D * FF) ** 0.5), 0.00015258789, ((0, 4), (1, 8)), jnp.float32)
    bucket_first = centred(keys[13], (NB, H), (0.044 / (4 * D * H * DH + 3 * D * FF) ** 0.5), 0.00010681152, (), jnp.float32)
    gains_first = centred(keys[14], (2, D), (0.22 / (4 * D * H * DH + 3 * D * FF) ** 0.5), 0.00048828125, ((1, 8),), jnp.float32)
    project_second = jnp.clip(jnp.exp(math.log(7.064254070598963e-09) - 2.7806209 * jax.random.uniform(keys[15], (3, D, H * DH), jnp.float32) ** steps_of(keys[15], (3, D, H * DH), ((1, 8), (2, 4)), -0.2, 0.2)), 4.379837603707415e-10, 7.064254070598963e-09)
    output_second = jnp.clip(jnp.exp(math.log(1.0172526015983507e-10) - 2.7725887 * jax.random.uniform(keys[16], (H * DH, D), jnp.float32) ** steps_of(keys[16], (H * DH, D), ((0, 4), (1, 8)), -0.2, 0.2)), 6.357828759989692e-12, 1.0172526015983507e-10)
    expand_second = jnp.clip(jnp.exp(math.log(4.0972675252604063e-10) - 2.7795092 * jax.random.uniform(keys[17], (2, D, FF), jnp.float32) ** steps_of(keys[17], (2, D, FF), ((1, 8), (2, 4)), -0.2, 0.2)), 2.543131503995877e-11, 4.0972675252604063e-10)
    shrink_second = jnp.clip(jnp.exp(math.log(4.0972675252604063e-10) - 2.7795092 * jax.random.uniform(keys[18], (FF, D), jnp.float32) ** steps_of(keys[18], (FF, D), ((0, 4), (1, 8)), -0.2, 0.2)), 2.543131503995877e-11, 4.0972675252604063e-10)
    bucket_second = jnp.clip(jnp.exp(jax.random.uniform(keys[19], (NB, H), jnp.float32, math.log(1.1302806780799646e-11), math.log(1.8084490849279433e-10))), 1.1302806780799646e-11, 1.8084490849279433e-10)
    gains_second = jnp.clip(jnp.exp(math.log(4.521122587419768e-09) - 2.7725887 * jax.random.uniform(keys[20], (2, D), jnp.float32) ** steps_of(keys[20], (2, D), ((1, 8),), -0.2, 0.2)), 2.825701617137355e-10, 4.521122587419768e-09)
    return {"block_input": block_input, "cotangent": cotangent, "lengths": lengths, "project_weight": project_weight, "output_weight": output_weight, "expand_weight": expand_weight, "shrink_weight": shrink_weight, "bucket_bias": bucket_bias, "norm_gains": norm_gains, "project_first": project_first, "output_first": output_first, "expand_first": expand_first, "shrink_first": shrink_first, "bucket_first": bucket_first, "gains_first": gains_first, "project_second": project_second, "output_second": output_second, "expand_second": expand_second, "shrink_second": shrink_second, "bucket_second": bucket_second, "gains_second": gains_second}


@jax.custom_vjp
def low(v):
    return lax.optimization_barrier(v.astype(jnp.bfloat16)).astype(jnp.float32)

@jax.custom_vjp
def low_back(v):
    return v

def low_keep(v):
    return (low(v), None)

def low_pass(kept, grad):
    return (grad,)

def back_keep(v):
    return (v, None)

def back_low(kept, grad):
    return (low(grad),)
low.defvjp(low_keep, low_pass)
low_back.defvjp(back_keep, back_low)
bucket_edges = (12, 16, 23, 32, 46, 64, 91)
norm_eps = 1e-06
clip_limit = 1.0
beta_one = 0.9
beta_two = 0.999
adam_eps = 1e-08
step_rates = (0.06, 0.3, 0.07, 0.06, 1.0, 0.3)
decay_rates = (0.01, 0.01, 0.01, 0.01, 0.0, 0.0)
masked_score = -1000000000.0

def bucket_of(offsets):
    distance = jnp.abs(offsets)
    far_bucket = 8 + sum(((distance >= threshold).astype(jnp.int32) for threshold in bucket_edges))
    return (jnp.where(distance < 8, distance, far_bucket) + 16 * (offsets > 0).astype(jnp.int32)).astype(jnp.int32)

def round_both(values):
    return low_back(low(values))

def matmul(left, right):
    return jnp.dot(left, right, precision=lax.Precision.HIGHEST)

def rms_norm(values, gain_vec):
    return values * lax.rsqrt(lax.optimization_barrier(jnp.mean(values * values, axis=-1, keepdims=True)) + norm_eps) * gain_vec

def segment_row(lengths_row):
    segment_ends = jnp.cumsum(lengths_row).astype(jnp.int32)
    positions = jnp.arange(BUF_LEN, dtype=jnp.int32)
    return lax.optimization_barrier(jnp.sum((positions[:, None] >= segment_ends[None, :]).astype(jnp.int32), axis=1)).astype(jnp.int32)

def buffer_attention(queries, keys_rows, values_rows, segments, table):
    positions = jnp.arange(BUF_LEN, dtype=jnp.int32)
    buckets = bucket_of(positions[None, :] - positions[:, None])
    bias_full = jnp.transpose(jnp.take(table, buckets, axis=0), (2, 0, 1))
    scores = jnp.einsum('qhd,khd->hqk', queries, keys_rows, precision=lax.Precision.HIGHEST) + bias_full
    scores = low_back(scores)
    same_segment = segments[:, None] == segments[None, :]
    scores = jnp.where(same_segment[None], scores, masked_score)
    probs_soft = jax.nn.softmax(scores, axis=-1)
    return round_both(jnp.einsum('hqk,khd->qhd', low(probs_soft), values_rows, precision=lax.Precision.HIGHEST))
checkpointed = jax.checkpoint(buffer_attention)

def forward(inputs, project_weight, output_weight, expand_weight, shrink_weight, bucket_bias, norm_gains, segment_ids):
    gains_low = low(norm_gains)
    normed_one = low(rms_norm(inputs, gains_low[0]))
    project_low = low(project_weight)
    heads_shape = (BUFS, BUF_LEN, H, DH)
    queries = round_both(matmul(normed_one, project_low[0])).reshape(heads_shape)
    keys_rows = round_both(matmul(normed_one, project_low[1])).reshape(heads_shape)
    values_rows = round_both(matmul(normed_one, project_low[2])).reshape(heads_shape)
    attended = lax.map(lambda block_items: checkpointed(block_items[0], block_items[1], block_items[2], block_items[3], bucket_bias), (queries, keys_rows, values_rows, segment_ids))
    attended = attended.reshape(TOKENS, H * DH)
    middle = inputs + low_back(matmul(attended, low(output_weight)))
    normed_two = low(rms_norm(middle, gains_low[1]))
    expand_low = low(expand_weight)
    gate_pre = low_back(matmul(normed_two, expand_low[0]))
    up_pre = low_back(matmul(normed_two, expand_low[1]))
    hidden = low(jax.nn.gelu(gate_pre, approximate=True) * up_pre)
    return middle + low_back(matmul(hidden, low(shrink_weight)))

def adam_update(weight, moment_one, moment_two, gradient, step_rate, decay_rate):
    new_first = beta_one * moment_one + (1.0 - beta_one) * gradient
    new_second = beta_two * moment_two + (1.0 - beta_two) * gradient * gradient
    first_hat = new_first / (1.0 - beta_one ** STEP)
    second_hat = new_second / (1.0 - beta_two ** STEP)
    new_weight = weight - step_rate * (first_hat / (jnp.sqrt(second_hat) + adam_eps) + decay_rate * weight)
    return (new_weight, new_first, new_second)

def reference(block_input, cotangent, lengths, project_weight, output_weight, expand_weight, shrink_weight, bucket_bias, norm_gains, project_first, output_first, expand_first, shrink_first, bucket_first, gains_first, project_second, output_second, expand_second, shrink_second, bucket_second, gains_second):
    segment_ids = lax.map(segment_row, lengths)
    params = (project_weight, output_weight, expand_weight, shrink_weight, bucket_bias, norm_gains)

    def run_forward(inputs, *weights):
        return forward(inputs, *weights, segment_ids)
    output_value, pull_back = jax.vjp(run_forward, block_input.astype(jnp.float32), *params)
    gradients = pull_back(cotangent.astype(jnp.float32))
    input_gradient = gradients[0]
    weight_grads = gradients[1:]
    global_norm = jnp.sqrt(sum((jnp.sum(gradient * gradient) for gradient in weight_grads)))
    factor = jnp.minimum(1.0, clip_limit / (global_norm + 1e-06))
    firsts = (project_first, output_first, expand_first, shrink_first, bucket_first, gains_first)
    seconds = (project_second, output_second, expand_second, shrink_second, bucket_second, gains_second)
    results = [adam_update(weight, moment_one, moment_two, factor * gradient, step_rate, decay_rate) for weight, moment_one, moment_two, gradient, step_rate, decay_rate in zip(params, firsts, seconds, weight_grads, step_rates, decay_rates)]
    return (output_value.astype(jnp.bfloat16), input_gradient.astype(jnp.bfloat16), global_norm, results[0][0], results[1][0], results[2][0], results[3][0], results[4][0], results[5][0], results[0][1], results[1][1], results[2][1], results[3][1], results[4][1], results[5][1], results[0][2], results[1][2], results[2][2], results[3][2], results[4][2], results[5][2])
```

```python
import functools

import jax
import jax.numpy as jnp
from jax import lax
from jax.experimental import pallas as pl
from jax.experimental.pallas import tpu as pltpu
from jax.sharding import PartitionSpec as P

DH = 64
STEP = 10
LANES = 128
MESH = pl.DeviceIdType.MESH
F32 = jnp.float32
BF16 = jnp.bfloat16
ANY = pl.ANY

bucket_edges = (12, 16, 23, 32, 46, 64, 91)
norm_eps = 1e-06
clip_limit = 1.0
beta_one = 0.9
beta_two = 0.999
adam_eps = 1e-08
step_rates = (0.06, 0.3, 0.07, 0.06, 1.0, 0.3)
decay_rates = (0.01, 0.01, 0.01, 0.01, 0.0, 0.0)
masked_score = -1000000000.0
VMEM_LIMIT = 58 << 20

NN = (((1,), (0,)), ((), ()))
NT = (((1,), (1,)), ((), ()))
TN = (((0,), (0,)), ((), ()))


def mm(left, right, dims=NN):
    return lax.dot_general(left, right, dims, preferred_element_type=F32)


def bucket_of(offsets):
    distance = jnp.abs(offsets)
    far_bucket = 8 + sum(((distance >= threshold).astype(jnp.int32) for threshold in bucket_edges))
    return jnp.where(distance < 8, distance, far_bucket) + 16 * (offsets > 0).astype(jnp.int32)


def rms_scale(values):
    return lax.rsqrt(jnp.mean(values * values, axis=-1, keepdims=True) + norm_eps)


def norm_back(values, scale_vec, gain_vec, upstream):
    weighted = upstream * gain_vec
    inner_mean = jnp.mean(weighted * values, axis=-1, keepdims=True)
    return scale_vec * weighted - values * (scale_vec * scale_vec * scale_vec) * inner_mean


def adam_update(weight, moment_one, moment_two, gradient, step_rate, decay_rate):
    new_first = beta_one * moment_one + (1.0 - beta_one) * gradient
    new_second = beta_two * moment_two + (1.0 - beta_two) * gradient * gradient
    first_hat = new_first / (1.0 - beta_one**STEP)
    second_hat = new_second / (1.0 - beta_two**STEP)
    new_weight = weight - step_rate * (
        first_hat / (jnp.sqrt(second_hat) + adam_eps) + decay_rate * weight
    )
    return (new_weight, new_first, new_second)


def fold_rows(values):
    rows, cols = values.shape
    return jnp.sum(values.reshape(rows // 8, 8, cols), axis=0)


def start_rows(pieces, target, offs_ref, sems):
    copies = []
    for at, piece in enumerate(pieces):
        rows = piece.shape[0]
        begin = pl.multiple_of(offs_ref[at], 16)
        copies.append(
            pltpu.make_async_copy(piece, target.at[pl.ds(begin, rows)], sems.at[at])
        )
    for copy in copies:
        copy.start()
    return copies


def segments(index, ends_ref, buffer, slots):
    total = jnp.zeros(index.shape, jnp.int32)
    for slot in range(slots):
        total = total + (index >= ends_ref[buffer, slot]).astype(jnp.int32)
    return total


def params(**more):
    return pltpu.CompilerParams(vmem_limit_bytes=VMEM_LIMIT, **more)


def attend_kernel(
    buffer, slots, heads, count, ends_ref, offs_ref, x_ref, strip_ref, *refs
):
    pieces = refs[:count]
    normed_ref, qkv_ref, att_ref, log_ref, gains_ref, wbuf, qs, ks, vs, os, sems = refs[count:]
    length, width = x_ref.shape
    head_cols = heads * DH
    copies = start_rows(pieces, wbuf, offs_ref, sems)
    for copy in copies:
        copy.wait()
    gain_cols = wbuf[:, 4 * LANES :].astype(F32).T
    first = 3 * head_cols - 4 * LANES
    gains = gain_cols[first : first + 8]
    gains_ref[...] = gains
    gain_one = gains[0:1]
    step = 256

    @pl.loop(0, length // step)
    def _(block):
        rows = pl.ds(pl.multiple_of(block * step, step), step)
        values = x_ref[rows].astype(F32)
        normed = (values * rms_scale(values) * gain_one).astype(BF16)
        normed_ref[rows] = normed
        qkv = mm(normed, wbuf[...]).astype(BF16)
        qkv_ref[rows] = qkv[:, : 3 * head_cols]
        for h in range(heads):
            qs[h, rows] = qkv[:, h * DH : (h + 1) * DH]
            ks[h, rows] = qkv[:, head_cols + h * DH : head_cols + (h + 1) * DH]
            vs[h, rows] = qkv[:, 2 * head_cols + h * DH : 2 * head_cols + (h + 1) * DH]

    blocks = length // LANES
    seg_keys = segments(
        lax.broadcasted_iota(jnp.int32, (1, length), 1), ends_ref, buffer, slots
    )

    @pl.loop(0, blocks)
    def _(block):
        begin = pl.multiple_of(block * LANES, LANES)
        rows = pl.ds(begin, LANES)
        window = pl.ds(pl.multiple_of((blocks - 1 - block) * LANES, LANES), length)
        seg_rows = segments(
            lax.broadcasted_iota(jnp.int32, (LANES, 1), 0) + begin, ends_ref, buffer, slots
        )
        same = seg_rows == seg_keys
        lane = lax.broadcasted_iota(jnp.int32, (LANES, LANES), 1)
        logs = jnp.zeros((LANES, LANES), F32)
        for h in range(heads):
            scores = mm(qs[h, rows], ks[h], NT) + strip_ref[h, :, window]
            scores = jnp.where(same, scores, masked_score)
            row_max = jnp.max(scores, axis=1, keepdims=True)
            raised = jnp.exp(scores - row_max)
            total = jnp.sum(raised, axis=1, keepdims=True)
            probs = (raised * (1.0 / total)).astype(BF16)
            os[h, rows] = mm(probs, vs[h]).astype(BF16)
            logs = jnp.where(lane == h, row_max + jnp.log(total), logs)
        log_ref[rows] = logs

    att_ref[...] = jnp.concatenate([os[h] for h in range(heads)], axis=1)


def attend(buffer, ends, offs, x, strip, pieces, length, heads):
    width = x.shape[1]
    count = len(pieces)
    cols = pieces[0].shape[1]
    head_cols = heads * DH
    whole = lambda i, *_: (0, 0)
    spec = pltpu.PrefetchScalarGridSpec(
        num_scalar_prefetch=2,
        grid=(1,),
        in_specs=[
            pl.BlockSpec((length, width), lambda i, *_: (buffer, 0)),
            pl.BlockSpec(strip.shape, lambda i, *_: (0, 0, 0)),
        ]
        + [pl.BlockSpec(memory_space=ANY)] * count,
        out_specs=[
            pl.BlockSpec((length, width), whole),
            pl.BlockSpec((length, 3 * head_cols), whole),
            pl.BlockSpec((length, head_cols), whole),
            pl.BlockSpec((length, LANES), whole),
            pl.BlockSpec((8, width), whole),
        ],
        scratch_shapes=[
            pltpu.VMEM((width, cols), BF16),
            pltpu.VMEM((heads, length, DH), BF16),
            pltpu.VMEM((heads, length, DH), BF16),
            pltpu.VMEM((heads, length, DH), BF16),
            pltpu.VMEM((heads, length, DH), BF16),
            pltpu.SemaphoreType.DMA((count,)),
        ],
    )
    flops = 2 * length * (width * cols + 2 * heads * DH * length)
    return pl.pallas_call(
        functools.partial(attend_kernel, buffer, ends.shape[1], heads, count),
        grid_spec=spec,
        out_shape=[
            jax.ShapeDtypeStruct((length, width), BF16),
            jax.ShapeDtypeStruct((length, 3 * head_cols), BF16),
            jax.ShapeDtypeStruct((length, head_cols), BF16),
            jax.ShapeDtypeStruct((length, LANES), F32),
            jax.ShapeDtypeStruct((8, width), F32),
        ],
        compiler_params=params(),
        cost_estimate=pl.CostEstimate(
            flops=4 * flops, bytes_accessed=8 << 20, transcendentals=heads * length * length
        ),
        name="attend",
    )(ends, offs, x, strip, *pieces)


def feed_kernel(hidden_cols, counts, order_ref, offs_ref, *refs):
    own, across, beside, diagonal, x_ref, cot_ref, gains_ref = refs[:7]
    at = 7
    groups = []
    for count in counts:
        groups.append(refs[at : at + count])
        at += count
    (
        normed_ref,
        hidden_ref,
        gate_ref,
        ff_send,
        ff_keep,
        dn_send,
        dn_keep,
        middle_keep,
        gain_sum,
        ebuf,
        sbuf,
        oabuf,
        obbuf,
        sems,
    ) = refs[at:]
    step = pl.program_id(0)
    bufs = (oabuf, obbuf, ebuf, sbuf)

    @pl.when(step == 0)
    def _():
        copies = []
        for which, (group, target) in enumerate(zip(groups, bufs)):
            copies += start_rows(group, target, offs_ref, sems.at[which])
        for copy in copies:
            copy.wait()

    cols = own.shape[1]
    upper = order_ref[2] == 0
    pairs = []
    for near, far, weights in ((own, across, oabuf), (beside, diagonal, obbuf)):
        near_sum = mm(near[...], weights[:, :cols], NT)
        far_sum = mm(far[...], weights[:, cols:], NT)
        pairs.append(
            jnp.where(upper, near_sum, far_sum) + jnp.where(upper, far_sum, near_sum)
        )
    swap = order_ref[0] == 0
    attention = jnp.where(swap, pairs[0], pairs[1]) + jnp.where(swap, pairs[1], pairs[0])
    middle = x_ref[...].astype(F32) + attention
    scale_two = rms_scale(middle)
    gain_two = gains_ref[1:2]
    normed = (middle * scale_two * gain_two).astype(BF16)
    normed_ref[...] = normed
    cot = cot_ref[...]
    part = 256
    k0 = 0.7978845608028654
    k1 = 0.044715
    for begin in range(0, hidden_cols, part):
        gate = mm(normed, ebuf[:, begin : begin + part])
        up = mm(normed, ebuf[:, hidden_cols + begin : hidden_cols + begin + part])
        square = gate * gate
        tanh = jnp.tanh(k0 * (gate + k1 * (square * gate)))
        half = 0.5 * (1.0 + tanh)
        active = gate * half
        slope = half + (0.5 * gate) * (1.0 - tanh * tanh) * (k0 + (3.0 * k0 * k1) * square)
        d_hidden = mm(cot, sbuf[:, begin : begin + part])
        hidden_ref[:, begin : begin + part] = (active * up).astype(BF16)
        gate_ref[:, begin : begin + part] = (d_hidden * up * slope).astype(BF16)
        gate_ref[:, hidden_cols + begin : hidden_cols + begin + part] = (
            d_hidden * active
        ).astype(BF16)
    ff = mm(hidden_ref[...], sbuf[...], NT).astype(BF16)
    dn = mm(gate_ref[...], ebuf[...], NT)
    sums = fold_rows(dn * middle * scale_two)
    dn = dn.astype(BF16)

    @pl.when(step == 0)
    def _():
        ff_send[...] = ff
        dn_send[...] = dn
        gain_sum[...] = sums

    @pl.when(step == 1)
    def _():
        ff_keep[...] = ff
        dn_keep[...] = dn
        middle_keep[...] = middle
        gain_sum[...] = gain_sum[...] + sums


def feed(buffer, order, offs, parts, x, cot, gains, groups, length, hidden_cols):
    width = x.shape[1]
    half = length // 2
    cols = parts[0].shape[1]
    counts = [len(group) for group in groups]
    natural = lambda i, order, *_: (order[i], 0)
    rows = lambda i, order, *_: (2 * buffer + order[i], 0)
    whole = lambda i, *_: (0, 0)
    spec = pltpu.PrefetchScalarGridSpec(
        num_scalar_prefetch=2,
        grid=(2,),
        in_specs=[pl.BlockSpec((half, cols), natural)] * 4
        + [pl.BlockSpec((half, width), rows)] * 2
        + [pl.BlockSpec((8, width), whole)]
        + [pl.BlockSpec(memory_space=ANY)] * sum(counts),
        out_specs=[
            pl.BlockSpec((half, width), natural),
            pl.BlockSpec((half, hidden_cols), natural),
            pl.BlockSpec((half, 2 * hidden_cols), natural),
        ]
        + [pl.BlockSpec((half, width), whole)] * 5
        + [pl.BlockSpec((8, width), whole)],
        scratch_shapes=[
            pltpu.VMEM((width, 2 * hidden_cols), BF16),
            pltpu.VMEM((width, hidden_cols), BF16),
            pltpu.VMEM((width, 2 * cols), BF16),
            pltpu.VMEM((width, 2 * cols), BF16),
            pltpu.SemaphoreType.DMA((4, max(counts))),
        ],
    )
    flops = 2 * length * width * (4 * cols + 7 * hidden_cols)
    return pl.pallas_call(
        functools.partial(feed_kernel, hidden_cols, counts),
        grid_spec=spec,
        out_shape=[
            jax.ShapeDtypeStruct((length, width), BF16),
            jax.ShapeDtypeStruct((length, hidden_cols), BF16),
            jax.ShapeDtypeStruct((length, 2 * hidden_cols), BF16),
            jax.ShapeDtypeStruct((half, width), BF16),
            jax.ShapeDtypeStruct((half, width), BF16),
            jax.ShapeDtypeStruct((half, width), BF16),
            jax.ShapeDtypeStruct((half, width), BF16),
            jax.ShapeDtypeStruct((half, width), F32),
            jax.ShapeDtypeStruct((8, width), F32),
        ],
        compiler_params=params(),
        cost_estimate=pl.CostEstimate(
            flops=flops, bytes_accessed=12 << 20, transcendentals=length * hidden_cols
        ),
        name="feed",
    )(order, offs, *parts, x, cot, gains, *[piece for group in groups for piece in group])


def middle_kernel(order_ref, near, far, middle_ref, cot_ref, gains_ref, d_ref, low_ref):
    upstream = near[...].astype(F32) + far[...].astype(F32)
    middle = middle_ref[...]
    d_middle = cot_ref[...].astype(F32) + norm_back(
        middle, rms_scale(middle), gains_ref[1:2], upstream
    )
    d_ref[...] = d_middle
    low_ref[...] = d_middle.astype(BF16)


def input_kernel(order_ref, near, far, x_ref, d_ref, gains_ref, out_ref):
    upstream = near[...].astype(F32) + far[...].astype(F32)
    values = x_ref[...].astype(F32)
    out_ref[...] = (
        d_ref[...] + norm_back(values, rms_scale(values), gains_ref[0:1], upstream)
    ).astype(BF16)


def output_kernel(order_ref, near, far, middle_ref, out_ref):
    out_ref[...] = (
        middle_ref[...] + (near[...].astype(F32) + far[...].astype(F32)).astype(BF16).astype(F32)
    ).astype(BF16)


def half_call(kernel, name, buffer, order, arrays, placed, outs, gains=None):
    half, width = arrays[0].shape
    steps = 3
    block = half // steps
    mine = lambda i, *_: (i, 0)
    rows = lambda i, order, *_: ((2 * buffer + order[1]) * steps + i, 0)
    in_specs = [
        pl.BlockSpec((block, width), rows if at in placed else mine)
        for at in range(len(arrays))
    ]
    operands = list(arrays)
    if gains is not None:
        in_specs.append(pl.BlockSpec((8, width), lambda i, *_: (0, 0)))
        operands.append(gains)
    return pl.pallas_call(
        kernel,
        grid_spec=pltpu.PrefetchScalarGridSpec(
            num_scalar_prefetch=1,
            grid=(steps,),
            in_specs=in_specs,
            out_specs=[pl.BlockSpec((block, width), mine) for _ in outs],
        ),
        out_shape=[jax.ShapeDtypeStruct((half, width), kind) for kind in outs],
        compiler_params=params(),
        cost_estimate=pl.CostEstimate(
            flops=20 * half * width, bytes_accessed=12 * half * width, transcendentals=0
        ),
        name=name,
    )(order, *operands)


def back_kernel(buffer, slots, heads, counts, ends_ref, offs_ref, order_ref, *refs):
    near, far, qkv_ref, log_ref, strip_ref, x_ref = refs[:6]
    at = 6
    o_pieces = refs[at : at + counts[0]]
    at += counts[0]
    p_pieces = refs[at : at + counts[1]]
    at += counts[1]
    (
        low_ref,
        dqkv_ref,
        dn_send,
        dn_keep,
        gain_sum,
        dstrip,
        wbuf,
        obuf,
        qs,
        ks,
        vs,
        gs,
        qt,
        gt,
        dkt,
        dvt,
        dq,
        sems,
    ) = refs[at:]
    length = qkv_ref.shape[0]
    half = length // 2
    head_cols = heads * DH
    o_copies = start_rows(o_pieces, obuf, offs_ref, sems.at[0])
    p_copies = start_rows(p_pieces, wbuf, offs_ref, sems.at[1])
    mine = pl.ds(pl.multiple_of(order_ref[1] * half, LANES), half)
    other = pl.ds(pl.multiple_of(order_ref[0] * half, LANES), half)
    low_ref[mine] = near[...]
    low_ref[other] = far[...]
    for h in range(heads):
        qs[h] = qkv_ref[:, h * DH : (h + 1) * DH]
        ks[h] = qkv_ref[:, head_cols + h * DH : head_cols + (h + 1) * DH]
        vs[h] = qkv_ref[:, 2 * head_cols + h * DH : 2 * head_cols + (h + 1) * DH]
        qt[h] = qs[h].T
    dstrip[...] = jnp.zeros_like(dstrip)
    dkt[...] = jnp.zeros_like(dkt)
    dvt[...] = jnp.zeros_like(dvt)
    for copy in o_copies + p_copies:
        copy.wait()
    grads = mm(low_ref[...], obuf[:, :head_cols]).astype(BF16)
    for h in range(heads):
        gs[h] = grads[:, h * DH : (h + 1) * DH]
        gt[h] = gs[h].T
    blocks = length // LANES
    seg_keys = segments(
        lax.broadcasted_iota(jnp.int32, (1, length), 1), ends_ref, buffer, slots
    )

    @pl.loop(0, blocks)
    def _(block):
        begin = pl.multiple_of(block * LANES, LANES)
        rows = pl.ds(begin, LANES)
        window = pl.ds(pl.multiple_of((blocks - 1 - block) * LANES, LANES), length)
        seg_rows = segments(
            lax.broadcasted_iota(jnp.int32, (LANES, 1), 0) + begin, ends_ref, buffer, slots
        )
        same = seg_rows == seg_keys
        logs = log_ref[rows]
        for h in range(heads):
            scores = mm(qs[h, rows], ks[h], NT) + strip_ref[h, :, window]
            scores = jnp.where(same, scores, masked_score)
            probs = jnp.exp(scores - logs[:, h : h + 1])
            d_probs = mm(gs[h, rows], vs[h], NT)
            inner = jnp.sum(probs * d_probs, axis=1, keepdims=True)
            d_scores = (probs * (d_probs - inner)).astype(BF16)
            dstrip[h, :, window] = dstrip[h, :, window] + d_scores.astype(F32)
            dq[h, rows] = mm(d_scores, ks[h]).astype(BF16)
            dkt[h] = dkt[h] + mm(qt[h, :, rows], d_scores)
            dvt[h] = dvt[h] + mm(gt[h, :, rows], probs.astype(BF16))

    outs = [dq[h] for h in range(heads)]
    outs += [dkt[h].T.astype(BF16) for h in range(heads)]
    outs += [dvt[h].T.astype(BF16) for h in range(heads)]
    dqkv_ref[...] = jnp.concatenate(outs, axis=1)
    sums = []
    for target, which in ((dn_send, other), (dn_keep, mine)):
        dn = mm(dqkv_ref[which], wbuf[:, : 3 * head_cols], NT)
        values = x_ref[which].astype(F32)
        sums.append(fold_rows(dn * values * rms_scale(values)))
        target[...] = dn.astype(BF16)
    gain_sum[...] = sums[0] + sums[1]


def back(buffer, ends, offs, order, near, far, qkv, logs, strip, x, o_pieces, p_pieces, heads):
    length = qkv.shape[0]
    half = length // 2
    width = x.shape[1]
    head_cols = heads * DH
    counts = (len(o_pieces), len(p_pieces))
    whole = lambda i, *_: (0, 0)
    whole3 = lambda i, *_: (0, 0, 0)
    spec = pltpu.PrefetchScalarGridSpec(
        num_scalar_prefetch=3,
        grid=(1,),
        in_specs=[
            pl.BlockSpec((half, width), whole),
            pl.BlockSpec((half, width), whole),
            pl.BlockSpec(qkv.shape, whole),
            pl.BlockSpec(logs.shape, whole),
            pl.BlockSpec(strip.shape, whole3),
            pl.BlockSpec((length, width), lambda i, *_: (buffer, 0)),
        ]
        + [pl.BlockSpec(memory_space=ANY)] * sum(counts),
        out_specs=[
            pl.BlockSpec((length, width), whole),
            pl.BlockSpec((length, 3 * head_cols), whole),
            pl.BlockSpec((half, width), whole),
            pl.BlockSpec((half, width), whole),
            pl.BlockSpec((8, width), whole),
            pl.BlockSpec(strip.shape, whole3),
        ],
        scratch_shapes=[
            pltpu.VMEM((width, p_pieces[0].shape[1]), BF16),
            pltpu.VMEM((width, o_pieces[0].shape[1]), BF16),
            pltpu.VMEM((heads, length, DH), BF16),
            pltpu.VMEM((heads, length, DH), BF16),
            pltpu.VMEM((heads, length, DH), BF16),
            pltpu.VMEM((heads, length, DH), BF16),
            pltpu.VMEM((heads, DH, length), BF16),
            pltpu.VMEM((heads, DH, length), BF16),
            pltpu.VMEM((heads, DH, length), F32),
            pltpu.VMEM((heads, DH, length), F32),
            pltpu.VMEM((heads, length, DH), BF16),
            pltpu.SemaphoreType.DMA((2, max(counts))),
        ],
    )
    return pl.pallas_call(
        functools.partial(back_kernel, buffer, ends.shape[1], heads, counts),
        grid_spec=spec,
        out_shape=[
            jax.ShapeDtypeStruct((length, width), BF16),
            jax.ShapeDtypeStruct((length, 3 * head_cols), BF16),
            jax.ShapeDtypeStruct((half, width), BF16),
            jax.ShapeDtypeStruct((half, width), BF16),
            jax.ShapeDtypeStruct((8, width), F32),
            jax.ShapeDtypeStruct(strip.shape, F32),
        ],
        compiler_params=params(),
        cost_estimate=pl.CostEstimate(
            flops=40 * heads * DH * length * length,
            bytes_accessed=16 << 20,
            transcendentals=heads * length * length,
        ),
        name="back",
    )(ends, offs, order, near, far, qkv, logs, strip, x, *o_pieces, *p_pieces)


def scatter_rows(total, offs_ref, evens, odds):
    rows = evens[0].shape[0]
    for at in range(2 * len(evens)):
        begin = pl.multiple_of(offs_ref[at], 8)
        block = total[pl.ds(begin, rows)]
        if at % 2:
            odds[at // 2][...] = block.astype(BF16)
        else:
            evens[at // 2][...] = block


def feed_grad_kernel(count, hidden_cols, offs_ref, *refs):
    buffers = 2
    normed = refs[:buffers]
    gates = refs[buffers : 2 * buffers]
    hiddens = refs[2 * buffers : 3 * buffers]
    cot_ref = refs[3 * buffers]
    outs = refs[3 * buffers + 1 : -1]
    total = refs[-1]
    length = normed[0].shape[0]
    width = normed[0].shape[1]
    part = 256
    for begin in range(0, width, part):
        cols = slice(begin, begin + part)
        total[cols, : 2 * hidden_cols] = mm(normed[0][:, cols], gates[0][...], TN) + mm(
            normed[1][:, cols], gates[1][...], TN
        )
        total[cols, 2 * hidden_cols :] = mm(
            cot_ref[:length, cols], hiddens[0][...], TN
        ) + mm(cot_ref[length:, cols], hiddens[1][...], TN)
    if count > 1:
        scatter_rows(total, offs_ref, outs[: count // 2], outs[count // 2 :])
    else:
        outs[0][...] = total[...]


def attend_grad_kernel(count, heads, offs_ref, *refs):
    buffers = 2
    normed = refs[:buffers]
    dqkv = refs[buffers : 2 * buffers]
    lows = refs[2 * buffers : 3 * buffers]
    atts = refs[3 * buffers : 4 * buffers]
    sums_ref = refs[4 * buffers]
    outs = refs[4 * buffers + 1 : -1]
    total = refs[-1]
    width = normed[0].shape[1]
    head_cols = heads * DH
    qkv_cols = 3 * head_cols
    part = 256
    rows = lax.broadcasted_iota(jnp.int32, (LANES, width), 0)
    first = sums_ref[0] + sums_ref[1]
    second = sums_ref[2] + sums_ref[3]
    gain_rows = jnp.where(
        rows == DH,
        jnp.sum(first, axis=0, keepdims=True),
        jnp.where(rows == DH + 1, jnp.sum(second, axis=0, keepdims=True), 0.0),
    )
    gain_cols = gain_rows.T
    for begin in range(0, width, part):
        cols = slice(begin, begin + part)
        total[cols, :qkv_cols] = mm(normed[0][:, cols], dqkv[0][...], TN) + mm(
            normed[1][:, cols], dqkv[1][...], TN
        )
        total[cols, qkv_cols : qkv_cols + DH] = gain_cols[cols, DH:]
        total[cols, qkv_cols + DH : qkv_cols + DH + head_cols] = mm(
            lows[0][:, cols], atts[0][...], TN
        ) + mm(lows[1][:, cols], atts[1][...], TN)
    if count > 1:
        scatter_rows(total, offs_ref, outs[: count // 2], outs[count // 2 :])
    else:
        outs[0][...] = total[...]


def grad_call(kernel, name, offs, operands, width, cols, count, rows, flops):
    vmem = pl.BlockSpec(memory_space=pltpu.VMEM)
    if count > 1:
        shapes = [jax.ShapeDtypeStruct((rows, cols), F32)] * (count // 2)
        shapes += [jax.ShapeDtypeStruct((rows, cols), BF16)] * (count // 2)
    else:
        shapes = [jax.ShapeDtypeStruct((width, cols), F32)]
    return pl.pallas_call(
        kernel,
        in_specs=[pl.BlockSpec(memory_space=pltpu.SMEM)] + [vmem] * len(operands),
        out_specs=[vmem] * len(shapes),
        out_shape=shapes,
        scratch_shapes=[pltpu.VMEM((width, cols), F32)],
        compiler_params=params(),
        cost_estimate=pl.CostEstimate(flops=2 * flops, bytes_accessed=14 << 20, transcendentals=0),
        name=name,
    )(offs, *operands)


def bucket_kernel(heads, near_ref, far_ref, out_ref):
    lanes = near_ref.shape[2]
    blocks = (lanes // LANES + 1) // 2
    begin = (blocks - 2) * LANES
    end = begin + 3 * LANES
    rows = lax.broadcasted_iota(jnp.int32, (LANES, 3 * LANES), 0)
    ids = bucket_of(
        lax.broadcasted_iota(jnp.int32, (LANES, 3 * LANES), 1) - LANES - rows
    )
    lane = lax.broadcasted_iota(jnp.int32, (1, LANES), 1)
    out = jnp.zeros((1, LANES), F32)
    for h in range(heads):
        strip = near_ref[h] + far_ref[h]
        left = jnp.sum(jnp.sum(strip[:, :begin], axis=0, keepdims=True), axis=1, keepdims=True)
        right = jnp.sum(jnp.sum(strip[:, end:], axis=0, keepdims=True), axis=1, keepdims=True)
        out = out + jnp.where(lane == h * 32 + 15, left, 0.0)
        out = out + jnp.where(lane == h * 32 + 31, right, 0.0)
        middle = strip[:, begin:end]
        for b in range(32):
            if b == 16:
                continue
            part = jnp.sum(jnp.where(ids == b, middle, 0.0), axis=0, keepdims=True)
            part = jnp.sum(part, axis=1, keepdims=True)
            out = out + jnp.where(lane == h * 32 + b, part, 0.0)
    out_ref[...] = jnp.broadcast_to(out, (8, LANES))


def norm_kernel(wide, narrow, lists, gain_at, *refs):
    at = 0
    groups = []
    for count in lists:
        groups.append(refs[at : at + count])
        at += count
    bucket_ref = refs[at]
    outs = refs[at + 1 : at + 1 + len(lists)]
    stat_ref, gain_ref, table_ref, block, inbox, padded, send_sems, recv_sems = refs[
        at + 1 + len(lists) :
    ]
    total = wide * narrow
    w = lax.axis_index("wide")
    n = lax.axis_index("narrow")
    me = w * narrow + n
    barrier = pltpu.get_barrier_semaphore()

    @pl.loop(1, total)
    def _(k):
        peer = (me + k) % total
        pl.semaphore_signal(
            barrier, inc=1, device_id=(peer // narrow, peer % narrow), device_id_type=MESH
        )

    squares = jnp.zeros((8, LANES), F32)
    for which, (group, out) in enumerate(zip(groups, outs)):
        value = group[0][...].astype(F32)
        for more in group[1:]:
            value = value + more[...].astype(F32)
        out[...] = value
        squared = value * value
        if which == 0:
            lane = lax.broadcasted_iota(jnp.int32, value.shape, 1)
            inside = (lane >= gain_at) & (lane < gain_at + DH)
            squared = jnp.where(inside, 0.0, squared)
        squared = jnp.sum(squared, axis=1, keepdims=True)
        squares = squares + jnp.sum(squared, axis=0, keepdims=True)
    rows = outs[0].shape[0]
    low = gain_at // LANES * LANES
    padded[...] = jnp.zeros_like(padded)
    padded[0:rows] = outs[0][:, low : low + LANES]
    turned = padded[...].T
    row = lax.broadcasted_iota(jnp.int32, (8, LANES), 0)
    here = gain_at - low
    mine = jnp.where(row == 0, squares, 0.0)
    mine = jnp.where(row == 1, turned[here : here + 1], mine)
    mine = jnp.where(row == 2, turned[here + 1 : here + 2], mine)
    mine = jnp.where(row == 3, bucket_ref[...], mine)
    block[...] = mine
    inbox[me] = mine
    pl.semaphore_wait(barrier, total - 1)

    @pl.loop(1, total)
    def _(k):
        peer = (me + k) % total
        pltpu.make_async_remote_copy(
            src_ref=block,
            dst_ref=inbox.at[me],
            send_sem=send_sems.at[k],
            recv_sem=recv_sems.at[total - k],
            device_id=(peer // narrow, peer % narrow),
            device_id_type=MESH,
        ).start()

    @pl.loop(1, total)
    def _(k):
        peer = (me + k) % total
        copy = pltpu.make_async_remote_copy(
            src_ref=block,
            dst_ref=inbox.at[peer],
            send_sem=send_sems.at[k],
            recv_sem=recv_sems.at[k],
            device_id=(peer // narrow, peer % narrow),
            device_id_type=MESH,
        )
        copy.wait_send()
        copy.wait_recv()

    columns = [jnp.zeros((8, LANES), F32) for _ in range(narrow)]
    gain_square = jnp.zeros((8, LANES), F32)
    square_total = jnp.zeros((8, LANES), F32)
    for a in range(wide):
        gains = jnp.zeros((8, LANES), F32)
        for b in range(narrow):
            got = inbox[a * narrow + b]
            gains = gains + got
            columns[b] = columns[b] + got
        square_total = square_total + gains
        gain_square = gain_square + gains * gains
    own = inbox[w * narrow]
    for b in range(1, narrow):
        own = own + inbox[w * narrow + b]
    gain_ref[...] = own
    pick = (row == 1) | (row == 2)
    gain_square = jnp.where(pick, gain_square, 0.0)
    norm_square = square_total[0:1, 0:1] + jnp.sum(
        jnp.sum(gain_square, axis=0, keepdims=True), axis=1, keepdims=True
    )
    heads = LANES // 32 - 1
    lane = lax.broadcasted_iota(jnp.int32, (32, LANES), 1)
    depth = lax.broadcasted_iota(jnp.int32, (32, LANES), 0)
    table = jnp.zeros((32, LANES), F32)
    for b in range(narrow):
        line = columns[b][3:4]
        norm_square = norm_square + jnp.sum(line * line, axis=1, keepdims=True)
        for h in range(heads):
            column = jnp.sum(
                jnp.where(lane == depth + 32 * h, line, 0.0), axis=1, keepdims=True
            )
            table = jnp.where(lane == b * heads + h, column, table)
    table_ref[...] = table
    global_norm = jnp.sqrt(norm_square)
    factor = jnp.minimum(1.0, clip_limit / (global_norm + 1e-06))
    stat_ref[...] = jnp.where(row == 0, global_norm, factor)


def norm_call(wide, narrow, groups, bucket, gain_at):
    vmem = pl.BlockSpec(memory_space=pltpu.VMEM)
    lists = tuple(len(group) for group in groups)
    total = wide * narrow
    operands = [piece for group in groups for piece in group] + [bucket]
    return pl.pallas_call(
        functools.partial(norm_kernel, wide, narrow, lists, gain_at),
        in_specs=[vmem] * len(operands),
        out_specs=[vmem] * (len(lists) + 3),
        out_shape=[jax.ShapeDtypeStruct(group[0].shape, F32) for group in groups]
        + [
            jax.ShapeDtypeStruct((8, LANES), F32),
            jax.ShapeDtypeStruct((8, LANES), F32),
            jax.ShapeDtypeStruct((32, LANES), F32),
        ],
        scratch_shapes=[
            pltpu.VMEM((8, LANES), F32),
            pltpu.VMEM((total, 8, LANES), F32),
            pltpu.VMEM((LANES, LANES), F32),
            pltpu.SemaphoreType.DMA((total,)),
            pltpu.SemaphoreType.DMA((total,)),
        ],
        compiler_params=params(collective_id=0, has_side_effects=True),
        cost_estimate=pl.CostEstimate(flops=1 << 20, bytes_accessed=4 << 20, transcendentals=0),
        name="norm",
    )(*operands)


def adam_kernel(heads, hidden_cols, att_ref, feed_ref, gain_ref, table_ref, stat_ref, *refs):
    weights, firsts, seconds = refs[:6], refs[6:12], refs[12:18]
    outs = refs[18:36]
    o_pad, s_pad = refs[36:]
    factor = stat_ref[1:2, 0:1]
    head_cols = heads * DH
    rows = att_ref.shape[0]
    gain_at = 3 * head_cols

    def update(which, index, gradient):
        results = adam_update(
            weights[which][index],
            firsts[which][index],
            seconds[which][index],
            factor * gradient,
            step_rates[which],
            decay_rates[which],
        )
        for at in range(3):
            outs[6 * at + which][index] = results[at]

    for i in range(3):
        update(0, i, att_ref[:, i * head_cols : (i + 1) * head_cols])
    for i in range(2):
        update(2, i, feed_ref[:, i * hidden_cols : (i + 1) * hidden_cols])
    o_pad[...] = jnp.zeros_like(o_pad)
    s_pad[...] = jnp.zeros_like(s_pad)
    o_pad[0:rows] = att_ref[:, gain_at + DH :]
    s_pad[0:rows] = feed_ref[:, 2 * hidden_cols :]
    update(1, slice(None), o_pad[...].T[:head_cols, :rows])
    update(3, slice(None), s_pad[...].T[:, :rows])
    columns = weights[4].shape[1]
    update(4, slice(None), table_ref[:, :columns])
    update(5, slice(None), gain_ref[1:3, :rows])


def adam_call(att, feed_grad, gain, table, stat, params_in, firsts, seconds, heads, hidden_cols):
    vmem = pl.BlockSpec(memory_space=pltpu.VMEM)
    operands = [att, feed_grad, gain, table, stat, *params_in, *firsts, *seconds]
    pad_cols = att.shape[1] - (3 * heads * DH + DH)
    return pl.pallas_call(
        functools.partial(adam_kernel, heads, hidden_cols),
        in_specs=[vmem] * len(operands),
        out_specs=[vmem] * 18,
        out_shape=[jax.ShapeDtypeStruct(a.shape, F32) for a in params_in] * 3,
        scratch_shapes=[
            pltpu.VMEM((LANES, pad_cols), F32),
            pltpu.VMEM((LANES, hidden_cols), F32),
        ],
        compiler_params=params(),
        cost_estimate=pl.CostEstimate(flops=4 << 20, bytes_accessed=8 << 20, transcendentals=0),
        name="adam",
    )(*operands)


def place_kernel(half, offs_ref, *refs):
    pieces = refs[:-2]
    out_ref, sems = refs[-2:]
    copies = []
    for at, piece in enumerate(pieces):
        begin = pl.multiple_of(offs_ref[at], LANES)
        copies.append(
            pltpu.make_async_copy(piece, out_ref.at[pl.ds(begin, half)], sems.at[at])
        )
    for copy in copies:
        copy.start()
    for copy in copies:
        copy.wait()


def place(pieces, offs, rows):
    half, width = pieces[0].shape
    hbm = pl.BlockSpec(memory_space=ANY)
    return pl.pallas_call(
        functools.partial(place_kernel, half),
        in_specs=[pl.BlockSpec(memory_space=pltpu.SMEM)] + [hbm] * len(pieces),
        out_specs=hbm,
        out_shape=jax.ShapeDtypeStruct((rows, width), pieces[0].dtype),
        scratch_shapes=[pltpu.SemaphoreType.DMA((len(pieces),))],
        compiler_params=params(),
        cost_estimate=pl.CostEstimate(
            flops=0, bytes_accessed=4 * rows * width, transcendentals=0
        ),
        name="place",
    )(offs, *pieces)


def body(wide, narrow, *arguments):
    (
        block_input,
        cotangent,
        lengths,
        project_weight,
        output_weight,
        expand_weight,
        shrink_weight,
        bucket_bias,
        norm_gains,
    ) = arguments[:9]
    firsts = arguments[9:15]
    seconds = arguments[15:21]
    tokens, width = block_input.shape
    buffers = lengths.shape[0]
    length = tokens // buffers
    rows = norm_gains.shape[1]
    head_cols = project_weight.shape[2]
    heads = head_cols // DH
    hidden_cols = expand_weight.shape[2]
    w = lax.axis_index("wide")
    n = lax.axis_index("narrow")
    core = n % 2
    direct = wide == 8 and rows % 16 == 0

    def swap(value, wide_mask, narrow_mask):
        pairs = [
            (a * narrow + b, (a ^ wide_mask) * narrow + (b ^ narrow_mask))
            for a in range(wide)
            for b in range(narrow)
        ]
        return lax.ppermute(value, ("wide", "narrow"), pairs)

    def gather(piece):
        if not direct:
            return [lax.all_gather(piece, "wide", axis=0, tiled=True)]
        found = {0: piece}
        for mask in (2, 4, 6):
            found[mask] = swap(piece, mask, 0)
        for mask in (0, 2, 4, 6):
            found[mask + 1] = swap(found[mask], 1, 0)
        return [found[mask] for mask in range(8)]

    def reduce_wide(outs):
        if not direct:
            return [lax.psum_scatter(outs[0], "wide", scatter_dimension=0, tiled=True)]
        evens, odds = outs[:4], outs[4:]
        got = []
        for e in (1, 2, 3, 0):
            came = swap(odds[e], 1, 0)
            if e:
                mixed = (evens[e] + came.astype(F32)).astype(BF16)
                got.append(swap(mixed, 2 * e, 0))
            else:
                kept = [evens[0], came]
        return kept + got

    if direct:
        offs = (jnp.arange(8, dtype=jnp.int32) ^ w) * rows
    else:
        offs = jnp.zeros((1,), jnp.int32)
    order = jnp.stack([1 - core, core, n // 2])

    p_piece = jnp.concatenate(
        [
            project_weight[0],
            project_weight[1],
            project_weight[2],
            norm_gains.T,
            jnp.zeros((rows, DH - 2), F32),
        ],
        axis=1,
    ).astype(BF16)
    p_pieces = gather(p_piece)
    o_piece = output_weight.astype(BF16).T
    o_pair = jnp.concatenate([o_piece, swap(o_piece, 0, 2)], axis=1)
    oa_pieces = gather(o_pair)
    ob_pieces = [swap(piece, 0, 1) for piece in oa_pieces]
    e_pieces = gather(
        jnp.concatenate([expand_weight[0], expand_weight[1]], axis=1).astype(BF16)
    )
    s_pieces = gather(shrink_weight.astype(BF16).T)

    ends = jnp.cumsum(lengths, axis=1)
    table = lax.dynamic_slice_in_dim(bucket_bias, n * heads, heads, 1).T
    blocks = length // LANES
    near_r = (
        jnp.arange(3 * LANES, dtype=jnp.int32)[None, :]
        - LANES
        - jnp.arange(LANES, dtype=jnp.int32)[:, None]
    )
    near_ids = bucket_of(near_r)
    near = sum(
        jnp.where(near_ids == b, table[:, b][:, None, None], 0.0) for b in range(32) if b != 16
    )
    far_shape = (heads, LANES, (blocks - 2) * LANES)
    strip = jnp.concatenate(
        [
            jnp.broadcast_to(table[:, 15][:, None, None], far_shape),
            near,
            jnp.broadcast_to(table[:, 31][:, None, None], far_shape),
        ],
        axis=2,
    )

    normed_one, qkv, atts, logs, fours = [], [], [], [], []
    for b in range(buffers):
        normed, rows_b, att, log, gains = attend(
            b, ends, offs, block_input, strip, p_pieces, length, heads
        )
        normed_one.append(normed)
        qkv.append(rows_b)
        atts.append(att)
        logs.append(log)
        across = swap(att, 0, 2)
        fours.append((att, across, swap(att, 0, 1), swap(across, 0, 1)))

    def core_sum(kept, sent):
        return (kept.astype(F32) + swap(sent, 0, 1).astype(F32)).astype(BF16)

    normed_two, hiddens, gates, middles, ff_sums, dn_sums, sums_two = [], [], [], [], [], [], []
    for b in range(buffers):
        normed, hidden, gate, ff_send, ff_keep, dn_send, dn_keep, middle, sums = feed(
            b,
            order,
            offs,
            fours[b],
            block_input,
            cotangent,
            gains,
            (oa_pieces, ob_pieces, e_pieces, s_pieces),
            length,
            hidden_cols,
        )
        normed_two.append(normed)
        hiddens.append(hidden)
        gates.append(gate)
        middles.append(middle)
        sums_two.append(sums)
        dn_sums.append(core_sum(dn_keep, dn_send))
        ff_sums.append(core_sum(ff_keep, ff_send))

    d_middles, lows = [], []
    for b in range(buffers):
        d_middle, low = half_call(
            middle_kernel,
            "middle",
            b,
            order,
            [dn_sums[b], swap(dn_sums[b], 0, 2), middles[b], cotangent],
            (3,),
            (F32, BF16),
            gains,
        )
        d_middles.append(d_middle)
        lows.append((low, swap(low, 0, 1)))

    count = 8 if direct else 1
    feed_outs = grad_call(
        functools.partial(feed_grad_kernel, count, hidden_cols),
        "feed_grad",
        offs,
        [*normed_two, *gates, *hiddens, cotangent],
        width,
        3 * hidden_cols,
        count,
        rows,
        2 * tokens * width * 3 * hidden_cols,
    )
    feed_group = reduce_wide(feed_outs)

    low_full, dqkv, dn_one, sums_one, strips = [], [], [], [], []
    for b in range(buffers):
        low, grads, dn_send, dn_keep, sums, dstrip = back(
            b,
            ends,
            offs,
            order,
            lows[b][0],
            lows[b][1],
            qkv[b],
            logs[b],
            strip,
            block_input,
            oa_pieces,
            p_pieces,
            heads,
        )
        low_full.append(low)
        dqkv.append(grads)
        sums_one.append(sums)
        strips.append(dstrip)
        dn_one.append(core_sum(dn_keep, dn_send))

    gain_at = 3 * head_cols
    att_outs = grad_call(
        functools.partial(attend_grad_kernel, count, heads),
        "attend_grad",
        offs,
        [*normed_one, *dqkv, *low_full, *atts, jnp.stack(sums_one + sums_two)],
        width,
        gain_at + DH + head_cols,
        count,
        rows,
        2 * tokens * width * 4 * head_cols,
    )
    att_group = reduce_wide(att_outs)
    vmem = pl.BlockSpec(memory_space=pltpu.VMEM)
    bucket = pl.pallas_call(
        functools.partial(bucket_kernel, heads),
        in_specs=[vmem, vmem],
        out_specs=vmem,
        out_shape=jax.ShapeDtypeStruct((8, LANES), F32),
        compiler_params=params(),
        cost_estimate=pl.CostEstimate(flops=8 << 20, bytes_accessed=4 << 20, transcendentals=0),
        name="bucket",
    )(*strips)

    half_offs = jnp.stack(
        [
            b * length + which * (length // 2)
            for b in range(buffers)
            for which in (core, 1 - core)
        ]
    )
    out_halves, in_halves = [], []
    for b in range(buffers):
        (half,) = half_call(
            output_kernel,
            "output",
            b,
            order,
            [ff_sums[b], swap(ff_sums[b], 0, 2), middles[b]],
            (),
            (BF16,),
        )
        out_halves += [half, swap(half, 0, 1)]
        (half,) = half_call(
            input_kernel,
            "input",
            b,
            order,
            [dn_one[b], swap(dn_one[b], 0, 2), block_input, d_middles[b]],
            (2,),
            (BF16,),
            gains,
        )
        in_halves += [half, swap(half, 0, 1)]
    block_output = place(out_halves, half_offs, tokens)
    input_gradient = place(in_halves, half_offs, tokens)

    att_grad, feed_grad, stat, gain, table_sum = norm_call(
        wide, narrow, [att_group, feed_group], bucket, gain_at
    )
    results = adam_call(
        att_grad,
        feed_grad,
        gain,
        table_sum,
        stat,
        arguments[3:9],
        firsts,
        seconds,
        heads,
        hidden_cols,
    )
    return (block_output, input_gradient, stat[0, 0], *results)


def solution(mesh):
    wide, narrow = mesh.shape["wide"], mesh.shape["narrow"]
    state = (
        P(None, "wide", "narrow"),
        P("narrow", "wide"),
        P(None, "wide", "narrow"),
        P("narrow", "wide"),
        P(),
        P(None, "wide"),
    )
    rows = P("wide", None)
    return jax.shard_map(
        functools.partial(body, wide, narrow),
        mesh=mesh,
        in_specs=(rows, rows, rows, *state, *state, *state),
        out_specs=(rows, rows, P(), *state, *state, *state),
        check_vma=False,
    )
```

```python
import functools

import jax
import jax.numpy as jnp
from jax import lax
from jax.experimental import pallas as pl
from jax.experimental.pallas import tpu as pltpu
from jax.sharding import PartitionSpec as P

DH = 64
STEP = 10
LANES = 128
MESH = pl.DeviceIdType.MESH
F32 = jnp.float32
BF16 = jnp.bfloat16
ANY = pl.ANY

bucket_edges = (12, 16, 23, 32, 46, 64, 91)
norm_eps = 1e-06
clip_limit = 1.0
beta_one = 0.9
beta_two = 0.999
adam_eps = 1e-08
step_rates = (0.06, 0.3, 0.07, 0.06, 1.0, 0.3)
decay_rates = (0.01, 0.01, 0.01, 0.01, 0.0, 0.0)
masked_score = -1000000000.0
VMEM_LIMIT = 58 << 20

NN = (((1,), (0,)), ((), ()))
NT = (((1,), (1,)), ((), ()))
TN = (((0,), (0,)), ((), ()))


def mm(left, right, dims=NN):
    return lax.dot_general(left, right, dims, preferred_element_type=F32)


def bucket_of(offsets):
    distance = jnp.abs(offsets)
    far_bucket = 8 + sum(((distance >= threshold).astype(jnp.int32) for threshold in bucket_edges))
    return jnp.where(distance < 8, distance, far_bucket) + 16 * (offsets > 0).astype(jnp.int32)


def rms_scale(values):
    return lax.rsqrt(jnp.mean(values * values, axis=-1, keepdims=True) + norm_eps)


def norm_back(values, scale_vec, gain_vec, upstream):
    weighted = upstream * gain_vec
    inner_mean = jnp.mean(weighted * values, axis=-1, keepdims=True)
    return scale_vec * weighted - values * (scale_vec * scale_vec * scale_vec) * inner_mean


def adam_update(weight, moment_one, moment_two, gradient, step_rate, decay_rate):
    new_first = beta_one * moment_one + (1.0 - beta_one) * gradient
    new_second = beta_two * moment_two + (1.0 - beta_two) * gradient * gradient
    first_hat = new_first / (1.0 - beta_one**STEP)
    second_hat = new_second / (1.0 - beta_two**STEP)
    new_weight = weight - step_rate * (
        first_hat / (jnp.sqrt(second_hat) + adam_eps) + decay_rate * weight
    )
    return (new_weight, new_first, new_second)


def fold_rows(values):
    rows, cols = values.shape
    return jnp.sum(values.reshape(rows // 8, 8, cols), axis=0)


def start_rows(pieces, target, offs_ref, sems):
    copies = []
    for at, piece in enumerate(pieces):
        rows = piece.shape[0]
        begin = pl.multiple_of(offs_ref[at], 16)
        copies.append(
            pltpu.make_async_copy(piece, target.at[pl.ds(begin, rows)], sems.at[at])
        )
    for copy in copies:
        copy.start()
    return copies


def segments(index, ends_ref, buffer, slots):
    total = jnp.zeros(index.shape, jnp.int32)
    for slot in range(slots):
        total = total + (index >= ends_ref[buffer, slot]).astype(jnp.int32)
    return total


def params(**more):
    return pltpu.CompilerParams(vmem_limit_bytes=VMEM_LIMIT, **more)


def attend_kernel(
    buffer, slots, heads, count, ends_ref, offs_ref, x_ref, strip_ref, *refs
):
    pieces = refs[:count]
    normed_ref, qkv_ref, att_ref, log_ref, gains_ref, wbuf, qs, ks, vs, os, sems = refs[count:]
    length, width = x_ref.shape
    head_cols = heads * DH
    copies = start_rows(pieces, wbuf, offs_ref, sems)
    for copy in copies:
        copy.wait()
    gain_cols = wbuf[:, 4 * LANES :].astype(F32).T
    first = 3 * head_cols - 4 * LANES
    gains = gain_cols[first : first + 8]
    gains_ref[...] = gains
    gain_one = gains[0:1]
    step = 256

    @pl.loop(0, length // step)
    def _(block):
        rows = pl.ds(pl.multiple_of(block * step, step), step)
        values = x_ref[rows].astype(F32)
        normed = (values * rms_scale(values) * gain_one).astype(BF16)
        normed_ref[rows] = normed
        qkv = mm(normed, wbuf[...]).astype(BF16)
        qkv_ref[rows] = qkv[:, : 3 * head_cols]
        for h in range(heads):
            qs[h, rows] = qkv[:, h * DH : (h + 1) * DH]
            ks[h, rows] = qkv[:, head_cols + h * DH : head_cols + (h + 1) * DH]
            vs[h, rows] = qkv[:, 2 * head_cols + h * DH : 2 * head_cols + (h + 1) * DH]

    blocks = length // LANES
    seg_keys = segments(
        lax.broadcasted_iota(jnp.int32, (1, length), 1), ends_ref, buffer, slots
    )

    @pl.loop(0, blocks)
    def _(block):
        begin = pl.multiple_of(block * LANES, LANES)
        rows = pl.ds(begin, LANES)
        window = pl.ds(pl.multiple_of((blocks - 1 - block) * LANES, LANES), length)
        seg_rows = segments(
            lax.broadcasted_iota(jnp.int32, (LANES, 1), 0) + begin, ends_ref, buffer, slots
        )
        same = seg_rows == seg_keys
        lane = lax.broadcasted_iota(jnp.int32, (LANES, LANES), 1)
        logs = jnp.zeros((LANES, LANES), F32)
        for h in range(heads):
            scores = mm(qs[h, rows], ks[h], NT) + strip_ref[h, :, window]
            scores = jnp.where(same, scores, masked_score)
            row_max = jnp.max(scores, axis=1, keepdims=True)
            raised = jnp.exp(scores - row_max)
            total = jnp.sum(raised, axis=1, keepdims=True)
            probs = (raised * (1.0 / total)).astype(BF16)
            os[h, rows] = mm(probs, vs[h]).astype(BF16)
            logs = jnp.where(lane == h, row_max + jnp.log(total), logs)
        log_ref[rows] = logs

    att_ref[...] = jnp.concatenate([os[h] for h in range(heads)], axis=1)


def attend(buffer, ends, offs, x, strip, pieces, length, heads):
    width = x.shape[1]
    count = len(pieces)
    cols = pieces[0].shape[1]
    head_cols = heads * DH
    whole = lambda i, *_: (0, 0)
    spec = pltpu.PrefetchScalarGridSpec(
        num_scalar_prefetch=2,
        grid=(1,),
        in_specs=[
            pl.BlockSpec((length, width), lambda i, *_: (buffer, 0)),
            pl.BlockSpec(strip.shape, lambda i, *_: (0, 0, 0)),
        ]
        + [pl.BlockSpec(memory_space=ANY)] * count,
        out_specs=[
            pl.BlockSpec((length, width), whole),
            pl.BlockSpec((length, 3 * head_cols), whole),
            pl.BlockSpec((length, head_cols), whole),
            pl.BlockSpec((length, LANES), whole),
            pl.BlockSpec((8, width), whole),
        ],
        scratch_shapes=[
            pltpu.VMEM((width, cols), BF16),
            pltpu.VMEM((heads, length, DH), BF16),
            pltpu.VMEM((heads, length, DH), BF16),
            pltpu.VMEM((heads, length, DH), BF16),
            pltpu.VMEM((heads, length, DH), BF16),
            pltpu.SemaphoreType.DMA((count,)),
        ],
    )
    flops = 2 * length * (width * cols + 2 * heads * DH * length)
    return pl.pallas_call(
        functools.partial(attend_kernel, buffer, ends.shape[1], heads, count),
        grid_spec=spec,
        out_shape=[
            jax.ShapeDtypeStruct((length, width), BF16),
            jax.ShapeDtypeStruct((length, 3 * head_cols), BF16),
            jax.ShapeDtypeStruct((length, head_cols), BF16),
            jax.ShapeDtypeStruct((length, LANES), F32),
            jax.ShapeDtypeStruct((8, width), F32),
        ],
        compiler_params=params(),
        cost_estimate=pl.CostEstimate(
            flops=4 * flops, bytes_accessed=8 << 20, transcendentals=heads * length * length
        ),
        name="attend",
    )(ends, offs, x, strip, *pieces)


def feed_kernel(hidden_cols, counts, order_ref, offs_ref, *refs):
    own, across, beside, diagonal, x_ref, cot_ref, gains_ref = refs[:7]
    at = 7
    groups = []
    for count in counts:
        groups.append(refs[at : at + count])
        at += count
    (
        normed_ref,
        hidden_ref,
        gate_ref,
        ff_send,
        ff_keep,
        dn_send,
        dn_keep,
        middle_keep,
        gain_sum,
        ebuf,
        sbuf,
        oabuf,
        obbuf,
        sems,
    ) = refs[at:]
    step = pl.program_id(0)
    bufs = (oabuf, obbuf, ebuf, sbuf)

    @pl.when(step == 0)
    def _():
        copies = []
        for which, (group, target) in enumerate(zip(groups, bufs)):
            copies += start_rows(group, target, offs_ref, sems.at[which])
        for copy in copies:
            copy.wait()

    cols = own.shape[1]
    upper = order_ref[2] == 0
    pairs = []
    for near, far, weights in ((own, across, oabuf), (beside, diagonal, obbuf)):
        near_sum = mm(near[...], weights[:, :cols], NT)
        far_sum = mm(far[...], weights[:, cols:], NT)
        pairs.append(
            jnp.where(upper, near_sum, far_sum) + jnp.where(upper, far_sum, near_sum)
        )
    swap = order_ref[0] == 0
    attention = jnp.where(swap, pairs[0], pairs[1]) + jnp.where(swap, pairs[1], pairs[0])
    middle = x_ref[...].astype(F32) + attention
    scale_two = rms_scale(middle)
    gain_two = gains_ref[1:2]
    normed = (middle * scale_two * gain_two).astype(BF16)
    normed_ref[...] = normed
    cot = cot_ref[...]
    part = 256
    k0 = 0.7978845608028654
    k1 = 0.044715
    for begin in range(0, hidden_cols, part):
        gate = mm(normed, ebuf[:, begin : begin + part])
        up = mm(normed, ebuf[:, hidden_cols + begin : hidden_cols + begin + part])
        square = gate * gate
        tanh = jnp.tanh(k0 * (gate + k1 * (square * gate)))
        half = 0.5 * (1.0 + tanh)
        active = gate * half
        slope = half + (0.5 * gate) * (1.0 - tanh * tanh) * (k0 + (3.0 * k0 * k1) * square)
        d_hidden = mm(cot, sbuf[:, begin : begin + part])
        hidden_ref[:, begin : begin + part] = (active * up).astype(BF16)
        gate_ref[:, begin : begin + part] = (d_hidden * up * slope).astype(BF16)
        gate_ref[:, hidden_cols + begin : hidden_cols + begin + part] = (
            d_hidden * active
        ).astype(BF16)
    ff = mm(hidden_ref[...], sbuf[...], NT).astype(BF16)
    dn = mm(gate_ref[...], ebuf[...], NT)
    sums = fold_rows(dn * middle * scale_two)
    dn = dn.astype(BF16)

    @pl.when(step == 0)
    def _():
        ff_send[...] = ff
        dn_send[...] = dn
        gain_sum[...] = sums

    @pl.when(step == 1)
    def _():
        ff_keep[...] = ff
        dn_keep[...] = dn
        middle_keep[...] = middle
        gain_sum[...] = gain_sum[...] + sums


def feed(buffer, order, offs, parts, x, cot, gains, groups, length, hidden_cols):
    width = x.shape[1]
    half = length // 2
    cols = parts[0].shape[1]
    counts = [len(group) for group in groups]
    natural = lambda i, order, *_: (order[i], 0)
    rows = lambda i, order, *_: (2 * buffer + order[i], 0)
    whole = lambda i, *_: (0, 0)
    spec = pltpu.PrefetchScalarGridSpec(
        num_scalar_prefetch=2,
        grid=(2,),
        in_specs=[pl.BlockSpec((half, cols), natural)] * 4
        + [pl.BlockSpec((half, width), rows)] * 2
        + [pl.BlockSpec((8, width), whole)]
        + [pl.BlockSpec(memory_space=ANY)] * sum(counts),
        out_specs=[
            pl.BlockSpec((half, width), natural),
            pl.BlockSpec((half, hidden_cols), natural),
            pl.BlockSpec((half, 2 * hidden_cols), natural),
        ]
        + [pl.BlockSpec((half, width), whole)] * 5
        + [pl.BlockSpec((8, width), whole)],
        scratch_shapes=[
            pltpu.VMEM((width, 2 * hidden_cols), BF16),
            pltpu.VMEM((width, hidden_cols), BF16),
            pltpu.VMEM((width, 2 * cols), BF16),
            pltpu.VMEM((width, 2 * cols), BF16),
            pltpu.SemaphoreType.DMA((4, max(counts))),
        ],
    )
    flops = 2 * length * width * (4 * cols + 7 * hidden_cols)
    return pl.pallas_call(
        functools.partial(feed_kernel, hidden_cols, counts),
        grid_spec=spec,
        out_shape=[
            jax.ShapeDtypeStruct((length, width), BF16),
            jax.ShapeDtypeStruct((length, hidden_cols), BF16),
            jax.ShapeDtypeStruct((length, 2 * hidden_cols), BF16),
            jax.ShapeDtypeStruct((half, width), BF16),
            jax.ShapeDtypeStruct((half, width), BF16),
            jax.ShapeDtypeStruct((half, width), BF16),
            jax.ShapeDtypeStruct((half, width), BF16),
            jax.ShapeDtypeStruct((half, width), F32),
            jax.ShapeDtypeStruct((8, width), F32),
        ],
        compiler_params=params(),
        cost_estimate=pl.CostEstimate(
            flops=flops, bytes_accessed=12 << 20, transcendentals=length * hidden_cols
        ),
        name="feed",
    )(order, offs, *parts, x, cot, gains, *[piece for group in groups for piece in group])


def middle_kernel(order_ref, near, far, middle_ref, cot_ref, gains_ref, d_ref, low_ref):
    upstream = near[...].astype(F32) + far[...].astype(F32)
    middle = middle_ref[...]
    d_middle = cot_ref[...].astype(F32) + norm_back(
        middle, rms_scale(middle), gains_ref[1:2], upstream
    )
    d_ref[...] = d_middle
    low_ref[...] = d_middle.astype(BF16)


def input_kernel(order_ref, near, far, x_ref, d_ref, gains_ref, out_ref):
    upstream = near[...].astype(F32) + far[...].astype(F32)
    values = x_ref[...].astype(F32)
    out_ref[...] = (
        d_ref[...] + norm_back(values, rms_scale(values), gains_ref[0:1], upstream)
    ).astype(BF16)


def output_kernel(order_ref, near, far, middle_ref, out_ref):
    out_ref[...] = (
        middle_ref[...] + (near[...].astype(F32) + far[...].astype(F32)).astype(BF16).astype(F32)
    ).astype(BF16)


def half_call(kernel, name, buffer, order, arrays, placed, outs, gains=None):
    half, width = arrays[0].shape
    steps = 3
    block = half // steps
    mine = lambda i, *_: (i, 0)
    rows = lambda i, order, *_: ((2 * buffer + order[1]) * steps + i, 0)
    in_specs = [
        pl.BlockSpec((block, width), rows if at in placed else mine)
        for at in range(len(arrays))
    ]
    operands = list(arrays)
    if gains is not None:
        in_specs.append(pl.BlockSpec((8, width), lambda i, *_: (0, 0)))
        operands.append(gains)
    return pl.pallas_call(
        kernel,
        grid_spec=pltpu.PrefetchScalarGridSpec(
            num_scalar_prefetch=1,
            grid=(steps,),
            in_specs=in_specs,
            out_specs=[pl.BlockSpec((block, width), mine) for _ in outs],
        ),
        out_shape=[jax.ShapeDtypeStruct((half, width), kind) for kind in outs],
        compiler_params=params(),
        cost_estimate=pl.CostEstimate(
            flops=20 * half * width, bytes_accessed=12 * half * width, transcendentals=0
        ),
        name=name,
    )(order, *operands)


def back_kernel(buffer, slots, heads, counts, ends_ref, offs_ref, order_ref, *refs):
    near, far, qkv_ref, log_ref, strip_ref, x_ref = refs[:6]
    at = 6
    o_pieces = refs[at : at + counts[0]]
    at += counts[0]
    p_pieces = refs[at : at + counts[1]]
    at += counts[1]
    (
        low_ref,
        dqkv_ref,
        dn_send,
        dn_keep,
        gain_sum,
        dstrip,
        wbuf,
        obuf,
        qs,
        ks,
        vs,
        gs,
        qt,
        gt,
        dkt,
        dvt,
        dq,
        sems,
    ) = refs[at:]
    length = qkv_ref.shape[0]
    half = length // 2
    head_cols = heads * DH
    o_copies = start_rows(o_pieces, obuf, offs_ref, sems.at[0])
    p_copies = start_rows(p_pieces, wbuf, offs_ref, sems.at[1])
    mine = pl.ds(pl.multiple_of(order_ref[1] * half, LANES), half)
    other = pl.ds(pl.multiple_of(order_ref[0] * half, LANES), half)
    low_ref[mine] = near[...]
    low_ref[other] = far[...]
    for h in range(heads):
        qs[h] = qkv_ref[:, h * DH : (h + 1) * DH]
        ks[h] = qkv_ref[:, head_cols + h * DH : head_cols + (h + 1) * DH]
        vs[h] = qkv_ref[:, 2 * head_cols + h * DH : 2 * head_cols + (h + 1) * DH]
        qt[h] = qs[h].T
    dstrip[...] = jnp.zeros_like(dstrip)
    dkt[...] = jnp.zeros_like(dkt)
    dvt[...] = jnp.zeros_like(dvt)
    for copy in o_copies + p_copies:
        copy.wait()
    grads = mm(low_ref[...], obuf[:, :head_cols]).astype(BF16)
    for h in range(heads):
        gs[h] = grads[:, h * DH : (h + 1) * DH]
        gt[h] = gs[h].T
    blocks = length // LANES
    seg_keys = segments(
        lax.broadcasted_iota(jnp.int32, (1, length), 1), ends_ref, buffer, slots
    )

    @pl.loop(0, blocks)
    def _(block):
        begin = pl.multiple_of(block * LANES, LANES)
        rows = pl.ds(begin, LANES)
        window = pl.ds(pl.multiple_of((blocks - 1 - block) * LANES, LANES), length)
        seg_rows = segments(
            lax.broadcasted_iota(jnp.int32, (LANES, 1), 0) + begin, ends_ref, buffer, slots
        )
        same = seg_rows == seg_keys
        logs = log_ref[rows]
        for h in range(heads):
            scores = mm(qs[h, rows], ks[h], NT) + strip_ref[h, :, window]
            scores = jnp.where(same, scores, masked_score)
            probs = jnp.exp(scores - logs[:, h : h + 1])
            d_probs = mm(gs[h, rows], vs[h], NT)
            inner = jnp.sum(probs * d_probs, axis=1, keepdims=True)
            d_scores = (probs * (d_probs - inner)).astype(BF16)
            dstrip[h, :, window] = dstrip[h, :, window] + d_scores.astype(F32)
            dq[h, rows] = mm(d_scores, ks[h]).astype(BF16)
            dkt[h] = dkt[h] + mm(qt[h, :, rows], d_scores)
            dvt[h] = dvt[h] + mm(gt[h, :, rows], probs.astype(BF16))

    outs = [dq[h] for h in range(heads)]
    outs += [dkt[h].T.astype(BF16) for h in range(heads)]
    outs += [dvt[h].T.astype(BF16) for h in range(heads)]
    dqkv_ref[...] = jnp.concatenate(outs, axis=1)
    sums = []
    for target, which in ((dn_send, other), (dn_keep, mine)):
        dn = mm(dqkv_ref[which], wbuf[:, : 3 * head_cols], NT)
        values = x_ref[which].astype(F32)
        sums.append(fold_rows(dn * values * rms_scale(values)))
        target[...] = dn.astype(BF16)
    gain_sum[...] = sums[0] + sums[1]


def back(buffer, ends, offs, order, near, far, qkv, logs, strip, x, o_pieces, p_pieces, heads):
    length = qkv.shape[0]
    half = length // 2
    width = x.shape[1]
    head_cols = heads * DH
    counts = (len(o_pieces), len(p_pieces))
    whole = lambda i, *_: (0, 0)
    whole3 = lambda i, *_: (0, 0, 0)
    spec = pltpu.PrefetchScalarGridSpec(
        num_scalar_prefetch=3,
        grid=(1,),
        in_specs=[
            pl.BlockSpec((half, width), whole),
            pl.BlockSpec((half, width), whole),
            pl.BlockSpec(qkv.shape, whole),
            pl.BlockSpec(logs.shape, whole),
            pl.BlockSpec(strip.shape, whole3),
            pl.BlockSpec((length, width), lambda i, *_: (buffer, 0)),
        ]
        + [pl.BlockSpec(memory_space=ANY)] * sum(counts),
        out_specs=[
            pl.BlockSpec((length, width), whole),
            pl.BlockSpec((length, 3 * head_cols), whole),
            pl.BlockSpec((half, width), whole),
            pl.BlockSpec((half, width), whole),
            pl.BlockSpec((8, width), whole),
            pl.BlockSpec(strip.shape, whole3),
        ],
        scratch_shapes=[
            pltpu.VMEM((width, p_pieces[0].shape[1]), BF16),
            pltpu.VMEM((width, o_pieces[0].shape[1]), BF16),
            pltpu.VMEM((heads, length, DH), BF16),
            pltpu.VMEM((heads, length, DH), BF16),
            pltpu.VMEM((heads, length, DH), BF16),
            pltpu.VMEM((heads, length, DH), BF16),
            pltpu.VMEM((heads, DH, length), BF16),
            pltpu.VMEM((heads, DH, length), BF16),
            pltpu.VMEM((heads, DH, length), F32),
            pltpu.VMEM((heads, DH, length), F32),
            pltpu.VMEM((heads, length, DH), BF16),
            pltpu.SemaphoreType.DMA((2, max(counts))),
        ],
    )
    return pl.pallas_call(
        functools.partial(back_kernel, buffer, ends.shape[1], heads, counts),
        grid_spec=spec,
        out_shape=[
            jax.ShapeDtypeStruct((length, width), BF16),
            jax.ShapeDtypeStruct((length, 3 * head_cols), BF16),
            jax.ShapeDtypeStruct((half, width), BF16),
            jax.ShapeDtypeStruct((half, width), BF16),
            jax.ShapeDtypeStruct((8, width), F32),
            jax.ShapeDtypeStruct(strip.shape, F32),
        ],
        compiler_params=params(),
        cost_estimate=pl.CostEstimate(
            flops=40 * heads * DH * length * length,
            bytes_accessed=16 << 20,
            transcendentals=heads * length * length,
        ),
        name="back",
    )(ends, offs, order, near, far, qkv, logs, strip, x, *o_pieces, *p_pieces)


def scatter_rows(total, offs_ref, evens, odds):
    rows = evens[0].shape[0]
    for at in range(2 * len(evens)):
        begin = pl.multiple_of(offs_ref[at], 8)
        block = total[pl.ds(begin, rows)]
        if at % 2:
            odds[at // 2][...] = block.astype(BF16)
        else:
            evens[at // 2][...] = block


def feed_grad_kernel(count, hidden_cols, offs_ref, *refs):
    buffers = 2
    normed = refs[:buffers]
    gates = refs[buffers : 2 * buffers]
    hiddens = refs[2 * buffers : 3 * buffers]
    cot_ref = refs[3 * buffers]
    outs = refs[3 * buffers + 1 : -1]
    total = refs[-1]
    length = normed[0].shape[0]
    width = normed[0].shape[1]
    part = 256
    for begin in range(0, width, part):
        cols = slice(begin, begin + part)
        total[cols, : 2 * hidden_cols] = mm(normed[0][:, cols], gates[0][...], TN) + mm(
            normed[1][:, cols], gates[1][...], TN
        )
        total[cols, 2 * hidden_cols :] = mm(
            cot_ref[:length, cols], hiddens[0][...], TN
        ) + mm(cot_ref[length:, cols], hiddens[1][...], TN)
    if count > 1:
        scatter_rows(total, offs_ref, outs[: count // 2], outs[count // 2 :])
    else:
        outs[0][...] = total[...]


def attend_grad_kernel(count, heads, offs_ref, *refs):
    buffers = 2
    normed = refs[:buffers]
    dqkv = refs[buffers : 2 * buffers]
    lows = refs[2 * buffers : 3 * buffers]
    atts = refs[3 * buffers : 4 * buffers]
    sums_ref = refs[4 * buffers]
    outs = refs[4 * buffers + 1 : -1]
    total = refs[-1]
    width = normed[0].shape[1]
    head_cols = heads * DH
    qkv_cols = 3 * head_cols
    part = 256
    rows = lax.broadcasted_iota(jnp.int32, (LANES, width), 0)
    first = sums_ref[0] + sums_ref[1]
    second = sums_ref[2] + sums_ref[3]
    gain_rows = jnp.where(
        rows == DH,
        jnp.sum(first, axis=0, keepdims=True),
        jnp.where(rows == DH + 1, jnp.sum(second, axis=0, keepdims=True), 0.0),
    )
    gain_cols = gain_rows.T
    for begin in range(0, width, part):
        cols = slice(begin, begin + part)
        total[cols, :qkv_cols] = mm(normed[0][:, cols], dqkv[0][...], TN) + mm(
            normed[1][:, cols], dqkv[1][...], TN
        )
        total[cols, qkv_cols : qkv_cols + DH] = gain_cols[cols, DH:]
        total[cols, qkv_cols + DH : qkv_cols + DH + head_cols] = mm(
            lows[0][:, cols], atts[0][...], TN
        ) + mm(lows[1][:, cols], atts[1][...], TN)
    if count > 1:
        scatter_rows(total, offs_ref, outs[: count // 2], outs[count // 2 :])
    else:
        outs[0][...] = total[...]


def grad_call(kernel, name, offs, operands, width, cols, count, rows, flops):
    vmem = pl.BlockSpec(memory_space=pltpu.VMEM)
    if count > 1:
        shapes = [jax.ShapeDtypeStruct((rows, cols), F32)] * (count // 2)
        shapes += [jax.ShapeDtypeStruct((rows, cols), BF16)] * (count // 2)
    else:
        shapes = [jax.ShapeDtypeStruct((width, cols), F32)]
    return pl.pallas_call(
        kernel,
        in_specs=[pl.BlockSpec(memory_space=pltpu.SMEM)] + [vmem] * len(operands),
        out_specs=[vmem] * len(shapes),
        out_shape=shapes,
        scratch_shapes=[pltpu.VMEM((width, cols), F32)],
        compiler_params=params(),
        cost_estimate=pl.CostEstimate(flops=2 * flops, bytes_accessed=14 << 20, transcendentals=0),
        name=name,
    )(offs, *operands)


def bucket_kernel(heads, near_ref, far_ref, out_ref):
    lanes = near_ref.shape[2]
    blocks = (lanes // LANES + 1) // 2
    begin = (blocks - 2) * LANES
    end = begin + 3 * LANES
    rows = lax.broadcasted_iota(jnp.int32, (LANES, 3 * LANES), 0)
    ids = bucket_of(
        lax.broadcasted_iota(jnp.int32, (LANES, 3 * LANES), 1) - LANES - rows
    )
    lane = lax.broadcasted_iota(jnp.int32, (1, LANES), 1)
    out = jnp.zeros((1, LANES), F32)
    for h in range(heads):
        strip = near_ref[h] + far_ref[h]
        left = jnp.sum(jnp.sum(strip[:, :begin], axis=0, keepdims=True), axis=1, keepdims=True)
        right = jnp.sum(jnp.sum(strip[:, end:], axis=0, keepdims=True), axis=1, keepdims=True)
        out = out + jnp.where(lane == h * 32 + 15, left, 0.0)
        out = out + jnp.where(lane == h * 32 + 31, right, 0.0)
        middle = strip[:, begin:end]
        for b in range(32):
            if b == 16:
                continue
            part = jnp.sum(jnp.where(ids == b, middle, 0.0), axis=0, keepdims=True)
            part = jnp.sum(part, axis=1, keepdims=True)
            out = out + jnp.where(lane == h * 32 + b, part, 0.0)
    out_ref[...] = jnp.broadcast_to(out, (8, LANES))


def norm_kernel(wide, narrow, lists, gain_at, *refs):
    at = 0
    groups = []
    for count in lists:
        groups.append(refs[at : at + count])
        at += count
    bucket_ref = refs[at]
    outs = refs[at + 1 : at + 1 + len(lists)]
    stat_ref, gain_ref, table_ref, block, inbox, padded, send_sems, recv_sems = refs[
        at + 1 + len(lists) :
    ]
    total = wide * narrow
    w = lax.axis_index("wide")
    n = lax.axis_index("narrow")
    me = w * narrow + n
    barrier = pltpu.get_barrier_semaphore()

    @pl.loop(1, total)
    def _(k):
        peer = (me + k) % total
        pl.semaphore_signal(
            barrier, inc=1, device_id=(peer // narrow, peer % narrow), device_id_type=MESH
        )

    squares = jnp.zeros((8, LANES), F32)
    for which, (group, out) in enumerate(zip(groups, outs)):
        value = group[0][...].astype(F32)
        for more in group[1:]:
            value = value + more[...].astype(F32)
        out[...] = value
        squared = value * value
        if which == 0:
            lane = lax.broadcasted_iota(jnp.int32, value.shape, 1)
            inside = (lane >= gain_at) & (lane < gain_at + DH)
            squared = jnp.where(inside, 0.0, squared)
        squared = jnp.sum(squared, axis=1, keepdims=True)
        squares = squares + jnp.sum(squared, axis=0, keepdims=True)
    rows = outs[0].shape[0]
    low = gain_at // LANES * LANES
    padded[...] = jnp.zeros_like(padded)
    padded[0:rows] = outs[0][:, low : low + LANES]
    turned = padded[...].T
    row = lax.broadcasted_iota(jnp.int32, (8, LANES), 0)
    here = gain_at - low
    mine = jnp.where(row == 0, squares, 0.0)
    mine = jnp.where(row == 1, turned[here : here + 1], mine)
    mine = jnp.where(row == 2, turned[here + 1 : here + 2], mine)
    mine = jnp.where(row == 3, bucket_ref[...], mine)
    block[...] = mine
    inbox[me] = mine
    pl.semaphore_wait(barrier, total - 1)

    @pl.loop(1, total)
    def _(k):
        peer = (me + k) % total
        pltpu.make_async_remote_copy(
            src_ref=block,
            dst_ref=inbox.at[me],
            send_sem=send_sems.at[k],
            recv_sem=recv_sems.at[total - k],
            device_id=(peer // narrow, peer % narrow),
            device_id_type=MESH,
        ).start()

    @pl.loop(1, total)
    def _(k):
        peer = (me + k) % total
        copy = pltpu.make_async_remote_copy(
            src_ref=block,
            dst_ref=inbox.at[peer],
            send_sem=send_sems.at[k],
            recv_sem=recv_sems.at[k],
            device_id=(peer // narrow, peer % narrow),
            device_id_type=MESH,
        )
        copy.wait_send()
        copy.wait_recv()

    columns = [jnp.zeros((8, LANES), F32) for _ in range(narrow)]
    gain_square = jnp.zeros((8, LANES), F32)
    square_total = jnp.zeros((8, LANES), F32)
    for a in range(wide):
        gains = jnp.zeros((8, LANES), F32)
        for b in range(narrow):
            got = inbox[a * narrow + b]
            gains = gains + got
            columns[b] = columns[b] + got
        square_total = square_total + gains
        gain_square = gain_square + gains * gains
    own = inbox[w * narrow]
    for b in range(1, narrow):
        own = own + inbox[w * narrow + b]
    gain_ref[...] = own
    pick = (row == 1) | (row == 2)
    gain_square = jnp.where(pick, gain_square, 0.0)
    norm_square = square_total[0:1, 0:1] + jnp.sum(
        jnp.sum(gain_square, axis=0, keepdims=True), axis=1, keepdims=True
    )
    heads = LANES // 32 - 1
    lane = lax.broadcasted_iota(jnp.int32, (32, LANES), 1)
    depth = lax.broadcasted_iota(jnp.int32, (32, LANES), 0)
    table = jnp.zeros((32, LANES), F32)
    for b in range(narrow):
        line = columns[b][3:4]
        norm_square = norm_square + jnp.sum(line * line, axis=1, keepdims=True)
        for h in range(heads):
            column = jnp.sum(
                jnp.where(lane == depth + 32 * h, line, 0.0), axis=1, keepdims=True
            )
            table = jnp.where(lane == b * heads + h, column, table)
    table_ref[...] = table
    global_norm = jnp.sqrt(norm_square)
    factor = jnp.minimum(1.0, clip_limit / (global_norm + 1e-06))
    stat_ref[...] = jnp.where(row == 0, global_norm, factor)


def norm_call(wide, narrow, groups, bucket, gain_at):
    vmem = pl.BlockSpec(memory_space=pltpu.VMEM)
    lists = tuple(len(group) for group in groups)
    total = wide * narrow
    operands = [piece for group in groups for piece in group] + [bucket]
    return pl.pallas_call(
        functools.partial(norm_kernel, wide, narrow, lists, gain_at),
        in_specs=[vmem] * len(operands),
        out_specs=[vmem] * (len(lists) + 3),
        out_shape=[jax.ShapeDtypeStruct(group[0].shape, F32) for group in groups]
        + [
            jax.ShapeDtypeStruct((8, LANES), F32),
            jax.ShapeDtypeStruct((8, LANES), F32),
            jax.ShapeDtypeStruct((32, LANES), F32),
        ],
        scratch_shapes=[
            pltpu.VMEM((8, LANES), F32),
            pltpu.VMEM((total, 8, LANES), F32),
            pltpu.VMEM((LANES, LANES), F32),
            pltpu.SemaphoreType.DMA((total,)),
            pltpu.SemaphoreType.DMA((total,)),
        ],
        compiler_params=params(collective_id=0, has_side_effects=True),
        cost_estimate=pl.CostEstimate(flops=1 << 20, bytes_accessed=4 << 20, transcendentals=0),
        name="norm",
    )(*operands)


def adam_kernel(heads, hidden_cols, parts, att_ref, feed_ref, gain_ref, table_ref, stat_ref, *refs):
    weights, firsts, seconds = refs[:6], refs[6:12], refs[12:18]
    outs = refs[18:36]
    o_pad, s_pad = refs[36:]
    factor = stat_ref[1:2, 0:1]
    head_cols = heads * DH
    rows = att_ref.shape[0]
    gain_at = 3 * head_cols

    def update(which, index, gradient):
        results = adam_update(
            weights[which][index],
            firsts[which][index],
            seconds[which][index],
            factor * gradient,
            step_rates[which],
            decay_rates[which],
        )
        for at in range(3):
            outs[6 * at + which][index] = results[at]

    for i in range(3):
        update(0, i, att_ref[:, i * head_cols : (i + 1) * head_cols])
    part = hidden_cols // parts
    for j in range(parts):
        span = slice(j * part, (j + 1) * part)
        for i in range(2):
            begin = (3 * j + i) * part if parts > 1 else i * part
            update(2, (i, slice(None), span), feed_ref[:, begin : begin + part])
    o_pad[...] = jnp.zeros_like(o_pad)
    s_pad[...] = jnp.zeros_like(s_pad)
    o_pad[0:rows] = att_ref[:, gain_at + DH :]
    for j in range(parts):
        begin = (3 * j + 2) * part
        s_pad[0:rows, j * part : (j + 1) * part] = feed_ref[:, begin : begin + part]
    update(1, slice(None), o_pad[...].T[:head_cols, :rows])
    update(3, slice(None), s_pad[...].T[:, :rows])
    columns = weights[4].shape[1]
    update(4, slice(None), table_ref[:, :columns])
    update(5, slice(None), gain_ref[1:3, :rows])


def adam_call(
    att, feed_grad, gain, table, stat, params_in, firsts, seconds, heads, hidden_cols, direct=False
):
    vmem = pl.BlockSpec(memory_space=pltpu.VMEM)
    operands = [att, feed_grad, gain, table, stat, *params_in, *firsts, *seconds]
    pad_cols = att.shape[1] - (3 * heads * DH + DH)
    return pl.pallas_call(
        functools.partial(adam_kernel, heads, hidden_cols, 2 if direct else 1),
        in_specs=[vmem] * len(operands),
        out_specs=[vmem] * 18,
        out_shape=[jax.ShapeDtypeStruct(a.shape, F32) for a in params_in] * 3,
        scratch_shapes=[
            pltpu.VMEM((LANES, pad_cols), F32),
            pltpu.VMEM((LANES, hidden_cols), F32),
        ],
        compiler_params=params(),
        cost_estimate=pl.CostEstimate(flops=4 << 20, bytes_accessed=8 << 20, transcendentals=0),
        name="adam",
    )(*operands)


def place_kernel(offs_ref, *refs):
    step = pl.program_id(0)
    for at, piece in enumerate(refs[:-1]):

        @pl.when(step == at)
        def _(piece=piece):
            refs[-1][...] = piece[...]


def place(pieces, offs, rows):
    half, width = pieces[0].shape
    count = len(pieces)
    return pl.pallas_call(
        place_kernel,
        grid_spec=pltpu.PrefetchScalarGridSpec(
            num_scalar_prefetch=1,
            grid=(count,),
            in_specs=[pl.BlockSpec((half, width), lambda i, *_: (0, 0))] * count,
            out_specs=pl.BlockSpec((half, width), lambda i, offs: (offs[i] // half, 0)),
        ),
        out_shape=jax.ShapeDtypeStruct((rows, width), pieces[0].dtype),
        compiler_params=params(),
        cost_estimate=pl.CostEstimate(
            flops=0, bytes_accessed=4 * rows * width, transcendentals=0
        ),
        name="place",
    )(offs, *pieces)


def bias_strip(bucket_bias, n, heads, length):
    table = lax.dynamic_slice_in_dim(bucket_bias, n * heads, heads, 1).T
    blocks = length // LANES
    near_r = (
        jnp.arange(3 * LANES, dtype=jnp.int32)[None, :]
        - LANES
        - jnp.arange(LANES, dtype=jnp.int32)[:, None]
    )
    near_ids = bucket_of(near_r)
    near = sum(
        jnp.where(near_ids == b, table[:, b][:, None, None], 0.0) for b in range(32) if b != 16
    )
    far_shape = (heads, LANES, (blocks - 2) * LANES)
    return jnp.concatenate(
        [
            jnp.broadcast_to(table[:, 15][:, None, None], far_shape),
            near,
            jnp.broadcast_to(table[:, 31][:, None, None], far_shape),
        ],
        axis=2,
    )


def general_body(wide, narrow, *arguments):
    (
        block_input,
        cotangent,
        lengths,
        project_weight,
        output_weight,
        expand_weight,
        shrink_weight,
        bucket_bias,
        norm_gains,
    ) = arguments[:9]
    firsts = arguments[9:15]
    seconds = arguments[15:21]
    tokens, width = block_input.shape
    buffers = lengths.shape[0]
    length = tokens // buffers
    rows = norm_gains.shape[1]
    head_cols = project_weight.shape[2]
    heads = head_cols // DH
    hidden_cols = expand_weight.shape[2]
    w = lax.axis_index("wide")
    n = lax.axis_index("narrow")
    core = n % 2

    def swap(value, wide_mask, narrow_mask):
        pairs = [
            (a * narrow + b, (a ^ wide_mask) * narrow + (b ^ narrow_mask))
            for a in range(wide)
            for b in range(narrow)
        ]
        return lax.ppermute(value, ("wide", "narrow"), pairs)

    def gather(piece):
        return [lax.all_gather(piece, "wide", axis=0, tiled=True)]

    def reduce_wide(outs):
        return [lax.psum_scatter(outs[0], "wide", scatter_dimension=0, tiled=True)]

    offs = jnp.zeros((1,), jnp.int32)
    order = jnp.stack([1 - core, core, n // 2])

    p_piece = jnp.concatenate(
        [
            project_weight[0],
            project_weight[1],
            project_weight[2],
            norm_gains.T,
            jnp.zeros((rows, DH - 2), F32),
        ],
        axis=1,
    ).astype(BF16)
    p_pieces = gather(p_piece)
    o_piece = output_weight.astype(BF16).T
    o_pair = jnp.concatenate([o_piece, swap(o_piece, 0, 2)], axis=1)
    oa_pieces = gather(o_pair)
    ob_pieces = [swap(piece, 0, 1) for piece in oa_pieces]
    e_pieces = gather(
        jnp.concatenate([expand_weight[0], expand_weight[1]], axis=1).astype(BF16)
    )
    s_pieces = gather(shrink_weight.astype(BF16).T)

    ends = jnp.cumsum(lengths, axis=1)
    strip = bias_strip(bucket_bias, n, heads, length)

    normed_one, qkv, atts, logs, fours = [], [], [], [], []
    for b in range(buffers):
        normed, rows_b, att, log, gains = attend(
            b, ends, offs, block_input, strip, p_pieces, length, heads
        )
        normed_one.append(normed)
        qkv.append(rows_b)
        atts.append(att)
        logs.append(log)
        across = swap(att, 0, 2)
        fours.append((att, across, swap(att, 0, 1), swap(across, 0, 1)))

    def core_sum(kept, sent):
        return (kept.astype(F32) + swap(sent, 0, 1).astype(F32)).astype(BF16)

    normed_two, hiddens, gates, middles, ff_sums, dn_sums, sums_two = [], [], [], [], [], [], []
    for b in range(buffers):
        normed, hidden, gate, ff_send, ff_keep, dn_send, dn_keep, middle, sums = feed(
            b,
            order,
            offs,
            fours[b],
            block_input,
            cotangent,
            gains,
            (oa_pieces, ob_pieces, e_pieces, s_pieces),
            length,
            hidden_cols,
        )
        normed_two.append(normed)
        hiddens.append(hidden)
        gates.append(gate)
        middles.append(middle)
        sums_two.append(sums)
        dn_sums.append(core_sum(dn_keep, dn_send))
        ff_sums.append(core_sum(ff_keep, ff_send))

    d_middles, lows = [], []
    for b in range(buffers):
        d_middle, low = half_call(
            middle_kernel,
            "middle",
            b,
            order,
            [dn_sums[b], swap(dn_sums[b], 0, 2), middles[b], cotangent],
            (3,),
            (F32, BF16),
            gains,
        )
        d_middles.append(d_middle)
        lows.append((low, swap(low, 0, 1)))

    count = 1
    feed_outs = grad_call(
        functools.partial(feed_grad_kernel, count, hidden_cols),
        "feed_grad",
        offs,
        [*normed_two, *gates, *hiddens, cotangent],
        width,
        3 * hidden_cols,
        count,
        rows,
        2 * tokens * width * 3 * hidden_cols,
    )
    feed_group = reduce_wide(feed_outs)

    low_full, dqkv, dn_one, sums_one, strips = [], [], [], [], []
    for b in range(buffers):
        low, grads, dn_send, dn_keep, sums, dstrip = back(
            b,
            ends,
            offs,
            order,
            lows[b][0],
            lows[b][1],
            qkv[b],
            logs[b],
            strip,
            block_input,
            oa_pieces,
            p_pieces,
            heads,
        )
        low_full.append(low)
        dqkv.append(grads)
        sums_one.append(sums)
        strips.append(dstrip)
        dn_one.append(core_sum(dn_keep, dn_send))

    gain_at = 3 * head_cols
    att_outs = grad_call(
        functools.partial(attend_grad_kernel, count, heads),
        "attend_grad",
        offs,
        [*normed_one, *dqkv, *low_full, *atts, jnp.stack(sums_one + sums_two)],
        width,
        gain_at + DH + head_cols,
        count,
        rows,
        2 * tokens * width * 4 * head_cols,
    )
    att_group = reduce_wide(att_outs)
    vmem = pl.BlockSpec(memory_space=pltpu.VMEM)
    bucket = pl.pallas_call(
        functools.partial(bucket_kernel, heads),
        in_specs=[vmem, vmem],
        out_specs=vmem,
        out_shape=jax.ShapeDtypeStruct((8, LANES), F32),
        compiler_params=params(),
        cost_estimate=pl.CostEstimate(flops=8 << 20, bytes_accessed=4 << 20, transcendentals=0),
        name="bucket",
    )(*strips)

    half_offs = jnp.stack(
        [
            b * length + which * (length // 2)
            for b in range(buffers)
            for which in (core, 1 - core)
        ]
    )
    out_halves, in_halves = [], []
    for b in range(buffers):
        (half,) = half_call(
            output_kernel,
            "output",
            b,
            order,
            [ff_sums[b], swap(ff_sums[b], 0, 2), middles[b]],
            (),
            (BF16,),
        )
        out_halves += [half, swap(half, 0, 1)]
        (half,) = half_call(
            input_kernel,
            "input",
            b,
            order,
            [dn_one[b], swap(dn_one[b], 0, 2), block_input, d_middles[b]],
            (2,),
            (BF16,),
            gains,
        )
        in_halves += [half, swap(half, 0, 1)]
    block_output = place(out_halves, half_offs, tokens)
    input_gradient = place(in_halves, half_offs, tokens)

    att_grad, feed_grad, stat, gain, table_sum = norm_call(
        wide, narrow, [att_group, feed_group], bucket, gain_at
    )
    results = adam_call(
        att_grad,
        feed_grad,
        gain,
        table_sum,
        stat,
        arguments[3:9],
        firsts,
        seconds,
        heads,
        hidden_cols,
    )
    return (block_output, input_gradient, stat[0, 0], *results)


class Place:
    def __init__(self):
        self.w = lax.axis_index("wide")
        self.n = lax.axis_index("narrow")
        self.z, self.x = self.w // 2, self.w % 2
        self.y, self.core = self.n // 2, self.n % 2
        self.n_far = (self.n + 2) % 4
        self.across = (self.w, self.n_far)
        self.beside = (self.w, self.n + 1 - 2 * self.core)
        self.flip = (self.z * 2 + 1 - self.x, self.n)

    def along(self, m):
        return (((self.z + m) % 4) * 2 + self.x, self.n)

    def from_z(self, m):
        return ((self.z + 4 - m) % 4) * 2 + self.x

    def from_x(self, m):
        return ((self.z + 4 - m) % 4) * 2 + 1 - self.x

    def meet(self):
        barrier = pltpu.get_barrier_semaphore()
        peers = [self.along(1), self.along(2), self.along(3), self.flip, self.across, self.beside]
        for peer in peers:
            pl.semaphore_signal(barrier, inc=1, device_id=peer, device_id_type=MESH)
        pl.semaphore_wait(barrier, len(peers))


def remote(source, target, send_sem, recv_sem, peer):
    return pltpu.make_async_remote_copy(
        src_ref=source,
        dst_ref=target,
        send_sem=send_sem,
        recv_sem=recv_sem,
        device_id=peer,
        device_id_type=MESH,
    )


class Gather:
    def __init__(self, spot, view, ssem, rsem):
        self.spot, self.view, self.ssem, self.rsem = spot, view, ssem, rsem
        self.sent = []

    def push(self, owner, slot, peer):
        copy = remote(
            self.view(owner), self.view(owner), self.ssem.at[slot], self.rsem.at[owner], peer
        )
        copy.start()
        self.sent.append((owner, slot, peer))

    def begin(self):
        for m in (1, 2, 3):
            self.push(self.spot.w, m - 1, self.spot.along(m))
        self.push(self.spot.w, 3, self.spot.flip)

    def arrived(self, owner):
        remote(
            self.view(owner), self.view(owner), self.ssem.at[0], self.rsem.at[owner], self.spot.flip
        ).wait_recv()

    def forward(self, m):
        owner = self.spot.from_z(m)
        self.arrived(owner)
        self.push(owner, 3 + m, self.spot.flip)

    def finish(self):
        for m in range(4):
            self.arrived(self.spot.from_x(m))

    def drain(self):
        for m in (1, 2, 3):
            remote(
                self.view(self.spot.w),
                self.view(self.spot.w),
                self.ssem.at[m - 1],
                self.rsem.at[0],
                self.spot.along(m),
            ).wait_send()
        for m in range(4):
            owner = self.spot.from_z(m)
            remote(
                self.view(owner), self.view(owner), self.ssem.at[3 + m], self.rsem.at[0], self.spot.flip
            ).wait_send()


def gather_attend_kernel(
    buffers,
    slots,
    heads,
    hidden_cols,
    ends_ref,
    x_ref,
    strip_ref,
    pw_ref,
    ow_ref,
    ew_ref,
    sw_ref,
    gn_ref,
    normed_ref,
    qkv_ref,
    att_ref,
    log_ref,
    gains_ref,
    pbuf,
    obuf,
    fbuf,
    qs,
    kt,
    vs,
    opad,
    spad,
    gpad,
    ssems,
    rsems,
    lone_s,
    lone_r,
):
    spot = Place()
    spot.meet()
    tokens, width = x_ref.shape
    length = tokens // buffers
    head_cols = heads * DH
    rows = gn_ref.shape[1]
    part = hidden_cols // 2
    chunk = 3 * part

    def at_rows(owner):
        return pl.ds(pl.multiple_of(owner * rows, 16), rows)

    mine = at_rows(spot.w)
    gpad[...] = jnp.zeros_like(gpad)
    gpad[0:2, 0:rows] = gn_ref[...]
    pbuf[mine] = jnp.concatenate(
        [pw_ref[0], pw_ref[1], pw_ref[2], gpad[...].T[:rows, :DH]], axis=1
    ).astype(BF16)
    projection = Gather(spot, lambda v: pbuf.at[at_rows(v)], ssems.at[0], rsems.at[0])
    projection.begin()
    opad[...] = jnp.zeros_like(opad)
    opad[0:head_cols, 0:rows] = ow_ref[...]
    obuf[spot.n, mine] = opad[...].T[:rows, :head_cols].astype(BF16)

    def o_view(which):
        return lambda v: obuf.at[which, at_rows(v)]

    def o_across():
        return remote(
            obuf.at[spot.n, mine],
            obuf.at[spot.n, mine],
            lone_s.at[0],
            lone_r.at[0],
            spot.across,
        )

    def o_across_in():
        return remote(
            obuf.at[spot.n_far, mine],
            obuf.at[spot.n_far, mine],
            lone_s.at[0],
            lone_r.at[0],
            spot.across,
        )

    o_across().start()
    spad[...] = jnp.zeros_like(spad)
    spad[:, 0:rows] = sw_ref[...]
    turned = spad[...].T[:rows].astype(BF16)
    for j in range(2):
        span = slice(j * part, (j + 1) * part)
        fbuf[mine, j * chunk : j * chunk + part] = ew_ref[0, :, span].astype(BF16)
        fbuf[mine, j * chunk + part : j * chunk + 2 * part] = ew_ref[1, :, span].astype(BF16)
        fbuf[mine, j * chunk + 2 * part : (j + 1) * chunk] = turned[:, span]
    out_near = Gather(spot, o_view(spot.n), ssems.at[1], rsems.at[1])
    out_far = Gather(spot, o_view(spot.n_far), ssems.at[2], rsems.at[2])
    feeds = [
        Gather(
            spot,
            lambda v, j=j: fbuf.at[at_rows(v), j * chunk : (j + 1) * chunk],
            ssems.at[3 + j],
            rsems.at[3 + j],
        )
        for j in range(2)
    ]
    for m in (1, 2, 3):
        projection.forward(m)
    o_across_in().wait_recv()
    out_near.begin()
    out_far.begin()
    feeds[0].begin()
    projection.finish()

    gain_cols = pbuf[:, 4 * LANES :].astype(F32).T
    first = 3 * head_cols - 4 * LANES
    gains = gain_cols[first : first + 8]
    gains_ref[...] = gains
    gain_one = gains[0:1]
    step = 256
    per = length // step

    for b in range(buffers):

        @pl.loop(0, per)
        def _(block, b=b):
            begin = pl.multiple_of(block * step, step)
            here = pl.ds(begin, step)
            span = pl.ds(pl.multiple_of(b * length + begin, step), step)
            values = x_ref[span].astype(F32)
            normed = (values * rms_scale(values) * gain_one).astype(BF16)
            normed_ref[span] = normed
            qkv = mm(normed, pbuf[...]).astype(BF16)
            qkv_ref[span] = qkv[:, : 3 * head_cols]
            for h in range(heads):
                qs[b, h, here] = qkv[:, h * DH : (h + 1) * DH]
                kt[b, h, :, here] = qkv[:, head_cols + h * DH : head_cols + (h + 1) * DH].T
                vs[b, h, here] = qkv[:, 2 * head_cols + h * DH : 2 * head_cols + (h + 1) * DH]

    def relay_out():
        for m in (1, 2, 3):
            out_near.forward(m)
            out_far.forward(m)

    def att_view(which, b):
        return att_ref.at[which, b * length : (b + 1) * length]

    def share(which, slot, peer):
        return remote(which, which, lone_s.at[slot], lone_r.at[slot], peer)

    n_beside = spot.beside[1]
    n_diag = (n_beside + 2) % 4

    def out_beside():
        out_near.finish()
        out_far.finish()
        share(obuf.at[spot.n], 1, spot.beside).start()
        share(obuf.at[spot.n_far], 2, spot.beside).start()

    def att_send(b):
        share(att_view(spot.n, b), 3 + 3 * b, spot.across).start()
        share(att_view(spot.n, b), 4 + 3 * b, spot.beside).start()

    def att_relay(b):
        share(att_view(spot.n_far, b), 3 + 3 * b, spot.across).wait_recv()
        share(att_view(spot.n_far, b), 5 + 3 * b, spot.beside).start()

    blocks = length // LANES

    def run(b, events):
        seg_keys = segments(
            lax.broadcasted_iota(jnp.int32, (1, length), 1), ends_ref, b, slots
        )

        @pl.loop(0, blocks)
        def _(block):
            for when, what in events.items():
                pl.when(block == when)(what)
            begin = pl.multiple_of(block * LANES, LANES)
            here = pl.ds(begin, LANES)
            span = pl.ds(pl.multiple_of(b * length + begin, LANES), LANES)
            window = pl.ds(pl.multiple_of((blocks - 1 - block) * LANES, LANES), length)
            seg_rows = segments(
                lax.broadcasted_iota(jnp.int32, (LANES, 1), 0) + begin, ends_ref, b, slots
            )
            same = seg_rows == seg_keys
            lane = lax.broadcasted_iota(jnp.int32, (LANES, LANES), 1)
            logs = jnp.zeros((LANES, LANES), F32)
            outs = []
            for h in range(heads):
                scores = mm(qs[b, h, here], kt[b, h]) + strip_ref[h, :, window]
                scores = jnp.where(same, scores, masked_score)
                row_max = jnp.max(scores, axis=1, keepdims=True)
                raised = jnp.exp(scores - row_max)
                total = jnp.sum(raised, axis=1, keepdims=True)
                probs = (raised * (1.0 / total)).astype(BF16)
                outs.append(mm(probs, vs[b, h]).astype(BF16))
                logs = jnp.where(lane == h, row_max + jnp.log(total), logs)
            log_ref[span] = logs
            att_ref[spot.n, span] = jnp.concatenate(outs, axis=1)

    def feed_turn():
        feeds[0].forward(3)
        feeds[1].begin()

    run(
        0,
        {
            0: relay_out,
            2: lambda: feeds[0].forward(1),
            3: lambda: feeds[0].forward(2),
            4: feed_turn,
            5: out_beside,
        },
    )
    att_send(0)
    run(
        1,
        {
            2: lambda: att_relay(0),
            3: lambda: feeds[1].forward(1),
            4: lambda: feeds[1].forward(2),
            5: lambda: feeds[1].forward(3),
        },
    )
    att_send(1)
    att_relay(1)
    feeds[0].finish()
    feeds[1].finish()
    share(obuf.at[n_beside], 1, spot.beside).wait_recv()
    share(obuf.at[n_diag], 2, spot.beside).wait_recv()
    for b in range(buffers):
        share(att_view(n_beside, b), 4 + 3 * b, spot.beside).wait_recv()
        share(att_view(n_diag, b), 5 + 3 * b, spot.beside).wait_recv()
    o_across().wait_send()
    for group in (projection, out_near, out_far, *feeds):
        group.drain()
    share(obuf.at[spot.n], 1, spot.beside).wait_send()
    share(obuf.at[spot.n_far], 2, spot.beside).wait_send()
    for b in range(buffers):
        share(att_view(spot.n, b), 3 + 3 * b, spot.across).wait_send()
        share(att_view(spot.n, b), 4 + 3 * b, spot.beside).wait_send()
        share(att_view(spot.n_far, b), 5 + 3 * b, spot.beside).wait_send()


def gather_attend(ends, x, strip, pw, ow, ew, sw, gn, length):
    tokens, width = x.shape
    buffers = tokens // length
    heads = strip.shape[0]
    head_cols = heads * DH
    hidden_cols = ew.shape[2]
    vmem = pl.BlockSpec(memory_space=pltpu.VMEM)
    return pl.pallas_call(
        functools.partial(gather_attend_kernel, buffers, ends.shape[1], heads, hidden_cols),
        in_specs=[pl.BlockSpec(memory_space=pltpu.SMEM)] + [vmem] * 7,
        out_specs=[vmem] * 8,
        out_shape=[
            jax.ShapeDtypeStruct((tokens, width), BF16),
            jax.ShapeDtypeStruct((tokens, 3 * head_cols), BF16),
            jax.ShapeDtypeStruct((4, tokens, head_cols), BF16),
            jax.ShapeDtypeStruct((tokens, LANES), F32),
            jax.ShapeDtypeStruct((8, width), F32),
            jax.ShapeDtypeStruct((width, 3 * head_cols + DH), BF16),
            jax.ShapeDtypeStruct((4, width, head_cols), BF16),
            jax.ShapeDtypeStruct((width, 3 * hidden_cols), BF16),
        ],
        scratch_shapes=[
            pltpu.VMEM((buffers, heads, length, DH), BF16),
            pltpu.VMEM((buffers, heads, DH, length), BF16),
            pltpu.VMEM((buffers, heads, length, DH), BF16),
            pltpu.VMEM((2 * LANES, LANES), F32),
            pltpu.VMEM((hidden_cols, LANES), F32),
            pltpu.VMEM((LANES, LANES), F32),
            pltpu.SemaphoreType.DMA((5, 7)),
            pltpu.SemaphoreType.DMA((5, 8)),
            pltpu.SemaphoreType.DMA((9,)),
            pltpu.SemaphoreType.DMA((9,)),
        ],
        compiler_params=params(collective_id=1, has_side_effects=True),
        cost_estimate=pl.CostEstimate(
            flops=16 << 30, bytes_accessed=24 << 20, transcendentals=8 << 20
        ),
        name="gather_attend",
    )(ends, x, strip, pw, ow, ew, sw, gn)


def feed_forward_kernel(
    buffers,
    hidden_cols,
    x_ref,
    cot_ref,
    att_ref,
    gains_ref,
    obuf,
    fbuf,
    low_ref,
    d_ref,
    middle_ref,
    ff_sum,
    gain_sum,
    even_ref,
    odd_ref,
    normed,
    hid,
    dg,
    total,
    ff_out,
    ff_in,
    dn_out,
    dn_keep,
    dn_in,
    dn_sum,
    dn_far,
    sends,
    recvs,
):
    spot = Place()
    spot.meet()
    tokens, width = x_ref.shape
    length = tokens // buffers
    half = length // 2
    part = hidden_cols // 2
    chunk = 3 * part
    core = spot.core
    k0 = 0.7978845608028654
    k1 = 0.044715
    gain_two = gains_ref[1:2]

    def ff_core(b):
        return remote(ff_out.at[b], ff_in.at[b], sends.at[b], recvs.at[b], spot.beside)

    def dn_core(b):
        return remote(dn_out.at[b], dn_in.at[b], sends.at[2 + b], recvs.at[2 + b], spot.beside)

    def dn_across(b):
        return remote(dn_sum.at[b], dn_far.at[b], sends.at[4 + b], recvs.at[4 + b], spot.across)

    def low_rows(b, which):
        return pl.ds(pl.multiple_of(b * length + which * half, LANES), half)

    def low_core(b):
        view = low_ref.at[low_rows(b, core)]
        return remote(view, view, sends.at[6 + b], recvs.at[6 + b], spot.beside)

    def low_core_in(b):
        view = low_ref.at[low_rows(b, 1 - core)]
        return remote(view, view, sends.at[6 + b], recvs.at[6 + b], spot.beside)

    gain_sum[...] = jnp.zeros_like(gain_sum)

    @pl.loop(0, 2 * buffers)
    def _(i):
        b = i // 2
        keep = i % 2
        which = (1 - core) * (1 - keep) + core * keep
        rows = low_rows(b, which)
        attention = jnp.zeros((half, width), F32)
        for a in range(4):
            attention = attention + mm(att_ref[a, rows], obuf[a], NT)
        middle = x_ref[rows].astype(F32) + attention
        scale_two = rms_scale(middle)
        normed_rows = (middle * scale_two * gain_two).astype(BF16)
        normed[rows] = normed_rows
        cot = cot_ref[rows]
        ff = jnp.zeros((half, width), F32)
        dn = jnp.zeros((half, width), F32)
        for j in range(2):
            at = j * chunk
            both = mm(normed_rows, fbuf[:, at : at + 2 * part])
            gate, up = both[:, :part], both[:, part:]
            square = gate * gate
            tanh = jnp.tanh(k0 * (gate + k1 * (square * gate)))
            lift = 0.5 * (1.0 + tanh)
            active = gate * lift
            slope = lift + (0.5 * gate) * (1.0 - tanh * tanh) * (k0 + (3.0 * k0 * k1) * square)
            d_hidden = mm(cot, fbuf[:, at + 2 * part : at + 3 * part])
            hid[rows, j * part : (j + 1) * part] = (active * up).astype(BF16)
            dg[rows, 2 * j * part : (2 * j + 1) * part] = (d_hidden * up * slope).astype(BF16)
            dg[rows, (2 * j + 1) * part : (2 * j + 2) * part] = (d_hidden * active).astype(BF16)
            ff = ff + mm(
                hid[rows, j * part : (j + 1) * part], fbuf[:, at + 2 * part : at + 3 * part], NT
            )
            dn = dn + mm(
                dg[rows, 2 * j * part : (2 * j + 2) * part], fbuf[:, at : at + 2 * part], NT
            )
        gain_sum[...] = gain_sum[...] + fold_rows(dn * middle * scale_two)

        @pl.when(keep == 0)
        def _():
            dn_out[b] = dn.astype(BF16)
            dn_core(b).start()
            ff_out[b] = ff.astype(BF16)
            ff_core(b).start()

        @pl.when(keep == 1)
        def _():
            middle_ref[b] = middle
            dn_core(b).wait_recv()
            dn_sum[b] = (dn.astype(BF16).astype(F32) + dn_in[b].astype(F32)).astype(BF16)
            dn_across(b).start()
            ff_core(b).wait_recv()
            ff_sum[b] = (ff.astype(BF16).astype(F32) + ff_in[b].astype(F32)).astype(BF16)

    def finish_middle(b):
        dn_across(b).wait_recv()

        @pl.loop(0, 3)
        def _(i):
            span = pl.ds(pl.multiple_of(i * LANES, LANES), LANES)
            rows = pl.ds(
                pl.multiple_of(b * length + core * half + i * LANES, LANES), LANES
            )
            upstream = dn_sum[b, span].astype(F32) + dn_far[b, span].astype(F32)
            middle = middle_ref[b, span]
            d_middle = cot_ref[rows].astype(F32) + norm_back(
                middle, rms_scale(middle), gain_two, upstream
            )
            d_ref[b, span] = d_middle
            low_ref[rows] = d_middle.astype(BF16)

        low_core(b).start()

    finish_middle(0)
    step = 256
    for begin in range(0, width, step):
        cols = slice(begin, begin + step)
        for j in range(2):
            at = j * chunk
            total[cols, at : at + 2 * part] = mm(
                normed[:, cols], dg[:, 2 * j * part : (2 * j + 2) * part], TN
            )
            total[cols, at + 2 * part : at + 3 * part] = mm(
                cot_ref[:, cols], hid[:, j * part : (j + 1) * part], TN
            )
    spread(spot, total, even_ref, odd_ref)
    finish_middle(1)
    for b in range(buffers):
        low_core_in(b).wait_recv()
        ff_core(b).wait_send()
        dn_core(b).wait_send()
        dn_across(b).wait_send()
        low_core(b).wait_send()


def spread(spot, total, even_ref, odd_ref):
    rows = even_ref.shape[1]
    for m in range(4):
        base = ((spot.z + m) % 4) * 2
        near = pl.ds(pl.multiple_of((base + spot.x) * rows, 8), rows)
        far = pl.ds(pl.multiple_of((base + 1 - spot.x) * rows, 8), rows)
        even_ref[m] = total[near]
        odd_ref[m] = total[far].astype(BF16)


def feed_forward(x, cot, att, gains, obuf, fbuf, length, rows):
    tokens, width = x.shape
    buffers = tokens // length
    half = length // 2
    hidden_cols = fbuf.shape[1] // 3
    vmem = pl.BlockSpec(memory_space=pltpu.VMEM)
    return pl.pallas_call(
        functools.partial(feed_forward_kernel, buffers, hidden_cols),
        in_specs=[vmem] * 6,
        out_specs=[vmem] * 7,
        out_shape=[
            jax.ShapeDtypeStruct((tokens, width), BF16),
            jax.ShapeDtypeStruct((buffers, half, width), F32),
            jax.ShapeDtypeStruct((buffers, half, width), F32),
            jax.ShapeDtypeStruct((buffers, half, width), BF16),
            jax.ShapeDtypeStruct((8, width), F32),
            jax.ShapeDtypeStruct((4, rows, 3 * hidden_cols), F32),
            jax.ShapeDtypeStruct((4, rows, 3 * hidden_cols), BF16),
        ],
        scratch_shapes=[
            pltpu.VMEM((tokens, width), BF16),
            pltpu.VMEM((tokens, hidden_cols), BF16),
            pltpu.VMEM((tokens, 2 * hidden_cols), BF16),
            pltpu.VMEM((width, 3 * hidden_cols), F32),
        ]
        + [pltpu.VMEM((buffers, half, width), BF16)] * 7
        + [pltpu.SemaphoreType.DMA((8,)), pltpu.SemaphoreType.DMA((8,))],
        compiler_params=params(collective_id=2, has_side_effects=True),
        cost_estimate=pl.CostEstimate(
            flops=20 << 30, bytes_accessed=24 << 20, transcendentals=1 << 20
        ),
        name="feed_forward",
    )(x, cot, att, gains, obuf, fbuf)


def direct_body(wide, narrow, *arguments):
    (
        block_input,
        cotangent,
        lengths,
        project_weight,
        output_weight,
        expand_weight,
        shrink_weight,
        bucket_bias,
        norm_gains,
    ) = arguments[:9]
    firsts = arguments[9:15]
    seconds = arguments[15:21]
    tokens, width = block_input.shape
    buffers = lengths.shape[0]
    length = tokens // buffers
    rows = norm_gains.shape[1]
    head_cols = project_weight.shape[2]
    heads = head_cols // DH
    hidden_cols = expand_weight.shape[2]
    w = lax.axis_index("wide")
    n = lax.axis_index("narrow")
    core = n % 2

    def move(value, wide_step=0, flip=0, narrow_mask=0):
        def target(a):
            return ((a // 2 + wide_step) % 4) * 2 + (a % 2 ^ flip)

        pairs = [
            (a * narrow + b, target(a) * narrow + (b ^ narrow_mask))
            for a in range(wide)
            for b in range(narrow)
        ]
        return lax.ppermute(value, ("wide", "narrow"), pairs)

    def reduce_wide(evens, odds):
        kept = [evens[0], move(odds[0], flip=1)]
        for m in (1, 2, 3):
            mixed = (evens[m] + move(odds[m], flip=1).astype(F32)).astype(BF16)
            kept.append(move(mixed, wide_step=m))
        return kept

    ends = jnp.cumsum(lengths, axis=1)
    order = jnp.stack([1 - core, core, n // 2])
    strip = bias_strip(bucket_bias, n, heads, length)
    normed_one, qkv, att, logs, gains, pbuf, obuf, fbuf = gather_attend(
        ends,
        block_input,
        strip,
        project_weight,
        output_weight,
        expand_weight,
        shrink_weight,
        norm_gains,
        length,
    )
    low, d_middle, middle, ff_sum, gain_two, feed_even, feed_odd = feed_forward(
        block_input, cotangent, att, gains, obuf, fbuf, length, rows
    )
    feed_group = reduce_wide(feed_even, feed_odd)

    def core_sum(kept, sent):
        return (kept.astype(F32) + move(sent, narrow_mask=1).astype(F32)).astype(BF16)

    offs = jnp.zeros((1,), jnp.int32)
    own = lax.dynamic_index_in_dim(obuf, n, 0, keepdims=False)
    att_own = lax.dynamic_index_in_dim(att, n, 0, keepdims=False)
    dqkv, dn_one, sums_one, strips = [], [], [], []
    half = length // 2
    for b in range(buffers):
        part = lambda which: lax.dynamic_slice_in_dim(low, b * length + which * half, half, 0)
        span = slice(b * length, (b + 1) * length)
        _, grads, dn_send, dn_keep, sums, dstrip = back(
            b,
            ends,
            offs,
            order,
            part(core),
            part(1 - core),
            qkv[span],
            logs[span],
            strip,
            block_input,
            [own],
            [pbuf],
            heads,
        )
        dqkv.append(grads)
        sums_one.append(sums)
        strips.append(dstrip)
        dn_one.append(core_sum(dn_keep, dn_send))

    gain_at = 3 * head_cols
    halves = lambda value: [value[b * length : (b + 1) * length] for b in range(buffers)]
    (att_total,) = grad_call(
        functools.partial(attend_grad_kernel, 1, heads),
        "attend_grad",
        offs,
        [
            *halves(normed_one),
            *dqkv,
            *halves(low),
            *halves(att_own),
            jnp.stack(sums_one + [gain_two, jnp.zeros_like(gain_two)]),
        ],
        width,
        gain_at + DH + head_cols,
        1,
        rows,
        2 * tokens * width * 4 * head_cols,
    )
    near = [
        lax.dynamic_slice_in_dim(att_total, ((w // 2 + m) % 4 * 2 + w % 2) * rows, rows, 0)
        for m in range(4)
    ]
    far = [
        lax.dynamic_slice_in_dim(att_total, ((w // 2 + m) % 4 * 2 + 1 - w % 2) * rows, rows, 0)
        for m in range(4)
    ]
    att_group = reduce_wide(near, [value.astype(BF16) for value in far])
    vmem = pl.BlockSpec(memory_space=pltpu.VMEM)
    bucket = pl.pallas_call(
        functools.partial(bucket_kernel, heads),
        in_specs=[vmem, vmem],
        out_specs=vmem,
        out_shape=jax.ShapeDtypeStruct((8, LANES), F32),
        compiler_params=params(),
        cost_estimate=pl.CostEstimate(flops=8 << 20, bytes_accessed=4 << 20, transcendentals=0),
        name="bucket",
    )(*strips)

    half_offs = jnp.stack(
        [b * length + which * half for b in range(buffers) for which in (core, 1 - core)]
    )
    out_halves, in_halves = [], []
    for b in range(buffers):
        (out_half,) = half_call(
            output_kernel,
            "output",
            b,
            order,
            [ff_sum[b], move(ff_sum[b], narrow_mask=2), middle[b]],
            (),
            (BF16,),
        )
        out_halves += [out_half, move(out_half, narrow_mask=1)]
        (in_half,) = half_call(
            input_kernel,
            "input",
            b,
            order,
            [dn_one[b], move(dn_one[b], narrow_mask=2), block_input, d_middle[b]],
            (2,),
            (BF16,),
            gains,
        )
        in_halves += [in_half, move(in_half, narrow_mask=1)]
    block_output = place(out_halves, half_offs, tokens)
    input_gradient = place(in_halves, half_offs, tokens)

    att_grad, feed_grad, stat, gain, table_sum = norm_call(
        wide, narrow, [att_group, feed_group], bucket, gain_at
    )
    results = adam_call(
        att_grad,
        feed_grad,
        gain,
        table_sum,
        stat,
        arguments[3:9],
        firsts,
        seconds,
        heads,
        hidden_cols,
        direct=True,
    )
    return (block_output, input_gradient, stat[0, 0], *results)


def solution(mesh):
    wide, narrow = mesh.shape["wide"], mesh.shape["narrow"]
    body = direct_body if (wide, narrow) == (8, 4) else general_body
    state = (
        P(None, "wide", "narrow"),
        P("narrow", "wide"),
        P(None, "wide", "narrow"),
        P("narrow", "wide"),
        P(),
        P(None, "wide"),
    )
    rows = P("wide", None)
    return jax.shard_map(
        functools.partial(body, wide, narrow),
        mesh=mesh,
        in_specs=(rows, rows, rows, *state, *state, *state),
        out_specs=(rows, rows, P(), *state, *state, *state),
        check_vma=False,
    )
```

```python
import functools

import jax
import jax.numpy as jnp
from jax import lax
from jax.experimental import pallas as pl
from jax.experimental.pallas import tpu as pltpu
from jax.sharding import PartitionSpec as P

DH = 64
STEP = 10
LANES = 128
MESH = pl.DeviceIdType.MESH
F32 = jnp.float32
BF16 = jnp.bfloat16
ANY = pl.ANY

bucket_edges = (12, 16, 23, 32, 46, 64, 91)
norm_eps = 1e-06
clip_limit = 1.0
beta_one = 0.9
beta_two = 0.999
adam_eps = 1e-08
step_rates = (0.06, 0.3, 0.07, 0.06, 1.0, 0.3)
decay_rates = (0.01, 0.01, 0.01, 0.01, 0.0, 0.0)
masked_score = -1000000000.0
VMEM_LIMIT = 58 << 20

NN = (((1,), (0,)), ((), ()))
NT = (((1,), (1,)), ((), ()))
TN = (((0,), (0,)), ((), ()))


def mm(left, right, dims=NN):
    return lax.dot_general(left, right, dims, preferred_element_type=F32)


def bucket_of(offsets):
    distance = jnp.abs(offsets)
    far_bucket = 8 + sum(((distance >= threshold).astype(jnp.int32) for threshold in bucket_edges))
    return jnp.where(distance < 8, distance, far_bucket) + 16 * (offsets > 0).astype(jnp.int32)


def rms_scale(values):
    return lax.rsqrt(jnp.mean(values * values, axis=-1, keepdims=True) + norm_eps)


def norm_back(values, scale_vec, gain_vec, upstream):
    weighted = upstream * gain_vec
    inner_mean = jnp.mean(weighted * values, axis=-1, keepdims=True)
    return scale_vec * weighted - values * (scale_vec * scale_vec * scale_vec) * inner_mean


def adam_update(weight, moment_one, moment_two, gradient, step_rate, decay_rate):
    new_first = beta_one * moment_one + (1.0 - beta_one) * gradient
    new_second = beta_two * moment_two + (1.0 - beta_two) * gradient * gradient
    first_hat = new_first / (1.0 - beta_one**STEP)
    second_hat = new_second / (1.0 - beta_two**STEP)
    new_weight = weight - step_rate * (
        first_hat / (jnp.sqrt(second_hat) + adam_eps) + decay_rate * weight
    )
    return (new_weight, new_first, new_second)


def fold_rows(values):
    rows, cols = values.shape
    return jnp.sum(values.reshape(rows // 8, 8, cols), axis=0)


def start_rows(pieces, target, offs_ref, sems):
    copies = []
    for at, piece in enumerate(pieces):
        rows = piece.shape[0]
        begin = pl.multiple_of(offs_ref[at], 16)
        copies.append(
            pltpu.make_async_copy(piece, target.at[pl.ds(begin, rows)], sems.at[at])
        )
    for copy in copies:
        copy.start()
    return copies


def segments(index, ends_ref, buffer, slots):
    total = jnp.zeros(index.shape, jnp.int32)
    for slot in range(slots):
        total = total + (index >= ends_ref[buffer, slot]).astype(jnp.int32)
    return total


def params(**more):
    return pltpu.CompilerParams(vmem_limit_bytes=VMEM_LIMIT, **more)


def attend_kernel(
    buffer, slots, heads, count, ends_ref, offs_ref, x_ref, strip_ref, *refs
):
    pieces = refs[:count]
    normed_ref, qkv_ref, att_ref, log_ref, gains_ref, wbuf, qs, ks, vs, os, sems = refs[count:]
    length, width = x_ref.shape
    head_cols = heads * DH
    copies = start_rows(pieces, wbuf, offs_ref, sems)
    for copy in copies:
        copy.wait()
    gain_cols = wbuf[:, 4 * LANES :].astype(F32).T
    first = 3 * head_cols - 4 * LANES
    gains = gain_cols[first : first + 8]
    gains_ref[...] = gains
    gain_one = gains[0:1]
    step = 256

    @pl.loop(0, length // step)
    def _(block):
        rows = pl.ds(pl.multiple_of(block * step, step), step)
        values = x_ref[rows].astype(F32)
        normed = (values * rms_scale(values) * gain_one).astype(BF16)
        normed_ref[rows] = normed
        qkv = mm(normed, wbuf[...]).astype(BF16)
        qkv_ref[rows] = qkv[:, : 3 * head_cols]
        for h in range(heads):
            qs[h, rows] = qkv[:, h * DH : (h + 1) * DH]
            ks[h, rows] = qkv[:, head_cols + h * DH : head_cols + (h + 1) * DH]
            vs[h, rows] = qkv[:, 2 * head_cols + h * DH : 2 * head_cols + (h + 1) * DH]

    blocks = length // LANES
    seg_keys = segments(
        lax.broadcasted_iota(jnp.int32, (1, length), 1), ends_ref, buffer, slots
    )

    @pl.loop(0, blocks)
    def _(block):
        begin = pl.multiple_of(block * LANES, LANES)
        rows = pl.ds(begin, LANES)
        window = pl.ds(pl.multiple_of((blocks - 1 - block) * LANES, LANES), length)
        seg_rows = segments(
            lax.broadcasted_iota(jnp.int32, (LANES, 1), 0) + begin, ends_ref, buffer, slots
        )
        same = seg_rows == seg_keys
        lane = lax.broadcasted_iota(jnp.int32, (LANES, LANES), 1)
        logs = jnp.zeros((LANES, LANES), F32)
        for h in range(heads):
            scores = mm(qs[h, rows], ks[h], NT) + strip_ref[h, :, window]
            scores = jnp.where(same, scores, masked_score)
            row_max = jnp.max(scores, axis=1, keepdims=True)
            raised = jnp.exp(scores - row_max)
            total = jnp.sum(raised, axis=1, keepdims=True)
            probs = (raised * (1.0 / total)).astype(BF16)
            os[h, rows] = mm(probs, vs[h]).astype(BF16)
            logs = jnp.where(lane == h, row_max + jnp.log(total), logs)
        log_ref[rows] = logs

    att_ref[...] = jnp.concatenate([os[h] for h in range(heads)], axis=1)


def attend(buffer, ends, offs, x, strip, pieces, length, heads):
    width = x.shape[1]
    count = len(pieces)
    cols = pieces[0].shape[1]
    head_cols = heads * DH
    whole = lambda i, *_: (0, 0)
    spec = pltpu.PrefetchScalarGridSpec(
        num_scalar_prefetch=2,
        grid=(1,),
        in_specs=[
            pl.BlockSpec((length, width), lambda i, *_: (buffer, 0)),
            pl.BlockSpec(strip.shape, lambda i, *_: (0, 0, 0)),
        ]
        + [pl.BlockSpec(memory_space=ANY)] * count,
        out_specs=[
            pl.BlockSpec((length, width), whole),
            pl.BlockSpec((length, 3 * head_cols), whole),
            pl.BlockSpec((length, head_cols), whole),
            pl.BlockSpec((length, LANES), whole),
            pl.BlockSpec((8, width), whole),
        ],
        scratch_shapes=[
            pltpu.VMEM((width, cols), BF16),
            pltpu.VMEM((heads, length, DH), BF16),
            pltpu.VMEM((heads, length, DH), BF16),
            pltpu.VMEM((heads, length, DH), BF16),
            pltpu.VMEM((heads, length, DH), BF16),
            pltpu.SemaphoreType.DMA((count,)),
        ],
    )
    flops = 2 * length * (width * cols + 2 * heads * DH * length)
    return pl.pallas_call(
        functools.partial(attend_kernel, buffer, ends.shape[1], heads, count),
        grid_spec=spec,
        out_shape=[
            jax.ShapeDtypeStruct((length, width), BF16),
            jax.ShapeDtypeStruct((length, 3 * head_cols), BF16),
            jax.ShapeDtypeStruct((length, head_cols), BF16),
            jax.ShapeDtypeStruct((length, LANES), F32),
            jax.ShapeDtypeStruct((8, width), F32),
        ],
        compiler_params=params(),
        cost_estimate=pl.CostEstimate(
            flops=4 * flops, bytes_accessed=8 << 20, transcendentals=heads * length * length
        ),
        name="attend",
    )(ends, offs, x, strip, *pieces)


def feed_kernel(hidden_cols, counts, order_ref, offs_ref, *refs):
    own, across, beside, diagonal, x_ref, cot_ref, gains_ref = refs[:7]
    at = 7
    groups = []
    for count in counts:
        groups.append(refs[at : at + count])
        at += count
    (
        normed_ref,
        hidden_ref,
        gate_ref,
        ff_send,
        ff_keep,
        dn_send,
        dn_keep,
        middle_keep,
        gain_sum,
        ebuf,
        sbuf,
        oabuf,
        obbuf,
        sems,
    ) = refs[at:]
    step = pl.program_id(0)
    bufs = (oabuf, obbuf, ebuf, sbuf)

    @pl.when(step == 0)
    def _():
        copies = []
        for which, (group, target) in enumerate(zip(groups, bufs)):
            copies += start_rows(group, target, offs_ref, sems.at[which])
        for copy in copies:
            copy.wait()

    cols = own.shape[1]
    upper = order_ref[2] == 0
    pairs = []
    for near, far, weights in ((own, across, oabuf), (beside, diagonal, obbuf)):
        near_sum = mm(near[...], weights[:, :cols], NT)
        far_sum = mm(far[...], weights[:, cols:], NT)
        pairs.append(
            jnp.where(upper, near_sum, far_sum) + jnp.where(upper, far_sum, near_sum)
        )
    swap = order_ref[0] == 0
    attention = jnp.where(swap, pairs[0], pairs[1]) + jnp.where(swap, pairs[1], pairs[0])
    middle = x_ref[...].astype(F32) + attention
    scale_two = rms_scale(middle)
    gain_two = gains_ref[1:2]
    normed = (middle * scale_two * gain_two).astype(BF16)
    normed_ref[...] = normed
    cot = cot_ref[...]
    part = 256
    k0 = 0.7978845608028654
    k1 = 0.044715
    for begin in range(0, hidden_cols, part):
        gate = mm(normed, ebuf[:, begin : begin + part])
        up = mm(normed, ebuf[:, hidden_cols + begin : hidden_cols + begin + part])
        square = gate * gate
        tanh = jnp.tanh(k0 * (gate + k1 * (square * gate)))
        half = 0.5 * (1.0 + tanh)
        active = gate * half
        slope = half + (0.5 * gate) * (1.0 - tanh * tanh) * (k0 + (3.0 * k0 * k1) * square)
        d_hidden = mm(cot, sbuf[:, begin : begin + part])
        hidden_ref[:, begin : begin + part] = (active * up).astype(BF16)
        gate_ref[:, begin : begin + part] = (d_hidden * up * slope).astype(BF16)
        gate_ref[:, hidden_cols + begin : hidden_cols + begin + part] = (
            d_hidden * active
        ).astype(BF16)
    ff = mm(hidden_ref[...], sbuf[...], NT).astype(BF16)
    dn = mm(gate_ref[...], ebuf[...], NT)
    sums = fold_rows(dn * middle * scale_two)
    dn = dn.astype(BF16)

    @pl.when(step == 0)
    def _():
        ff_send[...] = ff
        dn_send[...] = dn
        gain_sum[...] = sums

    @pl.when(step == 1)
    def _():
        ff_keep[...] = ff
        dn_keep[...] = dn
        middle_keep[...] = middle
        gain_sum[...] = gain_sum[...] + sums


def feed(buffer, order, offs, parts, x, cot, gains, groups, length, hidden_cols):
    width = x.shape[1]
    half = length // 2
    cols = parts[0].shape[1]
    counts = [len(group) for group in groups]
    natural = lambda i, order, *_: (order[i], 0)
    rows = lambda i, order, *_: (2 * buffer + order[i], 0)
    whole = lambda i, *_: (0, 0)
    spec = pltpu.PrefetchScalarGridSpec(
        num_scalar_prefetch=2,
        grid=(2,),
        in_specs=[pl.BlockSpec((half, cols), natural)] * 4
        + [pl.BlockSpec((half, width), rows)] * 2
        + [pl.BlockSpec((8, width), whole)]
        + [pl.BlockSpec(memory_space=ANY)] * sum(counts),
        out_specs=[
            pl.BlockSpec((half, width), natural),
            pl.BlockSpec((half, hidden_cols), natural),
            pl.BlockSpec((half, 2 * hidden_cols), natural),
        ]
        + [pl.BlockSpec((half, width), whole)] * 5
        + [pl.BlockSpec((8, width), whole)],
        scratch_shapes=[
            pltpu.VMEM((width, 2 * hidden_cols), BF16),
            pltpu.VMEM((width, hidden_cols), BF16),
            pltpu.VMEM((width, 2 * cols), BF16),
            pltpu.VMEM((width, 2 * cols), BF16),
            pltpu.SemaphoreType.DMA((4, max(counts))),
        ],
    )
    flops = 2 * length * width * (4 * cols + 7 * hidden_cols)
    return pl.pallas_call(
        functools.partial(feed_kernel, hidden_cols, counts),
        grid_spec=spec,
        out_shape=[
            jax.ShapeDtypeStruct((length, width), BF16),
            jax.ShapeDtypeStruct((length, hidden_cols), BF16),
            jax.ShapeDtypeStruct((length, 2 * hidden_cols), BF16),
            jax.ShapeDtypeStruct((half, width), BF16),
            jax.ShapeDtypeStruct((half, width), BF16),
            jax.ShapeDtypeStruct((half, width), BF16),
            jax.ShapeDtypeStruct((half, width), BF16),
            jax.ShapeDtypeStruct((half, width), F32),
            jax.ShapeDtypeStruct((8, width), F32),
        ],
        compiler_params=params(),
        cost_estimate=pl.CostEstimate(
            flops=flops, bytes_accessed=12 << 20, transcendentals=length * hidden_cols
        ),
        name="feed",
    )(order, offs, *parts, x, cot, gains, *[piece for group in groups for piece in group])


def middle_kernel(order_ref, near, far, middle_ref, cot_ref, gains_ref, d_ref, low_ref):
    upstream = near[...].astype(F32) + far[...].astype(F32)
    middle = middle_ref[...]
    d_middle = cot_ref[...].astype(F32) + norm_back(
        middle, rms_scale(middle), gains_ref[1:2], upstream
    )
    d_ref[...] = d_middle
    low_ref[...] = d_middle.astype(BF16)


def input_kernel(order_ref, near, far, x_ref, d_ref, gains_ref, out_ref):
    upstream = near[...].astype(F32) + far[...].astype(F32)
    values = x_ref[...].astype(F32)
    out_ref[...] = (
        d_ref[...] + norm_back(values, rms_scale(values), gains_ref[0:1], upstream)
    ).astype(BF16)


def output_kernel(order_ref, near, far, middle_ref, out_ref):
    out_ref[...] = (
        middle_ref[...] + (near[...].astype(F32) + far[...].astype(F32)).astype(BF16).astype(F32)
    ).astype(BF16)


def half_call(kernel, name, buffer, order, arrays, placed, outs, gains=None):
    half, width = arrays[0].shape
    steps = 3
    block = half // steps
    mine = lambda i, *_: (i, 0)
    rows = lambda i, order, *_: ((2 * buffer + order[1]) * steps + i, 0)
    in_specs = [
        pl.BlockSpec((block, width), rows if at in placed else mine)
        for at in range(len(arrays))
    ]
    operands = list(arrays)
    if gains is not None:
        in_specs.append(pl.BlockSpec((8, width), lambda i, *_: (0, 0)))
        operands.append(gains)
    return pl.pallas_call(
        kernel,
        grid_spec=pltpu.PrefetchScalarGridSpec(
            num_scalar_prefetch=1,
            grid=(steps,),
            in_specs=in_specs,
            out_specs=[pl.BlockSpec((block, width), mine) for _ in outs],
        ),
        out_shape=[jax.ShapeDtypeStruct((half, width), kind) for kind in outs],
        compiler_params=params(),
        cost_estimate=pl.CostEstimate(
            flops=20 * half * width, bytes_accessed=12 * half * width, transcendentals=0
        ),
        name=name,
    )(order, *operands)


def back_kernel(buffer, slots, heads, counts, ends_ref, offs_ref, order_ref, *refs):
    near, far, qkv_ref, log_ref, strip_ref, x_ref = refs[:6]
    at = 6
    o_pieces = refs[at : at + counts[0]]
    at += counts[0]
    p_pieces = refs[at : at + counts[1]]
    at += counts[1]
    (
        low_ref,
        dqkv_ref,
        dn_send,
        dn_keep,
        gain_sum,
        dstrip,
        wbuf,
        obuf,
        qs,
        ks,
        vs,
        gs,
        qt,
        gt,
        dkt,
        dvt,
        dq,
        sems,
    ) = refs[at:]
    length = qkv_ref.shape[0]
    half = length // 2
    head_cols = heads * DH
    o_copies = start_rows(o_pieces, obuf, offs_ref, sems.at[0])
    p_copies = start_rows(p_pieces, wbuf, offs_ref, sems.at[1])
    mine = pl.ds(pl.multiple_of(order_ref[1] * half, LANES), half)
    other = pl.ds(pl.multiple_of(order_ref[0] * half, LANES), half)
    low_ref[mine] = near[...]
    low_ref[other] = far[...]
    for h in range(heads):
        qs[h] = qkv_ref[:, h * DH : (h + 1) * DH]
        ks[h] = qkv_ref[:, head_cols + h * DH : head_cols + (h + 1) * DH]
        vs[h] = qkv_ref[:, 2 * head_cols + h * DH : 2 * head_cols + (h + 1) * DH]
        qt[h] = qs[h].T
    dstrip[...] = jnp.zeros_like(dstrip)
    dkt[...] = jnp.zeros_like(dkt)
    dvt[...] = jnp.zeros_like(dvt)
    for copy in o_copies + p_copies:
        copy.wait()
    grads = mm(low_ref[...], obuf[:, :head_cols]).astype(BF16)
    for h in range(heads):
        gs[h] = grads[:, h * DH : (h + 1) * DH]
        gt[h] = gs[h].T
    blocks = length // LANES
    seg_keys = segments(
        lax.broadcasted_iota(jnp.int32, (1, length), 1), ends_ref, buffer, slots
    )

    @pl.loop(0, blocks)
    def _(block):
        begin = pl.multiple_of(block * LANES, LANES)
        rows = pl.ds(begin, LANES)
        window = pl.ds(pl.multiple_of((blocks - 1 - block) * LANES, LANES), length)
        seg_rows = segments(
            lax.broadcasted_iota(jnp.int32, (LANES, 1), 0) + begin, ends_ref, buffer, slots
        )
        same = seg_rows == seg_keys
        logs = log_ref[rows]
        for h in range(heads):
            scores = mm(qs[h, rows], ks[h], NT) + strip_ref[h, :, window]
            scores = jnp.where(same, scores, masked_score)
            probs = jnp.exp(scores - logs[:, h : h + 1])
            d_probs = mm(gs[h, rows], vs[h], NT)
            inner = jnp.sum(probs * d_probs, axis=1, keepdims=True)
            d_scores = (probs * (d_probs - inner)).astype(BF16)
            dstrip[h, :, window] = dstrip[h, :, window] + d_scores.astype(F32)
            dq[h, rows] = mm(d_scores, ks[h]).astype(BF16)
            dkt[h] = dkt[h] + mm(qt[h, :, rows], d_scores)
            dvt[h] = dvt[h] + mm(gt[h, :, rows], probs.astype(BF16))

    outs = [dq[h] for h in range(heads)]
    outs += [dkt[h].T.astype(BF16) for h in range(heads)]
    outs += [dvt[h].T.astype(BF16) for h in range(heads)]
    dqkv_ref[...] = jnp.concatenate(outs, axis=1)
    sums = []
    for target, which in ((dn_send, other), (dn_keep, mine)):
        dn = mm(dqkv_ref[which], wbuf[:, : 3 * head_cols], NT)
        values = x_ref[which].astype(F32)
        sums.append(fold_rows(dn * values * rms_scale(values)))
        target[...] = dn.astype(BF16)
    gain_sum[...] = sums[0] + sums[1]


def back(buffer, ends, offs, order, near, far, qkv, logs, strip, x, o_pieces, p_pieces, heads):
    length = qkv.shape[0]
    half = length // 2
    width = x.shape[1]
    head_cols = heads * DH
    counts = (len(o_pieces), len(p_pieces))
    whole = lambda i, *_: (0, 0)
    whole3 = lambda i, *_: (0, 0, 0)
    spec = pltpu.PrefetchScalarGridSpec(
        num_scalar_prefetch=3,
        grid=(1,),
        in_specs=[
            pl.BlockSpec((half, width), whole),
            pl.BlockSpec((half, width), whole),
            pl.BlockSpec(qkv.shape, whole),
            pl.BlockSpec(logs.shape, whole),
            pl.BlockSpec(strip.shape, whole3),
            pl.BlockSpec((length, width), lambda i, *_: (buffer, 0)),
        ]
        + [pl.BlockSpec(memory_space=ANY)] * sum(counts),
        out_specs=[
            pl.BlockSpec((length, width), whole),
            pl.BlockSpec((length, 3 * head_cols), whole),
            pl.BlockSpec((half, width), whole),
            pl.BlockSpec((half, width), whole),
            pl.BlockSpec((8, width), whole),
            pl.BlockSpec(strip.shape, whole3),
        ],
        scratch_shapes=[
            pltpu.VMEM((width, p_pieces[0].shape[1]), BF16),
            pltpu.VMEM((width, o_pieces[0].shape[1]), BF16),
            pltpu.VMEM((heads, length, DH), BF16),
            pltpu.VMEM((heads, length, DH), BF16),
            pltpu.VMEM((heads, length, DH), BF16),
            pltpu.VMEM((heads, length, DH), BF16),
            pltpu.VMEM((heads, DH, length), BF16),
            pltpu.VMEM((heads, DH, length), BF16),
            pltpu.VMEM((heads, DH, length), F32),
            pltpu.VMEM((heads, DH, length), F32),
            pltpu.VMEM((heads, length, DH), BF16),
            pltpu.SemaphoreType.DMA((2, max(counts))),
        ],
    )
    return pl.pallas_call(
        functools.partial(back_kernel, buffer, ends.shape[1], heads, counts),
        grid_spec=spec,
        out_shape=[
            jax.ShapeDtypeStruct((length, width), BF16),
            jax.ShapeDtypeStruct((length, 3 * head_cols), BF16),
            jax.ShapeDtypeStruct((half, width), BF16),
            jax.ShapeDtypeStruct((half, width), BF16),
            jax.ShapeDtypeStruct((8, width), F32),
            jax.ShapeDtypeStruct(strip.shape, F32),
        ],
        compiler_params=params(),
        cost_estimate=pl.CostEstimate(
            flops=40 * heads * DH * length * length,
            bytes_accessed=16 << 20,
            transcendentals=heads * length * length,
        ),
        name="back",
    )(ends, offs, order, near, far, qkv, logs, strip, x, *o_pieces, *p_pieces)


def scatter_rows(total, offs_ref, evens, odds):
    rows = evens[0].shape[0]
    for at in range(2 * len(evens)):
        begin = pl.multiple_of(offs_ref[at], 8)
        block = total[pl.ds(begin, rows)]
        if at % 2:
            odds[at // 2][...] = block.astype(BF16)
        else:
            evens[at // 2][...] = block


def feed_grad_kernel(count, hidden_cols, offs_ref, *refs):
    buffers = 2
    normed = refs[:buffers]
    gates = refs[buffers : 2 * buffers]
    hiddens = refs[2 * buffers : 3 * buffers]
    cot_ref = refs[3 * buffers]
    outs = refs[3 * buffers + 1 : -1]
    total = refs[-1]
    length = normed[0].shape[0]
    width = normed[0].shape[1]
    part = 256
    for begin in range(0, width, part):
        cols = slice(begin, begin + part)
        total[cols, : 2 * hidden_cols] = mm(normed[0][:, cols], gates[0][...], TN) + mm(
            normed[1][:, cols], gates[1][...], TN
        )
        total[cols, 2 * hidden_cols :] = mm(
            cot_ref[:length, cols], hiddens[0][...], TN
        ) + mm(cot_ref[length:, cols], hiddens[1][...], TN)
    if count > 1:
        scatter_rows(total, offs_ref, outs[: count // 2], outs[count // 2 :])
    else:
        outs[0][...] = total[...]


def attend_grad_kernel(count, heads, offs_ref, *refs):
    buffers = 2
    normed = refs[:buffers]
    dqkv = refs[buffers : 2 * buffers]
    lows = refs[2 * buffers : 3 * buffers]
    atts = refs[3 * buffers : 4 * buffers]
    sums_ref = refs[4 * buffers]
    outs = refs[4 * buffers + 1 : -1]
    total = refs[-1]
    width = normed[0].shape[1]
    head_cols = heads * DH
    qkv_cols = 3 * head_cols
    part = 256
    rows = lax.broadcasted_iota(jnp.int32, (LANES, width), 0)
    first = sums_ref[0] + sums_ref[1]
    second = sums_ref[2] + sums_ref[3]
    gain_rows = jnp.where(
        rows == DH,
        jnp.sum(first, axis=0, keepdims=True),
        jnp.where(rows == DH + 1, jnp.sum(second, axis=0, keepdims=True), 0.0),
    )
    gain_cols = gain_rows.T
    for begin in range(0, width, part):
        cols = slice(begin, begin + part)
        total[cols, :qkv_cols] = mm(normed[0][:, cols], dqkv[0][...], TN) + mm(
            normed[1][:, cols], dqkv[1][...], TN
        )
        total[cols, qkv_cols : qkv_cols + DH] = gain_cols[cols, DH:]
        total[cols, qkv_cols + DH : qkv_cols + DH + head_cols] = mm(
            lows[0][:, cols], atts[0][...], TN
        ) + mm(lows[1][:, cols], atts[1][...], TN)
    if count > 1:
        scatter_rows(total, offs_ref, outs[: count // 2], outs[count // 2 :])
    else:
        outs[0][...] = total[...]


def grad_call(kernel, name, offs, operands, width, cols, count, rows, flops):
    vmem = pl.BlockSpec(memory_space=pltpu.VMEM)
    if count > 1:
        shapes = [jax.ShapeDtypeStruct((rows, cols), F32)] * (count // 2)
        shapes += [jax.ShapeDtypeStruct((rows, cols), BF16)] * (count // 2)
    else:
        shapes = [jax.ShapeDtypeStruct((width, cols), F32)]
    return pl.pallas_call(
        kernel,
        in_specs=[pl.BlockSpec(memory_space=pltpu.SMEM)] + [vmem] * len(operands),
        out_specs=[vmem] * len(shapes),
        out_shape=shapes,
        scratch_shapes=[pltpu.VMEM((width, cols), F32)],
        compiler_params=params(),
        cost_estimate=pl.CostEstimate(flops=2 * flops, bytes_accessed=14 << 20, transcendentals=0),
        name=name,
    )(offs, *operands)


def bucket_kernel(heads, near_ref, far_ref, out_ref):
    lanes = near_ref.shape[2]
    blocks = (lanes // LANES + 1) // 2
    begin = (blocks - 2) * LANES
    end = begin + 3 * LANES
    rows = lax.broadcasted_iota(jnp.int32, (LANES, 3 * LANES), 0)
    ids = bucket_of(
        lax.broadcasted_iota(jnp.int32, (LANES, 3 * LANES), 1) - LANES - rows
    )
    lane = lax.broadcasted_iota(jnp.int32, (1, LANES), 1)
    out = jnp.zeros((1, LANES), F32)
    for h in range(heads):
        strip = near_ref[h] + far_ref[h]
        left = jnp.sum(jnp.sum(strip[:, :begin], axis=0, keepdims=True), axis=1, keepdims=True)
        right = jnp.sum(jnp.sum(strip[:, end:], axis=0, keepdims=True), axis=1, keepdims=True)
        out = out + jnp.where(lane == h * 32 + 15, left, 0.0)
        out = out + jnp.where(lane == h * 32 + 31, right, 0.0)
        middle = strip[:, begin:end]
        for b in range(32):
            if b == 16:
                continue
            part = jnp.sum(jnp.where(ids == b, middle, 0.0), axis=0, keepdims=True)
            part = jnp.sum(part, axis=1, keepdims=True)
            out = out + jnp.where(lane == h * 32 + b, part, 0.0)
    out_ref[...] = jnp.broadcast_to(out, (8, LANES))


def norm_kernel(wide, narrow, lists, gain_at, *refs):
    at = 0
    groups = []
    for count in lists:
        groups.append(refs[at : at + count])
        at += count
    bucket_ref = refs[at]
    outs = refs[at + 1 : at + 1 + len(lists)]
    stat_ref, gain_ref, table_ref, block, inbox, padded, send_sems, recv_sems = refs[
        at + 1 + len(lists) :
    ]
    total = wide * narrow
    w = lax.axis_index("wide")
    n = lax.axis_index("narrow")
    me = w * narrow + n
    barrier = pltpu.get_barrier_semaphore()

    @pl.loop(1, total)
    def _(k):
        peer = (me + k) % total
        pl.semaphore_signal(
            barrier, inc=1, device_id=(peer // narrow, peer % narrow), device_id_type=MESH
        )

    squares = jnp.zeros((8, LANES), F32)
    for which, (group, out) in enumerate(zip(groups, outs)):
        value = group[0][...].astype(F32)
        for more in group[1:]:
            value = value + more[...].astype(F32)
        out[...] = value
        squared = value * value
        if which == 0:
            lane = lax.broadcasted_iota(jnp.int32, value.shape, 1)
            inside = (lane >= gain_at) & (lane < gain_at + DH)
            squared = jnp.where(inside, 0.0, squared)
        squared = jnp.sum(squared, axis=1, keepdims=True)
        squares = squares + jnp.sum(squared, axis=0, keepdims=True)
    rows = outs[0].shape[0]
    low = gain_at // LANES * LANES
    padded[...] = jnp.zeros_like(padded)
    padded[0:rows] = outs[0][:, low : low + LANES]
    turned = padded[...].T
    row = lax.broadcasted_iota(jnp.int32, (8, LANES), 0)
    here = gain_at - low
    mine = jnp.where(row == 0, squares, 0.0)
    mine = jnp.where(row == 1, turned[here : here + 1], mine)
    mine = jnp.where(row == 2, turned[here + 1 : here + 2], mine)
    mine = jnp.where(row == 3, bucket_ref[...], mine)
    block[...] = mine
    inbox[me] = mine
    pl.semaphore_wait(barrier, total - 1)

    @pl.loop(1, total)
    def _(k):
        peer = (me + k) % total
        pltpu.make_async_remote_copy(
            src_ref=block,
            dst_ref=inbox.at[me],
            send_sem=send_sems.at[k],
            recv_sem=recv_sems.at[total - k],
            device_id=(peer // narrow, peer % narrow),
            device_id_type=MESH,
        ).start()

    @pl.loop(1, total)
    def _(k):
        peer = (me + k) % total
        copy = pltpu.make_async_remote_copy(
            src_ref=block,
            dst_ref=inbox.at[peer],
            send_sem=send_sems.at[k],
            recv_sem=recv_sems.at[k],
            device_id=(peer // narrow, peer % narrow),
            device_id_type=MESH,
        )
        copy.wait_send()
        copy.wait_recv()

    columns = [jnp.zeros((8, LANES), F32) for _ in range(narrow)]
    gain_square = jnp.zeros((8, LANES), F32)
    square_total = jnp.zeros((8, LANES), F32)
    for a in range(wide):
        gains = jnp.zeros((8, LANES), F32)
        for b in range(narrow):
            got = inbox[a * narrow + b]
            gains = gains + got
            columns[b] = columns[b] + got
        square_total = square_total + gains
        gain_square = gain_square + gains * gains
    own = inbox[w * narrow]
    for b in range(1, narrow):
        own = own + inbox[w * narrow + b]
    gain_ref[...] = own
    pick = (row == 1) | (row == 2)
    gain_square = jnp.where(pick, gain_square, 0.0)
    norm_square = square_total[0:1, 0:1] + jnp.sum(
        jnp.sum(gain_square, axis=0, keepdims=True), axis=1, keepdims=True
    )
    heads = LANES // 32 - 1
    lane = lax.broadcasted_iota(jnp.int32, (32, LANES), 1)
    depth = lax.broadcasted_iota(jnp.int32, (32, LANES), 0)
    table = jnp.zeros((32, LANES), F32)
    for b in range(narrow):
        line = columns[b][3:4]
        norm_square = norm_square + jnp.sum(line * line, axis=1, keepdims=True)
        for h in range(heads):
            column = jnp.sum(
                jnp.where(lane == depth + 32 * h, line, 0.0), axis=1, keepdims=True
            )
            table = jnp.where(lane == b * heads + h, column, table)
    table_ref[...] = table
    global_norm = jnp.sqrt(norm_square)
    factor = jnp.minimum(1.0, clip_limit / (global_norm + 1e-06))
    stat_ref[...] = jnp.where(row == 0, global_norm, factor)


def norm_call(wide, narrow, groups, bucket, gain_at):
    vmem = pl.BlockSpec(memory_space=pltpu.VMEM)
    lists = tuple(len(group) for group in groups)
    total = wide * narrow
    operands = [piece for group in groups for piece in group] + [bucket]
    return pl.pallas_call(
        functools.partial(norm_kernel, wide, narrow, lists, gain_at),
        in_specs=[vmem] * len(operands),
        out_specs=[vmem] * (len(lists) + 3),
        out_shape=[jax.ShapeDtypeStruct(group[0].shape, F32) for group in groups]
        + [
            jax.ShapeDtypeStruct((8, LANES), F32),
            jax.ShapeDtypeStruct((8, LANES), F32),
            jax.ShapeDtypeStruct((32, LANES), F32),
        ],
        scratch_shapes=[
            pltpu.VMEM((8, LANES), F32),
            pltpu.VMEM((total, 8, LANES), F32),
            pltpu.VMEM((LANES, LANES), F32),
            pltpu.SemaphoreType.DMA((total,)),
            pltpu.SemaphoreType.DMA((total,)),
        ],
        compiler_params=params(collective_id=0, has_side_effects=True),
        cost_estimate=pl.CostEstimate(flops=1 << 20, bytes_accessed=4 << 20, transcendentals=0),
        name="norm",
    )(*operands)


def adam_kernel(heads, hidden_cols, parts, att_ref, feed_ref, gain_ref, table_ref, stat_ref, *refs):
    weights, firsts, seconds = refs[:6], refs[6:12], refs[12:18]
    outs = refs[18:36]
    o_pad, s_pad = refs[36:]
    factor = stat_ref[1:2, 0:1]
    head_cols = heads * DH
    rows = att_ref.shape[0]
    gain_at = 3 * head_cols

    def update(which, index, gradient):
        results = adam_update(
            weights[which][index],
            firsts[which][index],
            seconds[which][index],
            factor * gradient,
            step_rates[which],
            decay_rates[which],
        )
        for at in range(3):
            outs[6 * at + which][index] = results[at]

    for i in range(3):
        update(0, i, att_ref[:, i * head_cols : (i + 1) * head_cols])
    part = hidden_cols // parts
    for j in range(parts):
        span = slice(j * part, (j + 1) * part)
        for i in range(2):
            begin = (3 * j + i) * part if parts > 1 else i * part
            update(2, (i, slice(None), span), feed_ref[:, begin : begin + part])
    o_pad[...] = jnp.zeros_like(o_pad)
    s_pad[...] = jnp.zeros_like(s_pad)
    o_pad[0:rows] = att_ref[:, gain_at + DH :]
    for j in range(parts):
        begin = (3 * j + 2) * part
        s_pad[0:rows, j * part : (j + 1) * part] = feed_ref[:, begin : begin + part]
    update(1, slice(None), o_pad[...].T[:head_cols, :rows])
    update(3, slice(None), s_pad[...].T[:, :rows])
    columns = weights[4].shape[1]
    update(4, slice(None), table_ref[:, :columns])
    update(5, slice(None), gain_ref[1:3, :rows])


def adam_call(
    att, feed_grad, gain, table, stat, params_in, firsts, seconds, heads, hidden_cols, direct=False
):
    vmem = pl.BlockSpec(memory_space=pltpu.VMEM)
    operands = [att, feed_grad, gain, table, stat, *params_in, *firsts, *seconds]
    pad_cols = att.shape[1] - (3 * heads * DH + DH)
    return pl.pallas_call(
        functools.partial(adam_kernel, heads, hidden_cols, 2 if direct else 1),
        in_specs=[vmem] * len(operands),
        out_specs=[vmem] * 18,
        out_shape=[jax.ShapeDtypeStruct(a.shape, F32) for a in params_in] * 3,
        scratch_shapes=[
            pltpu.VMEM((LANES, pad_cols), F32),
            pltpu.VMEM((LANES, hidden_cols), F32),
        ],
        compiler_params=params(),
        cost_estimate=pl.CostEstimate(flops=4 << 20, bytes_accessed=8 << 20, transcendentals=0),
        name="adam",
    )(*operands)


def place_kernel(offs_ref, *refs):
    step = pl.program_id(0)
    for at, piece in enumerate(refs[:-1]):

        @pl.when(step == at)
        def _(piece=piece):
            refs[-1][...] = piece[...]


def place(pieces, offs, rows):
    half, width = pieces[0].shape
    count = len(pieces)
    return pl.pallas_call(
        place_kernel,
        grid_spec=pltpu.PrefetchScalarGridSpec(
            num_scalar_prefetch=1,
            grid=(count,),
            in_specs=[pl.BlockSpec((half, width), lambda i, *_: (0, 0))] * count,
            out_specs=pl.BlockSpec((half, width), lambda i, offs: (offs[i] // half, 0)),
        ),
        out_shape=jax.ShapeDtypeStruct((rows, width), pieces[0].dtype),
        compiler_params=params(),
        cost_estimate=pl.CostEstimate(
            flops=0, bytes_accessed=4 * rows * width, transcendentals=0
        ),
        name="place",
    )(offs, *pieces)


def bias_strip(bucket_bias, n, heads, length):
    table = lax.dynamic_slice_in_dim(bucket_bias, n * heads, heads, 1).T
    blocks = length // LANES
    near_r = (
        jnp.arange(3 * LANES, dtype=jnp.int32)[None, :]
        - LANES
        - jnp.arange(LANES, dtype=jnp.int32)[:, None]
    )
    near_ids = bucket_of(near_r)
    near = sum(
        jnp.where(near_ids == b, table[:, b][:, None, None], 0.0) for b in range(32) if b != 16
    )
    far_shape = (heads, LANES, (blocks - 2) * LANES)
    return jnp.concatenate(
        [
            jnp.broadcast_to(table[:, 15][:, None, None], far_shape),
            near,
            jnp.broadcast_to(table[:, 31][:, None, None], far_shape),
        ],
        axis=2,
    )


def general_body(wide, narrow, *arguments):
    (
        block_input,
        cotangent,
        lengths,
        project_weight,
        output_weight,
        expand_weight,
        shrink_weight,
        bucket_bias,
        norm_gains,
    ) = arguments[:9]
    firsts = arguments[9:15]
    seconds = arguments[15:21]
    tokens, width = block_input.shape
    buffers = lengths.shape[0]
    length = tokens // buffers
    rows = norm_gains.shape[1]
    head_cols = project_weight.shape[2]
    heads = head_cols // DH
    hidden_cols = expand_weight.shape[2]
    w = lax.axis_index("wide")
    n = lax.axis_index("narrow")
    core = n % 2

    def swap(value, wide_mask, narrow_mask):
        pairs = [
            (a * narrow + b, (a ^ wide_mask) * narrow + (b ^ narrow_mask))
            for a in range(wide)
            for b in range(narrow)
        ]
        return lax.ppermute(value, ("wide", "narrow"), pairs)

    def gather(piece):
        return [lax.all_gather(piece, "wide", axis=0, tiled=True)]

    def reduce_wide(outs):
        return [lax.psum_scatter(outs[0], "wide", scatter_dimension=0, tiled=True)]

    offs = jnp.zeros((1,), jnp.int32)
    order = jnp.stack([1 - core, core, n // 2])

    p_piece = jnp.concatenate(
        [
            project_weight[0],
            project_weight[1],
            project_weight[2],
            norm_gains.T,
            jnp.zeros((rows, DH - 2), F32),
        ],
        axis=1,
    ).astype(BF16)
    p_pieces = gather(p_piece)
    o_piece = output_weight.astype(BF16).T
    o_pair = jnp.concatenate([o_piece, swap(o_piece, 0, 2)], axis=1)
    oa_pieces = gather(o_pair)
    ob_pieces = [swap(piece, 0, 1) for piece in oa_pieces]
    e_pieces = gather(
        jnp.concatenate([expand_weight[0], expand_weight[1]], axis=1).astype(BF16)
    )
    s_pieces = gather(shrink_weight.astype(BF16).T)

    ends = jnp.cumsum(lengths, axis=1)
    strip = bias_strip(bucket_bias, n, heads, length)

    normed_one, qkv, atts, logs, fours = [], [], [], [], []
    for b in range(buffers):
        normed, rows_b, att, log, gains = attend(
            b, ends, offs, block_input, strip, p_pieces, length, heads
        )
        normed_one.append(normed)
        qkv.append(rows_b)
        atts.append(att)
        logs.append(log)
        across = swap(att, 0, 2)
        fours.append((att, across, swap(att, 0, 1), swap(across, 0, 1)))

    def core_sum(kept, sent):
        return (kept.astype(F32) + swap(sent, 0, 1).astype(F32)).astype(BF16)

    normed_two, hiddens, gates, middles, ff_sums, dn_sums, sums_two = [], [], [], [], [], [], []
    for b in range(buffers):
        normed, hidden, gate, ff_send, ff_keep, dn_send, dn_keep, middle, sums = feed(
            b,
            order,
            offs,
            fours[b],
            block_input,
            cotangent,
            gains,
            (oa_pieces, ob_pieces, e_pieces, s_pieces),
            length,
            hidden_cols,
        )
        normed_two.append(normed)
        hiddens.append(hidden)
        gates.append(gate)
        middles.append(middle)
        sums_two.append(sums)
        dn_sums.append(core_sum(dn_keep, dn_send))
        ff_sums.append(core_sum(ff_keep, ff_send))

    d_middles, lows = [], []
    for b in range(buffers):
        d_middle, low = half_call(
            middle_kernel,
            "middle",
            b,
            order,
            [dn_sums[b], swap(dn_sums[b], 0, 2), middles[b], cotangent],
            (3,),
            (F32, BF16),
            gains,
        )
        d_middles.append(d_middle)
        lows.append((low, swap(low, 0, 1)))

    count = 1
    feed_outs = grad_call(
        functools.partial(feed_grad_kernel, count, hidden_cols),
        "feed_grad",
        offs,
        [*normed_two, *gates, *hiddens, cotangent],
        width,
        3 * hidden_cols,
        count,
        rows,
        2 * tokens * width * 3 * hidden_cols,
    )
    feed_group = reduce_wide(feed_outs)

    low_full, dqkv, dn_one, sums_one, strips = [], [], [], [], []
    for b in range(buffers):
        low, grads, dn_send, dn_keep, sums, dstrip = back(
            b,
            ends,
            offs,
            order,
            lows[b][0],
            lows[b][1],
            qkv[b],
            logs[b],
            strip,
            block_input,
            oa_pieces,
            p_pieces,
            heads,
        )
        low_full.append(low)
        dqkv.append(grads)
        sums_one.append(sums)
        strips.append(dstrip)
        dn_one.append(core_sum(dn_keep, dn_send))

    gain_at = 3 * head_cols
    att_outs = grad_call(
        functools.partial(attend_grad_kernel, count, heads),
        "attend_grad",
        offs,
        [*normed_one, *dqkv, *low_full, *atts, jnp.stack(sums_one + sums_two)],
        width,
        gain_at + DH + head_cols,
        count,
        rows,
        2 * tokens * width * 4 * head_cols,
    )
    att_group = reduce_wide(att_outs)
    vmem = pl.BlockSpec(memory_space=pltpu.VMEM)
    bucket = pl.pallas_call(
        functools.partial(bucket_kernel, heads),
        in_specs=[vmem, vmem],
        out_specs=vmem,
        out_shape=jax.ShapeDtypeStruct((8, LANES), F32),
        compiler_params=params(),
        cost_estimate=pl.CostEstimate(flops=8 << 20, bytes_accessed=4 << 20, transcendentals=0),
        name="bucket",
    )(*strips)

    half_offs = jnp.stack(
        [
            b * length + which * (length // 2)
            for b in range(buffers)
            for which in (core, 1 - core)
        ]
    )
    out_halves, in_halves = [], []
    for b in range(buffers):
        (half,) = half_call(
            output_kernel,
            "output",
            b,
            order,
            [ff_sums[b], swap(ff_sums[b], 0, 2), middles[b]],
            (),
            (BF16,),
        )
        out_halves += [half, swap(half, 0, 1)]
        (half,) = half_call(
            input_kernel,
            "input",
            b,
            order,
            [dn_one[b], swap(dn_one[b], 0, 2), block_input, d_middles[b]],
            (2,),
            (BF16,),
            gains,
        )
        in_halves += [half, swap(half, 0, 1)]
    block_output = place(out_halves, half_offs, tokens)
    input_gradient = place(in_halves, half_offs, tokens)

    att_grad, feed_grad, stat, gain, table_sum = norm_call(
        wide, narrow, [att_group, feed_group], bucket, gain_at
    )
    results = adam_call(
        att_grad,
        feed_grad,
        gain,
        table_sum,
        stat,
        arguments[3:9],
        firsts,
        seconds,
        heads,
        hidden_cols,
    )
    return (block_output, input_gradient, stat[0, 0], *results)


class Place:
    def __init__(self):
        self.w = lax.axis_index("wide")
        self.n = lax.axis_index("narrow")
        self.z, self.x = self.w // 2, self.w % 2
        self.y, self.core = self.n // 2, self.n % 2
        self.n_far = (self.n + 2) % 4
        self.across = (self.w, self.n_far)
        self.beside = (self.w, self.n + 1 - 2 * self.core)
        self.flip = (self.z * 2 + 1 - self.x, self.n)

    def along(self, m):
        return (((self.z + m) % 4) * 2 + self.x, self.n)

    def from_z(self, m):
        return ((self.z + 4 - m) % 4) * 2 + self.x

    def from_x(self, m):
        return ((self.z + 4 - m) % 4) * 2 + 1 - self.x

    def meet(self):
        barrier = pltpu.get_barrier_semaphore()
        peers = [self.along(1), self.along(2), self.along(3), self.flip, self.across, self.beside]
        for peer in peers:
            pl.semaphore_signal(barrier, inc=1, device_id=peer, device_id_type=MESH)
        pl.semaphore_wait(barrier, len(peers))


def remote(source, target, send_sem, recv_sem, peer):
    return pltpu.make_async_remote_copy(
        src_ref=source,
        dst_ref=target,
        send_sem=send_sem,
        recv_sem=recv_sem,
        device_id=peer,
        device_id_type=MESH,
    )


class Gather:
    def __init__(self, spot, view, ssem, rsem):
        self.spot, self.view, self.ssem, self.rsem = spot, view, ssem, rsem
        self.sent = []

    def push(self, owner, slot, peer):
        copy = remote(
            self.view(owner), self.view(owner), self.ssem.at[slot], self.rsem.at[owner], peer
        )
        copy.start()
        self.sent.append((owner, slot, peer))

    def begin(self):
        for m in (1, 2, 3):
            self.push(self.spot.w, m - 1, self.spot.along(m))
        self.push(self.spot.w, 3, self.spot.flip)

    def arrived(self, owner):
        remote(
            self.view(owner), self.view(owner), self.ssem.at[0], self.rsem.at[owner], self.spot.flip
        ).wait_recv()

    def forward(self, m):
        owner = self.spot.from_z(m)
        self.arrived(owner)
        self.push(owner, 3 + m, self.spot.flip)

    def finish(self):
        for m in range(4):
            self.arrived(self.spot.from_x(m))

    def drain(self):
        for m in (1, 2, 3):
            remote(
                self.view(self.spot.w),
                self.view(self.spot.w),
                self.ssem.at[m - 1],
                self.rsem.at[0],
                self.spot.along(m),
            ).wait_send()
        for m in range(4):
            owner = self.spot.from_z(m)
            remote(
                self.view(owner), self.view(owner), self.ssem.at[3 + m], self.rsem.at[0], self.spot.flip
            ).wait_send()


def gather_attend_kernel(
    buffers,
    slots,
    heads,
    hidden_cols,
    ends_ref,
    x_ref,
    strip_ref,
    pw_ref,
    ow_ref,
    ew_ref,
    sw_ref,
    gn_ref,
    normed_ref,
    qkv_ref,
    att_ref,
    log_ref,
    gains_ref,
    pbuf,
    obuf,
    fbuf,
    qs,
    kt,
    vs,
    opad,
    spad,
    gpad,
    ssems,
    rsems,
    lone_s,
    lone_r,
):
    spot = Place()
    spot.meet()
    tokens, width = x_ref.shape
    length = tokens // buffers
    head_cols = heads * DH
    rows = gn_ref.shape[1]
    part = hidden_cols // 2
    chunk = 3 * part

    def at_rows(owner):
        return pl.ds(pl.multiple_of(owner * rows, 16), rows)

    mine = at_rows(spot.w)
    gpad[...] = jnp.zeros_like(gpad)
    gpad[0:2, 0:rows] = gn_ref[...]
    pbuf[mine] = jnp.concatenate(
        [pw_ref[0], pw_ref[1], pw_ref[2], gpad[...].T[:rows, :DH]], axis=1
    ).astype(BF16)
    projection = Gather(spot, lambda v: pbuf.at[at_rows(v)], ssems.at[0], rsems.at[0])
    projection.begin()
    opad[...] = jnp.zeros_like(opad)
    opad[0:head_cols, 0:rows] = ow_ref[...]
    obuf[spot.n, mine] = opad[...].T[:rows, :head_cols].astype(BF16)

    def o_view(which):
        return lambda v: obuf.at[which, at_rows(v)]

    def o_across():
        return remote(
            obuf.at[spot.n, mine],
            obuf.at[spot.n, mine],
            lone_s.at[0],
            lone_r.at[0],
            spot.across,
        )

    def o_across_in():
        return remote(
            obuf.at[spot.n_far, mine],
            obuf.at[spot.n_far, mine],
            lone_s.at[0],
            lone_r.at[0],
            spot.across,
        )

    o_across().start()
    spad[...] = jnp.zeros_like(spad)
    spad[:, 0:rows] = sw_ref[...]
    turned = spad[...].T[:rows].astype(BF16)
    for j in range(2):
        span = slice(j * part, (j + 1) * part)
        fbuf[mine, j * chunk : j * chunk + part] = ew_ref[0, :, span].astype(BF16)
        fbuf[mine, j * chunk + part : j * chunk + 2 * part] = ew_ref[1, :, span].astype(BF16)
        fbuf[mine, j * chunk + 2 * part : (j + 1) * chunk] = turned[:, span]
    out_near = Gather(spot, o_view(spot.n), ssems.at[1], rsems.at[1])
    out_far = Gather(spot, o_view(spot.n_far), ssems.at[2], rsems.at[2])
    feeds = [
        Gather(
            spot,
            lambda v, j=j: fbuf.at[at_rows(v), j * chunk : (j + 1) * chunk],
            ssems.at[3 + j],
            rsems.at[3 + j],
        )
        for j in range(2)
    ]
    for m in (1, 2, 3):
        projection.forward(m)
    o_across_in().wait_recv()
    out_near.begin()
    out_far.begin()
    feeds[0].begin()
    projection.finish()

    gain_cols = pbuf[:, 4 * LANES :].astype(F32).T
    first = 3 * head_cols - 4 * LANES
    gains = gain_cols[first : first + 8]
    gains_ref[...] = gains
    gain_one = gains[0:1]
    step = 256
    per = length // step

    for b in range(buffers):

        @pl.loop(0, per)
        def _(block, b=b):
            begin = pl.multiple_of(block * step, step)
            here = pl.ds(begin, step)
            span = pl.ds(pl.multiple_of(b * length + begin, step), step)
            values = x_ref[span].astype(F32)
            normed = (values * rms_scale(values) * gain_one).astype(BF16)
            normed_ref[span] = normed
            qkv = mm(normed, pbuf[...]).astype(BF16)
            qkv_ref[span] = qkv[:, : 3 * head_cols]
            for h in range(heads):
                qs[b, h, here] = qkv[:, h * DH : (h + 1) * DH]
                kt[b, h, :, here] = qkv[:, head_cols + h * DH : head_cols + (h + 1) * DH].T
                vs[b, h, here] = qkv[:, 2 * head_cols + h * DH : 2 * head_cols + (h + 1) * DH]

    def relay_out():
        for m in (1, 2, 3):
            out_near.forward(m)
            out_far.forward(m)

    def att_view(which, b):
        return att_ref.at[which, b * length : (b + 1) * length]

    def share(which, slot, peer):
        return remote(which, which, lone_s.at[slot], lone_r.at[slot], peer)

    n_beside = spot.beside[1]
    n_diag = (n_beside + 2) % 4

    def out_beside():
        out_near.finish()
        out_far.finish()
        share(obuf.at[spot.n], 1, spot.beside).start()
        share(obuf.at[spot.n_far], 2, spot.beside).start()

    def att_send(b):
        share(att_view(spot.n, b), 3 + 3 * b, spot.across).start()
        share(att_view(spot.n, b), 4 + 3 * b, spot.beside).start()

    def att_relay(b):
        share(att_view(spot.n_far, b), 3 + 3 * b, spot.across).wait_recv()
        share(att_view(spot.n_far, b), 5 + 3 * b, spot.beside).start()

    blocks = length // LANES

    def run(b, events):
        seg_keys = segments(
            lax.broadcasted_iota(jnp.int32, (1, length), 1), ends_ref, b, slots
        )

        @pl.loop(0, blocks)
        def _(block):
            for when, what in events.items():
                pl.when(block == when)(what)
            begin = pl.multiple_of(block * LANES, LANES)
            here = pl.ds(begin, LANES)
            span = pl.ds(pl.multiple_of(b * length + begin, LANES), LANES)
            window = pl.ds(pl.multiple_of((blocks - 1 - block) * LANES, LANES), length)
            seg_rows = segments(
                lax.broadcasted_iota(jnp.int32, (LANES, 1), 0) + begin, ends_ref, b, slots
            )
            same = seg_rows == seg_keys
            lane = lax.broadcasted_iota(jnp.int32, (LANES, LANES), 1)
            logs = jnp.zeros((LANES, LANES), F32)
            outs = []
            for h in range(heads):
                scores = mm(qs[b, h, here], kt[b, h]) + strip_ref[h, :, window]
                scores = jnp.where(same, scores, masked_score)
                row_max = jnp.max(scores, axis=1, keepdims=True)
                raised = jnp.exp(scores - row_max)
                total = jnp.sum(raised, axis=1, keepdims=True)
                probs = (raised * (1.0 / total)).astype(BF16)
                outs.append(mm(probs, vs[b, h]).astype(BF16))
                logs = jnp.where(lane == h, row_max + jnp.log(total), logs)
            log_ref[span] = logs
            att_ref[spot.n, span] = jnp.concatenate(outs, axis=1)

    def feed_turn():
        feeds[0].forward(3)
        feeds[1].begin()

    run(
        0,
        {
            0: relay_out,
            2: lambda: feeds[0].forward(1),
            3: lambda: feeds[0].forward(2),
            4: feed_turn,
            5: out_beside,
        },
    )
    att_send(0)
    run(
        1,
        {
            2: lambda: att_relay(0),
            3: lambda: feeds[1].forward(1),
            4: lambda: feeds[1].forward(2),
            5: lambda: feeds[1].forward(3),
        },
    )
    att_send(1)
    att_relay(1)
    feeds[0].finish()
    feeds[1].finish()
    share(obuf.at[n_beside], 1, spot.beside).wait_recv()
    share(obuf.at[n_diag], 2, spot.beside).wait_recv()
    for b in range(buffers):
        share(att_view(n_beside, b), 4 + 3 * b, spot.beside).wait_recv()
        share(att_view(n_diag, b), 5 + 3 * b, spot.beside).wait_recv()
    o_across().wait_send()
    for group in (projection, out_near, out_far, *feeds):
        group.drain()
    share(obuf.at[spot.n], 1, spot.beside).wait_send()
    share(obuf.at[spot.n_far], 2, spot.beside).wait_send()
    for b in range(buffers):
        share(att_view(spot.n, b), 3 + 3 * b, spot.across).wait_send()
        share(att_view(spot.n, b), 4 + 3 * b, spot.beside).wait_send()
        share(att_view(spot.n_far, b), 5 + 3 * b, spot.beside).wait_send()


def gather_attend(ends, x, strip, pw, ow, ew, sw, gn, length):
    tokens, width = x.shape
    buffers = tokens // length
    heads = strip.shape[0]
    head_cols = heads * DH
    hidden_cols = ew.shape[2]
    vmem = pl.BlockSpec(memory_space=pltpu.VMEM)
    return pl.pallas_call(
        functools.partial(gather_attend_kernel, buffers, ends.shape[1], heads, hidden_cols),
        in_specs=[pl.BlockSpec(memory_space=pltpu.SMEM)] + [vmem] * 7,
        out_specs=[vmem] * 8,
        out_shape=[
            jax.ShapeDtypeStruct((tokens, width), BF16),
            jax.ShapeDtypeStruct((tokens, 3 * head_cols), BF16),
            jax.ShapeDtypeStruct((4, tokens, head_cols), BF16),
            jax.ShapeDtypeStruct((tokens, LANES), F32),
            jax.ShapeDtypeStruct((8, width), F32),
            jax.ShapeDtypeStruct((width, 3 * head_cols + DH), BF16),
            jax.ShapeDtypeStruct((4, width, head_cols), BF16),
            jax.ShapeDtypeStruct((width, 3 * hidden_cols), BF16),
        ],
        scratch_shapes=[
            pltpu.VMEM((buffers, heads, length, DH), BF16),
            pltpu.VMEM((buffers, heads, DH, length), BF16),
            pltpu.VMEM((buffers, heads, length, DH), BF16),
            pltpu.VMEM((2 * LANES, LANES), F32),
            pltpu.VMEM((hidden_cols, LANES), F32),
            pltpu.VMEM((LANES, LANES), F32),
            pltpu.SemaphoreType.DMA((5, 7)),
            pltpu.SemaphoreType.DMA((5, 8)),
            pltpu.SemaphoreType.DMA((9,)),
            pltpu.SemaphoreType.DMA((9,)),
        ],
        compiler_params=params(collective_id=1, has_side_effects=True),
        cost_estimate=pl.CostEstimate(
            flops=16 << 30, bytes_accessed=24 << 20, transcendentals=8 << 20
        ),
        name="gather_attend",
    )(ends, x, strip, pw, ow, ew, sw, gn)


def feed_forward_kernel(
    buffers,
    hidden_cols,
    x_ref,
    cot_ref,
    att_ref,
    gains_ref,
    obuf,
    fbuf,
    low_ref,
    d_ref,
    middle_ref,
    ff_sum,
    gain_sum,
    even_ref,
    odd_ref,
    normed,
    hid,
    dg,
    total,
    ff_out,
    ff_in,
    dn_out,
    dn_keep,
    dn_in,
    dn_sum,
    dn_far,
    sends,
    recvs,
):
    spot = Place()
    spot.meet()
    tokens, width = x_ref.shape
    length = tokens // buffers
    half = length // 2
    part = hidden_cols // 2
    chunk = 3 * part
    core = spot.core
    k0 = 0.7978845608028654
    k1 = 0.044715
    gain_two = gains_ref[1:2]

    def ff_core(b):
        return remote(ff_out.at[b], ff_in.at[b], sends.at[b], recvs.at[b], spot.beside)

    def dn_core(b):
        return remote(dn_out.at[b], dn_in.at[b], sends.at[2 + b], recvs.at[2 + b], spot.beside)

    def dn_across(b):
        return remote(dn_sum.at[b], dn_far.at[b], sends.at[4 + b], recvs.at[4 + b], spot.across)

    def low_rows(b, which):
        return pl.ds(pl.multiple_of(b * length + which * half, LANES), half)

    def low_core(b):
        view = low_ref.at[low_rows(b, core)]
        return remote(view, view, sends.at[6 + b], recvs.at[6 + b], spot.beside)

    def low_core_in(b):
        view = low_ref.at[low_rows(b, 1 - core)]
        return remote(view, view, sends.at[6 + b], recvs.at[6 + b], spot.beside)

    gain_sum[...] = jnp.zeros_like(gain_sum)

    @pl.loop(0, 2 * buffers)
    def _(i):
        b = i // 2
        keep = i % 2
        which = (1 - core) * (1 - keep) + core * keep
        rows = low_rows(b, which)
        attention = jnp.zeros((half, width), F32)
        for a in range(4):
            attention = attention + mm(att_ref[a, rows], obuf[a], NT)
        middle = x_ref[rows].astype(F32) + attention
        scale_two = rms_scale(middle)
        normed_rows = (middle * scale_two * gain_two).astype(BF16)
        normed[rows] = normed_rows
        cot = cot_ref[rows]
        ff = jnp.zeros((half, width), F32)
        dn = jnp.zeros((half, width), F32)
        for j in range(2):
            at = j * chunk
            both = mm(normed_rows, fbuf[:, at : at + 2 * part])
            gate, up = both[:, :part], both[:, part:]
            square = gate * gate
            tanh = jnp.tanh(k0 * (gate + k1 * (square * gate)))
            lift = 0.5 * (1.0 + tanh)
            active = gate * lift
            slope = lift + (0.5 * gate) * (1.0 - tanh * tanh) * (k0 + (3.0 * k0 * k1) * square)
            d_hidden = mm(cot, fbuf[:, at + 2 * part : at + 3 * part])
            hid[rows, j * part : (j + 1) * part] = (active * up).astype(BF16)
            dg[rows, 2 * j * part : (2 * j + 1) * part] = (d_hidden * up * slope).astype(BF16)
            dg[rows, (2 * j + 1) * part : (2 * j + 2) * part] = (d_hidden * active).astype(BF16)
            ff = ff + mm(
                hid[rows, j * part : (j + 1) * part], fbuf[:, at + 2 * part : at + 3 * part], NT
            )
            dn = dn + mm(
                dg[rows, 2 * j * part : (2 * j + 2) * part], fbuf[:, at : at + 2 * part], NT
            )
        gain_sum[...] = gain_sum[...] + fold_rows(dn * middle * scale_two)

        @pl.when(keep == 0)
        def _():
            dn_out[b] = dn.astype(BF16)
            dn_core(b).start()
            ff_out[b] = ff.astype(BF16)
            ff_core(b).start()

        @pl.when(keep == 1)
        def _():
            middle_ref[b] = middle
            dn_core(b).wait_recv()
            dn_sum[b] = (dn.astype(BF16).astype(F32) + dn_in[b].astype(F32)).astype(BF16)
            dn_across(b).start()
            ff_core(b).wait_recv()
            ff_sum[b] = (ff.astype(BF16).astype(F32) + ff_in[b].astype(F32)).astype(BF16)

    def finish_middle(b):
        dn_across(b).wait_recv()

        @pl.loop(0, 3)
        def _(i):
            span = pl.ds(pl.multiple_of(i * LANES, LANES), LANES)
            rows = pl.ds(
                pl.multiple_of(b * length + core * half + i * LANES, LANES), LANES
            )
            upstream = dn_sum[b, span].astype(F32) + dn_far[b, span].astype(F32)
            middle = middle_ref[b, span]
            d_middle = cot_ref[rows].astype(F32) + norm_back(
                middle, rms_scale(middle), gain_two, upstream
            )
            d_ref[b, span] = d_middle
            low_ref[rows] = d_middle.astype(BF16)

        low_core(b).start()

    finish_middle(0)
    step = 256
    for begin in range(0, width, step):
        cols = slice(begin, begin + step)
        for j in range(2):
            at = j * chunk
            total[cols, at : at + 2 * part] = mm(
                normed[:, cols], dg[:, 2 * j * part : (2 * j + 2) * part], TN
            )
            total[cols, at + 2 * part : at + 3 * part] = mm(
                cot_ref[:, cols], hid[:, j * part : (j + 1) * part], TN
            )
    spread(spot, total, even_ref, odd_ref)
    finish_middle(1)
    for b in range(buffers):
        low_core_in(b).wait_recv()
        ff_core(b).wait_send()
        dn_core(b).wait_send()
        dn_across(b).wait_send()
        low_core(b).wait_send()


def spread(spot, total, even_ref, odd_ref):
    rows = even_ref.shape[1]
    for m in range(4):
        base = ((spot.z + m) % 4) * 2
        near = pl.ds(pl.multiple_of((base + spot.x) * rows, 8), rows)
        far = pl.ds(pl.multiple_of((base + 1 - spot.x) * rows, 8), rows)
        even_ref[m] = total[near]
        odd_ref[m] = total[far].astype(BF16)


def feed_forward(x, cot, att, gains, obuf, fbuf, length, rows):
    tokens, width = x.shape
    buffers = tokens // length
    half = length // 2
    hidden_cols = fbuf.shape[1] // 3
    vmem = pl.BlockSpec(memory_space=pltpu.VMEM)
    return pl.pallas_call(
        functools.partial(feed_forward_kernel, buffers, hidden_cols),
        in_specs=[vmem] * 6,
        out_specs=[vmem] * 7,
        out_shape=[
            jax.ShapeDtypeStruct((tokens, width), BF16),
            jax.ShapeDtypeStruct((buffers, half, width), F32),
            jax.ShapeDtypeStruct((buffers, half, width), F32),
            jax.ShapeDtypeStruct((buffers, half, width), BF16),
            jax.ShapeDtypeStruct((8, width), F32),
            jax.ShapeDtypeStruct((4, rows, 3 * hidden_cols), F32),
            jax.ShapeDtypeStruct((4, rows, 3 * hidden_cols), BF16),
        ],
        scratch_shapes=[
            pltpu.VMEM((tokens, width), BF16),
            pltpu.VMEM((tokens, hidden_cols), BF16),
            pltpu.VMEM((tokens, 2 * hidden_cols), BF16),
            pltpu.VMEM((width, 3 * hidden_cols), F32),
        ]
        + [pltpu.VMEM((buffers, half, width), BF16)] * 7
        + [pltpu.SemaphoreType.DMA((8,)), pltpu.SemaphoreType.DMA((8,))],
        compiler_params=params(collective_id=2, has_side_effects=True),
        cost_estimate=pl.CostEstimate(
            flops=20 << 30, bytes_accessed=24 << 20, transcendentals=1 << 20
        ),
        name="feed_forward",
    )(x, cot, att, gains, obuf, fbuf)


class Reduce:
    def __init__(self, spot, even, odd, flipped, mixed, landed, sems_s, sems_r):
        self.spot, self.even, self.odd = spot, even, odd
        self.flipped, self.mixed, self.landed = flipped, mixed, landed
        self.sems_s, self.sems_r = sems_s, sems_r

    def over(self, m):
        return remote(
            self.odd.at[m], self.flipped.at[m], self.sems_s.at[m], self.sems_r.at[m], self.spot.flip
        )

    def along(self, m):
        return remote(
            self.mixed.at[m - 1],
            self.landed.at[m - 1],
            self.sems_s.at[3 + m],
            self.sems_r.at[3 + m],
            self.spot.along(m),
        )

    def begin(self):
        for m in (2, 1, 3, 0):
            self.over(m).start()

    def relay(self, m):
        self.over(m).wait_recv()
        self.mixed[m - 1] = (self.even(m) + self.flipped[m].astype(F32)).astype(BF16)
        self.along(m).start()

    def result(self):
        self.over(0).wait_recv()
        value = self.even(0) + self.flipped[0].astype(F32)
        for m in (1, 2, 3):
            self.along(m).wait_recv()
            value = value + self.landed[m - 1].astype(F32)
        return value

    def drain(self):
        for m in range(4):
            self.over(m).wait_send()
        for m in (1, 2, 3):
            self.along(m).wait_send()


def back_all_kernel(
    buffers,
    slots,
    heads,
    ends_ref,
    x_ref,
    strip_ref,
    qkv_ref,
    log_ref,
    low_ref,
    att_ref,
    normed_ref,
    gains_ref,
    pbuf,
    obuf,
    ff_sum,
    middle_ref,
    d_ref,
    gain_two_ref,
    feed_even,
    feed_odd,
    out_ref,
    in_ref,
    att_grad,
    feed_grad,
    bucket_ref,
    qs,
    kt,
    ks,
    vt,
    gs,
    qt,
    gt,
    dkt,
    dvt,
    dq,
    dqkv,
    dstrip,
    total,
    att_odd,
    att_flip,
    att_mix,
    att_land,
    feed_flip,
    feed_mix,
    feed_land,
    ff_far,
    dn_out,
    dn_in,
    dn_sum,
    dn_far,
    sends,
    recvs,
    red_s,
    red_r,
):
    spot = Place()
    spot.meet()
    tokens, width = x_ref.shape
    length = tokens // buffers
    half = length // 2
    head_cols = heads * DH
    qkv_cols = 3 * head_cols
    core = spot.core
    rows_of = feed_even.shape[1]
    gain_one = gains_ref[0:1]

    def half_rows(b, which):
        return pl.ds(pl.multiple_of(b * length + which * half, LANES), half)

    def ff_across(b):
        return remote(ff_sum.at[b], ff_far.at[b], sends.at[b], recvs.at[b], spot.across)

    def dn_core(b):
        return remote(dn_out.at[b], dn_in.at[b], sends.at[2 + b], recvs.at[2 + b], spot.beside)

    def dn_across(b):
        return remote(dn_sum.at[b], dn_far.at[b], sends.at[4 + b], recvs.at[4 + b], spot.across)

    def out_core(b, which):
        view = out_ref.at[half_rows(b, which)]
        return remote(view, view, sends.at[6 + b], recvs.at[6 + b], spot.beside)

    def in_core(b, which):
        view = in_ref.at[half_rows(b, which)]
        return remote(view, view, sends.at[8 + b], recvs.at[8 + b], spot.beside)

    feed = Reduce(
        spot,
        lambda m: feed_even[m],
        feed_odd,
        feed_flip,
        feed_mix,
        feed_land,
        red_s.at[0],
        red_r.at[0],
    )

    def att_even(m):
        owner = ((spot.z + m) % 4) * 2 + spot.x
        return total[pl.ds(pl.multiple_of(owner * rows_of, 8), rows_of)]

    att = Reduce(
        spot, att_even, att_odd, att_flip, att_mix, att_land, red_s.at[1], red_r.at[1]
    )
    feed.begin()
    for b in range(buffers):
        ff_across(b).start()
    dstrip[...] = jnp.zeros_like(dstrip)
    blocks = length // LANES
    gain_sums = jnp.zeros((8, width), F32)

    for b in range(buffers):
        base = b * length
        rows = slice(base, base + length)
        grads = mm(low_ref[rows], obuf[spot.n]).astype(BF16)
        for h in range(heads):
            qs[h] = qkv_ref[rows, h * DH : (h + 1) * DH]
            ks[h] = qkv_ref[rows, head_cols + h * DH : head_cols + (h + 1) * DH]
            values = qkv_ref[rows, 2 * head_cols + h * DH : 2 * head_cols + (h + 1) * DH]
            qt[h] = qs[h].T
            kt[h] = ks[h].T
            vt[h] = values.T
            gs[h] = grads[:, h * DH : (h + 1) * DH]
            gt[h] = gs[h].T
        dkt[...] = jnp.zeros_like(dkt)
        dvt[...] = jnp.zeros_like(dvt)
        seg_keys = segments(
            lax.broadcasted_iota(jnp.int32, (1, length), 1), ends_ref, b, slots
        )
        events = {1: lambda: feed.relay(2), 2: lambda: feed.relay(1), 3: lambda: feed.relay(3)}

        @pl.loop(0, blocks)
        def _(block, b=b, base=base, seg_keys=seg_keys):
            if b == 0:
                for when, what in events.items():
                    pl.when(block == when)(what)
            begin = pl.multiple_of(block * LANES, LANES)
            here = pl.ds(begin, LANES)
            window = pl.ds(pl.multiple_of((blocks - 1 - block) * LANES, LANES), length)
            seg_rows = segments(
                lax.broadcasted_iota(jnp.int32, (LANES, 1), 0) + begin, ends_ref, b, slots
            )
            same = seg_rows == seg_keys
            logs = log_ref[pl.ds(pl.multiple_of(base + begin, LANES), LANES)]
            for h in range(heads):
                scores = mm(qs[h, here], kt[h]) + strip_ref[h, :, window]
                scores = jnp.where(same, scores, masked_score)
                probs = jnp.exp(scores - logs[:, h : h + 1])
                d_probs = mm(gs[h, here], vt[h])
                inner = jnp.sum(probs * d_probs, axis=1, keepdims=True)
                d_scores = (probs * (d_probs - inner)).astype(BF16)
                dstrip[h, :, window] = dstrip[h, :, window] + d_scores.astype(F32)
                dq[h, here] = mm(d_scores, ks[h]).astype(BF16)
                dkt[h] = dkt[h] + mm(qt[h, :, here], d_scores)
                dvt[h] = dvt[h] + mm(gt[h, :, here], probs.astype(BF16))

        outs = [dq[h] for h in range(heads)]
        outs += [dkt[h].T.astype(BF16) for h in range(heads)]
        outs += [dvt[h].T.astype(BF16) for h in range(heads)]
        dqkv[rows] = jnp.concatenate(outs, axis=1)
        for keep in range(2):
            which = core if keep else 1 - core
            here = half_rows(b, which)
            dn = mm(dqkv[here], pbuf[:, :qkv_cols], NT)
            values = x_ref[here].astype(F32)
            gain_sums = gain_sums + fold_rows(dn * values * rms_scale(values))
            dn = dn.astype(BF16)
            if keep:
                dn_core(b).wait_recv()
                dn_sum[b] = (dn.astype(F32) + dn_in[b].astype(F32)).astype(BF16)
                dn_across(b).start()
            else:
                dn_out[b] = dn
                dn_core(b).start()

    def finish_out(b):
        ff_across(b).wait_recv()

        @pl.loop(0, 3)
        def _(i):
            span = pl.ds(pl.multiple_of(i * LANES, LANES), LANES)
            here = pl.ds(pl.multiple_of(b * length + core * half + i * LANES, LANES), LANES)
            joined = (ff_sum[b, span].astype(F32) + ff_far[b, span].astype(F32)).astype(BF16)
            out_ref[here] = (middle_ref[b, span] + joined.astype(F32)).astype(BF16)

        out_core(b, core).start()

    def finish_in(b):
        dn_across(b).wait_recv()

        @pl.loop(0, 3)
        def _(i):
            span = pl.ds(pl.multiple_of(i * LANES, LANES), LANES)
            here = pl.ds(pl.multiple_of(b * length + core * half + i * LANES, LANES), LANES)
            upstream = dn_sum[b, span].astype(F32) + dn_far[b, span].astype(F32)
            values = x_ref[here].astype(F32)
            in_ref[here] = (
                d_ref[b, span] + norm_back(values, rms_scale(values), gain_one, upstream)
            ).astype(BF16)

        in_core(b, core).start()

    row = lax.broadcasted_iota(jnp.int32, (LANES, width), 0)
    gain_rows = jnp.where(
        row == DH,
        jnp.sum(gain_sums, axis=0, keepdims=True),
        jnp.where(row == DH + 1, jnp.sum(gain_two_ref[...], axis=0, keepdims=True), 0.0),
    )
    gain_cols = gain_rows.T
    step = 256
    for begin in range(0, width, step):
        cols = slice(begin, begin + step)
        total[cols, :qkv_cols] = mm(normed_ref[:, cols], dqkv[...], TN)
        total[cols, qkv_cols : qkv_cols + DH] = gain_cols[cols, DH:]
        total[cols, qkv_cols + DH :] = mm(low_ref[:, cols], att_ref[spot.n], TN)
    for m in range(4):
        owner = ((spot.z + m) % 4) * 2 + 1 - spot.x
        att_odd[m] = total[pl.ds(pl.multiple_of(owner * rows_of, 8), rows_of)].astype(BF16)
    att.begin()
    feed_grad[...] = feed.result()
    finish_out(0)
    att.relay(2)
    att.relay(1)
    att.relay(3)
    finish_out(1)
    finish_in(0)

    near_at = (blocks - 2) * LANES
    near_row = lax.broadcasted_iota(jnp.int32, (LANES, 4 * LANES), 0)
    diag = lax.broadcasted_iota(jnp.int32, (LANES, 4 * LANES), 1)[0:1]
    offset = jnp.where(diag < 3 * LANES, diag - LANES, diag - 5 * LANES)
    ids = bucket_of(offset)
    lane = lax.broadcasted_iota(jnp.int32, (1, LANES), 1)
    pick = lax.broadcasted_iota(jnp.int32, (LANES, 4 * LANES), 0)
    onehot = jnp.where(pick == ids, 1.0, 0.0)
    out = jnp.zeros((1, LANES), F32)
    for h in range(heads):
        left = jnp.sum(jnp.sum(dstrip[h, :, :near_at], axis=0, keepdims=True), axis=1, keepdims=True)
        right = jnp.sum(
            jnp.sum(dstrip[h, :, near_at + 3 * LANES :], axis=0, keepdims=True), axis=1, keepdims=True
        )
        near = jnp.concatenate(
            [dstrip[h, :, near_at : near_at + 3 * LANES], jnp.zeros((LANES, LANES), F32)], axis=1
        )
        for k in range(7):
            near = jnp.where(
                (near_row // (1 << k)) % 2 == 1, pltpu.roll(near, 4 * LANES - (1 << k), 1), near
            )
        sums = jnp.sum(near, axis=0, keepdims=True)
        binned = lax.dot_general(
            jnp.broadcast_to(sums, (8, 4 * LANES)),
            onehot,
            NT,
            precision=lax.Precision.HIGHEST,
            preferred_element_type=F32,
        )[0:1]
        binned = binned + jnp.where(lane == 15, left, 0.0) + jnp.where(lane == 31, right, 0.0)
        binned = jnp.where(lane < 32, binned, 0.0)
        out = out + (pltpu.roll(binned, 32 * h, 1) if h else binned)
    bucket_ref[...] = jnp.broadcast_to(out, (8, LANES))

    att_grad[...] = att.result()
    finish_in(1)
    for b in range(buffers):
        out_core(b, 1 - core).wait_recv()
        in_core(b, 1 - core).wait_recv()
        ff_across(b).wait_send()
        dn_core(b).wait_send()
        dn_across(b).wait_send()
        out_core(b, core).wait_send()
        in_core(b, core).wait_send()
    feed.drain()
    att.drain()


def back_all(
    ends, x, strip, qkv, logs, low, att, normed, gains, pbuf, obuf, ff_sum, middle, d_middle,
    gain_two, feed_even, feed_odd, length
):
    tokens, width = x.shape
    buffers = tokens // length
    half = length // 2
    heads = strip.shape[0]
    rows, feed_cols = feed_even.shape[1:]
    head_cols = heads * DH
    att_cols = 4 * head_cols + DH
    vmem = pl.BlockSpec(memory_space=pltpu.VMEM)
    operands = [
        x, strip, qkv, logs, low, att, normed, gains, pbuf, obuf, ff_sum, middle, d_middle,
        gain_two, feed_even, feed_odd
    ]
    wide_heads = pltpu.VMEM((heads, length, DH), BF16)
    tall_heads = pltpu.VMEM((heads, DH, length), BF16)
    return pl.pallas_call(
        functools.partial(back_all_kernel, buffers, ends.shape[1], heads),
        in_specs=[pl.BlockSpec(memory_space=pltpu.SMEM)] + [vmem] * len(operands),
        out_specs=[vmem] * 5,
        out_shape=[
            jax.ShapeDtypeStruct((tokens, width), BF16),
            jax.ShapeDtypeStruct((tokens, width), BF16),
            jax.ShapeDtypeStruct((rows, att_cols), F32),
            jax.ShapeDtypeStruct((rows, feed_cols), F32),
            jax.ShapeDtypeStruct((8, LANES), F32),
        ],
        scratch_shapes=[
            wide_heads,
            tall_heads,
            wide_heads,
            tall_heads,
            wide_heads,
            tall_heads,
            tall_heads,
            pltpu.VMEM((heads, DH, length), F32),
            pltpu.VMEM((heads, DH, length), F32),
            wide_heads,
            pltpu.VMEM((tokens, 3 * head_cols), BF16),
            pltpu.VMEM(strip.shape, F32),
            pltpu.VMEM((width, att_cols), F32),
            pltpu.VMEM((4, rows, att_cols), BF16),
            pltpu.VMEM((4, rows, att_cols), BF16),
            pltpu.VMEM((3, rows, att_cols), BF16),
            pltpu.VMEM((3, rows, att_cols), BF16),
            pltpu.VMEM((4, rows, feed_cols), BF16),
            pltpu.VMEM((3, rows, feed_cols), BF16),
            pltpu.VMEM((3, rows, feed_cols), BF16),
        ]
        + [pltpu.VMEM((buffers, half, width), BF16)] * 5
        + [
            pltpu.SemaphoreType.DMA((10,)),
            pltpu.SemaphoreType.DMA((10,)),
            pltpu.SemaphoreType.DMA((2, 7)),
            pltpu.SemaphoreType.DMA((2, 7)),
        ],
        compiler_params=params(collective_id=3, has_side_effects=True),
        cost_estimate=pl.CostEstimate(
            flops=20 << 30, bytes_accessed=32 << 20, transcendentals=4 << 20
        ),
        name="back_all",
    )(ends, *operands)


def direct_body(wide, narrow, *arguments):
    (
        block_input,
        cotangent,
        lengths,
        project_weight,
        output_weight,
        expand_weight,
        shrink_weight,
        bucket_bias,
        norm_gains,
    ) = arguments[:9]
    firsts = arguments[9:15]
    seconds = arguments[15:21]
    tokens, width = block_input.shape
    buffers = lengths.shape[0]
    length = tokens // buffers
    rows = norm_gains.shape[1]
    head_cols = project_weight.shape[2]
    heads = head_cols // DH
    hidden_cols = expand_weight.shape[2]
    n = lax.axis_index("narrow")

    ends = jnp.cumsum(lengths, axis=1)
    strip = bias_strip(bucket_bias, n, heads, length)
    normed_one, qkv, att, logs, gains, pbuf, obuf, fbuf = gather_attend(
        ends,
        block_input,
        strip,
        project_weight,
        output_weight,
        expand_weight,
        shrink_weight,
        norm_gains,
        length,
    )
    low, d_middle, middle, ff_sum, gain_two, feed_even, feed_odd = feed_forward(
        block_input, cotangent, att, gains, obuf, fbuf, length, rows
    )
    block_output, input_gradient, att_grad, feed_grad, bucket = back_all(
        ends,
        block_input,
        strip,
        qkv,
        logs,
        low,
        att,
        normed_one,
        gains,
        pbuf,
        obuf,
        ff_sum,
        middle,
        d_middle,
        gain_two,
        feed_even,
        feed_odd,
        length,
    )
    gain_at = 3 * head_cols
    att_grad, feed_grad, stat, gain, table_sum = norm_call(
        wide, narrow, [[att_grad], [feed_grad]], bucket, gain_at
    )
    results = adam_call(
        att_grad,
        feed_grad,
        gain,
        table_sum,
        stat,
        arguments[3:9],
        firsts,
        seconds,
        heads,
        hidden_cols,
        direct=True,
    )
    return (block_output, input_gradient, stat[0, 0], *results)


def solution(mesh):
    wide, narrow = mesh.shape["wide"], mesh.shape["narrow"]
    body = direct_body if (wide, narrow) == (8, 4) else general_body
    state = (
        P(None, "wide", "narrow"),
        P("narrow", "wide"),
        P(None, "wide", "narrow"),
        P("narrow", "wide"),
        P(),
        P(None, "wide"),
    )
    rows = P("wide", None)
    return jax.shard_map(
        functools.partial(body, wide, narrow),
        mesh=mesh,
        in_specs=(rows, rows, rows, *state, *state, *state),
        out_specs=(rows, rows, P(), *state, *state, *state),
        check_vma=False,
    )
```

```python
import functools

import jax
import jax.numpy as jnp
from jax import lax
from jax.experimental import pallas as pl
from jax.experimental.pallas import tpu as pltpu
from jax.sharding import PartitionSpec as P

DH = 64
STEP = 10
LANES = 128
MESH = pl.DeviceIdType.MESH
F32 = jnp.float32
BF16 = jnp.bfloat16
ANY = pl.ANY

bucket_edges = (12, 16, 23, 32, 46, 64, 91)
norm_eps = 1e-06
clip_limit = 1.0
beta_one = 0.9
beta_two = 0.999
adam_eps = 1e-08
step_rates = (0.06, 0.3, 0.07, 0.06, 1.0, 0.3)
decay_rates = (0.01, 0.01, 0.01, 0.01, 0.0, 0.0)
masked_score = -1000000000.0
VMEM_LIMIT = 58 << 20

NN = (((1,), (0,)), ((), ()))
NT = (((1,), (1,)), ((), ()))
TN = (((0,), (0,)), ((), ()))


def mm(left, right, dims=NN):
    return lax.dot_general(left, right, dims, preferred_element_type=F32)


def bucket_of(offsets):
    distance = jnp.abs(offsets)
    far_bucket = 8 + sum(((distance >= threshold).astype(jnp.int32) for threshold in bucket_edges))
    return jnp.where(distance < 8, distance, far_bucket) + 16 * (offsets > 0).astype(jnp.int32)


def rms_scale(values):
    return lax.rsqrt(jnp.mean(values * values, axis=-1, keepdims=True) + norm_eps)


def norm_back(values, scale_vec, gain_vec, upstream):
    weighted = upstream * gain_vec
    inner_mean = jnp.mean(weighted * values, axis=-1, keepdims=True)
    return scale_vec * weighted - values * (scale_vec * scale_vec * scale_vec) * inner_mean


def adam_update(weight, moment_one, moment_two, gradient, step_rate, decay_rate):
    new_first = beta_one * moment_one + (1.0 - beta_one) * gradient
    new_second = beta_two * moment_two + (1.0 - beta_two) * gradient * gradient
    first_hat = new_first / (1.0 - beta_one**STEP)
    second_hat = new_second / (1.0 - beta_two**STEP)
    new_weight = weight - step_rate * (
        first_hat / (jnp.sqrt(second_hat) + adam_eps) + decay_rate * weight
    )
    return (new_weight, new_first, new_second)


def fold_rows(values):
    rows, cols = values.shape
    return jnp.sum(values.reshape(rows // 8, 8, cols), axis=0)


def start_rows(pieces, target, offs_ref, sems):
    copies = []
    for at, piece in enumerate(pieces):
        rows = piece.shape[0]
        begin = pl.multiple_of(offs_ref[at], 16)
        copies.append(
            pltpu.make_async_copy(piece, target.at[pl.ds(begin, rows)], sems.at[at])
        )
    for copy in copies:
        copy.start()
    return copies


def segments(index, ends_ref, buffer, slots):
    total = jnp.zeros(index.shape, jnp.int32)
    for slot in range(slots):
        total = total + (index >= ends_ref[buffer, slot]).astype(jnp.int32)
    return total


def params(**more):
    return pltpu.CompilerParams(vmem_limit_bytes=VMEM_LIMIT, **more)


def attend_kernel(
    buffer, slots, heads, count, ends_ref, offs_ref, x_ref, strip_ref, *refs
):
    pieces = refs[:count]
    normed_ref, qkv_ref, att_ref, log_ref, gains_ref, wbuf, qs, ks, vs, os, sems = refs[count:]
    length, width = x_ref.shape
    head_cols = heads * DH
    copies = start_rows(pieces, wbuf, offs_ref, sems)
    for copy in copies:
        copy.wait()
    gain_cols = wbuf[:, 4 * LANES :].astype(F32).T
    first = 3 * head_cols - 4 * LANES
    gains = gain_cols[first : first + 8]
    gains_ref[...] = gains
    gain_one = gains[0:1]
    step = 256

    @pl.loop(0, length // step)
    def _(block):
        rows = pl.ds(pl.multiple_of(block * step, step), step)
        values = x_ref[rows].astype(F32)
        normed = (values * rms_scale(values) * gain_one).astype(BF16)
        normed_ref[rows] = normed
        qkv = mm(normed, wbuf[...]).astype(BF16)
        qkv_ref[rows] = qkv[:, : 3 * head_cols]
        for h in range(heads):
            qs[h, rows] = qkv[:, h * DH : (h + 1) * DH]
            ks[h, rows] = qkv[:, head_cols + h * DH : head_cols + (h + 1) * DH]
            vs[h, rows] = qkv[:, 2 * head_cols + h * DH : 2 * head_cols + (h + 1) * DH]

    blocks = length // LANES
    seg_keys = segments(
        lax.broadcasted_iota(jnp.int32, (1, length), 1), ends_ref, buffer, slots
    )

    @pl.loop(0, blocks)
    def _(block):
        begin = pl.multiple_of(block * LANES, LANES)
        rows = pl.ds(begin, LANES)
        window = pl.ds(pl.multiple_of((blocks - 1 - block) * LANES, LANES), length)
        seg_rows = segments(
            lax.broadcasted_iota(jnp.int32, (LANES, 1), 0) + begin, ends_ref, buffer, slots
        )
        same = seg_rows == seg_keys
        lane = lax.broadcasted_iota(jnp.int32, (LANES, LANES), 1)
        logs = jnp.zeros((LANES, LANES), F32)
        for h in range(heads):
            scores = mm(qs[h, rows], ks[h], NT) + strip_ref[h, :, window]
            scores = jnp.where(same, scores, masked_score)
            row_max = jnp.max(scores, axis=1, keepdims=True)
            raised = jnp.exp(scores - row_max)
            total = jnp.sum(raised, axis=1, keepdims=True)
            probs = (raised * (1.0 / total)).astype(BF16)
            os[h, rows] = mm(probs, vs[h]).astype(BF16)
            logs = jnp.where(lane == h, row_max + jnp.log(total), logs)
        log_ref[rows] = logs

    att_ref[...] = jnp.concatenate([os[h] for h in range(heads)], axis=1)


def attend(buffer, ends, offs, x, strip, pieces, length, heads):
    width = x.shape[1]
    count = len(pieces)
    cols = pieces[0].shape[1]
    head_cols = heads * DH
    whole = lambda i, *_: (0, 0)
    spec = pltpu.PrefetchScalarGridSpec(
        num_scalar_prefetch=2,
        grid=(1,),
        in_specs=[
            pl.BlockSpec((length, width), lambda i, *_: (buffer, 0)),
            pl.BlockSpec(strip.shape, lambda i, *_: (0, 0, 0)),
        ]
        + [pl.BlockSpec(memory_space=ANY)] * count,
        out_specs=[
            pl.BlockSpec((length, width), whole),
            pl.BlockSpec((length, 3 * head_cols), whole),
            pl.BlockSpec((length, head_cols), whole),
            pl.BlockSpec((length, LANES), whole),
            pl.BlockSpec((8, width), whole),
        ],
        scratch_shapes=[
            pltpu.VMEM((width, cols), BF16),
            pltpu.VMEM((heads, length, DH), BF16),
            pltpu.VMEM((heads, length, DH), BF16),
            pltpu.VMEM((heads, length, DH), BF16),
            pltpu.VMEM((heads, length, DH), BF16),
            pltpu.SemaphoreType.DMA((count,)),
        ],
    )
    flops = 2 * length * (width * cols + 2 * heads * DH * length)
    return pl.pallas_call(
        functools.partial(attend_kernel, buffer, ends.shape[1], heads, count),
        grid_spec=spec,
        out_shape=[
            jax.ShapeDtypeStruct((length, width), BF16),
            jax.ShapeDtypeStruct((length, 3 * head_cols), BF16),
            jax.ShapeDtypeStruct((length, head_cols), BF16),
            jax.ShapeDtypeStruct((length, LANES), F32),
            jax.ShapeDtypeStruct((8, width), F32),
        ],
        compiler_params=params(),
        cost_estimate=pl.CostEstimate(
            flops=4 * flops, bytes_accessed=8 << 20, transcendentals=heads * length * length
        ),
        name="attend",
    )(ends, offs, x, strip, *pieces)


def feed_kernel(hidden_cols, counts, order_ref, offs_ref, *refs):
    own, across, beside, diagonal, x_ref, cot_ref, gains_ref = refs[:7]
    at = 7
    groups = []
    for count in counts:
        groups.append(refs[at : at + count])
        at += count
    (
        normed_ref,
        hidden_ref,
        gate_ref,
        ff_send,
        ff_keep,
        dn_send,
        dn_keep,
        middle_keep,
        gain_sum,
        ebuf,
        sbuf,
        oabuf,
        obbuf,
        sems,
    ) = refs[at:]
    step = pl.program_id(0)
    bufs = (oabuf, obbuf, ebuf, sbuf)

    @pl.when(step == 0)
    def _():
        copies = []
        for which, (group, target) in enumerate(zip(groups, bufs)):
            copies += start_rows(group, target, offs_ref, sems.at[which])
        for copy in copies:
            copy.wait()

    cols = own.shape[1]
    upper = order_ref[2] == 0
    pairs = []
    for near, far, weights in ((own, across, oabuf), (beside, diagonal, obbuf)):
        near_sum = mm(near[...], weights[:, :cols], NT)
        far_sum = mm(far[...], weights[:, cols:], NT)
        pairs.append(
            jnp.where(upper, near_sum, far_sum) + jnp.where(upper, far_sum, near_sum)
        )
    swap = order_ref[0] == 0
    attention = jnp.where(swap, pairs[0], pairs[1]) + jnp.where(swap, pairs[1], pairs[0])
    middle = x_ref[...].astype(F32) + attention
    scale_two = rms_scale(middle)
    gain_two = gains_ref[1:2]
    normed = (middle * scale_two * gain_two).astype(BF16)
    normed_ref[...] = normed
    cot = cot_ref[...]
    part = 256
    k0 = 0.7978845608028654
    k1 = 0.044715
    for begin in range(0, hidden_cols, part):
        gate = mm(normed, ebuf[:, begin : begin + part])
        up = mm(normed, ebuf[:, hidden_cols + begin : hidden_cols + begin + part])
        square = gate * gate
        tanh = jnp.tanh(k0 * (gate + k1 * (square * gate)))
        half = 0.5 * (1.0 + tanh)
        active = gate * half
        slope = half + (0.5 * gate) * (1.0 - tanh * tanh) * (k0 + (3.0 * k0 * k1) * square)
        d_hidden = mm(cot, sbuf[:, begin : begin + part])
        hidden_ref[:, begin : begin + part] = (active * up).astype(BF16)
        gate_ref[:, begin : begin + part] = (d_hidden * up * slope).astype(BF16)
        gate_ref[:, hidden_cols + begin : hidden_cols + begin + part] = (
            d_hidden * active
        ).astype(BF16)
    ff = mm(hidden_ref[...], sbuf[...], NT).astype(BF16)
    dn = mm(gate_ref[...], ebuf[...], NT)
    sums = fold_rows(dn * middle * scale_two)
    dn = dn.astype(BF16)

    @pl.when(step == 0)
    def _():
        ff_send[...] = ff
        dn_send[...] = dn
        gain_sum[...] = sums

    @pl.when(step == 1)
    def _():
        ff_keep[...] = ff
        dn_keep[...] = dn
        middle_keep[...] = middle
        gain_sum[...] = gain_sum[...] + sums


def feed(buffer, order, offs, parts, x, cot, gains, groups, length, hidden_cols):
    width = x.shape[1]
    half = length // 2
    cols = parts[0].shape[1]
    counts = [len(group) for group in groups]
    natural = lambda i, order, *_: (order[i], 0)
    rows = lambda i, order, *_: (2 * buffer + order[i], 0)
    whole = lambda i, *_: (0, 0)
    spec = pltpu.PrefetchScalarGridSpec(
        num_scalar_prefetch=2,
        grid=(2,),
        in_specs=[pl.BlockSpec((half, cols), natural)] * 4
        + [pl.BlockSpec((half, width), rows)] * 2
        + [pl.BlockSpec((8, width), whole)]
        + [pl.BlockSpec(memory_space=ANY)] * sum(counts),
        out_specs=[
            pl.BlockSpec((half, width), natural),
            pl.BlockSpec((half, hidden_cols), natural),
            pl.BlockSpec((half, 2 * hidden_cols), natural),
        ]
        + [pl.BlockSpec((half, width), whole)] * 5
        + [pl.BlockSpec((8, width), whole)],
        scratch_shapes=[
            pltpu.VMEM((width, 2 * hidden_cols), BF16),
            pltpu.VMEM((width, hidden_cols), BF16),
            pltpu.VMEM((width, 2 * cols), BF16),
            pltpu.VMEM((width, 2 * cols), BF16),
            pltpu.SemaphoreType.DMA((4, max(counts))),
        ],
    )
    flops = 2 * length * width * (4 * cols + 7 * hidden_cols)
    return pl.pallas_call(
        functools.partial(feed_kernel, hidden_cols, counts),
        grid_spec=spec,
        out_shape=[
            jax.ShapeDtypeStruct((length, width), BF16),
            jax.ShapeDtypeStruct((length, hidden_cols), BF16),
            jax.ShapeDtypeStruct((length, 2 * hidden_cols), BF16),
            jax.ShapeDtypeStruct((half, width), BF16),
            jax.ShapeDtypeStruct((half, width), BF16),
            jax.ShapeDtypeStruct((half, width), BF16),
            jax.ShapeDtypeStruct((half, width), BF16),
            jax.ShapeDtypeStruct((half, width), F32),
            jax.ShapeDtypeStruct((8, width), F32),
        ],
        compiler_params=params(),
        cost_estimate=pl.CostEstimate(
            flops=flops, bytes_accessed=12 << 20, transcendentals=length * hidden_cols
        ),
        name="feed",
    )(order, offs, *parts, x, cot, gains, *[piece for group in groups for piece in group])


def middle_kernel(order_ref, near, far, middle_ref, cot_ref, gains_ref, d_ref, low_ref):
    upstream = near[...].astype(F32) + far[...].astype(F32)
    middle = middle_ref[...]
    d_middle = cot_ref[...].astype(F32) + norm_back(
        middle, rms_scale(middle), gains_ref[1:2], upstream
    )
    d_ref[...] = d_middle
    low_ref[...] = d_middle.astype(BF16)


def input_kernel(order_ref, near, far, x_ref, d_ref, gains_ref, out_ref):
    upstream = near[...].astype(F32) + far[...].astype(F32)
    values = x_ref[...].astype(F32)
    out_ref[...] = (
        d_ref[...] + norm_back(values, rms_scale(values), gains_ref[0:1], upstream)
    ).astype(BF16)


def output_kernel(order_ref, near, far, middle_ref, out_ref):
    out_ref[...] = (
        middle_ref[...] + (near[...].astype(F32) + far[...].astype(F32)).astype(BF16).astype(F32)
    ).astype(BF16)


def half_call(kernel, name, buffer, order, arrays, placed, outs, gains=None):
    half, width = arrays[0].shape
    steps = 3
    block = half // steps
    mine = lambda i, *_: (i, 0)
    rows = lambda i, order, *_: ((2 * buffer + order[1]) * steps + i, 0)
    in_specs = [
        pl.BlockSpec((block, width), rows if at in placed else mine)
        for at in range(len(arrays))
    ]
    operands = list(arrays)
    if gains is not None:
        in_specs.append(pl.BlockSpec((8, width), lambda i, *_: (0, 0)))
        operands.append(gains)
    return pl.pallas_call(
        kernel,
        grid_spec=pltpu.PrefetchScalarGridSpec(
            num_scalar_prefetch=1,
            grid=(steps,),
            in_specs=in_specs,
            out_specs=[pl.BlockSpec((block, width), mine) for _ in outs],
        ),
        out_shape=[jax.ShapeDtypeStruct((half, width), kind) for kind in outs],
        compiler_params=params(),
        cost_estimate=pl.CostEstimate(
            flops=20 * half * width, bytes_accessed=12 * half * width, transcendentals=0
        ),
        name=name,
    )(order, *operands)


def back_kernel(buffer, slots, heads, counts, ends_ref, offs_ref, order_ref, *refs):
    near, far, qkv_ref, log_ref, strip_ref, x_ref = refs[:6]
    at = 6
    o_pieces = refs[at : at + counts[0]]
    at += counts[0]
    p_pieces = refs[at : at + counts[1]]
    at += counts[1]
    (
        low_ref,
        dqkv_ref,
        dn_send,
        dn_keep,
        gain_sum,
        dstrip,
        wbuf,
        obuf,
        qs,
        ks,
        vs,
        gs,
        qt,
        gt,
        dkt,
        dvt,
        dq,
        sems,
    ) = refs[at:]
    length = qkv_ref.shape[0]
    half = length // 2
    head_cols = heads * DH
    o_copies = start_rows(o_pieces, obuf, offs_ref, sems.at[0])
    p_copies = start_rows(p_pieces, wbuf, offs_ref, sems.at[1])
    mine = pl.ds(pl.multiple_of(order_ref[1] * half, LANES), half)
    other = pl.ds(pl.multiple_of(order_ref[0] * half, LANES), half)
    low_ref[mine] = near[...]
    low_ref[other] = far[...]
    for h in range(heads):
        qs[h] = qkv_ref[:, h * DH : (h + 1) * DH]
        ks[h] = qkv_ref[:, head_cols + h * DH : head_cols + (h + 1) * DH]
        vs[h] = qkv_ref[:, 2 * head_cols + h * DH : 2 * head_cols + (h + 1) * DH]
        qt[h] = qs[h].T
    dstrip[...] = jnp.zeros_like(dstrip)
    dkt[...] = jnp.zeros_like(dkt)
    dvt[...] = jnp.zeros_like(dvt)
    for copy in o_copies + p_copies:
        copy.wait()
    grads = mm(low_ref[...], obuf[:, :head_cols]).astype(BF16)
    for h in range(heads):
        gs[h] = grads[:, h * DH : (h + 1) * DH]
        gt[h] = gs[h].T
    blocks = length // LANES
    seg_keys = segments(
        lax.broadcasted_iota(jnp.int32, (1, length), 1), ends_ref, buffer, slots
    )

    @pl.loop(0, blocks)
    def _(block):
        begin = pl.multiple_of(block * LANES, LANES)
        rows = pl.ds(begin, LANES)
        window = pl.ds(pl.multiple_of((blocks - 1 - block) * LANES, LANES), length)
        seg_rows = segments(
            lax.broadcasted_iota(jnp.int32, (LANES, 1), 0) + begin, ends_ref, buffer, slots
        )
        same = seg_rows == seg_keys
        logs = log_ref[rows]
        for h in range(heads):
            scores = mm(qs[h, rows], ks[h], NT) + strip_ref[h, :, window]
            scores = jnp.where(same, scores, masked_score)
            probs = jnp.exp(scores - logs[:, h : h + 1])
            d_probs = mm(gs[h, rows], vs[h], NT)
            inner = jnp.sum(probs * d_probs, axis=1, keepdims=True)
            d_scores = (probs * (d_probs - inner)).astype(BF16)
            dstrip[h, :, window] = dstrip[h, :, window] + d_scores.astype(F32)
            dq[h, rows] = mm(d_scores, ks[h]).astype(BF16)
            dkt[h] = dkt[h] + mm(qt[h, :, rows], d_scores)
            dvt[h] = dvt[h] + mm(gt[h, :, rows], probs.astype(BF16))

    outs = [dq[h] for h in range(heads)]
    outs += [dkt[h].T.astype(BF16) for h in range(heads)]
    outs += [dvt[h].T.astype(BF16) for h in range(heads)]
    dqkv_ref[...] = jnp.concatenate(outs, axis=1)
    sums = []
    for target, which in ((dn_send, other), (dn_keep, mine)):
        dn = mm(dqkv_ref[which], wbuf[:, : 3 * head_cols], NT)
        values = x_ref[which].astype(F32)
        sums.append(fold_rows(dn * values * rms_scale(values)))
        target[...] = dn.astype(BF16)
    gain_sum[...] = sums[0] + sums[1]


def back(buffer, ends, offs, order, near, far, qkv, logs, strip, x, o_pieces, p_pieces, heads):
    length = qkv.shape[0]
    half = length // 2
    width = x.shape[1]
    head_cols = heads * DH
    counts = (len(o_pieces), len(p_pieces))
    whole = lambda i, *_: (0, 0)
    whole3 = lambda i, *_: (0, 0, 0)
    spec = pltpu.PrefetchScalarGridSpec(
        num_scalar_prefetch=3,
        grid=(1,),
        in_specs=[
            pl.BlockSpec((half, width), whole),
            pl.BlockSpec((half, width), whole),
            pl.BlockSpec(qkv.shape, whole),
            pl.BlockSpec(logs.shape, whole),
            pl.BlockSpec(strip.shape, whole3),
            pl.BlockSpec((length, width), lambda i, *_: (buffer, 0)),
        ]
        + [pl.BlockSpec(memory_space=ANY)] * sum(counts),
        out_specs=[
            pl.BlockSpec((length, width), whole),
            pl.BlockSpec((length, 3 * head_cols), whole),
            pl.BlockSpec((half, width), whole),
            pl.BlockSpec((half, width), whole),
            pl.BlockSpec((8, width), whole),
            pl.BlockSpec(strip.shape, whole3),
        ],
        scratch_shapes=[
            pltpu.VMEM((width, p_pieces[0].shape[1]), BF16),
            pltpu.VMEM((width, o_pieces[0].shape[1]), BF16),
            pltpu.VMEM((heads, length, DH), BF16),
            pltpu.VMEM((heads, length, DH), BF16),
            pltpu.VMEM((heads, length, DH), BF16),
            pltpu.VMEM((heads, length, DH), BF16),
            pltpu.VMEM((heads, DH, length), BF16),
            pltpu.VMEM((heads, DH, length), BF16),
            pltpu.VMEM((heads, DH, length), F32),
            pltpu.VMEM((heads, DH, length), F32),
            pltpu.VMEM((heads, length, DH), BF16),
            pltpu.SemaphoreType.DMA((2, max(counts))),
        ],
    )
    return pl.pallas_call(
        functools.partial(back_kernel, buffer, ends.shape[1], heads, counts),
        grid_spec=spec,
        out_shape=[
            jax.ShapeDtypeStruct((length, width), BF16),
            jax.ShapeDtypeStruct((length, 3 * head_cols), BF16),
            jax.ShapeDtypeStruct((half, width), BF16),
            jax.ShapeDtypeStruct((half, width), BF16),
            jax.ShapeDtypeStruct((8, width), F32),
            jax.ShapeDtypeStruct(strip.shape, F32),
        ],
        compiler_params=params(),
        cost_estimate=pl.CostEstimate(
            flops=40 * heads * DH * length * length,
            bytes_accessed=16 << 20,
            transcendentals=heads * length * length,
        ),
        name="back",
    )(ends, offs, order, near, far, qkv, logs, strip, x, *o_pieces, *p_pieces)


def scatter_rows(total, offs_ref, evens, odds):
    rows = evens[0].shape[0]
    for at in range(2 * len(evens)):
        begin = pl.multiple_of(offs_ref[at], 8)
        block = total[pl.ds(begin, rows)]
        if at % 2:
            odds[at // 2][...] = block.astype(BF16)
        else:
            evens[at // 2][...] = block


def feed_grad_kernel(count, hidden_cols, offs_ref, *refs):
    buffers = 2
    normed = refs[:buffers]
    gates = refs[buffers : 2 * buffers]
    hiddens = refs[2 * buffers : 3 * buffers]
    cot_ref = refs[3 * buffers]
    outs = refs[3 * buffers + 1 : -1]
    total = refs[-1]
    length = normed[0].shape[0]
    width = normed[0].shape[1]
    part = 256
    for begin in range(0, width, part):
        cols = slice(begin, begin + part)
        total[cols, : 2 * hidden_cols] = mm(normed[0][:, cols], gates[0][...], TN) + mm(
            normed[1][:, cols], gates[1][...], TN
        )
        total[cols, 2 * hidden_cols :] = mm(
            cot_ref[:length, cols], hiddens[0][...], TN
        ) + mm(cot_ref[length:, cols], hiddens[1][...], TN)
    if count > 1:
        scatter_rows(total, offs_ref, outs[: count // 2], outs[count // 2 :])
    else:
        outs[0][...] = total[...]


def attend_grad_kernel(count, heads, offs_ref, *refs):
    buffers = 2
    normed = refs[:buffers]
    dqkv = refs[buffers : 2 * buffers]
    lows = refs[2 * buffers : 3 * buffers]
    atts = refs[3 * buffers : 4 * buffers]
    sums_ref = refs[4 * buffers]
    outs = refs[4 * buffers + 1 : -1]
    total = refs[-1]
    width = normed[0].shape[1]
    head_cols = heads * DH
    qkv_cols = 3 * head_cols
    part = 256
    rows = lax.broadcasted_iota(jnp.int32, (LANES, width), 0)
    first = sums_ref[0] + sums_ref[1]
    second = sums_ref[2] + sums_ref[3]
    gain_rows = jnp.where(
        rows == DH,
        jnp.sum(first, axis=0, keepdims=True),
        jnp.where(rows == DH + 1, jnp.sum(second, axis=0, keepdims=True), 0.0),
    )
    gain_cols = gain_rows.T
    for begin in range(0, width, part):
        cols = slice(begin, begin + part)
        total[cols, :qkv_cols] = mm(normed[0][:, cols], dqkv[0][...], TN) + mm(
            normed[1][:, cols], dqkv[1][...], TN
        )
        total[cols, qkv_cols : qkv_cols + DH] = gain_cols[cols, DH:]
        total[cols, qkv_cols + DH : qkv_cols + DH + head_cols] = mm(
            lows[0][:, cols], atts[0][...], TN
        ) + mm(lows[1][:, cols], atts[1][...], TN)
    if count > 1:
        scatter_rows(total, offs_ref, outs[: count // 2], outs[count // 2 :])
    else:
        outs[0][...] = total[...]


def grad_call(kernel, name, offs, operands, width, cols, count, rows, flops):
    vmem = pl.BlockSpec(memory_space=pltpu.VMEM)
    if count > 1:
        shapes = [jax.ShapeDtypeStruct((rows, cols), F32)] * (count // 2)
        shapes += [jax.ShapeDtypeStruct((rows, cols), BF16)] * (count // 2)
    else:
        shapes = [jax.ShapeDtypeStruct((width, cols), F32)]
    return pl.pallas_call(
        kernel,
        in_specs=[pl.BlockSpec(memory_space=pltpu.SMEM)] + [vmem] * len(operands),
        out_specs=[vmem] * len(shapes),
        out_shape=shapes,
        scratch_shapes=[pltpu.VMEM((width, cols), F32)],
        compiler_params=params(),
        cost_estimate=pl.CostEstimate(flops=2 * flops, bytes_accessed=14 << 20, transcendentals=0),
        name=name,
    )(offs, *operands)


def bucket_kernel(heads, near_ref, far_ref, out_ref):
    lanes = near_ref.shape[2]
    blocks = (lanes // LANES + 1) // 2
    begin = (blocks - 2) * LANES
    end = begin + 3 * LANES
    rows = lax.broadcasted_iota(jnp.int32, (LANES, 3 * LANES), 0)
    ids = bucket_of(
        lax.broadcasted_iota(jnp.int32, (LANES, 3 * LANES), 1) - LANES - rows
    )
    lane = lax.broadcasted_iota(jnp.int32, (1, LANES), 1)
    out = jnp.zeros((1, LANES), F32)
    for h in range(heads):
        strip = near_ref[h] + far_ref[h]
        left = jnp.sum(jnp.sum(strip[:, :begin], axis=0, keepdims=True), axis=1, keepdims=True)
        right = jnp.sum(jnp.sum(strip[:, end:], axis=0, keepdims=True), axis=1, keepdims=True)
        out = out + jnp.where(lane == h * 32 + 15, left, 0.0)
        out = out + jnp.where(lane == h * 32 + 31, right, 0.0)
        middle = strip[:, begin:end]
        for b in range(32):
            if b == 16:
                continue
            part = jnp.sum(jnp.where(ids == b, middle, 0.0), axis=0, keepdims=True)
            part = jnp.sum(part, axis=1, keepdims=True)
            out = out + jnp.where(lane == h * 32 + b, part, 0.0)
    out_ref[...] = jnp.broadcast_to(out, (8, LANES))


def norm_kernel(wide, narrow, lists, gain_at, *refs):
    at = 0
    groups = []
    for count in lists:
        groups.append(refs[at : at + count])
        at += count
    bucket_ref = refs[at]
    outs = refs[at + 1 : at + 1 + len(lists)]
    stat_ref, gain_ref, table_ref, block, inbox, padded, send_sems, recv_sems = refs[
        at + 1 + len(lists) :
    ]
    total = wide * narrow
    w = lax.axis_index("wide")
    n = lax.axis_index("narrow")
    me = w * narrow + n
    barrier = pltpu.get_barrier_semaphore()

    @pl.loop(1, total)
    def _(k):
        peer = (me + k) % total
        pl.semaphore_signal(
            barrier, inc=1, device_id=(peer // narrow, peer % narrow), device_id_type=MESH
        )

    squares = jnp.zeros((8, LANES), F32)
    for which, (group, out) in enumerate(zip(groups, outs)):
        value = group[0][...].astype(F32)
        for more in group[1:]:
            value = value + more[...].astype(F32)
        out[...] = value
        squared = value * value
        if which == 0:
            lane = lax.broadcasted_iota(jnp.int32, value.shape, 1)
            inside = (lane >= gain_at) & (lane < gain_at + DH)
            squared = jnp.where(inside, 0.0, squared)
        squared = jnp.sum(squared, axis=1, keepdims=True)
        squares = squares + jnp.sum(squared, axis=0, keepdims=True)
    rows = outs[0].shape[0]
    low = gain_at // LANES * LANES
    padded[...] = jnp.zeros_like(padded)
    padded[0:rows] = outs[0][:, low : low + LANES]
    turned = padded[...].T
    row = lax.broadcasted_iota(jnp.int32, (8, LANES), 0)
    here = gain_at - low
    mine = jnp.where(row == 0, squares, 0.0)
    mine = jnp.where(row == 1, turned[here : here + 1], mine)
    mine = jnp.where(row == 2, turned[here + 1 : here + 2], mine)
    mine = jnp.where(row == 3, bucket_ref[...], mine)
    block[...] = mine
    inbox[me] = mine
    pl.semaphore_wait(barrier, total - 1)

    @pl.loop(1, total)
    def _(k):
        peer = (me + k) % total
        pltpu.make_async_remote_copy(
            src_ref=block,
            dst_ref=inbox.at[me],
            send_sem=send_sems.at[k],
            recv_sem=recv_sems.at[total - k],
            device_id=(peer // narrow, peer % narrow),
            device_id_type=MESH,
        ).start()

    @pl.loop(1, total)
    def _(k):
        peer = (me + k) % total
        copy = pltpu.make_async_remote_copy(
            src_ref=block,
            dst_ref=inbox.at[peer],
            send_sem=send_sems.at[k],
            recv_sem=recv_sems.at[k],
            device_id=(peer // narrow, peer % narrow),
            device_id_type=MESH,
        )
        copy.wait_send()
        copy.wait_recv()

    columns = [jnp.zeros((8, LANES), F32) for _ in range(narrow)]
    gain_square = jnp.zeros((8, LANES), F32)
    square_total = jnp.zeros((8, LANES), F32)
    for a in range(wide):
        gains = jnp.zeros((8, LANES), F32)
        for b in range(narrow):
            got = inbox[a * narrow + b]
            gains = gains + got
            columns[b] = columns[b] + got
        square_total = square_total + gains
        gain_square = gain_square + gains * gains
    own = inbox[w * narrow]
    for b in range(1, narrow):
        own = own + inbox[w * narrow + b]
    gain_ref[...] = own
    pick = (row == 1) | (row == 2)
    gain_square = jnp.where(pick, gain_square, 0.0)
    norm_square = square_total[0:1, 0:1] + jnp.sum(
        jnp.sum(gain_square, axis=0, keepdims=True), axis=1, keepdims=True
    )
    heads = LANES // 32 - 1
    lane = lax.broadcasted_iota(jnp.int32, (32, LANES), 1)
    depth = lax.broadcasted_iota(jnp.int32, (32, LANES), 0)
    table = jnp.zeros((32, LANES), F32)
    for b in range(narrow):
        line = columns[b][3:4]
        norm_square = norm_square + jnp.sum(line * line, axis=1, keepdims=True)
        for h in range(heads):
            column = jnp.sum(
                jnp.where(lane == depth + 32 * h, line, 0.0), axis=1, keepdims=True
            )
            table = jnp.where(lane == b * heads + h, column, table)
    table_ref[...] = table
    global_norm = jnp.sqrt(norm_square)
    factor = jnp.minimum(1.0, clip_limit / (global_norm + 1e-06))
    stat_ref[...] = jnp.where(row == 0, global_norm, factor)


def norm_call(wide, narrow, groups, bucket, gain_at):
    vmem = pl.BlockSpec(memory_space=pltpu.VMEM)
    lists = tuple(len(group) for group in groups)
    total = wide * narrow
    operands = [piece for group in groups for piece in group] + [bucket]
    return pl.pallas_call(
        functools.partial(norm_kernel, wide, narrow, lists, gain_at),
        in_specs=[vmem] * len(operands),
        out_specs=[vmem] * (len(lists) + 3),
        out_shape=[jax.ShapeDtypeStruct(group[0].shape, F32) for group in groups]
        + [
            jax.ShapeDtypeStruct((8, LANES), F32),
            jax.ShapeDtypeStruct((8, LANES), F32),
            jax.ShapeDtypeStruct((32, LANES), F32),
        ],
        scratch_shapes=[
            pltpu.VMEM((8, LANES), F32),
            pltpu.VMEM((total, 8, LANES), F32),
            pltpu.VMEM((LANES, LANES), F32),
            pltpu.SemaphoreType.DMA((total,)),
            pltpu.SemaphoreType.DMA((total,)),
        ],
        compiler_params=params(collective_id=0, has_side_effects=True),
        cost_estimate=pl.CostEstimate(flops=1 << 20, bytes_accessed=4 << 20, transcendentals=0),
        name="norm",
    )(*operands)


def adam_kernel(heads, hidden_cols, parts, att_ref, feed_ref, gain_ref, table_ref, stat_ref, *refs):
    weights, firsts, seconds = refs[:6], refs[6:12], refs[12:18]
    outs = refs[18:36]
    o_pad, s_pad = refs[36:]
    factor = stat_ref[1:2, 0:1]
    head_cols = heads * DH
    rows = att_ref.shape[0]
    gain_at = 3 * head_cols

    def update(which, index, gradient):
        results = adam_update(
            weights[which][index],
            firsts[which][index],
            seconds[which][index],
            factor * gradient,
            step_rates[which],
            decay_rates[which],
        )
        for at in range(3):
            outs[6 * at + which][index] = results[at]

    for i in range(3):
        update(0, i, att_ref[:, i * head_cols : (i + 1) * head_cols])
    part = hidden_cols // parts
    for j in range(parts):
        span = slice(j * part, (j + 1) * part)
        for i in range(2):
            begin = (3 * j + i) * part if parts > 1 else i * part
            update(2, (i, slice(None), span), feed_ref[:, begin : begin + part])
    o_pad[...] = jnp.zeros_like(o_pad)
    s_pad[...] = jnp.zeros_like(s_pad)
    o_pad[0:rows] = att_ref[:, gain_at + DH :]
    for j in range(parts):
        begin = (3 * j + 2) * part
        s_pad[0:rows, j * part : (j + 1) * part] = feed_ref[:, begin : begin + part]
    update(1, slice(None), o_pad[...].T[:head_cols, :rows])
    update(3, slice(None), s_pad[...].T[:, :rows])
    columns = weights[4].shape[1]
    update(4, slice(None), table_ref[:, :columns])
    update(5, slice(None), gain_ref[1:3, :rows])


def adam_call(
    att, feed_grad, gain, table, stat, params_in, firsts, seconds, heads, hidden_cols, direct=False
):
    vmem = pl.BlockSpec(memory_space=pltpu.VMEM)
    operands = [att, feed_grad, gain, table, stat, *params_in, *firsts, *seconds]
    pad_cols = att.shape[1] - (3 * heads * DH + DH)
    return pl.pallas_call(
        functools.partial(adam_kernel, heads, hidden_cols, 2 if direct else 1),
        in_specs=[vmem] * len(operands),
        out_specs=[vmem] * 18,
        out_shape=[jax.ShapeDtypeStruct(a.shape, F32) for a in params_in] * 3,
        scratch_shapes=[
            pltpu.VMEM((LANES, pad_cols), F32),
            pltpu.VMEM((LANES, hidden_cols), F32),
        ],
        compiler_params=params(),
        cost_estimate=pl.CostEstimate(flops=4 << 20, bytes_accessed=8 << 20, transcendentals=0),
        name="adam",
    )(*operands)


def place_kernel(offs_ref, *refs):
    step = pl.program_id(0)
    for at, piece in enumerate(refs[:-1]):

        @pl.when(step == at)
        def _(piece=piece):
            refs[-1][...] = piece[...]


def place(pieces, offs, rows):
    half, width = pieces[0].shape
    count = len(pieces)
    return pl.pallas_call(
        place_kernel,
        grid_spec=pltpu.PrefetchScalarGridSpec(
            num_scalar_prefetch=1,
            grid=(count,),
            in_specs=[pl.BlockSpec((half, width), lambda i, *_: (0, 0))] * count,
            out_specs=pl.BlockSpec((half, width), lambda i, offs: (offs[i] // half, 0)),
        ),
        out_shape=jax.ShapeDtypeStruct((rows, width), pieces[0].dtype),
        compiler_params=params(),
        cost_estimate=pl.CostEstimate(
            flops=0, bytes_accessed=4 * rows * width, transcendentals=0
        ),
        name="place",
    )(offs, *pieces)


def bias_strip(bucket_bias, n, heads, length):
    table = lax.dynamic_slice_in_dim(bucket_bias, n * heads, heads, 1).T
    blocks = length // LANES
    near_r = (
        jnp.arange(3 * LANES, dtype=jnp.int32)[None, :]
        - LANES
        - jnp.arange(LANES, dtype=jnp.int32)[:, None]
    )
    near_ids = bucket_of(near_r)
    near = sum(
        jnp.where(near_ids == b, table[:, b][:, None, None], 0.0) for b in range(32) if b != 16
    )
    far_shape = (heads, LANES, (blocks - 2) * LANES)
    return jnp.concatenate(
        [
            jnp.broadcast_to(table[:, 15][:, None, None], far_shape),
            near,
            jnp.broadcast_to(table[:, 31][:, None, None], far_shape),
        ],
        axis=2,
    )


def general_body(wide, narrow, *arguments):
    (
        block_input,
        cotangent,
        lengths,
        project_weight,
        output_weight,
        expand_weight,
        shrink_weight,
        bucket_bias,
        norm_gains,
    ) = arguments[:9]
    firsts = arguments[9:15]
    seconds = arguments[15:21]
    tokens, width = block_input.shape
    buffers = lengths.shape[0]
    length = tokens // buffers
    rows = norm_gains.shape[1]
    head_cols = project_weight.shape[2]
    heads = head_cols // DH
    hidden_cols = expand_weight.shape[2]
    w = lax.axis_index("wide")
    n = lax.axis_index("narrow")
    core = n % 2

    def swap(value, wide_mask, narrow_mask):
        pairs = [
            (a * narrow + b, (a ^ wide_mask) * narrow + (b ^ narrow_mask))
            for a in range(wide)
            for b in range(narrow)
        ]
        return lax.ppermute(value, ("wide", "narrow"), pairs)

    def gather(piece):
        return [lax.all_gather(piece, "wide", axis=0, tiled=True)]

    def reduce_wide(outs):
        return [lax.psum_scatter(outs[0], "wide", scatter_dimension=0, tiled=True)]

    offs = jnp.zeros((1,), jnp.int32)
    order = jnp.stack([1 - core, core, n // 2])

    p_piece = jnp.concatenate(
        [
            project_weight[0],
            project_weight[1],
            project_weight[2],
            norm_gains.T,
            jnp.zeros((rows, DH - 2), F32),
        ],
        axis=1,
    ).astype(BF16)
    p_pieces = gather(p_piece)
    o_piece = output_weight.astype(BF16).T
    o_pair = jnp.concatenate([o_piece, swap(o_piece, 0, 2)], axis=1)
    oa_pieces = gather(o_pair)
    ob_pieces = [swap(piece, 0, 1) for piece in oa_pieces]
    e_pieces = gather(
        jnp.concatenate([expand_weight[0], expand_weight[1]], axis=1).astype(BF16)
    )
    s_pieces = gather(shrink_weight.astype(BF16).T)

    ends = jnp.cumsum(lengths, axis=1)
    strip = bias_strip(bucket_bias, n, heads, length)

    normed_one, qkv, atts, logs, fours = [], [], [], [], []
    for b in range(buffers):
        normed, rows_b, att, log, gains = attend(
            b, ends, offs, block_input, strip, p_pieces, length, heads
        )
        normed_one.append(normed)
        qkv.append(rows_b)
        atts.append(att)
        logs.append(log)
        across = swap(att, 0, 2)
        fours.append((att, across, swap(att, 0, 1), swap(across, 0, 1)))

    def core_sum(kept, sent):
        return (kept.astype(F32) + swap(sent, 0, 1).astype(F32)).astype(BF16)

    normed_two, hiddens, gates, middles, ff_sums, dn_sums, sums_two = [], [], [], [], [], [], []
    for b in range(buffers):
        normed, hidden, gate, ff_send, ff_keep, dn_send, dn_keep, middle, sums = feed(
            b,
            order,
            offs,
            fours[b],
            block_input,
            cotangent,
            gains,
            (oa_pieces, ob_pieces, e_pieces, s_pieces),
            length,
            hidden_cols,
        )
        normed_two.append(normed)
        hiddens.append(hidden)
        gates.append(gate)
        middles.append(middle)
        sums_two.append(sums)
        dn_sums.append(core_sum(dn_keep, dn_send))
        ff_sums.append(core_sum(ff_keep, ff_send))

    d_middles, lows = [], []
    for b in range(buffers):
        d_middle, low = half_call(
            middle_kernel,
            "middle",
            b,
            order,
            [dn_sums[b], swap(dn_sums[b], 0, 2), middles[b], cotangent],
            (3,),
            (F32, BF16),
            gains,
        )
        d_middles.append(d_middle)
        lows.append((low, swap(low, 0, 1)))

    count = 1
    feed_outs = grad_call(
        functools.partial(feed_grad_kernel, count, hidden_cols),
        "feed_grad",
        offs,
        [*normed_two, *gates, *hiddens, cotangent],
        width,
        3 * hidden_cols,
        count,
        rows,
        2 * tokens * width * 3 * hidden_cols,
    )
    feed_group = reduce_wide(feed_outs)

    low_full, dqkv, dn_one, sums_one, strips = [], [], [], [], []
    for b in range(buffers):
        low, grads, dn_send, dn_keep, sums, dstrip = back(
            b,
            ends,
            offs,
            order,
            lows[b][0],
            lows[b][1],
            qkv[b],
            logs[b],
            strip,
            block_input,
            oa_pieces,
            p_pieces,
            heads,
        )
        low_full.append(low)
        dqkv.append(grads)
        sums_one.append(sums)
        strips.append(dstrip)
        dn_one.append(core_sum(dn_keep, dn_send))

    gain_at = 3 * head_cols
    att_outs = grad_call(
        functools.partial(attend_grad_kernel, count, heads),
        "attend_grad",
        offs,
        [*normed_one, *dqkv, *low_full, *atts, jnp.stack(sums_one + sums_two)],
        width,
        gain_at + DH + head_cols,
        count,
        rows,
        2 * tokens * width * 4 * head_cols,
    )
    att_group = reduce_wide(att_outs)
    vmem = pl.BlockSpec(memory_space=pltpu.VMEM)
    bucket = pl.pallas_call(
        functools.partial(bucket_kernel, heads),
        in_specs=[vmem, vmem],
        out_specs=vmem,
        out_shape=jax.ShapeDtypeStruct((8, LANES), F32),
        compiler_params=params(),
        cost_estimate=pl.CostEstimate(flops=8 << 20, bytes_accessed=4 << 20, transcendentals=0),
        name="bucket",
    )(*strips)

    half_offs = jnp.stack(
        [
            b * length + which * (length // 2)
            for b in range(buffers)
            for which in (core, 1 - core)
        ]
    )
    out_halves, in_halves = [], []
    for b in range(buffers):
        (half,) = half_call(
            output_kernel,
            "output",
            b,
            order,
            [ff_sums[b], swap(ff_sums[b], 0, 2), middles[b]],
            (),
            (BF16,),
        )
        out_halves += [half, swap(half, 0, 1)]
        (half,) = half_call(
            input_kernel,
            "input",
            b,
            order,
            [dn_one[b], swap(dn_one[b], 0, 2), block_input, d_middles[b]],
            (2,),
            (BF16,),
            gains,
        )
        in_halves += [half, swap(half, 0, 1)]
    block_output = place(out_halves, half_offs, tokens)
    input_gradient = place(in_halves, half_offs, tokens)

    att_grad, feed_grad, stat, gain, table_sum = norm_call(
        wide, narrow, [att_group, feed_group], bucket, gain_at
    )
    results = adam_call(
        att_grad,
        feed_grad,
        gain,
        table_sum,
        stat,
        arguments[3:9],
        firsts,
        seconds,
        heads,
        hidden_cols,
    )
    return (block_output, input_gradient, stat[0, 0], *results)


class Place:
    def __init__(self, wide, narrow):
        self.wide, self.narrow = wide, narrow
        self.w = lax.axis_index("wide")
        self.n = lax.axis_index("narrow")
        self.me = self.w * narrow + self.n
        self.z, self.x = self.w // 2, self.w % 2
        self.y, self.core = self.n // 2, self.n % 2
        self.n_far = (self.n + 2) % 4
        self.n_beside = self.n + 1 - 2 * self.core
        self.n_diag = (self.n_beside + 2) % 4
        self.across = (self.w, self.n_far)
        self.beside = (self.w, self.n_beside)
        self.flip = (self.z * 2 + 1 - self.x, self.n)

    def along(self, m):
        return (((self.z + m) % 4) * 2 + self.x, self.n)

    def near_owner(self, m):
        return ((self.z + m) % 4) * 2 + self.x

    def far_owner(self, m):
        return ((self.z + m) % 4) * 2 + 1 - self.x

    def peer(self, k):
        device = (self.me + k) % (self.wide * self.narrow)
        return device, (device // self.narrow, device % self.narrow)


def remote(source, target, send_sem, recv_sem, peer):
    return pltpu.make_async_remote_copy(
        src_ref=source,
        dst_ref=target,
        send_sem=send_sem,
        recv_sem=recv_sem,
        device_id=peer,
        device_id_type=MESH,
    )


class Gather:
    def __init__(self, spot, view, ssem, rsem):
        self.spot, self.view, self.ssem, self.rsem = spot, view, ssem, rsem

    def copy(self, owner, slot, peer):
        return remote(
            self.view(owner), self.view(owner), self.ssem.at[slot], self.rsem.at[owner], peer
        )

    def begin(self):
        for m in (2, 1, 3):
            self.copy(self.spot.w, m - 1, self.spot.along(m)).start()
        self.copy(self.spot.w, 3, self.spot.flip).start()

    def forward(self):
        for m in (3, 1, 2):
            owner = self.spot.near_owner(4 - m)
            self.copy(owner, 0, self.spot.flip).wait_recv()
            self.copy(owner, 3 + m, self.spot.flip).start()

    def finish(self):
        for m in range(4):
            self.copy(self.spot.far_owner(4 - m), 0, self.spot.flip).wait_recv()

    def drain(self):
        for m in (1, 2, 3):
            self.copy(self.spot.w, m - 1, self.spot.along(m)).wait_send()
        for m in range(4):
            self.copy(self.spot.near_owner(4 - m), 3 + m, self.spot.flip).wait_send()


class Reduce:
    def __init__(self, spot, even, odd, flipped, mixed, landed, sems_s, sems_r):
        self.spot, self.even, self.odd = spot, even, odd
        self.flipped, self.mixed, self.landed = flipped, mixed, landed
        self.sems_s, self.sems_r = sems_s, sems_r

    def over(self, m):
        return remote(
            self.odd(m), self.flipped.at[m], self.sems_s.at[m], self.sems_r.at[m], self.spot.flip
        )

    def along(self, m):
        return remote(
            self.mixed.at[m - 1],
            self.landed.at[m - 1],
            self.sems_s.at[3 + m],
            self.sems_r.at[3 + m],
            self.spot.along(m),
        )

    def begin(self):
        for m in (2, 1, 3, 0):
            self.over(m).start()

    def relay(self):
        for m in (2, 1, 3):
            self.over(m).wait_recv()
            self.mixed[m - 1] = (
                self.even(m).astype(F32) + self.flipped[m].astype(F32)
            ).astype(BF16)
            self.along(m).start()

    def result(self):
        self.over(0).wait_recv()
        value = self.even(0).astype(F32) + self.flipped[0].astype(F32)
        for m in (1, 2, 3):
            self.along(m).wait_recv()
            value = value + self.landed[m - 1].astype(F32)
        return value

    def drain(self):
        for m in range(4):
            self.over(m).wait_send()
        for m in (1, 2, 3):
            self.along(m).wait_send()


def segments_of(index, lengths_ref, buffer, slots):
    end = lengths_ref[buffer, 0]
    total = (index >= end).astype(jnp.int32)
    for slot in range(1, slots):
        end = end + lengths_ref[buffer, slot]
        total = total + (index >= end).astype(jnp.int32)
    return total


def layer_kernel(dims, *refs):
    buffers, slots, heads, hidden_cols, wide, narrow = dims
    (
        lengths_ref,
        bias_ref,
        x_ref,
        cot_ref,
        pw_ref,
        ow_ref,
        ew_ref,
        sw_ref,
        gn_ref,
        out_ref,
        in_ref,
        p_grad,
        o_grad,
        feed_grad,
        stat_ref,
        gain_ref,
        table_ref,
        strip,
        dstrip,
        pbuf,
        obuf,
        fbuf,
        att_ref,
        qkv_ref,
        log_ref,
        low_ref,
        middle_ref,
        hid,
        dg,
        total,
        opad,
        gpad,
        feed_flip,
        feed_mix,
        feed_land,
        o_even,
        o_odd,
        o_flip,
        o_mix,
        o_land,
        p_odd,
        p_flip,
        p_mix,
        p_land,
        ff_out,
        ff_in,
        ff_sum,
        dn_out,
        dn_in,
        dn_sum,
        dn_far,
        ws,
        kt,
        vt,
        qt,
        gt,
        dkt,
        dvt,
        gain_two_sum,
        block,
        inbox,
        gather_s,
        gather_r,
        lone_s,
        lone_r,
        red_s,
        red_r,
        norm_s,
        norm_r,
        credit,
    ) = refs
    spot = Place(wide, narrow)
    core = spot.core
    devices = wide * narrow
    tokens, width = x_ref.shape
    length = tokens // buffers
    half = length // 2
    head_cols = heads * DH
    qkv_cols = 3 * head_cols
    part = hidden_cols // 2
    chunk = 3 * part
    blocks = length // LANES
    owned = gn_ref.shape[1]
    normed_one, normed_two = in_ref, out_ref
    barrier = pltpu.get_barrier_semaphore()

    @pl.loop(1, devices)
    def _(k):
        pl.semaphore_signal(barrier, inc=1, device_id=spot.peer(k)[1], device_id_type=MESH)

    def at_rows(owner):
        return pl.ds(pl.multiple_of(owner * owned, 16), owned)

    def lone(view_from, view_to, slot, peer):
        return remote(view_from, view_to, lone_s.at[slot], lone_r.at[slot], peer)

    mine = at_rows(spot.w)
    gpad[...] = jnp.zeros_like(gpad)
    gpad[0:2, 0:owned] = gn_ref[...]
    pbuf[mine] = jnp.concatenate(
        [pw_ref[0], pw_ref[1], pw_ref[2], gpad[...].T[:owned, :DH]], axis=1
    ).astype(BF16)
    opad[...] = jnp.zeros_like(opad)
    opad[0:head_cols, 0:owned] = ow_ref[...]
    obuf[spot.n, mine] = opad[...].T[:owned, :head_cols].astype(BF16)
    pl.semaphore_wait(barrier, devices - 1)
    split = 3 * LANES
    projections = [
        Gather(
            spot,
            lambda v, span=span: pbuf.at[at_rows(v), span],
            gather_s.at[at],
            gather_r.at[at],
        )
        for at, span in enumerate((slice(0, split), slice(split, qkv_cols + DH)))
    ]
    for group in projections:
        group.begin()
    o_views = [
        lambda v: obuf.at[spot.n, at_rows(v)],
        lambda v: obuf.at[spot.n_far, at_rows(v)],
    ]
    outs_gather = [
        Gather(spot, view, gather_s.at[2 + at], gather_r.at[2 + at])
        for at, view in enumerate(o_views)
    ]
    lone(o_views[0](spot.w), o_views[0](spot.w), 0, spot.across).start()
    for j in range(2):
        span = slice(j * part, (j + 1) * part)
        fbuf[mine, j * chunk : j * chunk + part] = ew_ref[0, :, span].astype(BF16)
        fbuf[mine, j * chunk + part : j * chunk + 2 * part] = ew_ref[1, :, span].astype(BF16)
        fbuf[mine, j * chunk + 2 * part : (j + 1) * chunk] = sw_ref[:, span].astype(BF16)
    piece = chunk // 2
    feeds_gather = [
        Gather(
            spot,
            lambda v, at=at: fbuf.at[at_rows(v), at * piece : (at + 1) * piece],
            gather_s.at[4 + at],
            gather_r.at[4 + at],
        )
        for at in range(4)
    ]

    near_at = (blocks - 2) * LANES
    near_end = near_at + 3 * LANES
    near_ids = bucket_of(
        lax.broadcasted_iota(jnp.int32, (LANES, 3 * LANES), 1)
        - LANES
        - lax.broadcasted_iota(jnp.int32, (LANES, 3 * LANES), 0)
    )
    for h in range(heads):
        head = spot.n * heads + h
        near = jnp.zeros((LANES, 3 * LANES), F32)
        for b in range(32):
            if b != 16:
                near = jnp.where(near_ids == b, bias_ref[head, b], near)
        strip[h, :, near_at:near_end] = near
        strip[h, :, :near_at] = jnp.full((LANES, near_at), bias_ref[head, 15])
        strip[h, :, near_end:] = jnp.full((LANES, near_at), bias_ref[head, 31])
    dstrip[...] = jnp.zeros_like(dstrip)
    gain_two_sum[...] = jnp.zeros_like(gain_two_sum)

    for group in projections:
        group.forward()
    lone(o_views[1](spot.w), o_views[1](spot.w), 0, spot.across).wait_recv()
    for group in outs_gather:
        group.begin()
    feeds_gather[0].begin()
    for group in projections:
        group.finish()

    gains = pbuf[:, 4 * LANES :].astype(F32).T[qkv_cols - 4 * LANES : qkv_cols - 4 * LANES + 8]
    gain_one, gain_two = gains[0:1], gains[1:2]

    def relay_outs():
        for group in outs_gather:
            group.forward()
        feeds_gather[1].begin()

    def relay_feed(at):
        def act():
            feeds_gather[at].forward()
            if at + 2 < 4:
                feeds_gather[at + 2].begin()

        return act

    def outs_beside():
        for group in outs_gather:
            group.finish()
        lone(obuf.at[spot.n], obuf.at[spot.n], 1, spot.beside).start()
        lone(obuf.at[spot.n_far], obuf.at[spot.n_far], 2, spot.beside).start()

    def att_view(which, b):
        return att_ref.at[which, b * length : (b + 1) * length]

    def att_copy(which, b, slot, peer):
        return lone(att_view(which, b), att_view(which, b), 3 + 3 * b + slot, peer)

    def att_send(b):
        att_copy(spot.n, b, 0, spot.across).start()
        att_copy(spot.n, b, 1, spot.beside).start()

    def att_relay(b):
        att_copy(spot.n_far, b, 0, spot.across).wait_recv()
        att_copy(spot.n_far, b, 2, spot.beside).start()

    step = 256
    qkv_events = ({}, {1: relay_feed(2)})
    att_events = (
        {1: relay_outs, 3: relay_feed(0), 5: relay_feed(1)},
        {0: outs_beside, 1: relay_feed(3), 3: lambda: att_relay(0)},
    )

    def fire(events, at):
        for when, what in events.items():
            pl.when(at == when)(what)

    for b in range(buffers):
        base = b * length

        @pl.loop(0, length // step)
        def _(at, b=b, base=base):
            fire(qkv_events[b], at)
            begin = pl.multiple_of(at * step, step)
            here = pl.ds(begin, step)
            span = pl.ds(pl.multiple_of(base + begin, step), step)
            values = x_ref[span].astype(F32)
            normed = (values * rms_scale(values) * gain_one).astype(BF16)
            normed_one[span] = normed
            qkv = mm(normed, pbuf[...]).astype(BF16)
            qkv_ref[span] = qkv[:, :qkv_cols]
            for h in range(heads):
                k_at = head_cols + h * DH
                v_at = 2 * head_cols + h * DH
                kt[h, :, here] = qkv[:, k_at : k_at + DH].T
                ws[h, here] = qkv[:, v_at : v_at + DH]

        seg_keys = segments_of(
            lax.broadcasted_iota(jnp.int32, (1, length), 1), lengths_ref, b, slots
        )

        @pl.loop(0, blocks)
        def _(at, b=b, base=base, seg_keys=seg_keys):
            fire(att_events[b], at)
            begin = pl.multiple_of(at * LANES, LANES)
            span = pl.ds(pl.multiple_of(base + begin, LANES), LANES)
            window = pl.ds(pl.multiple_of((blocks - 1 - at) * LANES, LANES), length)
            seg_rows = segments_of(
                lax.broadcasted_iota(jnp.int32, (LANES, 1), 0) + begin, lengths_ref, b, slots
            )
            same = seg_rows == seg_keys
            lane = lax.broadcasted_iota(jnp.int32, (LANES, LANES), 1)
            logs = jnp.zeros((LANES, LANES), F32)
            queries = qkv_ref[span, :head_cols]
            outs = []
            for h in range(heads):
                scores = mm(queries[:, h * DH : (h + 1) * DH], kt[h]) + strip[h, :, window]
                scores = jnp.where(same, scores, masked_score)
                row_max = jnp.max(scores, axis=1, keepdims=True)
                raised = jnp.exp(scores - row_max)
                sums = jnp.sum(raised, axis=1, keepdims=True)
                probs = (raised * (1.0 / sums)).astype(BF16)
                outs.append(mm(probs, ws[h]).astype(BF16))
                logs = jnp.where(lane == h, row_max + jnp.log(sums), logs)
            log_ref[span] = logs
            att_ref[spot.n, span] = jnp.concatenate(outs, axis=1)

        att_send(b)

    k0 = 0.7978845608028654
    k1 = 0.044715

    def half_rows(b, which):
        return pl.ds(pl.multiple_of(b * length + which * half, LANES), half)

    def ff_core(b):
        return lone(ff_out.at[b], ff_in.at[b], 9 + b, spot.beside)

    def ff_across(b):
        return lone(ff_sum.at[b], ff_in.at[b], 11 + b, spot.across)

    def dn_core(b, turn):
        return lone(dn_out.at[b], dn_in.at[b], 13 + 2 * turn + b, spot.beside)

    def dn_across(b, turn):
        return lone(dn_sum.at[b], dn_far.at[b], 17 + 2 * turn + b, spot.across)

    def low_core(b, which):
        view = low_ref.at[half_rows(b, which)]
        return lone(view, view, 21 + b, spot.beside)

    def out_core(b, which):
        view = out_ref.at[half_rows(b, which)]
        return lone(view, view, 23 + b, spot.beside)

    def in_core(b, which):
        view = in_ref.at[half_rows(b, which)]
        return lone(view, view, 25 + b, spot.beside)

    def att_ready(b):
        att_copy(spot.n_beside, b, 1, spot.beside).wait_recv()
        att_copy(spot.n_diag, b, 2, spot.beside).wait_recv()

    def first_feed():
        att_ready(0)
        lone(obuf.at[spot.n_beside], obuf.at[spot.n_beside], 1, spot.beside).wait_recv()
        lone(obuf.at[spot.n_diag], obuf.at[spot.n_diag], 2, spot.beside).wait_recv()
        feeds_gather[0].finish()
        feeds_gather[1].finish()
        feeds_gather[2].finish()
        feeds_gather[3].finish()

    @pl.loop(0, 2 * buffers)
    def _(i):
        fire({0: first_feed, 1: lambda: att_relay(1), 2: lambda: att_ready(1)}, i)
        b = i // 2
        keep = i % 2
        which = (1 - core) * (1 - keep) + core * keep
        rows = half_rows(b, which)
        attention = mm(att_ref[0, rows], obuf[0], NT)
        for a in range(1, 4):
            attention = attention + mm(att_ref[a, rows], obuf[a], NT)
        middle = x_ref[rows].astype(F32) + attention
        scale_two = rms_scale(middle)
        normed_rows = (middle * scale_two * gain_two).astype(BF16)
        normed_two[rows] = normed_rows
        cot = cot_ref[rows]
        for j in range(2):
            at = j * chunk
            both = mm(normed_rows, fbuf[:, at : at + 2 * part])
            gate, up = both[:, :part], both[:, part:]
            square = gate * gate
            tanh = jnp.tanh(k0 * (gate + k1 * (square * gate)))
            lift = 0.5 * (1.0 + tanh)
            active = gate * lift
            slope = lift + (0.5 * gate) * (1.0 - tanh * tanh) * (k0 + (3.0 * k0 * k1) * square)
            d_hidden = mm(cot, fbuf[:, at + 2 * part : at + 3 * part])
            hid[rows, j * part : (j + 1) * part] = (active * up).astype(BF16)
            dg[rows, 2 * j * part : (2 * j + 1) * part] = (d_hidden * up * slope).astype(BF16)
            dg[rows, (2 * j + 1) * part : (2 * j + 2) * part] = (d_hidden * active).astype(BF16)
        dn = mm(dg[rows, : 2 * part], fbuf[:, : 2 * part], NT) + mm(
            dg[rows, 2 * part :], fbuf[:, chunk : chunk + 2 * part], NT
        )
        gain_two_sum[...] = gain_two_sum[...] + fold_rows(dn * middle * scale_two)
        dn = dn.astype(BF16)
        ff = (
            mm(hid[rows, :part], fbuf[:, 2 * part : chunk], NT)
            + mm(hid[rows, part:], fbuf[:, chunk + 2 * part :], NT)
        ).astype(BF16)

        @pl.when(keep == 0)
        def _():
            dn_out[b] = dn
            dn_core(b, 0).start()
            ff_out[b] = ff
            ff_core(b).start()

        @pl.when(keep == 1)
        def _():
            middle_ref[b] = middle
            ff_core(b).wait_recv()
            ff_sum[b] = (ff.astype(F32) + ff_in[b].astype(F32)).astype(BF16)
            dn_core(b, 0).wait_recv()
            dn_sum[b] = (dn.astype(F32) + dn_in[b].astype(F32)).astype(BF16)
            dn_across(b, 0).start()

    def own_block(b, i):
        span = pl.ds(pl.multiple_of(i * LANES, LANES), LANES)
        here = pl.ds(pl.multiple_of(b * length + core * half + i * LANES, LANES), LANES)
        return span, here

    def finish_middle(b):
        dn_across(b, 0).wait_recv()
        ff_across(b).start()

        @pl.loop(0, half // LANES)
        def _(i):
            span, here = own_block(b, i)
            upstream = dn_sum[b, span].astype(F32) + dn_far[b, span].astype(F32)
            middle = middle_ref[b, span]
            d_middle = cot_ref[here].astype(F32) + norm_back(
                middle, rms_scale(middle), gain_two, upstream
            )
            low_ref[here] = d_middle.astype(BF16)

        pl.semaphore_signal(credit.at[b], inc=1, device_id=spot.across, device_id_type=MESH)
        low_core(b, core).start()

    finish_middle(0)

    for group in feeds_gather:
        group.drain()
    for b in range(buffers):
        att_copy(spot.n_far, b, 2, spot.beside).wait_send()
    for j in range(2):
        for begin in range(0, width, step):
            cols = slice(begin, begin + step)
            total[cols, : 2 * part] = mm(
                normed_two[:, cols], dg[:, 2 * j * part : (2 * j + 2) * part], TN
            )
            total[cols, 2 * part :] = mm(cot_ref[:, cols], hid[:, j * part : (j + 1) * part], TN)
        span = slice(j * chunk, (j + 1) * chunk)
        for m in range(4):
            even = total[pl.ds(pl.multiple_of(spot.near_owner(m) * owned, 8), owned)]
            odd = total[pl.ds(pl.multiple_of(spot.far_owner(m) * owned, 8), owned)]
            fbuf[m * owned : (m + 1) * owned, span] = even.astype(BF16)
            fbuf[(4 + m) * owned : (5 + m) * owned, span] = odd.astype(BF16)
    feed_red = Reduce(
        spot,
        lambda m: fbuf[m * owned : (m + 1) * owned],
        lambda m: fbuf.at[(4 + m) * owned : (5 + m) * owned],
        feed_flip,
        feed_mix,
        feed_land,
        red_s.at[0],
        red_r.at[0],
    )
    feed_red.begin()

    out_red = Reduce(
        spot,
        lambda m: o_even[m],
        lambda m: o_odd.at[m],
        o_flip,
        o_mix,
        o_land,
        red_s.at[1],
        red_r.at[1],
    )

    def out_weight_grad():
        for begin in range(0, width, step):
            cols = slice(begin, begin + step)
            total[cols, :head_cols] = mm(low_ref[:, cols], att_ref[spot.n], TN)
        for m in range(4):
            even = total[pl.ds(pl.multiple_of(spot.near_owner(m) * owned, 8), owned), :head_cols]
            odd = total[pl.ds(pl.multiple_of(spot.far_owner(m) * owned, 8), owned), :head_cols]
            o_even[m] = even
            o_odd[m] = odd.astype(BF16)
        out_red.begin()

    gain_sums = jnp.zeros((8, width), F32)
    back_events = (
        {2: feed_red.relay, 4: lambda: finish_middle(1)},
        {2: out_red.relay},
    )
    for b in range(buffers):
        base = b * length
        rows = slice(base, base + length)
        low_core(b, 1 - core).wait_recv()
        if b == 1:
            out_weight_grad()
        grads = mm(low_ref[rows], obuf[spot.n]).astype(BF16)
        att_ref[spot.n_far, :length] = grads
        for h in range(heads):
            keys = qkv_ref[rows, head_cols + h * DH : head_cols + (h + 1) * DH]
            values = qkv_ref[rows, 2 * head_cols + h * DH : 2 * head_cols + (h + 1) * DH]
            ws[h] = keys
            kt[h] = keys.T
            vt[h] = values.T
            qt[h] = qkv_ref[rows, h * DH : (h + 1) * DH].T
            gt[h] = grads[:, h * DH : (h + 1) * DH].T
        dkt[...] = jnp.zeros_like(dkt)
        dvt[...] = jnp.zeros_like(dvt)
        seg_keys = segments_of(
            lax.broadcasted_iota(jnp.int32, (1, length), 1), lengths_ref, b, slots
        )

        @pl.loop(0, blocks)
        def _(at, b=b, base=base, seg_keys=seg_keys):
            fire(back_events[b], at)
            begin = pl.multiple_of(at * LANES, LANES)
            here = pl.ds(begin, LANES)
            span = pl.ds(pl.multiple_of(base + begin, LANES), LANES)
            window = pl.ds(pl.multiple_of((blocks - 1 - at) * LANES, LANES), length)
            seg_rows = segments_of(
                lax.broadcasted_iota(jnp.int32, (LANES, 1), 0) + begin, lengths_ref, b, slots
            )
            same = seg_rows == seg_keys
            logs = log_ref[span]
            queries = qkv_ref[span, :head_cols]
            incoming = att_ref[spot.n_far, here]
            outs = []
            for h in range(heads):
                cols = slice(h * DH, (h + 1) * DH)
                scores = mm(queries[:, cols], kt[h]) + strip[h, :, window]
                scores = jnp.where(same, scores, masked_score)
                probs = jnp.exp(scores - logs[:, h : h + 1])
                d_probs = mm(incoming[:, cols], vt[h])
                inner = jnp.sum(probs * d_probs, axis=1, keepdims=True)
                d_scores = (probs * (d_probs - inner)).astype(BF16)
                dstrip[h, :, window] = dstrip[h, :, window] + d_scores.astype(F32)
                outs.append(mm(d_scores, ws[h]).astype(BF16))
                dkt[h] = dkt[h] + mm(qt[h, :, here], d_scores)
                dvt[h] = dvt[h] + mm(gt[h, :, here], probs.astype(BF16))
            dg[span, :head_cols] = jnp.concatenate(outs, axis=1)

        outs = [dkt[h].T.astype(BF16) for h in range(heads)]
        outs += [dvt[h].T.astype(BF16) for h in range(heads)]
        dg[rows, head_cols:qkv_cols] = jnp.concatenate(outs, axis=1)
        for keep in range(2):
            which = core if keep else 1 - core
            here = half_rows(b, which)
            if keep == 0:
                dn_core(b, 0).wait_send()
            else:
                dn_across(b, 0).wait_send()
            dn = mm(dg[here, :qkv_cols], pbuf[:, :qkv_cols], NT)
            values = x_ref[here].astype(F32)
            gain_sums = gain_sums + fold_rows(dn * values * rms_scale(values))
            dn = dn.astype(BF16)
            if keep == 0:
                dn_out[b] = dn
                dn_core(b, 1).start()
            else:
                dn_core(b, 1).wait_recv()
                dn_sum[b] = (dn.astype(F32) + dn_in[b].astype(F32)).astype(BF16)
                pl.semaphore_wait(credit.at[b], 1)
                dn_across(b, 1).start()

    row = lax.broadcasted_iota(jnp.int32, (LANES, width), 0)
    gain_rows = jnp.where(
        row == DH,
        jnp.sum(gain_sums, axis=0, keepdims=True),
        jnp.where(row == DH + 1, jnp.sum(gain_two_sum[...], axis=0, keepdims=True), 0.0),
    )
    gain_cols = gain_rows.T
    p_cols = qkv_cols + DH
    for begin in range(0, width, step):
        cols = slice(begin, begin + step)
        total[cols, :qkv_cols] = mm(normed_one[:, cols], dg[:, :qkv_cols], TN)
        total[cols, qkv_cols:p_cols] = gain_cols[cols, DH:]
    for m in range(4):
        odd = total[pl.ds(pl.multiple_of(spot.far_owner(m) * owned, 8), owned), :p_cols]
        p_odd[m] = odd.astype(BF16)
    p_red = Reduce(
        spot,
        lambda m: total[pl.ds(pl.multiple_of(spot.near_owner(m) * owned, 8), owned), :p_cols],
        lambda m: p_odd.at[m],
        p_flip,
        p_mix,
        p_land,
        red_s.at[2],
        red_r.at[2],
    )
    p_red.begin()

    def finish_out(b):
        ff_across(b).wait_recv()

        @pl.loop(0, half // LANES)
        def _(i):
            span, here = own_block(b, i)
            joined = (ff_sum[b, span].astype(F32) + ff_in[b, span].astype(F32)).astype(BF16)
            out_ref[here] = (middle_ref[b, span] + joined.astype(F32)).astype(BF16)

        out_core(b, core).start()

    def finish_in(b):
        dn_across(b, 1).wait_recv()

        @pl.loop(0, half // LANES)
        def _(i):
            span, here = own_block(b, i)
            upstream = dn_sum[b, span].astype(F32) + dn_far[b, span].astype(F32)
            values = x_ref[here].astype(F32)
            in_ref[here] = (
                low_ref[here].astype(F32)
                + norm_back(values, rms_scale(values), gain_one, upstream)
            ).astype(BF16)

        in_core(b, core).start()

    finish_out(0)
    finish_out(1)
    feed_value = feed_red.result()
    feed_grad[...] = feed_value
    squares = jnp.sum(jnp.sum(feed_value * feed_value, axis=1, keepdims=True), axis=0, keepdims=True)
    o_value = out_red.result()
    o_grad[...] = o_value
    squares = squares + jnp.sum(
        jnp.sum(o_value * o_value, axis=1, keepdims=True), axis=0, keepdims=True
    )
    p_red.relay()
    for b in range(buffers):
        out_core(b, 1 - core).wait_recv()
    finish_in(0)

    near_row = lax.broadcasted_iota(jnp.int32, (LANES, 4 * LANES), 0)
    diag = lax.broadcasted_iota(jnp.int32, (1, 4 * LANES), 1)
    ids = bucket_of(jnp.where(diag < 3 * LANES, diag - LANES, diag - 5 * LANES))
    lane = lax.broadcasted_iota(jnp.int32, (1, LANES), 1)
    onehot = jnp.where(near_row == ids, 1.0, 0.0)
    bucket_line = jnp.zeros((1, LANES), F32)
    for h in range(heads):
        left = jnp.sum(jnp.sum(dstrip[h, :, :near_at], axis=0, keepdims=True), axis=1, keepdims=True)
        right = jnp.sum(
            jnp.sum(dstrip[h, :, near_end:], axis=0, keepdims=True), axis=1, keepdims=True
        )
        near = jnp.concatenate(
            [dstrip[h, :, near_at:near_end], jnp.zeros((LANES, LANES), F32)], axis=1
        )
        for k in range(7):
            near = jnp.where(
                (near_row // (1 << k)) % 2 == 1, pltpu.roll(near, 4 * LANES - (1 << k), 1), near
            )
        binned = lax.dot_general(
            jnp.broadcast_to(jnp.sum(near, axis=0, keepdims=True), (8, 4 * LANES)),
            onehot,
            NT,
            precision=lax.Precision.HIGHEST,
            preferred_element_type=F32,
        )[0:1]
        binned = binned + jnp.where(lane == 15, left, 0.0) + jnp.where(lane == 31, right, 0.0)
        binned = jnp.where(lane < 32, binned, 0.0)
        bucket_line = bucket_line + (pltpu.roll(binned, 32 * h, 1) if h else binned)

    p_value = p_red.result()
    p_grad[...] = p_value
    p_lane = lax.broadcasted_iota(jnp.int32, p_value.shape, 1)
    squared = jnp.where(p_lane < qkv_cols, p_value * p_value, 0.0)
    squares = squares + jnp.sum(jnp.sum(squared, axis=1, keepdims=True), axis=0, keepdims=True)
    low_lane = qkv_cols // LANES * LANES
    gpad[...] = jnp.zeros_like(gpad)
    gpad[0:owned, : p_cols - low_lane] = p_value[:, low_lane:]
    turned = gpad[...].T
    here = qkv_cols - low_lane
    row8 = lax.broadcasted_iota(jnp.int32, (8, LANES), 0)
    line = jnp.where(row8 == 0, squares, 0.0)
    line = jnp.where(row8 == 1, turned[here : here + 1], line)
    line = jnp.where(row8 == 2, turned[here + 1 : here + 2], line)
    line = jnp.where(row8 == 3, bucket_line, line)
    block[...] = line
    inbox[spot.me] = line

    @pl.loop(1, devices)
    def _(k):
        peer, where = spot.peer(k)
        remote(block, inbox.at[spot.me], norm_s.at[k], norm_r.at[devices - k], where).start()

    finish_in(1)

    @pl.loop(1, devices)
    def _(k):
        peer, where = spot.peer(k)
        copy = remote(block, inbox.at[peer], norm_s.at[k], norm_r.at[k], where)
        copy.wait_send()
        copy.wait_recv()

    columns = [jnp.zeros((8, LANES), F32) for _ in range(narrow)]
    gain_square = jnp.zeros((8, LANES), F32)
    square_total = jnp.zeros((8, LANES), F32)
    for a in range(wide):
        summed = jnp.zeros((8, LANES), F32)
        for c in range(narrow):
            got = inbox[a * narrow + c]
            summed = summed + got
            columns[c] = columns[c] + got
        square_total = square_total + summed
        gain_square = gain_square + summed * summed
    own = inbox[spot.w * narrow]
    for c in range(1, narrow):
        own = own + inbox[spot.w * narrow + c]
    gain_ref[...] = own
    gain_square = jnp.where((row8 == 1) | (row8 == 2), gain_square, 0.0)
    norm_square = square_total[0:1, 0:1] + jnp.sum(
        jnp.sum(gain_square, axis=1, keepdims=True), axis=0, keepdims=True
    )
    table_row = lax.broadcasted_iota(jnp.int32, (16, LANES), 0)
    table = jnp.zeros((16, LANES), F32)
    for c in range(narrow):
        got = columns[c][3:4]
        norm_square = norm_square + jnp.sum(got * got, axis=1, keepdims=True)
        for h in range(heads):
            moved = pltpu.roll(got, LANES - 32 * h, 1) if h else got
            table = jnp.where(table_row == c * heads + h, moved, table)
    table_ref[...] = table
    global_norm = jnp.sqrt(norm_square)
    factor = jnp.minimum(1.0, clip_limit / (global_norm + 1e-06))
    stat_ref[...] = jnp.where(row8 == 0, global_norm, factor)

    for b in range(buffers):
        in_core(b, 1 - core).wait_recv()
        for slot, which, peer in (
            (0, spot.n, spot.across),
            (1, spot.n, spot.beside),
        ):
            att_copy(which, b, slot, peer).wait_send()
        ff_core(b).wait_send()
        ff_across(b).wait_send()
        dn_core(b, 1).wait_send()
        dn_across(b, 1).wait_send()
        low_core(b, core).wait_send()
        out_core(b, core).wait_send()
        in_core(b, core).wait_send()
    lone(o_views[0](spot.w), o_views[0](spot.w), 0, spot.across).wait_send()
    lone(obuf.at[spot.n], obuf.at[spot.n], 1, spot.beside).wait_send()
    lone(obuf.at[spot.n_far], obuf.at[spot.n_far], 2, spot.beside).wait_send()
    for group in projections + outs_gather:
        group.drain()
    for group in (feed_red, out_red, p_red):
        group.drain()


def layer(wide, narrow, lengths, bias, x, cot, pw, ow, ew, sw, gn):
    tokens, width = x.shape
    buffers, slots = lengths.shape
    length = tokens // buffers
    half = length // 2
    head_cols = pw.shape[2]
    heads = head_cols // DH
    hidden_cols = ew.shape[2]
    rows = gn.shape[1]
    devices = wide * narrow
    qkv_cols = 3 * head_cols
    p_cols = qkv_cols + DH
    feed_cols = 3 * hidden_cols
    strip_shape = (heads, LANES, (2 * (length // LANES) - 1) * LANES)
    vmem = pl.BlockSpec(memory_space=pltpu.VMEM)
    smem = pl.BlockSpec(memory_space=pltpu.SMEM)
    halves = pltpu.VMEM((buffers, half, width), BF16)
    tall = pltpu.VMEM((heads, DH, length), BF16)
    dma = pltpu.SemaphoreType.DMA

    def pieces(count, cols, kind=BF16):
        return pltpu.VMEM((count, rows, cols), kind)

    return pl.pallas_call(
        functools.partial(layer_kernel, (buffers, slots, heads, hidden_cols, wide, narrow)),
        in_specs=[smem, smem] + [vmem] * 7,
        out_specs=[vmem] * 8,
        out_shape=[
            jax.ShapeDtypeStruct((tokens, width), BF16),
            jax.ShapeDtypeStruct((tokens, width), BF16),
            jax.ShapeDtypeStruct((rows, p_cols), F32),
            jax.ShapeDtypeStruct((rows, head_cols), F32),
            jax.ShapeDtypeStruct((rows, feed_cols), F32),
            jax.ShapeDtypeStruct((8, LANES), F32),
            jax.ShapeDtypeStruct((8, LANES), F32),
            jax.ShapeDtypeStruct((16, LANES), F32),
        ],
        scratch_shapes=[
            pltpu.VMEM(strip_shape, F32),
            pltpu.VMEM(strip_shape, F32),
            pltpu.VMEM((width, p_cols), BF16),
            pltpu.VMEM((narrow, width, head_cols), BF16),
            pltpu.VMEM((width, feed_cols), BF16),
            pltpu.VMEM((narrow, tokens, head_cols), BF16),
            pltpu.VMEM((tokens, qkv_cols), BF16),
            pltpu.VMEM((tokens, LANES), F32),
            pltpu.VMEM((tokens, width), BF16),
            pltpu.VMEM((buffers, half, width), F32),
            pltpu.VMEM((tokens, hidden_cols), BF16),
            pltpu.VMEM((tokens, 2 * hidden_cols), BF16),
            pltpu.VMEM((width, feed_cols // 2), F32),
            pltpu.VMEM((2 * LANES, LANES), F32),
            pltpu.VMEM((LANES, LANES), F32),
            pieces(4, feed_cols),
            pieces(3, feed_cols),
            pieces(3, feed_cols),
            pieces(4, head_cols, F32),
            pieces(4, head_cols),
            pieces(4, head_cols),
            pieces(3, head_cols),
            pieces(3, head_cols),
            pieces(4, p_cols),
            pieces(4, p_cols),
            pieces(3, p_cols),
            pieces(3, p_cols),
        ]
        + [halves] * 7
        + [
            pltpu.VMEM((heads, length, DH), BF16),
            tall,
            tall,
            tall,
            tall,
            pltpu.VMEM((heads, DH, length), F32),
            pltpu.VMEM((heads, DH, length), F32),
            pltpu.VMEM((8, width), F32),
            pltpu.VMEM((8, LANES), F32),
            pltpu.VMEM((devices, 8, LANES), F32),
            dma((8, 7)),
            dma((8, wide)),
            dma((27,)),
            dma((27,)),
            dma((3, 7)),
            dma((3, 7)),
            dma((devices,)),
            dma((devices,)),
            pltpu.SemaphoreType.REGULAR((buffers,)),
        ],
        compiler_params=pltpu.CompilerParams(
            vmem_limit_bytes=64 << 20, collective_id=0, has_side_effects=True
        ),
        cost_estimate=pl.CostEstimate(
            flops=60 << 30, bytes_accessed=24 << 20, transcendentals=16 << 20
        ),
        name="layer",
    )(lengths, bias, x, cot, pw, ow, ew, sw, gn)


def update_kernel(heads, hidden_cols, p_ref, o_ref, feed_ref, stat_ref, gain_ref, table_ref, *refs):
    weights, firsts, seconds = refs[:6], refs[6:12], refs[12:18]
    outs, norm_ref, o_pad = refs[18:36], refs[36], refs[37]
    factor = stat_ref[1:2, 0:1]
    norm_ref[0, 0] = jnp.sum(stat_ref[0:1, 0:1])
    head_cols = heads * DH
    rows = p_ref.shape[0]

    def update(which, index, gradient):
        results = adam_update(
            weights[which][index],
            firsts[which][index],
            seconds[which][index],
            factor * gradient,
            step_rates[which],
            decay_rates[which],
        )
        for at in range(3):
            outs[6 * at + which][index] = results[at]

    for i in range(3):
        update(0, i, p_ref[:, i * head_cols : (i + 1) * head_cols])
    part = hidden_cols // 2
    for j in range(2):
        span = slice(j * part, (j + 1) * part)
        for i in range(2):
            begin = (3 * j + i) * part
            update(2, (i, slice(None), span), feed_ref[:, begin : begin + part])
        begin = (3 * j + 2) * part
        update(3, (slice(None), span), feed_ref[:, begin : begin + part])
    o_pad[...] = jnp.zeros_like(o_pad)
    o_pad[0:rows, 0:head_cols] = o_ref[...]
    update(1, slice(None), o_pad[...].T[:head_cols, :rows])
    depth, columns = weights[4].shape
    update(4, slice(None), table_ref[:depth, :columns])
    update(5, slice(None), gain_ref[1:3, :rows])


def update_call(grads, params_in, firsts, seconds, heads, hidden_cols):
    vmem = pl.BlockSpec(memory_space=pltpu.VMEM)
    operands = [*grads, *params_in, *firsts, *seconds]
    return pl.pallas_call(
        functools.partial(update_kernel, heads, hidden_cols),
        in_specs=[vmem] * len(operands),
        out_specs=[vmem] * 18 + [pl.BlockSpec(memory_space=pltpu.SMEM)],
        out_shape=[jax.ShapeDtypeStruct(a.shape, F32) for a in params_in] * 3
        + [jax.ShapeDtypeStruct((1, 1), F32)],
        scratch_shapes=[pltpu.VMEM((LANES, 2 * LANES), F32)],
        compiler_params=params(),
        cost_estimate=pl.CostEstimate(flops=4 << 20, bytes_accessed=8 << 20, transcendentals=0),
        name="update",
    )(*operands)


def direct_body(wide, narrow, *arguments):
    block_input, cotangent, lengths = arguments[:3]
    turned = (3, 4)
    flat = [
        value.T if at % 6 in turned else value for at, value in enumerate(arguments[3:21])
    ]
    weights, firsts, seconds = flat[:6], flat[6:12], flat[12:18]
    project, output, expand, shrink, bias, gains = weights
    block_output, input_gradient, *grads = layer(
        wide,
        narrow,
        lengths,
        bias,
        block_input,
        cotangent,
        project,
        output,
        expand,
        shrink,
        gains,
    )
    heads = project.shape[2] // DH
    *results, norm = update_call(grads, weights, firsts, seconds, heads, expand.shape[2])
    results = [value.T if at % 6 in turned else value for at, value in enumerate(results)]
    return (block_output, input_gradient, norm.reshape(()), *results)


def solution(mesh):
    wide, narrow = mesh.shape["wide"], mesh.shape["narrow"]
    body = direct_body if (wide, narrow) == (8, 4) else general_body
    state = (
        P(None, "wide", "narrow"),
        P("narrow", "wide"),
        P(None, "wide", "narrow"),
        P("narrow", "wide"),
        P(),
        P(None, "wide"),
    )
    rows = P("wide", None)
    return jax.shard_map(
        functools.partial(body, wide, narrow),
        mesh=mesh,
        in_specs=(rows, rows, rows, *state, *state, *state),
        out_specs=(rows, rows, P(), *state, *state, *state),
        check_vma=False,
    )
```

```python
import functools

import jax
import jax.numpy as jnp
from jax import lax
from jax.experimental import pallas as pl
from jax.experimental.pallas import tpu as pltpu
from jax.sharding import PartitionSpec as P

DH = 64
STEP = 10
LANES = 128
MESH = pl.DeviceIdType.MESH
F32 = jnp.float32
BF16 = jnp.bfloat16
ANY = pl.ANY

bucket_edges = (12, 16, 23, 32, 46, 64, 91)
norm_eps = 1e-06
clip_limit = 1.0
beta_one = 0.9
beta_two = 0.999
adam_eps = 1e-08
step_rates = (0.06, 0.3, 0.07, 0.06, 1.0, 0.3)
decay_rates = (0.01, 0.01, 0.01, 0.01, 0.0, 0.0)
masked_score = -1000000000.0
VMEM_LIMIT = 58 << 20

NN = (((1,), (0,)), ((), ()))
NT = (((1,), (1,)), ((), ()))
TN = (((0,), (0,)), ((), ()))


def mm(left, right, dims=NN):
    return lax.dot_general(left, right, dims, preferred_element_type=F32)


def bucket_of(offsets):
    distance = jnp.abs(offsets)
    far_bucket = 8 + sum(((distance >= threshold).astype(jnp.int32) for threshold in bucket_edges))
    return jnp.where(distance < 8, distance, far_bucket) + 16 * (offsets > 0).astype(jnp.int32)


def rms_scale(values):
    return lax.rsqrt(jnp.mean(values * values, axis=-1, keepdims=True) + norm_eps)


def norm_back(values, scale_vec, gain_vec, upstream):
    weighted = upstream * gain_vec
    inner_mean = jnp.mean(weighted * values, axis=-1, keepdims=True)
    return scale_vec * weighted - values * (scale_vec * scale_vec * scale_vec) * inner_mean


def adam_update(weight, moment_one, moment_two, gradient, step_rate, decay_rate):
    new_first = beta_one * moment_one + (1.0 - beta_one) * gradient
    new_second = beta_two * moment_two + (1.0 - beta_two) * gradient * gradient
    first_hat = new_first / (1.0 - beta_one**STEP)
    second_hat = new_second / (1.0 - beta_two**STEP)
    new_weight = weight - step_rate * (
        first_hat / (jnp.sqrt(second_hat) + adam_eps) + decay_rate * weight
    )
    return (new_weight, new_first, new_second)


def fold_rows(values):
    rows, cols = values.shape
    return jnp.sum(values.reshape(rows // 8, 8, cols), axis=0)


def start_rows(pieces, target, offs_ref, sems):
    copies = []
    for at, piece in enumerate(pieces):
        rows = piece.shape[0]
        begin = pl.multiple_of(offs_ref[at], 16)
        copies.append(
            pltpu.make_async_copy(piece, target.at[pl.ds(begin, rows)], sems.at[at])
        )
    for copy in copies:
        copy.start()
    return copies


def segments(index, ends_ref, buffer, slots):
    total = jnp.zeros(index.shape, jnp.int32)
    for slot in range(slots):
        total = total + (index >= ends_ref[buffer, slot]).astype(jnp.int32)
    return total


def params(**more):
    return pltpu.CompilerParams(vmem_limit_bytes=VMEM_LIMIT, **more)


def attend_kernel(
    buffer, slots, heads, count, ends_ref, offs_ref, x_ref, strip_ref, *refs
):
    pieces = refs[:count]
    normed_ref, qkv_ref, att_ref, log_ref, gains_ref, wbuf, qs, ks, vs, os, sems = refs[count:]
    length, width = x_ref.shape
    head_cols = heads * DH
    copies = start_rows(pieces, wbuf, offs_ref, sems)
    for copy in copies:
        copy.wait()
    gain_cols = wbuf[:, 4 * LANES :].astype(F32).T
    first = 3 * head_cols - 4 * LANES
    gains = gain_cols[first : first + 8]
    gains_ref[...] = gains
    gain_one = gains[0:1]
    step = 256

    @pl.loop(0, length // step)
    def _(block):
        rows = pl.ds(pl.multiple_of(block * step, step), step)
        values = x_ref[rows].astype(F32)
        normed = (values * rms_scale(values) * gain_one).astype(BF16)
        normed_ref[rows] = normed
        qkv = mm(normed, wbuf[...]).astype(BF16)
        qkv_ref[rows] = qkv[:, : 3 * head_cols]
        for h in range(heads):
            qs[h, rows] = qkv[:, h * DH : (h + 1) * DH]
            ks[h, rows] = qkv[:, head_cols + h * DH : head_cols + (h + 1) * DH]
            vs[h, rows] = qkv[:, 2 * head_cols + h * DH : 2 * head_cols + (h + 1) * DH]

    blocks = length // LANES
    seg_keys = segments(
        lax.broadcasted_iota(jnp.int32, (1, length), 1), ends_ref, buffer, slots
    )

    @pl.loop(0, blocks)
    def _(block):
        begin = pl.multiple_of(block * LANES, LANES)
        rows = pl.ds(begin, LANES)
        window = pl.ds(pl.multiple_of((blocks - 1 - block) * LANES, LANES), length)
        seg_rows = segments(
            lax.broadcasted_iota(jnp.int32, (LANES, 1), 0) + begin, ends_ref, buffer, slots
        )
        same = seg_rows == seg_keys
        lane = lax.broadcasted_iota(jnp.int32, (LANES, LANES), 1)
        logs = jnp.zeros((LANES, LANES), F32)
        for h in range(heads):
            scores = mm(qs[h, rows], ks[h], NT) + strip_ref[h, :, window]
            scores = jnp.where(same, scores, masked_score)
            row_max = jnp.max(scores, axis=1, keepdims=True)
            raised = jnp.exp(scores - row_max)
            total = jnp.sum(raised, axis=1, keepdims=True)
            probs = (raised * (1.0 / total)).astype(BF16)
            os[h, rows] = mm(probs, vs[h]).astype(BF16)
            logs = jnp.where(lane == h, row_max + jnp.log(total), logs)
        log_ref[rows] = logs

    att_ref[...] = jnp.concatenate([os[h] for h in range(heads)], axis=1)


def attend(buffer, ends, offs, x, strip, pieces, length, heads):
    width = x.shape[1]
    count = len(pieces)
    cols = pieces[0].shape[1]
    head_cols = heads * DH
    whole = lambda i, *_: (0, 0)
    spec = pltpu.PrefetchScalarGridSpec(
        num_scalar_prefetch=2,
        grid=(1,),
        in_specs=[
            pl.BlockSpec((length, width), lambda i, *_: (buffer, 0)),
            pl.BlockSpec(strip.shape, lambda i, *_: (0, 0, 0)),
        ]
        + [pl.BlockSpec(memory_space=ANY)] * count,
        out_specs=[
            pl.BlockSpec((length, width), whole),
            pl.BlockSpec((length, 3 * head_cols), whole),
            pl.BlockSpec((length, head_cols), whole),
            pl.BlockSpec((length, LANES), whole),
            pl.BlockSpec((8, width), whole),
        ],
        scratch_shapes=[
            pltpu.VMEM((width, cols), BF16),
            pltpu.VMEM((heads, length, DH), BF16),
            pltpu.VMEM((heads, length, DH), BF16),
            pltpu.VMEM((heads, length, DH), BF16),
            pltpu.VMEM((heads, length, DH), BF16),
            pltpu.SemaphoreType.DMA((count,)),
        ],
    )
    flops = 2 * length * (width * cols + 2 * heads * DH * length)
    return pl.pallas_call(
        functools.partial(attend_kernel, buffer, ends.shape[1], heads, count),
        grid_spec=spec,
        out_shape=[
            jax.ShapeDtypeStruct((length, width), BF16),
            jax.ShapeDtypeStruct((length, 3 * head_cols), BF16),
            jax.ShapeDtypeStruct((length, head_cols), BF16),
            jax.ShapeDtypeStruct((length, LANES), F32),
            jax.ShapeDtypeStruct((8, width), F32),
        ],
        compiler_params=params(),
        cost_estimate=pl.CostEstimate(
            flops=4 * flops, bytes_accessed=8 << 20, transcendentals=heads * length * length
        ),
        name="attend",
    )(ends, offs, x, strip, *pieces)


def feed_kernel(hidden_cols, counts, order_ref, offs_ref, *refs):
    own, across, beside, diagonal, x_ref, cot_ref, gains_ref = refs[:7]
    at = 7
    groups = []
    for count in counts:
        groups.append(refs[at : at + count])
        at += count
    (
        normed_ref,
        hidden_ref,
        gate_ref,
        ff_send,
        ff_keep,
        dn_send,
        dn_keep,
        middle_keep,
        gain_sum,
        ebuf,
        sbuf,
        oabuf,
        obbuf,
        sems,
    ) = refs[at:]
    step = pl.program_id(0)
    bufs = (oabuf, obbuf, ebuf, sbuf)

    @pl.when(step == 0)
    def _():
        copies = []
        for which, (group, target) in enumerate(zip(groups, bufs)):
            copies += start_rows(group, target, offs_ref, sems.at[which])
        for copy in copies:
            copy.wait()

    cols = own.shape[1]
    upper = order_ref[2] == 0
    pairs = []
    for near, far, weights in ((own, across, oabuf), (beside, diagonal, obbuf)):
        near_sum = mm(near[...], weights[:, :cols], NT)
        far_sum = mm(far[...], weights[:, cols:], NT)
        pairs.append(
            jnp.where(upper, near_sum, far_sum) + jnp.where(upper, far_sum, near_sum)
        )
    swap = order_ref[0] == 0
    attention = jnp.where(swap, pairs[0], pairs[1]) + jnp.where(swap, pairs[1], pairs[0])
    middle = x_ref[...].astype(F32) + attention
    scale_two = rms_scale(middle)
    gain_two = gains_ref[1:2]
    normed = (middle * scale_two * gain_two).astype(BF16)
    normed_ref[...] = normed
    cot = cot_ref[...]
    part = 256
    k0 = 0.7978845608028654
    k1 = 0.044715
    for begin in range(0, hidden_cols, part):
        gate = mm(normed, ebuf[:, begin : begin + part])
        up = mm(normed, ebuf[:, hidden_cols + begin : hidden_cols + begin + part])
        square = gate * gate
        tanh = jnp.tanh(k0 * (gate + k1 * (square * gate)))
        half = 0.5 * (1.0 + tanh)
        active = gate * half
        slope = half + (0.5 * gate) * (1.0 - tanh * tanh) * (k0 + (3.0 * k0 * k1) * square)
        d_hidden = mm(cot, sbuf[:, begin : begin + part])
        hidden_ref[:, begin : begin + part] = (active * up).astype(BF16)
        gate_ref[:, begin : begin + part] = (d_hidden * up * slope).astype(BF16)
        gate_ref[:, hidden_cols + begin : hidden_cols + begin + part] = (
            d_hidden * active
        ).astype(BF16)
    ff = mm(hidden_ref[...], sbuf[...], NT).astype(BF16)
    dn = mm(gate_ref[...], ebuf[...], NT)
    sums = fold_rows(dn * middle * scale_two)
    dn = dn.astype(BF16)

    @pl.when(step == 0)
    def _():
        ff_send[...] = ff
        dn_send[...] = dn
        gain_sum[...] = sums

    @pl.when(step == 1)
    def _():
        ff_keep[...] = ff
        dn_keep[...] = dn
        middle_keep[...] = middle
        gain_sum[...] = gain_sum[...] + sums


def feed(buffer, order, offs, parts, x, cot, gains, groups, length, hidden_cols):
    width = x.shape[1]
    half = length // 2
    cols = parts[0].shape[1]
    counts = [len(group) for group in groups]
    natural = lambda i, order, *_: (order[i], 0)
    rows = lambda i, order, *_: (2 * buffer + order[i], 0)
    whole = lambda i, *_: (0, 0)
    spec = pltpu.PrefetchScalarGridSpec(
        num_scalar_prefetch=2,
        grid=(2,),
        in_specs=[pl.BlockSpec((half, cols), natural)] * 4
        + [pl.BlockSpec((half, width), rows)] * 2
        + [pl.BlockSpec((8, width), whole)]
        + [pl.BlockSpec(memory_space=ANY)] * sum(counts),
        out_specs=[
            pl.BlockSpec((half, width), natural),
            pl.BlockSpec((half, hidden_cols), natural),
            pl.BlockSpec((half, 2 * hidden_cols), natural),
        ]
        + [pl.BlockSpec((half, width), whole)] * 5
        + [pl.BlockSpec((8, width), whole)],
        scratch_shapes=[
            pltpu.VMEM((width, 2 * hidden_cols), BF16),
            pltpu.VMEM((width, hidden_cols), BF16),
            pltpu.VMEM((width, 2 * cols), BF16),
            pltpu.VMEM((width, 2 * cols), BF16),
            pltpu.SemaphoreType.DMA((4, max(counts))),
        ],
    )
    flops = 2 * length * width * (4 * cols + 7 * hidden_cols)
    return pl.pallas_call(
        functools.partial(feed_kernel, hidden_cols, counts),
        grid_spec=spec,
        out_shape=[
            jax.ShapeDtypeStruct((length, width), BF16),
            jax.ShapeDtypeStruct((length, hidden_cols), BF16),
            jax.ShapeDtypeStruct((length, 2 * hidden_cols), BF16),
            jax.ShapeDtypeStruct((half, width), BF16),
            jax.ShapeDtypeStruct((half, width), BF16),
            jax.ShapeDtypeStruct((half, width), BF16),
            jax.ShapeDtypeStruct((half, width), BF16),
            jax.ShapeDtypeStruct((half, width), F32),
            jax.ShapeDtypeStruct((8, width), F32),
        ],
        compiler_params=params(),
        cost_estimate=pl.CostEstimate(
            flops=flops, bytes_accessed=12 << 20, transcendentals=length * hidden_cols
        ),
        name="feed",
    )(order, offs, *parts, x, cot, gains, *[piece for group in groups for piece in group])


def middle_kernel(order_ref, near, far, middle_ref, cot_ref, gains_ref, d_ref, low_ref):
    upstream = near[...].astype(F32) + far[...].astype(F32)
    middle = middle_ref[...]
    d_middle = cot_ref[...].astype(F32) + norm_back(
        middle, rms_scale(middle), gains_ref[1:2], upstream
    )
    d_ref[...] = d_middle
    low_ref[...] = d_middle.astype(BF16)


def input_kernel(order_ref, near, far, x_ref, d_ref, gains_ref, out_ref):
    upstream = near[...].astype(F32) + far[...].astype(F32)
    values = x_ref[...].astype(F32)
    out_ref[...] = (
        d_ref[...] + norm_back(values, rms_scale(values), gains_ref[0:1], upstream)
    ).astype(BF16)


def output_kernel(order_ref, near, far, middle_ref, out_ref):
    out_ref[...] = (
        middle_ref[...] + (near[...].astype(F32) + far[...].astype(F32)).astype(BF16).astype(F32)
    ).astype(BF16)


def half_call(kernel, name, buffer, order, arrays, placed, outs, gains=None):
    half, width = arrays[0].shape
    steps = 3
    block = half // steps
    mine = lambda i, *_: (i, 0)
    rows = lambda i, order, *_: ((2 * buffer + order[1]) * steps + i, 0)
    in_specs = [
        pl.BlockSpec((block, width), rows if at in placed else mine)
        for at in range(len(arrays))
    ]
    operands = list(arrays)
    if gains is not None:
        in_specs.append(pl.BlockSpec((8, width), lambda i, *_: (0, 0)))
        operands.append(gains)
    return pl.pallas_call(
        kernel,
        grid_spec=pltpu.PrefetchScalarGridSpec(
            num_scalar_prefetch=1,
            grid=(steps,),
            in_specs=in_specs,
            out_specs=[pl.BlockSpec((block, width), mine) for _ in outs],
        ),
        out_shape=[jax.ShapeDtypeStruct((half, width), kind) for kind in outs],
        compiler_params=params(),
        cost_estimate=pl.CostEstimate(
            flops=20 * half * width, bytes_accessed=12 * half * width, transcendentals=0
        ),
        name=name,
    )(order, *operands)


def back_kernel(buffer, slots, heads, counts, ends_ref, offs_ref, order_ref, *refs):
    near, far, qkv_ref, log_ref, strip_ref, x_ref = refs[:6]
    at = 6
    o_pieces = refs[at : at + counts[0]]
    at += counts[0]
    p_pieces = refs[at : at + counts[1]]
    at += counts[1]
    (
        low_ref,
        dqkv_ref,
        dn_send,
        dn_keep,
        gain_sum,
        dstrip,
        wbuf,
        obuf,
        qs,
        ks,
        vs,
        gs,
        qt,
        gt,
        dkt,
        dvt,
        dq,
        sems,
    ) = refs[at:]
    length = qkv_ref.shape[0]
    half = length // 2
    head_cols = heads * DH
    o_copies = start_rows(o_pieces, obuf, offs_ref, sems.at[0])
    p_copies = start_rows(p_pieces, wbuf, offs_ref, sems.at[1])
    mine = pl.ds(pl.multiple_of(order_ref[1] * half, LANES), half)
    other = pl.ds(pl.multiple_of(order_ref[0] * half, LANES), half)
    low_ref[mine] = near[...]
    low_ref[other] = far[...]
    for h in range(heads):
        qs[h] = qkv_ref[:, h * DH : (h + 1) * DH]
        ks[h] = qkv_ref[:, head_cols + h * DH : head_cols + (h + 1) * DH]
        vs[h] = qkv_ref[:, 2 * head_cols + h * DH : 2 * head_cols + (h + 1) * DH]
        qt[h] = qs[h].T
    dstrip[...] = jnp.zeros_like(dstrip)
    dkt[...] = jnp.zeros_like(dkt)
    dvt[...] = jnp.zeros_like(dvt)
    for copy in o_copies + p_copies:
        copy.wait()
    grads = mm(low_ref[...], obuf[:, :head_cols]).astype(BF16)
    for h in range(heads):
        gs[h] = grads[:, h * DH : (h + 1) * DH]
        gt[h] = gs[h].T
    blocks = length // LANES
    seg_keys = segments(
        lax.broadcasted_iota(jnp.int32, (1, length), 1), ends_ref, buffer, slots
    )

    @pl.loop(0, blocks)
    def _(block):
        begin = pl.multiple_of(block * LANES, LANES)
        rows = pl.ds(begin, LANES)
        window = pl.ds(pl.multiple_of((blocks - 1 - block) * LANES, LANES), length)
        seg_rows = segments(
            lax.broadcasted_iota(jnp.int32, (LANES, 1), 0) + begin, ends_ref, buffer, slots
        )
        same = seg_rows == seg_keys
        logs = log_ref[rows]
        for h in range(heads):
            scores = mm(qs[h, rows], ks[h], NT) + strip_ref[h, :, window]
            scores = jnp.where(same, scores, masked_score)
            probs = jnp.exp(scores - logs[:, h : h + 1])
            d_probs = mm(gs[h, rows], vs[h], NT)
            inner = jnp.sum(probs * d_probs, axis=1, keepdims=True)
            d_scores = (probs * (d_probs - inner)).astype(BF16)
            dstrip[h, :, window] = dstrip[h, :, window] + d_scores.astype(F32)
            dq[h, rows] = mm(d_scores, ks[h]).astype(BF16)
            dkt[h] = dkt[h] + mm(qt[h, :, rows], d_scores)
            dvt[h] = dvt[h] + mm(gt[h, :, rows], probs.astype(BF16))

    outs = [dq[h] for h in range(heads)]
    outs += [dkt[h].T.astype(BF16) for h in range(heads)]
    outs += [dvt[h].T.astype(BF16) for h in range(heads)]
    dqkv_ref[...] = jnp.concatenate(outs, axis=1)
    sums = []
    for target, which in ((dn_send, other), (dn_keep, mine)):
        dn = mm(dqkv_ref[which], wbuf[:, : 3 * head_cols], NT)
        values = x_ref[which].astype(F32)
        sums.append(fold_rows(dn * values * rms_scale(values)))
        target[...] = dn.astype(BF16)
    gain_sum[...] = sums[0] + sums[1]


def back(buffer, ends, offs, order, near, far, qkv, logs, strip, x, o_pieces, p_pieces, heads):
    length = qkv.shape[0]
    half = length // 2
    width = x.shape[1]
    head_cols = heads * DH
    counts = (len(o_pieces), len(p_pieces))
    whole = lambda i, *_: (0, 0)
    whole3 = lambda i, *_: (0, 0, 0)
    spec = pltpu.PrefetchScalarGridSpec(
        num_scalar_prefetch=3,
        grid=(1,),
        in_specs=[
            pl.BlockSpec((half, width), whole),
            pl.BlockSpec((half, width), whole),
            pl.BlockSpec(qkv.shape, whole),
            pl.BlockSpec(logs.shape, whole),
            pl.BlockSpec(strip.shape, whole3),
            pl.BlockSpec((length, width), lambda i, *_: (buffer, 0)),
        ]
        + [pl.BlockSpec(memory_space=ANY)] * sum(counts),
        out_specs=[
            pl.BlockSpec((length, width), whole),
            pl.BlockSpec((length, 3 * head_cols), whole),
            pl.BlockSpec((half, width), whole),
            pl.BlockSpec((half, width), whole),
            pl.BlockSpec((8, width), whole),
            pl.BlockSpec(strip.shape, whole3),
        ],
        scratch_shapes=[
            pltpu.VMEM((width, p_pieces[0].shape[1]), BF16),
            pltpu.VMEM((width, o_pieces[0].shape[1]), BF16),
            pltpu.VMEM((heads, length, DH), BF16),
            pltpu.VMEM((heads, length, DH), BF16),
            pltpu.VMEM((heads, length, DH), BF16),
            pltpu.VMEM((heads, length, DH), BF16),
            pltpu.VMEM((heads, DH, length), BF16),
            pltpu.VMEM((heads, DH, length), BF16),
            pltpu.VMEM((heads, DH, length), F32),
            pltpu.VMEM((heads, DH, length), F32),
            pltpu.VMEM((heads, length, DH), BF16),
            pltpu.SemaphoreType.DMA((2, max(counts))),
        ],
    )
    return pl.pallas_call(
        functools.partial(back_kernel, buffer, ends.shape[1], heads, counts),
        grid_spec=spec,
        out_shape=[
            jax.ShapeDtypeStruct((length, width), BF16),
            jax.ShapeDtypeStruct((length, 3 * head_cols), BF16),
            jax.ShapeDtypeStruct((half, width), BF16),
            jax.ShapeDtypeStruct((half, width), BF16),
            jax.ShapeDtypeStruct((8, width), F32),
            jax.ShapeDtypeStruct(strip.shape, F32),
        ],
        compiler_params=params(),
        cost_estimate=pl.CostEstimate(
            flops=40 * heads * DH * length * length,
            bytes_accessed=16 << 20,
            transcendentals=heads * length * length,
        ),
        name="back",
    )(ends, offs, order, near, far, qkv, logs, strip, x, *o_pieces, *p_pieces)


def scatter_rows(total, offs_ref, evens, odds):
    rows = evens[0].shape[0]
    for at in range(2 * len(evens)):
        begin = pl.multiple_of(offs_ref[at], 8)
        block = total[pl.ds(begin, rows)]
        if at % 2:
            odds[at // 2][...] = block.astype(BF16)
        else:
            evens[at // 2][...] = block


def feed_grad_kernel(count, hidden_cols, offs_ref, *refs):
    buffers = 2
    normed = refs[:buffers]
    gates = refs[buffers : 2 * buffers]
    hiddens = refs[2 * buffers : 3 * buffers]
    cot_ref = refs[3 * buffers]
    outs = refs[3 * buffers + 1 : -1]
    total = refs[-1]
    length = normed[0].shape[0]
    width = normed[0].shape[1]
    part = 256
    for begin in range(0, width, part):
        cols = slice(begin, begin + part)
        total[cols, : 2 * hidden_cols] = mm(normed[0][:, cols], gates[0][...], TN) + mm(
            normed[1][:, cols], gates[1][...], TN
        )
        total[cols, 2 * hidden_cols :] = mm(
            cot_ref[:length, cols], hiddens[0][...], TN
        ) + mm(cot_ref[length:, cols], hiddens[1][...], TN)
    if count > 1:
        scatter_rows(total, offs_ref, outs[: count // 2], outs[count // 2 :])
    else:
        outs[0][...] = total[...]


def attend_grad_kernel(count, heads, offs_ref, *refs):
    buffers = 2
    normed = refs[:buffers]
    dqkv = refs[buffers : 2 * buffers]
    lows = refs[2 * buffers : 3 * buffers]
    atts = refs[3 * buffers : 4 * buffers]
    sums_ref = refs[4 * buffers]
    outs = refs[4 * buffers + 1 : -1]
    total = refs[-1]
    width = normed[0].shape[1]
    head_cols = heads * DH
    qkv_cols = 3 * head_cols
    part = 256
    rows = lax.broadcasted_iota(jnp.int32, (LANES, width), 0)
    first = sums_ref[0] + sums_ref[1]
    second = sums_ref[2] + sums_ref[3]
    gain_rows = jnp.where(
        rows == DH,
        jnp.sum(first, axis=0, keepdims=True),
        jnp.where(rows == DH + 1, jnp.sum(second, axis=0, keepdims=True), 0.0),
    )
    gain_cols = gain_rows.T
    for begin in range(0, width, part):
        cols = slice(begin, begin + part)
        total[cols, :qkv_cols] = mm(normed[0][:, cols], dqkv[0][...], TN) + mm(
            normed[1][:, cols], dqkv[1][...], TN
        )
        total[cols, qkv_cols : qkv_cols + DH] = gain_cols[cols, DH:]
        total[cols, qkv_cols + DH : qkv_cols + DH + head_cols] = mm(
            lows[0][:, cols], atts[0][...], TN
        ) + mm(lows[1][:, cols], atts[1][...], TN)
    if count > 1:
        scatter_rows(total, offs_ref, outs[: count // 2], outs[count // 2 :])
    else:
        outs[0][...] = total[...]


def grad_call(kernel, name, offs, operands, width, cols, count, rows, flops):
    vmem = pl.BlockSpec(memory_space=pltpu.VMEM)
    if count > 1:
        shapes = [jax.ShapeDtypeStruct((rows, cols), F32)] * (count // 2)
        shapes += [jax.ShapeDtypeStruct((rows, cols), BF16)] * (count // 2)
    else:
        shapes = [jax.ShapeDtypeStruct((width, cols), F32)]
    return pl.pallas_call(
        kernel,
        in_specs=[pl.BlockSpec(memory_space=pltpu.SMEM)] + [vmem] * len(operands),
        out_specs=[vmem] * len(shapes),
        out_shape=shapes,
        scratch_shapes=[pltpu.VMEM((width, cols), F32)],
        compiler_params=params(),
        cost_estimate=pl.CostEstimate(flops=2 * flops, bytes_accessed=14 << 20, transcendentals=0),
        name=name,
    )(offs, *operands)


def bucket_kernel(heads, near_ref, far_ref, out_ref):
    lanes = near_ref.shape[2]
    blocks = (lanes // LANES + 1) // 2
    begin = (blocks - 2) * LANES
    end = begin + 3 * LANES
    rows = lax.broadcasted_iota(jnp.int32, (LANES, 3 * LANES), 0)
    ids = bucket_of(
        lax.broadcasted_iota(jnp.int32, (LANES, 3 * LANES), 1) - LANES - rows
    )
    lane = lax.broadcasted_iota(jnp.int32, (1, LANES), 1)
    out = jnp.zeros((1, LANES), F32)
    for h in range(heads):
        strip = near_ref[h] + far_ref[h]
        left = jnp.sum(jnp.sum(strip[:, :begin], axis=0, keepdims=True), axis=1, keepdims=True)
        right = jnp.sum(jnp.sum(strip[:, end:], axis=0, keepdims=True), axis=1, keepdims=True)
        out = out + jnp.where(lane == h * 32 + 15, left, 0.0)
        out = out + jnp.where(lane == h * 32 + 31, right, 0.0)
        middle = strip[:, begin:end]
        for b in range(32):
            if b == 16:
                continue
            part = jnp.sum(jnp.where(ids == b, middle, 0.0), axis=0, keepdims=True)
            part = jnp.sum(part, axis=1, keepdims=True)
            out = out + jnp.where(lane == h * 32 + b, part, 0.0)
    out_ref[...] = jnp.broadcast_to(out, (8, LANES))


def norm_kernel(wide, narrow, lists, gain_at, *refs):
    at = 0
    groups = []
    for count in lists:
        groups.append(refs[at : at + count])
        at += count
    bucket_ref = refs[at]
    outs = refs[at + 1 : at + 1 + len(lists)]
    stat_ref, gain_ref, table_ref, block, inbox, padded, send_sems, recv_sems = refs[
        at + 1 + len(lists) :
    ]
    total = wide * narrow
    w = lax.axis_index("wide")
    n = lax.axis_index("narrow")
    me = w * narrow + n
    barrier = pltpu.get_barrier_semaphore()

    @pl.loop(1, total)
    def _(k):
        peer = (me + k) % total
        pl.semaphore_signal(
            barrier, inc=1, device_id=(peer // narrow, peer % narrow), device_id_type=MESH
        )

    squares = jnp.zeros((8, LANES), F32)
    for which, (group, out) in enumerate(zip(groups, outs)):
        value = group[0][...].astype(F32)
        for more in group[1:]:
            value = value + more[...].astype(F32)
        out[...] = value
        squared = value * value
        if which == 0:
            lane = lax.broadcasted_iota(jnp.int32, value.shape, 1)
            inside = (lane >= gain_at) & (lane < gain_at + DH)
            squared = jnp.where(inside, 0.0, squared)
        squared = jnp.sum(squared, axis=1, keepdims=True)
        squares = squares + jnp.sum(squared, axis=0, keepdims=True)
    rows = outs[0].shape[0]
    low = gain_at // LANES * LANES
    padded[...] = jnp.zeros_like(padded)
    padded[0:rows] = outs[0][:, low : low + LANES]
    turned = padded[...].T
    row = lax.broadcasted_iota(jnp.int32, (8, LANES), 0)
    here = gain_at - low
    mine = jnp.where(row == 0, squares, 0.0)
    mine = jnp.where(row == 1, turned[here : here + 1], mine)
    mine = jnp.where(row == 2, turned[here + 1 : here + 2], mine)
    mine = jnp.where(row == 3, bucket_ref[...], mine)
    block[...] = mine
    inbox[me] = mine
    pl.semaphore_wait(barrier, total - 1)

    @pl.loop(1, total)
    def _(k):
        peer = (me + k) % total
        pltpu.make_async_remote_copy(
            src_ref=block,
            dst_ref=inbox.at[me],
            send_sem=send_sems.at[k],
            recv_sem=recv_sems.at[total - k],
            device_id=(peer // narrow, peer % narrow),
            device_id_type=MESH,
        ).start()

    @pl.loop(1, total)
    def _(k):
        peer = (me + k) % total
        copy = pltpu.make_async_remote_copy(
            src_ref=block,
            dst_ref=inbox.at[peer],
            send_sem=send_sems.at[k],
            recv_sem=recv_sems.at[k],
            device_id=(peer // narrow, peer % narrow),
            device_id_type=MESH,
        )
        copy.wait_send()
        copy.wait_recv()

    columns = [jnp.zeros((8, LANES), F32) for _ in range(narrow)]
    gain_square = jnp.zeros((8, LANES), F32)
    square_total = jnp.zeros((8, LANES), F32)
    for a in range(wide):
        gains = jnp.zeros((8, LANES), F32)
        for b in range(narrow):
            got = inbox[a * narrow + b]
            gains = gains + got
            columns[b] = columns[b] + got
        square_total = square_total + gains
        gain_square = gain_square + gains * gains
    own = inbox[w * narrow]
    for b in range(1, narrow):
        own = own + inbox[w * narrow + b]
    gain_ref[...] = own
    pick = (row == 1) | (row == 2)
    gain_square = jnp.where(pick, gain_square, 0.0)
    norm_square = square_total[0:1, 0:1] + jnp.sum(
        jnp.sum(gain_square, axis=0, keepdims=True), axis=1, keepdims=True
    )
    heads = LANES // 32 - 1
    lane = lax.broadcasted_iota(jnp.int32, (32, LANES), 1)
    depth = lax.broadcasted_iota(jnp.int32, (32, LANES), 0)
    table = jnp.zeros((32, LANES), F32)
    for b in range(narrow):
        line = columns[b][3:4]
        norm_square = norm_square + jnp.sum(line * line, axis=1, keepdims=True)
        for h in range(heads):
            column = jnp.sum(
                jnp.where(lane == depth + 32 * h, line, 0.0), axis=1, keepdims=True
            )
            table = jnp.where(lane == b * heads + h, column, table)
    table_ref[...] = table
    global_norm = jnp.sqrt(norm_square)
    factor = jnp.minimum(1.0, clip_limit / (global_norm + 1e-06))
    stat_ref[...] = jnp.where(row == 0, global_norm, factor)


def norm_call(wide, narrow, groups, bucket, gain_at):
    vmem = pl.BlockSpec(memory_space=pltpu.VMEM)
    lists = tuple(len(group) for group in groups)
    total = wide * narrow
    operands = [piece for group in groups for piece in group] + [bucket]
    return pl.pallas_call(
        functools.partial(norm_kernel, wide, narrow, lists, gain_at),
        in_specs=[vmem] * len(operands),
        out_specs=[vmem] * (len(lists) + 3),
        out_shape=[jax.ShapeDtypeStruct(group[0].shape, F32) for group in groups]
        + [
            jax.ShapeDtypeStruct((8, LANES), F32),
            jax.ShapeDtypeStruct((8, LANES), F32),
            jax.ShapeDtypeStruct((32, LANES), F32),
        ],
        scratch_shapes=[
            pltpu.VMEM((8, LANES), F32),
            pltpu.VMEM((total, 8, LANES), F32),
            pltpu.VMEM((LANES, LANES), F32),
            pltpu.SemaphoreType.DMA((total,)),
            pltpu.SemaphoreType.DMA((total,)),
        ],
        compiler_params=params(collective_id=0, has_side_effects=True),
        cost_estimate=pl.CostEstimate(flops=1 << 20, bytes_accessed=4 << 20, transcendentals=0),
        name="norm",
    )(*operands)


def adam_kernel(heads, hidden_cols, parts, att_ref, feed_ref, gain_ref, table_ref, stat_ref, *refs):
    weights, firsts, seconds = refs[:6], refs[6:12], refs[12:18]
    outs = refs[18:36]
    o_pad, s_pad = refs[36:]
    factor = stat_ref[1:2, 0:1]
    head_cols = heads * DH
    rows = att_ref.shape[0]
    gain_at = 3 * head_cols

    def update(which, index, gradient):
        results = adam_update(
            weights[which][index],
            firsts[which][index],
            seconds[which][index],
            factor * gradient,
            step_rates[which],
            decay_rates[which],
        )
        for at in range(3):
            outs[6 * at + which][index] = results[at]

    for i in range(3):
        update(0, i, att_ref[:, i * head_cols : (i + 1) * head_cols])
    part = hidden_cols // parts
    for j in range(parts):
        span = slice(j * part, (j + 1) * part)
        for i in range(2):
            begin = (3 * j + i) * part if parts > 1 else i * part
            update(2, (i, slice(None), span), feed_ref[:, begin : begin + part])
    o_pad[...] = jnp.zeros_like(o_pad)
    s_pad[...] = jnp.zeros_like(s_pad)
    o_pad[0:rows] = att_ref[:, gain_at + DH :]
    for j in range(parts):
        begin = (3 * j + 2) * part
        s_pad[0:rows, j * part : (j + 1) * part] = feed_ref[:, begin : begin + part]
    update(1, slice(None), o_pad[...].T[:head_cols, :rows])
    update(3, slice(None), s_pad[...].T[:, :rows])
    columns = weights[4].shape[1]
    update(4, slice(None), table_ref[:, :columns])
    update(5, slice(None), gain_ref[1:3, :rows])


def adam_call(
    att, feed_grad, gain, table, stat, params_in, firsts, seconds, heads, hidden_cols, direct=False
):
    vmem = pl.BlockSpec(memory_space=pltpu.VMEM)
    operands = [att, feed_grad, gain, table, stat, *params_in, *firsts, *seconds]
    pad_cols = att.shape[1] - (3 * heads * DH + DH)
    return pl.pallas_call(
        functools.partial(adam_kernel, heads, hidden_cols, 2 if direct else 1),
        in_specs=[vmem] * len(operands),
        out_specs=[vmem] * 18,
        out_shape=[jax.ShapeDtypeStruct(a.shape, F32) for a in params_in] * 3,
        scratch_shapes=[
            pltpu.VMEM((LANES, pad_cols), F32),
            pltpu.VMEM((LANES, hidden_cols), F32),
        ],
        compiler_params=params(),
        cost_estimate=pl.CostEstimate(flops=4 << 20, bytes_accessed=8 << 20, transcendentals=0),
        name="adam",
    )(*operands)


def place_kernel(offs_ref, *refs):
    step = pl.program_id(0)
    for at, piece in enumerate(refs[:-1]):

        @pl.when(step == at)
        def _(piece=piece):
            refs[-1][...] = piece[...]


def place(pieces, offs, rows):
    half, width = pieces[0].shape
    count = len(pieces)
    return pl.pallas_call(
        place_kernel,
        grid_spec=pltpu.PrefetchScalarGridSpec(
            num_scalar_prefetch=1,
            grid=(count,),
            in_specs=[pl.BlockSpec((half, width), lambda i, *_: (0, 0))] * count,
            out_specs=pl.BlockSpec((half, width), lambda i, offs: (offs[i] // half, 0)),
        ),
        out_shape=jax.ShapeDtypeStruct((rows, width), pieces[0].dtype),
        compiler_params=params(),
        cost_estimate=pl.CostEstimate(
            flops=0, bytes_accessed=4 * rows * width, transcendentals=0
        ),
        name="place",
    )(offs, *pieces)


def bias_strip(bucket_bias, n, heads, length):
    table = lax.dynamic_slice_in_dim(bucket_bias, n * heads, heads, 1).T
    blocks = length // LANES
    near_r = (
        jnp.arange(3 * LANES, dtype=jnp.int32)[None, :]
        - LANES
        - jnp.arange(LANES, dtype=jnp.int32)[:, None]
    )
    near_ids = bucket_of(near_r)
    near = sum(
        jnp.where(near_ids == b, table[:, b][:, None, None], 0.0) for b in range(32) if b != 16
    )
    far_shape = (heads, LANES, (blocks - 2) * LANES)
    return jnp.concatenate(
        [
            jnp.broadcast_to(table[:, 15][:, None, None], far_shape),
            near,
            jnp.broadcast_to(table[:, 31][:, None, None], far_shape),
        ],
        axis=2,
    )


def general_body(wide, narrow, *arguments):
    (
        block_input,
        cotangent,
        lengths,
        project_weight,
        output_weight,
        expand_weight,
        shrink_weight,
        bucket_bias,
        norm_gains,
    ) = arguments[:9]
    firsts = arguments[9:15]
    seconds = arguments[15:21]
    tokens, width = block_input.shape
    buffers = lengths.shape[0]
    length = tokens // buffers
    rows = norm_gains.shape[1]
    head_cols = project_weight.shape[2]
    heads = head_cols // DH
    hidden_cols = expand_weight.shape[2]
    w = lax.axis_index("wide")
    n = lax.axis_index("narrow")
    core = n % 2

    def swap(value, wide_mask, narrow_mask):
        pairs = [
            (a * narrow + b, (a ^ wide_mask) * narrow + (b ^ narrow_mask))
            for a in range(wide)
            for b in range(narrow)
        ]
        return lax.ppermute(value, ("wide", "narrow"), pairs)

    def gather(piece):
        return [lax.all_gather(piece, "wide", axis=0, tiled=True)]

    def reduce_wide(outs):
        return [lax.psum_scatter(outs[0], "wide", scatter_dimension=0, tiled=True)]

    offs = jnp.zeros((1,), jnp.int32)
    order = jnp.stack([1 - core, core, n // 2])

    p_piece = jnp.concatenate(
        [
            project_weight[0],
            project_weight[1],
            project_weight[2],
            norm_gains.T,
            jnp.zeros((rows, DH - 2), F32),
        ],
        axis=1,
    ).astype(BF16)
    p_pieces = gather(p_piece)
    o_piece = output_weight.astype(BF16).T
    o_pair = jnp.concatenate([o_piece, swap(o_piece, 0, 2)], axis=1)
    oa_pieces = gather(o_pair)
    ob_pieces = [swap(piece, 0, 1) for piece in oa_pieces]
    e_pieces = gather(
        jnp.concatenate([expand_weight[0], expand_weight[1]], axis=1).astype(BF16)
    )
    s_pieces = gather(shrink_weight.astype(BF16).T)

    ends = jnp.cumsum(lengths, axis=1)
    strip = bias_strip(bucket_bias, n, heads, length)

    normed_one, qkv, atts, logs, fours = [], [], [], [], []
    for b in range(buffers):
        normed, rows_b, att, log, gains = attend(
            b, ends, offs, block_input, strip, p_pieces, length, heads
        )
        normed_one.append(normed)
        qkv.append(rows_b)
        atts.append(att)
        logs.append(log)
        across = swap(att, 0, 2)
        fours.append((att, across, swap(att, 0, 1), swap(across, 0, 1)))

    def core_sum(kept, sent):
        return (kept.astype(F32) + swap(sent, 0, 1).astype(F32)).astype(BF16)

    normed_two, hiddens, gates, middles, ff_sums, dn_sums, sums_two = [], [], [], [], [], [], []
    for b in range(buffers):
        normed, hidden, gate, ff_send, ff_keep, dn_send, dn_keep, middle, sums = feed(
            b,
            order,
            offs,
            fours[b],
            block_input,
            cotangent,
            gains,
            (oa_pieces, ob_pieces, e_pieces, s_pieces),
            length,
            hidden_cols,
        )
        normed_two.append(normed)
        hiddens.append(hidden)
        gates.append(gate)
        middles.append(middle)
        sums_two.append(sums)
        dn_sums.append(core_sum(dn_keep, dn_send))
        ff_sums.append(core_sum(ff_keep, ff_send))

    d_middles, lows = [], []
    for b in range(buffers):
        d_middle, low = half_call(
            middle_kernel,
            "middle",
            b,
            order,
            [dn_sums[b], swap(dn_sums[b], 0, 2), middles[b], cotangent],
            (3,),
            (F32, BF16),
            gains,
        )
        d_middles.append(d_middle)
        lows.append((low, swap(low, 0, 1)))

    count = 1
    feed_outs = grad_call(
        functools.partial(feed_grad_kernel, count, hidden_cols),
        "feed_grad",
        offs,
        [*normed_two, *gates, *hiddens, cotangent],
        width,
        3 * hidden_cols,
        count,
        rows,
        2 * tokens * width * 3 * hidden_cols,
    )
    feed_group = reduce_wide(feed_outs)

    low_full, dqkv, dn_one, sums_one, strips = [], [], [], [], []
    for b in range(buffers):
        low, grads, dn_send, dn_keep, sums, dstrip = back(
            b,
            ends,
            offs,
            order,
            lows[b][0],
            lows[b][1],
            qkv[b],
            logs[b],
            strip,
            block_input,
            oa_pieces,
            p_pieces,
            heads,
        )
        low_full.append(low)
        dqkv.append(grads)
        sums_one.append(sums)
        strips.append(dstrip)
        dn_one.append(core_sum(dn_keep, dn_send))

    gain_at = 3 * head_cols
    att_outs = grad_call(
        functools.partial(attend_grad_kernel, count, heads),
        "attend_grad",
        offs,
        [*normed_one, *dqkv, *low_full, *atts, jnp.stack(sums_one + sums_two)],
        width,
        gain_at + DH + head_cols,
        count,
        rows,
        2 * tokens * width * 4 * head_cols,
    )
    att_group = reduce_wide(att_outs)
    vmem = pl.BlockSpec(memory_space=pltpu.VMEM)
    bucket = pl.pallas_call(
        functools.partial(bucket_kernel, heads),
        in_specs=[vmem, vmem],
        out_specs=vmem,
        out_shape=jax.ShapeDtypeStruct((8, LANES), F32),
        compiler_params=params(),
        cost_estimate=pl.CostEstimate(flops=8 << 20, bytes_accessed=4 << 20, transcendentals=0),
        name="bucket",
    )(*strips)

    half_offs = jnp.stack(
        [
            b * length + which * (length // 2)
            for b in range(buffers)
            for which in (core, 1 - core)
        ]
    )
    out_halves, in_halves = [], []
    for b in range(buffers):
        (half,) = half_call(
            output_kernel,
            "output",
            b,
            order,
            [ff_sums[b], swap(ff_sums[b], 0, 2), middles[b]],
            (),
            (BF16,),
        )
        out_halves += [half, swap(half, 0, 1)]
        (half,) = half_call(
            input_kernel,
            "input",
            b,
            order,
            [dn_one[b], swap(dn_one[b], 0, 2), block_input, d_middles[b]],
            (2,),
            (BF16,),
            gains,
        )
        in_halves += [half, swap(half, 0, 1)]
    block_output = place(out_halves, half_offs, tokens)
    input_gradient = place(in_halves, half_offs, tokens)

    att_grad, feed_grad, stat, gain, table_sum = norm_call(
        wide, narrow, [att_group, feed_group], bucket, gain_at
    )
    results = adam_call(
        att_grad,
        feed_grad,
        gain,
        table_sum,
        stat,
        arguments[3:9],
        firsts,
        seconds,
        heads,
        hidden_cols,
    )
    return (block_output, input_gradient, stat[0, 0], *results)


class Place:
    def __init__(self, wide, narrow):
        self.wide, self.narrow = wide, narrow
        self.w = lax.axis_index("wide")
        self.n = lax.axis_index("narrow")
        self.me = self.w * narrow + self.n
        self.z, self.x = self.w // 2, self.w % 2
        self.y, self.core = self.n // 2, self.n % 2
        self.n_far = (self.n + 2) % 4
        self.n_beside = self.n + 1 - 2 * self.core
        self.n_diag = (self.n_beside + 2) % 4
        self.across = (self.w, self.n_far)
        self.beside = (self.w, self.n_beside)
        self.flip = (self.z * 2 + 1 - self.x, self.n)

    def along(self, m):
        return (((self.z + m) % 4) * 2 + self.x, self.n)

    def near_owner(self, m):
        return ((self.z + m) % 4) * 2 + self.x

    def far_owner(self, m):
        return ((self.z + m) % 4) * 2 + 1 - self.x

    def peer(self, k):
        device = (self.me + k) % (self.wide * self.narrow)
        return device, (device // self.narrow, device % self.narrow)


def remote(source, target, send_sem, recv_sem, peer):
    return pltpu.make_async_remote_copy(
        src_ref=source,
        dst_ref=target,
        send_sem=send_sem,
        recv_sem=recv_sem,
        device_id=peer,
        device_id_type=MESH,
    )


class Gather:
    def __init__(self, spot, view, ssem, rsem, flip_first=False):
        self.spot, self.view, self.ssem, self.rsem = spot, view, ssem, rsem
        self.flip_first = flip_first

    def copy(self, owner, slot, peer):
        return remote(
            self.view(owner), self.view(owner), self.ssem.at[slot], self.rsem.at[owner], peer
        )

    def landed(self, owner):
        self.copy(owner, 0, self.spot.flip).wait_recv()

    def begin(self):
        if self.flip_first:
            self.copy(self.spot.w, 3, self.spot.flip).start()
        for m in (2, 1, 3):
            self.copy(self.spot.w, m - 1, self.spot.along(m)).start()
        if not self.flip_first:
            self.copy(self.spot.w, 3, self.spot.flip).start()

    def forward(self):
        if self.flip_first:
            owner = self.spot.far_owner(0)
            self.landed(owner)
            for m in (2, 1, 3):
                self.copy(owner, 3 + m, self.spot.along(m)).start()
            return
        for m in (3, 1, 2):
            owner = self.spot.near_owner(4 - m)
            self.landed(owner)
            self.copy(owner, 3 + m, self.spot.flip).start()

    def finish(self):
        if self.flip_first:
            for m in (1, 2, 3):
                self.landed(self.spot.near_owner(4 - m))
        else:
            self.landed(self.spot.far_owner(0))
        for m in (1, 2, 3):
            self.landed(self.spot.far_owner(4 - m))

    def drain(self):
        self.copy(self.spot.w, 3, self.spot.flip).wait_send()
        for m in (1, 2, 3):
            self.copy(self.spot.w, m - 1, self.spot.along(m)).wait_send()
            if self.flip_first:
                owner, peer = self.spot.far_owner(0), self.spot.along(m)
            else:
                owner, peer = self.spot.near_owner(4 - m), self.spot.flip
            self.copy(owner, 3 + m, peer).wait_send()


class Reduce:
    def __init__(self, spot, even, odd, flipped, mixed, landed, sems_s, sems_r):
        self.spot, self.even, self.odd = spot, even, odd
        self.flipped, self.mixed, self.landed = flipped, mixed, landed
        self.sems_s, self.sems_r = sems_s, sems_r

    def over(self, m):
        return remote(
            self.odd(m), self.flipped(m), self.sems_s.at[m], self.sems_r.at[m], self.spot.flip
        )

    def along(self, m):
        return remote(
            self.mixed(m - 1),
            self.landed(m - 1),
            self.sems_s.at[3 + m],
            self.sems_r.at[3 + m],
            self.spot.along(m),
        )

    def begin(self):
        for m in (2, 1, 3, 0):
            self.over(m).start()

    def relay(self, *ms):
        for m in ms:
            self.over(m).wait_recv()
            self.mixed(m - 1)[...] = (
                self.even(m).astype(F32) + self.flipped(m)[...].astype(F32)
            ).astype(BF16)
            self.along(m).start()

    def result(self):
        self.over(0).wait_recv()
        value = self.even(0).astype(F32) + self.flipped(0)[...].astype(F32)
        for m in (1, 2, 3):
            self.along(m).wait_recv()
            value = value + self.landed(m - 1)[...].astype(F32)
        return value

    def drain(self):
        for m in range(4):
            self.over(m).wait_send()
        for m in (1, 2, 3):
            self.along(m).wait_send()


def segments_of(index, lengths_ref, buffer, slots):
    end = lengths_ref[buffer, 0]
    total = (index >= end).astype(jnp.int32)
    for slot in range(1, slots):
        end = end + lengths_ref[buffer, slot]
        total = total + (index >= end).astype(jnp.int32)
    return total


def layer_kernel(dims, *refs):
    buffers, slots, heads, hidden_cols, wide, narrow = dims
    (
        lengths_ref,
        bias_ref,
        x_hbm,
        cot_hbm,
        pw_ref,
        ow_ref,
        ew_ref,
        sw_ref,
        gn_ref,
        out_ref,
        in_ref,
        p_grad,
        o_grad,
        feed_grad,
        stat_ref,
        gain_ref,
        table_ref,
        x_ref,
        cot_ref,
        strip,
        dstrip,
        pbuf,
        obuf,
        fbuf,
        att_ref,
        qkv_ref,
        log_ref,
        low_ref,
        middle_ref,
        hid,
        dg,
        total,
        opad,
        gpad,
        feed_flip,
        feed_mix,
        feed_land,
        o_even,
        o_odd,
        o_flip,
        o_mix,
        o_land,
        p_odd,
        p_flip,
        p_mix,
        p_land,
        ff_out,
        ff_in,
        ff_sum,
        dn_out,
        dn_in,
        dn_sum,
        dn_far,
        ws,
        kt,
        vt,
        qt,
        gt,
        dkt,
        dvt,
        gain_two_sum,
        block,
        inbox,
        gather_s,
        gather_r,
        lone_s,
        lone_r,
        red_s,
        red_r,
        norm_s,
        norm_r,
        credit,
        load,
    ) = refs
    spot = Place(wide, narrow)
    core = spot.core
    devices = wide * narrow
    tokens, width = x_ref.shape
    length = tokens // buffers
    half = length // 2
    head_cols = heads * DH
    qkv_cols = 3 * head_cols
    part = hidden_cols // 2
    chunk = 3 * part
    blocks = length // LANES
    owned = gn_ref.shape[1]
    normed_one, normed_two = in_ref, out_ref
    loads = [
        pltpu.make_async_copy(x_hbm, x_ref, load.at[0]),
        pltpu.make_async_copy(cot_hbm, cot_ref, load.at[1]),
    ]
    for copy in loads:
        copy.start()
    barrier = pltpu.get_barrier_semaphore()

    @pl.loop(1, devices)
    def _(k):
        pl.semaphore_signal(barrier, inc=1, device_id=spot.peer(k)[1], device_id_type=MESH)

    def at_rows(owner):
        return pl.ds(pl.multiple_of(owner * owned, 16), owned)

    def lone(view_from, view_to, slot, peer):
        return remote(view_from, view_to, lone_s.at[slot], lone_r.at[slot], peer)

    mine = at_rows(spot.w)
    gpad[...] = jnp.zeros_like(gpad)
    gpad[0:2, 0:owned] = gn_ref[...]
    pbuf[mine] = jnp.concatenate(
        [pw_ref[0], pw_ref[1], pw_ref[2], gpad[...].T[:owned, :DH]], axis=1
    ).astype(BF16)
    pl.semaphore_wait(barrier, devices - 1)
    split = 3 * LANES
    projections = [
        Gather(
            spot,
            lambda v, span=span: pbuf.at[at_rows(v), span],
            gather_s.at[at],
            gather_r.at[at],
        )
        for at, span in enumerate((slice(0, split), slice(split, qkv_cols + DH)))
    ]
    for group in projections:
        group.begin()
    opad[...] = jnp.zeros_like(opad)
    opad[0:head_cols, 0:owned] = ow_ref[...]
    obuf[spot.n, mine] = opad[...].T[:owned, :head_cols].astype(BF16)
    o_views = [
        lambda v: obuf.at[spot.n, at_rows(v)],
        lambda v: obuf.at[spot.n_far, at_rows(v)],
    ]
    outs_gather = [
        Gather(spot, view, gather_s.at[2 + at], gather_r.at[2 + at])
        for at, view in enumerate(o_views)
    ]
    lone(o_views[0](spot.w), o_views[0](spot.w), 0, spot.across).start()
    for j in range(2):
        span = slice(j * part, (j + 1) * part)
        fbuf[mine, j * chunk : j * chunk + part] = ew_ref[0, :, span].astype(BF16)
        fbuf[mine, j * chunk + part : j * chunk + 2 * part] = ew_ref[1, :, span].astype(BF16)
        fbuf[mine, j * chunk + 2 * part : (j + 1) * chunk] = sw_ref[:, span].astype(BF16)
    piece = chunk // 2
    feeds_gather = [
        Gather(
            spot,
            lambda v, at=at: fbuf.at[at_rows(v), at * piece : (at + 1) * piece],
            gather_s.at[4 + at],
            gather_r.at[4 + at],
            flip_first=at == 3,
        )
        for at in range(4)
    ]

    near_at = (blocks - 2) * LANES
    near_end = near_at + 3 * LANES
    near_ids = bucket_of(
        lax.broadcasted_iota(jnp.int32, (LANES, 3 * LANES), 1)
        - LANES
        - lax.broadcasted_iota(jnp.int32, (LANES, 3 * LANES), 0)
    )
    for h in range(heads):
        head = spot.n * heads + h
        near = jnp.zeros((LANES, 3 * LANES), F32)
        for b in range(32):
            if b != 16:
                near = jnp.where(near_ids == b, bias_ref[head, b], near)
        strip[h, :, near_at:near_end] = near
        strip[h, :, :near_at] = jnp.full((LANES, near_at), bias_ref[head, 15])
        strip[h, :, near_end:] = jnp.full((LANES, near_at), bias_ref[head, 31])
    lone(o_views[1](spot.w), o_views[1](spot.w), 0, spot.across).wait_recv()
    for group in outs_gather + feeds_gather:
        group.begin()
    dstrip[...] = jnp.zeros_like(dstrip)
    gain_two_sum[...] = jnp.zeros_like(gain_two_sum)

    projections[0].forward()
    projections[1].forward()
    for group in projections:
        group.finish()
    loads[0].wait()

    gains = pbuf[:, 4 * LANES :].astype(F32).T[qkv_cols - 4 * LANES : qkv_cols - 4 * LANES + 8]
    gain_one, gain_two = gains[0:1], gains[1:2]

    def relay_outs():
        for group in outs_gather:
            group.forward()

    def outs_beside():
        for group in outs_gather:
            group.finish()
        lone(obuf.at[spot.n], obuf.at[spot.n], 1, spot.beside).start()
        lone(obuf.at[spot.n_far], obuf.at[spot.n_far], 2, spot.beside).start()

    def att_view(which, b):
        return att_ref.at[which, b * length : (b + 1) * length]

    def att_copy(which, b, slot, peer):
        return lone(att_view(which, b), att_view(which, b), 3 + 3 * b + slot, peer)

    def att_send(b):
        att_copy(spot.n, b, 0, spot.across).start()
        att_copy(spot.n, b, 1, spot.beside).start()

    def att_relay(b):
        att_copy(spot.n_far, b, 0, spot.across).wait_recv()
        att_copy(spot.n_far, b, 2, spot.beside).start()

    step = 256
    qkv_events = ({}, {0: feeds_gather[0].forward})
    att_events = (
        {2: relay_outs, 5: feeds_gather[3].forward},
        {0: outs_beside, 3: lambda: att_relay(0), 4: feeds_gather[1].forward},
    )

    def fire(events, at):
        for when, what in events.items():
            pl.when(at == when)(what)

    for b in range(buffers):
        base = b * length

        @pl.loop(0, length // step)
        def _(at, b=b, base=base):
            fire(qkv_events[b], at)
            begin = pl.multiple_of(at * step, step)
            here = pl.ds(begin, step)
            span = pl.ds(pl.multiple_of(base + begin, step), step)
            values = x_ref[span].astype(F32)
            normed = (values * rms_scale(values) * gain_one).astype(BF16)
            normed_one[span] = normed
            qkv = mm(normed, pbuf[...]).astype(BF16)
            qkv_ref[span] = qkv[:, :qkv_cols]
            for h in range(heads):
                k_at = head_cols + h * DH
                v_at = 2 * head_cols + h * DH
                kt[h, :, here] = qkv[:, k_at : k_at + DH].T
                ws[h, here] = qkv[:, v_at : v_at + DH]

        seg_keys = segments_of(
            lax.broadcasted_iota(jnp.int32, (1, length), 1), lengths_ref, b, slots
        )

        @pl.loop(0, blocks)
        def _(at, b=b, base=base, seg_keys=seg_keys):
            fire(att_events[b], at)
            begin = pl.multiple_of(at * LANES, LANES)
            span = pl.ds(pl.multiple_of(base + begin, LANES), LANES)
            window = pl.ds(pl.multiple_of((blocks - 1 - at) * LANES, LANES), length)
            seg_rows = segments_of(
                lax.broadcasted_iota(jnp.int32, (LANES, 1), 0) + begin, lengths_ref, b, slots
            )
            same = seg_rows == seg_keys
            lane = lax.broadcasted_iota(jnp.int32, (LANES, LANES), 1)
            logs = jnp.zeros((LANES, LANES), F32)
            queries = qkv_ref[span, :head_cols]
            outs = []
            for h in range(heads):
                scores = mm(queries[:, h * DH : (h + 1) * DH], kt[h]) + strip[h, :, window]
                scores = jnp.where(same, scores, masked_score)
                row_max = jnp.max(scores, axis=1, keepdims=True)
                raised = jnp.exp(scores - row_max)
                sums = jnp.sum(raised, axis=1, keepdims=True)
                probs = (raised * (1.0 / sums)).astype(BF16)
                outs.append(mm(probs, ws[h]).astype(BF16))
                logs = jnp.where(lane == h, row_max + jnp.log(sums), logs)
            log_ref[span] = logs
            att_ref[spot.n, span] = jnp.concatenate(outs, axis=1)

        att_send(b)

    k0 = 0.7978845608028654
    k1 = 0.044715

    def half_rows(b, which):
        return pl.ds(pl.multiple_of(b * length + which * half, LANES), half)

    def ff_core(b):
        return lone(ff_out.at[b], ff_in.at[b], 9 + b, spot.beside)

    def ff_across(b):
        return lone(ff_sum.at[b], ff_in.at[b], 11 + b, spot.across)

    def dn_core(b, turn):
        return lone(dn_out.at[b], dn_in.at[b], 13 + 2 * turn + b, spot.beside)

    def dn_across(b, turn):
        return lone(dn_sum.at[b], dn_far.at[b], 17 + 2 * turn + b, spot.across)

    def low_core(b, which):
        view = low_ref.at[half_rows(b, which)]
        return lone(view, view, 21 + b, spot.beside)

    def out_core(b, which):
        view = out_ref.at[half_rows(b, which)]
        return lone(view, view, 23 + b, spot.beside)

    def in_core(b, which):
        view = in_ref.at[half_rows(b, which)]
        return lone(view, view, 25 + b, spot.beside)

    def outs_ready():
        loads[1].wait()
        lone(obuf.at[spot.n_beside], obuf.at[spot.n_beside], 1, spot.beside).wait_recv()
        lone(obuf.at[spot.n_diag], obuf.at[spot.n_diag], 2, spot.beside).wait_recv()

    def first_feed():
        feeds_gather[2].forward()
        feeds_gather[0].finish()
        feeds_gather[1].finish()

    def last_feed():
        att_relay(1)
        feeds_gather[2].finish()
        feeds_gather[3].finish()

    def half_of(b, keep):
        return half_rows(b, (1 - core) * (1 - keep) + core * keep)

    def hidden_part(j, rows, normed_rows):
        at = j * chunk
        both = mm(normed_rows, fbuf[:, at : at + 2 * part])
        gate, up = both[:, :part], both[:, part:]
        square = gate * gate
        tanh = jnp.tanh(k0 * (gate + k1 * (square * gate)))
        lift = 0.5 * (1.0 + tanh)
        active = gate * lift
        slope = lift + (0.5 * gate) * (1.0 - tanh * tanh) * (k0 + (3.0 * k0 * k1) * square)
        d_hidden = mm(cot_ref[rows], fbuf[:, at + 2 * part : at + 3 * part])
        hid[rows, j * part : (j + 1) * part] = (active * up).astype(BF16)
        dg[rows, 2 * j * part : (2 * j + 1) * part] = (d_hidden * up * slope).astype(BF16)
        dg[rows, (2 * j + 1) * part : (2 * j + 2) * part] = (d_hidden * active).astype(BF16)

    @pl.loop(0, buffers)
    def _(b):
        def att_ready():
            span = pl.ds(pl.multiple_of(b * length, LANES), length)
            for slot, which in ((4, spot.n_beside), (5, spot.n_diag)):
                view = att_ref.at[which, span]
                lone(view, view, slot + 3 * b, spot.beside).wait_recv()

        att_ready()

        @pl.loop(0, 2)
        def _(keep):
            pl.when((b == 0) & (keep == 0))(outs_ready)
            rows = half_of(b, keep)
            attention = mm(att_ref[0, rows], obuf[0], NT)
            for a in range(1, 4):
                attention = attention + mm(att_ref[a, rows], obuf[a], NT)
            middle = x_ref[rows].astype(F32) + attention
            normed_rows = (middle * rms_scale(middle) * gain_two).astype(BF16)
            normed_two[rows] = normed_rows

            @pl.when(keep == 1)
            def _():
                middle_ref[b] = middle

            pl.when((b == 0) & (keep == 0))(first_feed)
            hidden_part(0, rows, normed_two[rows])

        pl.when(b == 0)(last_feed)

        @pl.loop(0, 2)
        def _(keep):
            rows = half_of(b, keep)
            normed_rows = normed_two[rows]
            hidden_part(1, rows, normed_rows)
            dn = mm(dg[rows, : 2 * part], fbuf[:, : 2 * part], NT) + mm(
                dg[rows, 2 * part :], fbuf[:, chunk : chunk + 2 * part], NT
            )
            gain_two_sum[...] = gain_two_sum[...] + fold_rows(dn * normed_rows.astype(F32))
            dn = dn.astype(BF16)

            @pl.when(keep == 0)
            def _():
                dn_out[b] = dn
                dn_core(b, 0).start()

            ff = (
                mm(hid[rows, :part], fbuf[:, 2 * part : chunk], NT)
                + mm(hid[rows, part:], fbuf[:, chunk + 2 * part :], NT)
            ).astype(BF16)

            @pl.when(keep == 0)
            def _():
                ff_out[b] = ff
                ff_core(b).start()

            @pl.when(keep == 1)
            def _():
                ff_core(b).wait_recv()
                ff_sum[b] = (ff.astype(F32) + ff_in[b].astype(F32)).astype(BF16)
                dn_core(b, 0).wait_recv()
                dn_sum[b] = (dn.astype(F32) + dn_in[b].astype(F32)).astype(BF16)
                dn_across(b, 0).start()

    def own_block(b, i):
        span = pl.ds(pl.multiple_of(i * LANES, LANES), LANES)
        here = pl.ds(pl.multiple_of(b * length + core * half + i * LANES, LANES), LANES)
        return span, here

    def finish_middle(b):
        dn_across(b, 0).wait_recv()

        @pl.loop(0, half // LANES)
        def _(i):
            span, here = own_block(b, i)
            upstream = dn_sum[b, span].astype(F32) + dn_far[b, span].astype(F32)
            middle = middle_ref[b, span]
            d_middle = cot_ref[here].astype(F32) + norm_back(
                middle, rms_scale(middle), gain_two, upstream
            )
            low_ref[here] = d_middle.astype(BF16)

        pl.semaphore_signal(credit.at[b], inc=1, device_id=spot.across, device_id_type=MESH)
        low_core(b, core).start()

    for group in feeds_gather:
        group.drain()
    for b in range(buffers):
        att_copy(spot.n_far, b, 2, spot.beside).wait_send()
    feed_reds = []
    for j in range(2):
        for begin in range(0, width, step):
            cols = slice(begin, begin + step)
            total[cols, : 2 * part] = mm(
                normed_two[:, cols], dg[:, 2 * j * part : (2 * j + 2) * part], TN
            )
            total[cols, 2 * part :] = mm(cot_ref[:, cols], hid[:, j * part : (j + 1) * part], TN)
        span = slice(j * chunk, (j + 1) * chunk)
        for m in range(4):
            even = total[pl.ds(pl.multiple_of(spot.near_owner(m) * owned, 8), owned)]
            odd = total[pl.ds(pl.multiple_of(spot.far_owner(m) * owned, 8), owned)]
            fbuf[m * owned : (m + 1) * owned, span] = even.astype(BF16)
            fbuf[(4 + m) * owned : (5 + m) * owned, span] = odd.astype(BF16)
        red = Reduce(
            spot,
            lambda m, span=span: fbuf[m * owned : (m + 1) * owned, span],
            lambda m, span=span: fbuf.at[(4 + m) * owned : (5 + m) * owned, span],
            lambda m, span=span: feed_flip.at[m, :, span],
            lambda m, span=span: feed_mix.at[m, :, span],
            lambda m, span=span: feed_land.at[m, :, span],
            red_s.at[j],
            red_r.at[j],
        )
        red.begin()
        feed_reds.append(red)
    finish_middle(0)
    feed_reds[0].relay(2, 1)

    out_red = Reduce(
        spot,
        lambda m: o_even[m],
        lambda m: o_odd.at[m],
        lambda m: o_flip.at[m],
        lambda m: o_mix.at[m],
        lambda m: o_land.at[m],
        red_s.at[2],
        red_r.at[2],
    )

    def out_weight_grad():
        for begin in range(0, width, step):
            cols = slice(begin, begin + step)
            total[cols, :head_cols] = mm(low_ref[:, cols], att_ref[spot.n], TN)
        for m in range(4):
            even = total[pl.ds(pl.multiple_of(spot.near_owner(m) * owned, 8), owned), :head_cols]
            odd = total[pl.ds(pl.multiple_of(spot.far_owner(m) * owned, 8), owned), :head_cols]
            o_even[m] = even
            o_odd[m] = odd.astype(BF16)
        out_red.begin()

    gain_sums = jnp.zeros((8, width), F32)
    def second_middle():
        finish_middle(1)
        ff_across(1).start()

    back_events = (
        {
            0: lambda: feed_reds[0].relay(3),
            2: lambda: ff_across(0).start(),
            3: lambda: feed_reds[1].relay(2),
            5: lambda: (feed_reds[1].relay(1), second_middle())[1],
        },
        {0: lambda: feed_reds[1].relay(3), 3: lambda: out_red.relay(2, 1), 4: lambda: out_red.relay(3)},
    )
    for b in range(buffers):
        base = b * length
        rows = slice(base, base + length)
        low_core(b, 1 - core).wait_recv()
        if b == 1:
            out_weight_grad()
        grads = mm(low_ref[rows], obuf[spot.n]).astype(BF16)
        att_ref[spot.n_far, :length] = grads
        for h in range(heads):
            keys = qkv_ref[rows, head_cols + h * DH : head_cols + (h + 1) * DH]
            values = qkv_ref[rows, 2 * head_cols + h * DH : 2 * head_cols + (h + 1) * DH]
            ws[h] = keys
            kt[h] = keys.T
            vt[h] = values.T
            qt[h] = qkv_ref[rows, h * DH : (h + 1) * DH].T
            gt[h] = grads[:, h * DH : (h + 1) * DH].T
        dkt[...] = jnp.zeros_like(dkt)
        dvt[...] = jnp.zeros_like(dvt)
        seg_keys = segments_of(
            lax.broadcasted_iota(jnp.int32, (1, length), 1), lengths_ref, b, slots
        )

        @pl.loop(0, blocks)
        def _(at, b=b, base=base, seg_keys=seg_keys):
            fire(back_events[b], at)
            begin = pl.multiple_of(at * LANES, LANES)
            here = pl.ds(begin, LANES)
            span = pl.ds(pl.multiple_of(base + begin, LANES), LANES)
            window = pl.ds(pl.multiple_of((blocks - 1 - at) * LANES, LANES), length)
            seg_rows = segments_of(
                lax.broadcasted_iota(jnp.int32, (LANES, 1), 0) + begin, lengths_ref, b, slots
            )
            same = seg_rows == seg_keys
            logs = log_ref[span]
            queries = qkv_ref[span, :head_cols]
            incoming = att_ref[spot.n_far, here]
            outs = []
            for h in range(heads):
                cols = slice(h * DH, (h + 1) * DH)
                scores = mm(queries[:, cols], kt[h]) + strip[h, :, window]
                scores = jnp.where(same, scores, masked_score)
                probs = jnp.exp(scores - logs[:, h : h + 1])
                d_probs = mm(incoming[:, cols], vt[h])
                inner = jnp.sum(probs * d_probs, axis=1, keepdims=True)
                d_scores = (probs * (d_probs - inner)).astype(BF16)
                dstrip[h, :, window] = dstrip[h, :, window] + d_scores.astype(F32)
                outs.append(mm(d_scores, ws[h]).astype(BF16))
                dkt[h] = dkt[h] + mm(qt[h, :, here], d_scores)
                dvt[h] = dvt[h] + mm(gt[h, :, here], probs.astype(BF16))
            dg[span, :head_cols] = jnp.concatenate(outs, axis=1)

        outs = [dkt[h].T.astype(BF16) for h in range(heads)]
        outs += [dvt[h].T.astype(BF16) for h in range(heads)]
        dg[rows, head_cols:qkv_cols] = jnp.concatenate(outs, axis=1)
        for keep in range(2):
            which = core if keep else 1 - core
            here = half_rows(b, which)
            if keep == 0:
                dn_core(b, 0).wait_send()
            else:
                dn_across(b, 0).wait_send()
            dn = mm(dg[here, :qkv_cols], pbuf[:, :qkv_cols], NT)
            values = x_ref[here].astype(F32)
            gain_sums = gain_sums + fold_rows(dn * values * rms_scale(values))
            dn = dn.astype(BF16)
            if keep == 0:
                dn_out[b] = dn
                dn_core(b, 1).start()
            else:
                dn_core(b, 1).wait_recv()
                dn_sum[b] = (dn.astype(F32) + dn_in[b].astype(F32)).astype(BF16)
                pl.semaphore_wait(credit.at[b], 1)
                dn_across(b, 1).start()

    row = lax.broadcasted_iota(jnp.int32, (LANES, width), 0)
    gain_rows = jnp.where(
        row == DH,
        jnp.sum(gain_sums, axis=0, keepdims=True),
        jnp.where(
            row == DH + 1, jnp.sum(gain_two_sum[...], axis=0, keepdims=True) / gain_two, 0.0
        ),
    )
    gain_cols = gain_rows.T
    p_cols = qkv_cols + DH
    p_reds = []
    for at, span in enumerate((slice(0, split), slice(split, p_cols))):
        stop = min(span.stop, qkv_cols)
        for begin in range(0, width, step):
            cols = slice(begin, begin + step)
            total[cols, span.start : stop] = mm(
                normed_one[:, cols], dg[:, span.start : stop], TN
            )
            if at:
                total[cols, qkv_cols:p_cols] = gain_cols[cols, DH:]
        for m in range(4):
            odd = total[pl.ds(pl.multiple_of(spot.far_owner(m) * owned, 8), owned), span]
            p_odd[m, :, span] = odd.astype(BF16)
        red = Reduce(
            spot,
            lambda m, span=span: total[
                pl.ds(pl.multiple_of(spot.near_owner(m) * owned, 8), owned), span
            ],
            lambda m, span=span: p_odd.at[m, :, span],
            lambda m, span=span: p_flip.at[m, :, span],
            lambda m, span=span: p_mix.at[m, :, span],
            lambda m, span=span: p_land.at[m, :, span],
            red_s.at[3 + at],
            red_r.at[3 + at],
        )
        red.begin()
        p_reds.append(red)

    def finish_out(b):
        ff_across(b).wait_recv()

        @pl.loop(0, half // LANES)
        def _(i):
            span, here = own_block(b, i)
            joined = (ff_sum[b, span].astype(F32) + ff_in[b, span].astype(F32)).astype(BF16)
            out_ref[here] = (middle_ref[b, span] + joined.astype(F32)).astype(BF16)

        out_core(b, core).start()

    def finish_in(b):
        dn_across(b, 1).wait_recv()

        @pl.loop(0, half // LANES)
        def _(i):
            span, here = own_block(b, i)
            upstream = dn_sum[b, span].astype(F32) + dn_far[b, span].astype(F32)
            values = x_ref[here].astype(F32)
            in_ref[here] = (
                low_ref[here].astype(F32)
                + norm_back(values, rms_scale(values), gain_one, upstream)
            ).astype(BF16)

        in_core(b, core).start()

    def square_of(value):
        return jnp.sum(jnp.sum(value * value, axis=1, keepdims=True), axis=0, keepdims=True)

    finish_out(0)
    p_reds[0].relay(2, 1, 3)
    finish_out(1)
    squares = jnp.zeros((1, 1), F32)
    for j in range(2):
        value = feed_reds[j].result()
        feed_grad[:, j * chunk : (j + 1) * chunk] = value
        squares = squares + square_of(value)
    p_reds[1].relay(2, 1, 3)
    value = out_red.result()
    o_grad[...] = value
    squares = squares + square_of(value)
    for b in range(buffers):
        out_core(b, 1 - core).wait_recv()
    finish_in(0)

    near_row = lax.broadcasted_iota(jnp.int32, (LANES, 4 * LANES), 0)
    diag = lax.broadcasted_iota(jnp.int32, (1, 4 * LANES), 1)
    ids = bucket_of(jnp.where(diag < 3 * LANES, diag - LANES, diag - 5 * LANES))
    lane = lax.broadcasted_iota(jnp.int32, (1, LANES), 1)
    onehot = jnp.where(near_row == ids, 1.0, 0.0)
    bucket_line = jnp.zeros((1, LANES), F32)
    for h in range(heads):
        left = jnp.sum(jnp.sum(dstrip[h, :, :near_at], axis=0, keepdims=True), axis=1, keepdims=True)
        right = jnp.sum(
            jnp.sum(dstrip[h, :, near_end:], axis=0, keepdims=True), axis=1, keepdims=True
        )
        near = jnp.concatenate(
            [dstrip[h, :, near_at:near_end], jnp.zeros((LANES, LANES), F32)], axis=1
        )
        for k in range(7):
            near = jnp.where(
                (near_row // (1 << k)) % 2 == 1, pltpu.roll(near, 4 * LANES - (1 << k), 1), near
            )
        binned = lax.dot_general(
            jnp.broadcast_to(jnp.sum(near, axis=0, keepdims=True), (8, 4 * LANES)),
            onehot,
            NT,
            precision=lax.Precision.HIGHEST,
            preferred_element_type=F32,
        )[0:1]
        binned = binned + jnp.where(lane == 15, left, 0.0) + jnp.where(lane == 31, right, 0.0)
        binned = jnp.where(lane < 32, binned, 0.0)
        bucket_line = bucket_line + (pltpu.roll(binned, 32 * h, 1) if h else binned)

    value = p_reds[0].result()
    p_grad[:, :split] = value
    squares = squares + square_of(value)
    value = p_reds[1].result()
    p_grad[:, split:] = value
    kept = lax.broadcasted_iota(jnp.int32, value.shape, 1) < qkv_cols - split
    squares = squares + square_of(jnp.where(kept, value, 0.0))
    low_lane = qkv_cols // LANES * LANES
    gpad[...] = jnp.zeros_like(gpad)
    gpad[0:owned, : p_cols - low_lane] = value[:, low_lane - split :]
    turned = gpad[...].T
    here = qkv_cols - low_lane
    row8 = lax.broadcasted_iota(jnp.int32, (8, LANES), 0)
    line = jnp.where(row8 == 0, squares, 0.0)
    line = jnp.where(row8 == 1, turned[here : here + 1], line)
    line = jnp.where(row8 == 2, turned[here + 1 : here + 2], line)
    line = jnp.where(row8 == 3, bucket_line, line)
    block[...] = line
    inbox[spot.me] = line

    @pl.loop(1, devices)
    def _(k):
        peer, where = spot.peer(k)
        remote(block, inbox.at[spot.me], norm_s.at[k], norm_r.at[devices - k], where).start()

    finish_in(1)

    @pl.loop(1, devices)
    def _(k):
        peer, where = spot.peer(k)
        copy = remote(block, inbox.at[peer], norm_s.at[k], norm_r.at[k], where)
        copy.wait_send()
        copy.wait_recv()

    columns = [jnp.zeros((8, LANES), F32) for _ in range(narrow)]
    gain_square = jnp.zeros((8, LANES), F32)
    square_total = jnp.zeros((8, LANES), F32)
    for a in range(wide):
        summed = jnp.zeros((8, LANES), F32)
        for c in range(narrow):
            got = inbox[a * narrow + c]
            summed = summed + got
            columns[c] = columns[c] + got
        square_total = square_total + summed
        gain_square = gain_square + summed * summed
    own = inbox[spot.w * narrow]
    for c in range(1, narrow):
        own = own + inbox[spot.w * narrow + c]
    gain_ref[...] = own
    gain_square = jnp.where((row8 == 1) | (row8 == 2), gain_square, 0.0)
    norm_square = square_total[0:1, 0:1] + jnp.sum(
        jnp.sum(gain_square, axis=1, keepdims=True), axis=0, keepdims=True
    )
    table_row = lax.broadcasted_iota(jnp.int32, (16, LANES), 0)
    table = jnp.zeros((16, LANES), F32)
    for c in range(narrow):
        got = columns[c][3:4]
        norm_square = norm_square + jnp.sum(got * got, axis=1, keepdims=True)
        for h in range(heads):
            moved = pltpu.roll(got, LANES - 32 * h, 1) if h else got
            table = jnp.where(table_row == c * heads + h, moved, table)
    table_ref[...] = table
    global_norm = jnp.sqrt(norm_square)
    factor = jnp.minimum(1.0, clip_limit / (global_norm + 1e-06))
    stat_ref[...] = jnp.where(row8 == 0, global_norm, factor)

    for b in range(buffers):
        in_core(b, 1 - core).wait_recv()
        for slot, which, peer in (
            (0, spot.n, spot.across),
            (1, spot.n, spot.beside),
        ):
            att_copy(which, b, slot, peer).wait_send()
        ff_core(b).wait_send()
        ff_across(b).wait_send()
        dn_core(b, 1).wait_send()
        dn_across(b, 1).wait_send()
        low_core(b, core).wait_send()
        out_core(b, core).wait_send()
        in_core(b, core).wait_send()
    lone(o_views[0](spot.w), o_views[0](spot.w), 0, spot.across).wait_send()
    lone(obuf.at[spot.n], obuf.at[spot.n], 1, spot.beside).wait_send()
    lone(obuf.at[spot.n_far], obuf.at[spot.n_far], 2, spot.beside).wait_send()
    for group in projections + outs_gather:
        group.drain()
    for group in feed_reds + p_reds + [out_red]:
        group.drain()


def layer(wide, narrow, lengths, bias, x, cot, pw, ow, ew, sw, gn):
    tokens, width = x.shape
    buffers, slots = lengths.shape
    length = tokens // buffers
    half = length // 2
    head_cols = pw.shape[2]
    heads = head_cols // DH
    hidden_cols = ew.shape[2]
    rows = gn.shape[1]
    devices = wide * narrow
    qkv_cols = 3 * head_cols
    p_cols = qkv_cols + DH
    feed_cols = 3 * hidden_cols
    strip_shape = (heads, LANES, (2 * (length // LANES) - 1) * LANES)
    vmem = pl.BlockSpec(memory_space=pltpu.VMEM)
    smem = pl.BlockSpec(memory_space=pltpu.SMEM)
    halves = pltpu.VMEM((buffers, half, width), BF16)
    tall = pltpu.VMEM((heads, DH, length), BF16)
    dma = pltpu.SemaphoreType.DMA

    def pieces(count, cols, kind=BF16):
        return pltpu.VMEM((count, rows, cols), kind)

    return pl.pallas_call(
        functools.partial(layer_kernel, (buffers, slots, heads, hidden_cols, wide, narrow)),
        in_specs=[smem, smem, pl.BlockSpec(memory_space=ANY), pl.BlockSpec(memory_space=ANY)]
        + [vmem] * 5,
        out_specs=[vmem] * 8,
        out_shape=[
            jax.ShapeDtypeStruct((tokens, width), BF16),
            jax.ShapeDtypeStruct((tokens, width), BF16),
            jax.ShapeDtypeStruct((rows, p_cols), F32),
            jax.ShapeDtypeStruct((rows, head_cols), F32),
            jax.ShapeDtypeStruct((rows, feed_cols), F32),
            jax.ShapeDtypeStruct((8, LANES), F32),
            jax.ShapeDtypeStruct((8, LANES), F32),
            jax.ShapeDtypeStruct((16, LANES), F32),
        ],
        scratch_shapes=[
            pltpu.VMEM((tokens, width), BF16),
            pltpu.VMEM((tokens, width), BF16),
            pltpu.VMEM(strip_shape, F32),
            pltpu.VMEM(strip_shape, F32),
            pltpu.VMEM((width, p_cols), BF16),
            pltpu.VMEM((narrow, width, head_cols), BF16),
            pltpu.VMEM((width, feed_cols), BF16),
            pltpu.VMEM((narrow, tokens, head_cols), BF16),
            pltpu.VMEM((tokens, qkv_cols), BF16),
            pltpu.VMEM((tokens, LANES), F32),
            pltpu.VMEM((tokens, width), BF16),
            pltpu.VMEM((buffers, half, width), F32),
            pltpu.VMEM((tokens, hidden_cols), BF16),
            pltpu.VMEM((tokens, 2 * hidden_cols), BF16),
            pltpu.VMEM((width, feed_cols // 2), F32),
            pltpu.VMEM((2 * LANES, LANES), F32),
            pltpu.VMEM((LANES, LANES), F32),
            pieces(4, feed_cols),
            pieces(3, feed_cols),
            pieces(3, feed_cols),
            pieces(4, head_cols, F32),
            pieces(4, head_cols),
            pieces(4, head_cols),
            pieces(3, head_cols),
            pieces(3, head_cols),
            pieces(4, p_cols),
            pieces(4, p_cols),
            pieces(3, p_cols),
            pieces(3, p_cols),
        ]
        + [halves] * 7
        + [
            pltpu.VMEM((heads, length, DH), BF16),
            tall,
            tall,
            tall,
            tall,
            pltpu.VMEM((heads, DH, length), F32),
            pltpu.VMEM((heads, DH, length), F32),
            pltpu.VMEM((8, width), F32),
            pltpu.VMEM((8, LANES), F32),
            pltpu.VMEM((devices, 8, LANES), F32),
            dma((8, 7)),
            dma((8, wide)),
            dma((27,)),
            dma((27,)),
            dma((5, 7)),
            dma((5, 7)),
            dma((devices,)),
            dma((devices,)),
            pltpu.SemaphoreType.REGULAR((buffers,)),
            dma((2,)),
        ],
        compiler_params=pltpu.CompilerParams(
            vmem_limit_bytes=64 << 20, collective_id=0, has_side_effects=True
        ),
        cost_estimate=pl.CostEstimate(
            flops=60 << 30, bytes_accessed=24 << 20, transcendentals=16 << 20
        ),
        name="layer",
    )(lengths, bias, x, cot, pw, ow, ew, sw, gn)


def update_kernel(
    heads, hidden_cols, from_out, from_in, p_ref, o_ref, feed_ref, stat_ref, gain_ref, table_ref, *refs
):
    weights, firsts, seconds = refs[:6], refs[6:12], refs[12:18]
    outs, norm_ref, to_out, to_in, o_pad, held, sems = refs[18:36], *refs[36:]
    pairs = ((from_out, to_out), (from_in, to_in))
    rows = from_out.shape[0] // 2
    ways = []
    for which, (source, target) in enumerate(pairs):
        for part in range(2):
            span = slice(part * rows, (part + 1) * rows)
            at = 2 * which + part
            ways.append(
                (
                    pltpu.make_async_copy(source.at[span], held.at[which, span], sems.at[0, at]),
                    pltpu.make_async_copy(held.at[which, span], target.at[span], sems.at[1, at]),
                )
            )
    for inward, _ in ways:
        inward.start()
    for inward, outward in ways:
        inward.wait()
        outward.start()
    factor = stat_ref[1:2, 0:1]
    norm_ref[0, 0] = jnp.sum(stat_ref[0:1, 0:1])
    head_cols = heads * DH
    rows = p_ref.shape[0]

    def update(which, index, gradient):
        results = adam_update(
            weights[which][index],
            firsts[which][index],
            seconds[which][index],
            factor * gradient,
            step_rates[which],
            decay_rates[which],
        )
        for at in range(3):
            outs[6 * at + which][index] = results[at]

    for i in range(3):
        update(0, i, p_ref[:, i * head_cols : (i + 1) * head_cols])
    part = hidden_cols // 2
    for j in range(2):
        span = slice(j * part, (j + 1) * part)
        for i in range(2):
            begin = (3 * j + i) * part
            update(2, (i, slice(None), span), feed_ref[:, begin : begin + part])
        begin = (3 * j + 2) * part
        update(3, (slice(None), span), feed_ref[:, begin : begin + part])
    o_pad[...] = jnp.zeros_like(o_pad)
    o_pad[0:rows, 0:head_cols] = o_ref[...]
    update(1, slice(None), o_pad[...].T[:head_cols, :rows])
    depth, columns = weights[4].shape
    update(4, slice(None), table_ref[:depth, :columns])
    update(5, slice(None), gain_ref[1:3, :rows])
    for _, outward in ways:
        outward.wait()


def update_call(activations, grads, params_in, firsts, seconds, heads, hidden_cols):
    vmem = pl.BlockSpec(memory_space=pltpu.VMEM)
    hbm = pl.BlockSpec(memory_space=ANY)
    operands = [*activations, *grads, *params_in, *firsts, *seconds]
    return pl.pallas_call(
        functools.partial(update_kernel, heads, hidden_cols),
        in_specs=[hbm] * 2 + [vmem] * (len(operands) - 2),
        out_specs=[vmem] * 18 + [pl.BlockSpec(memory_space=pltpu.SMEM)] + [hbm] * 2,
        out_shape=[jax.ShapeDtypeStruct(a.shape, F32) for a in params_in] * 3
        + [jax.ShapeDtypeStruct((1, 1), F32)]
        + [jax.ShapeDtypeStruct(a.shape, a.dtype) for a in activations],
        scratch_shapes=[
            pltpu.VMEM((LANES, 2 * LANES), F32),
            pltpu.VMEM((2, *activations[0].shape), BF16),
            pltpu.SemaphoreType.DMA((2, 4)),
        ],
        compiler_params=params(),
        cost_estimate=pl.CostEstimate(flops=4 << 20, bytes_accessed=16 << 20, transcendentals=0),
        name="update",
    )(*operands)


def direct_body(wide, narrow, *arguments):
    block_input, cotangent, lengths = arguments[:3]
    turned = (3, 4)
    flat = [
        value.T if at % 6 in turned else value for at, value in enumerate(arguments[3:21])
    ]
    weights, firsts, seconds = flat[:6], flat[6:12], flat[12:18]
    project, output, expand, shrink, bias, gains = weights
    block_output, input_gradient, *grads = layer(
        wide,
        narrow,
        lengths,
        bias,
        block_input,
        cotangent,
        project,
        output,
        expand,
        shrink,
        gains,
    )
    heads = project.shape[2] // DH
    *results, norm, block_output, input_gradient = update_call(
        (block_output, input_gradient), grads, weights, firsts, seconds, heads, expand.shape[2]
    )
    results = [value.T if at % 6 in turned else value for at, value in enumerate(results)]
    return (block_output, input_gradient, norm.reshape(()), *results)


def solution(mesh):
    wide, narrow = mesh.shape["wide"], mesh.shape["narrow"]
    body = direct_body if (wide, narrow) == (8, 4) else general_body
    state = (
        P(None, "wide", "narrow"),
        P("narrow", "wide"),
        P(None, "wide", "narrow"),
        P("narrow", "wide"),
        P(),
        P(None, "wide"),
    )
    rows = P("wide", None)
    return jax.shard_map(
        functools.partial(body, wide, narrow),
        mesh=mesh,
        in_specs=(rows, rows, rows, *state, *state, *state),
        out_specs=(rows, rows, P(), *state, *state, *state),
        check_vma=False,
    )
```

```python
import functools

import jax
import jax.numpy as jnp
from jax import lax
from jax.experimental import pallas as pl
from jax.experimental.pallas import tpu as pltpu
from jax.sharding import PartitionSpec as P

DH = 64
STEP = 10
LANES = 128
MESH = pl.DeviceIdType.MESH
F32 = jnp.float32
BF16 = jnp.bfloat16
ANY = pl.ANY

bucket_edges = (12, 16, 23, 32, 46, 64, 91)
norm_eps = 1e-06
clip_limit = 1.0
beta_one = 0.9
beta_two = 0.999
adam_eps = 1e-08
step_rates = (0.06, 0.3, 0.07, 0.06, 1.0, 0.3)
decay_rates = (0.01, 0.01, 0.01, 0.01, 0.0, 0.0)
masked_score = -1000000000.0
VMEM_LIMIT = 58 << 20

NN = (((1,), (0,)), ((), ()))
NT = (((1,), (1,)), ((), ()))
TN = (((0,), (0,)), ((), ()))


def mm(left, right, dims=NN):
    return lax.dot_general(left, right, dims, preferred_element_type=F32)


def bucket_of(offsets):
    distance = jnp.abs(offsets)
    far_bucket = 8 + sum(((distance >= threshold).astype(jnp.int32) for threshold in bucket_edges))
    return jnp.where(distance < 8, distance, far_bucket) + 16 * (offsets > 0).astype(jnp.int32)


def rms_scale(values):
    return lax.rsqrt(jnp.mean(values * values, axis=-1, keepdims=True) + norm_eps)


def norm_back(values, scale_vec, gain_vec, upstream):
    weighted = upstream * gain_vec
    inner_mean = jnp.mean(weighted * values, axis=-1, keepdims=True)
    return scale_vec * weighted - values * (scale_vec * scale_vec * scale_vec) * inner_mean


def adam_update(weight, moment_one, moment_two, gradient, step_rate, decay_rate):
    new_first = beta_one * moment_one + (1.0 - beta_one) * gradient
    new_second = beta_two * moment_two + (1.0 - beta_two) * gradient * gradient
    first_hat = new_first / (1.0 - beta_one**STEP)
    second_hat = new_second / (1.0 - beta_two**STEP)
    new_weight = weight - step_rate * (
        first_hat / (jnp.sqrt(second_hat) + adam_eps) + decay_rate * weight
    )
    return (new_weight, new_first, new_second)


def fold_rows(values):
    rows, cols = values.shape
    return jnp.sum(values.reshape(rows // 8, 8, cols), axis=0)


def start_rows(pieces, target, offs_ref, sems):
    copies = []
    for at, piece in enumerate(pieces):
        rows = piece.shape[0]
        begin = pl.multiple_of(offs_ref[at], 16)
        copies.append(
            pltpu.make_async_copy(piece, target.at[pl.ds(begin, rows)], sems.at[at])
        )
    for copy in copies:
        copy.start()
    return copies


def segments(index, ends_ref, buffer, slots):
    total = jnp.zeros(index.shape, jnp.int32)
    for slot in range(slots):
        total = total + (index >= ends_ref[buffer, slot]).astype(jnp.int32)
    return total


def params(**more):
    return pltpu.CompilerParams(vmem_limit_bytes=VMEM_LIMIT, **more)


def attend_kernel(
    buffer, slots, heads, count, ends_ref, offs_ref, x_ref, strip_ref, *refs
):
    pieces = refs[:count]
    normed_ref, qkv_ref, att_ref, log_ref, gains_ref, wbuf, qs, ks, vs, os, sems = refs[count:]
    length, width = x_ref.shape
    head_cols = heads * DH
    copies = start_rows(pieces, wbuf, offs_ref, sems)
    for copy in copies:
        copy.wait()
    gain_cols = wbuf[:, 4 * LANES :].astype(F32).T
    first = 3 * head_cols - 4 * LANES
    gains = gain_cols[first : first + 8]
    gains_ref[...] = gains
    gain_one = gains[0:1]
    step = 256

    @pl.loop(0, length // step)
    def _(block):
        rows = pl.ds(pl.multiple_of(block * step, step), step)
        values = x_ref[rows].astype(F32)
        normed = (values * rms_scale(values) * gain_one).astype(BF16)
        normed_ref[rows] = normed
        qkv = mm(normed, wbuf[...]).astype(BF16)
        qkv_ref[rows] = qkv[:, : 3 * head_cols]
        for h in range(heads):
            qs[h, rows] = qkv[:, h * DH : (h + 1) * DH]
            ks[h, rows] = qkv[:, head_cols + h * DH : head_cols + (h + 1) * DH]
            vs[h, rows] = qkv[:, 2 * head_cols + h * DH : 2 * head_cols + (h + 1) * DH]

    blocks = length // LANES
    seg_keys = segments(
        lax.broadcasted_iota(jnp.int32, (1, length), 1), ends_ref, buffer, slots
    )

    @pl.loop(0, blocks)
    def _(block):
        begin = pl.multiple_of(block * LANES, LANES)
        rows = pl.ds(begin, LANES)
        window = pl.ds(pl.multiple_of((blocks - 1 - block) * LANES, LANES), length)
        seg_rows = segments(
            lax.broadcasted_iota(jnp.int32, (LANES, 1), 0) + begin, ends_ref, buffer, slots
        )
        same = seg_rows == seg_keys
        lane = lax.broadcasted_iota(jnp.int32, (LANES, LANES), 1)
        logs = jnp.zeros((LANES, LANES), F32)
        for h in range(heads):
            scores = mm(qs[h, rows], ks[h], NT) + strip_ref[h, :, window]
            scores = jnp.where(same, scores, masked_score)
            row_max = jnp.max(scores, axis=1, keepdims=True)
            raised = jnp.exp(scores - row_max)
            total = jnp.sum(raised, axis=1, keepdims=True)
            probs = (raised * (1.0 / total)).astype(BF16)
            os[h, rows] = mm(probs, vs[h]).astype(BF16)
            logs = jnp.where(lane == h, row_max + jnp.log(total), logs)
        log_ref[rows] = logs

    att_ref[...] = jnp.concatenate([os[h] for h in range(heads)], axis=1)


def attend(buffer, ends, offs, x, strip, pieces, length, heads):
    width = x.shape[1]
    count = len(pieces)
    cols = pieces[0].shape[1]
    head_cols = heads * DH
    whole = lambda i, *_: (0, 0)
    spec = pltpu.PrefetchScalarGridSpec(
        num_scalar_prefetch=2,
        grid=(1,),
        in_specs=[
            pl.BlockSpec((length, width), lambda i, *_: (buffer, 0)),
            pl.BlockSpec(strip.shape, lambda i, *_: (0, 0, 0)),
        ]
        + [pl.BlockSpec(memory_space=ANY)] * count,
        out_specs=[
            pl.BlockSpec((length, width), whole),
            pl.BlockSpec((length, 3 * head_cols), whole),
            pl.BlockSpec((length, head_cols), whole),
            pl.BlockSpec((length, LANES), whole),
            pl.BlockSpec((8, width), whole),
        ],
        scratch_shapes=[
            pltpu.VMEM((width, cols), BF16),
            pltpu.VMEM((heads, length, DH), BF16),
            pltpu.VMEM((heads, length, DH), BF16),
            pltpu.VMEM((heads, length, DH), BF16),
            pltpu.VMEM((heads, length, DH), BF16),
            pltpu.SemaphoreType.DMA((count,)),
        ],
    )
    flops = 2 * length * (width * cols + 2 * heads * DH * length)
    return pl.pallas_call(
        functools.partial(attend_kernel, buffer, ends.shape[1], heads, count),
        grid_spec=spec,
        out_shape=[
            jax.ShapeDtypeStruct((length, width), BF16),
            jax.ShapeDtypeStruct((length, 3 * head_cols), BF16),
            jax.ShapeDtypeStruct((length, head_cols), BF16),
            jax.ShapeDtypeStruct((length, LANES), F32),
            jax.ShapeDtypeStruct((8, width), F32),
        ],
        compiler_params=params(),
        cost_estimate=pl.CostEstimate(
            flops=4 * flops, bytes_accessed=8 << 20, transcendentals=heads * length * length
        ),
        name="attend",
    )(ends, offs, x, strip, *pieces)


def feed_kernel(hidden_cols, counts, order_ref, offs_ref, *refs):
    own, across, beside, diagonal, x_ref, cot_ref, gains_ref = refs[:7]
    at = 7
    groups = []
    for count in counts:
        groups.append(refs[at : at + count])
        at += count
    (
        normed_ref,
        hidden_ref,
        gate_ref,
        ff_send,
        ff_keep,
        dn_send,
        dn_keep,
        middle_keep,
        gain_sum,
        ebuf,
        sbuf,
        oabuf,
        obbuf,
        sems,
    ) = refs[at:]
    step = pl.program_id(0)
    bufs = (oabuf, obbuf, ebuf, sbuf)

    @pl.when(step == 0)
    def _():
        copies = []
        for which, (group, target) in enumerate(zip(groups, bufs)):
            copies += start_rows(group, target, offs_ref, sems.at[which])
        for copy in copies:
            copy.wait()

    cols = own.shape[1]
    upper = order_ref[2] == 0
    pairs = []
    for near, far, weights in ((own, across, oabuf), (beside, diagonal, obbuf)):
        near_sum = mm(near[...], weights[:, :cols], NT)
        far_sum = mm(far[...], weights[:, cols:], NT)
        pairs.append(
            jnp.where(upper, near_sum, far_sum) + jnp.where(upper, far_sum, near_sum)
        )
    swap = order_ref[0] == 0
    attention = jnp.where(swap, pairs[0], pairs[1]) + jnp.where(swap, pairs[1], pairs[0])
    middle = x_ref[...].astype(F32) + attention
    scale_two = rms_scale(middle)
    gain_two = gains_ref[1:2]
    normed = (middle * scale_two * gain_two).astype(BF16)
    normed_ref[...] = normed
    cot = cot_ref[...]
    part = 256
    k0 = 0.7978845608028654
    k1 = 0.044715
    for begin in range(0, hidden_cols, part):
        gate = mm(normed, ebuf[:, begin : begin + part])
        up = mm(normed, ebuf[:, hidden_cols + begin : hidden_cols + begin + part])
        square = gate * gate
        tanh = jnp.tanh(k0 * (gate + k1 * (square * gate)))
        half = 0.5 * (1.0 + tanh)
        active = gate * half
        slope = half + (0.5 * gate) * (1.0 - tanh * tanh) * (k0 + (3.0 * k0 * k1) * square)
        d_hidden = mm(cot, sbuf[:, begin : begin + part])
        hidden_ref[:, begin : begin + part] = (active * up).astype(BF16)
        gate_ref[:, begin : begin + part] = (d_hidden * up * slope).astype(BF16)
        gate_ref[:, hidden_cols + begin : hidden_cols + begin + part] = (
            d_hidden * active
        ).astype(BF16)
    ff = mm(hidden_ref[...], sbuf[...], NT).astype(BF16)
    dn = mm(gate_ref[...], ebuf[...], NT)
    sums = fold_rows(dn * middle * scale_two)
    dn = dn.astype(BF16)

    @pl.when(step == 0)
    def _():
        ff_send[...] = ff
        dn_send[...] = dn
        gain_sum[...] = sums

    @pl.when(step == 1)
    def _():
        ff_keep[...] = ff
        dn_keep[...] = dn
        middle_keep[...] = middle
        gain_sum[...] = gain_sum[...] + sums


def feed(buffer, order, offs, parts, x, cot, gains, groups, length, hidden_cols):
    width = x.shape[1]
    half = length // 2
    cols = parts[0].shape[1]
    counts = [len(group) for group in groups]
    natural = lambda i, order, *_: (order[i], 0)
    rows = lambda i, order, *_: (2 * buffer + order[i], 0)
    whole = lambda i, *_: (0, 0)
    spec = pltpu.PrefetchScalarGridSpec(
        num_scalar_prefetch=2,
        grid=(2,),
        in_specs=[pl.BlockSpec((half, cols), natural)] * 4
        + [pl.BlockSpec((half, width), rows)] * 2
        + [pl.BlockSpec((8, width), whole)]
        + [pl.BlockSpec(memory_space=ANY)] * sum(counts),
        out_specs=[
            pl.BlockSpec((half, width), natural),
            pl.BlockSpec((half, hidden_cols), natural),
            pl.BlockSpec((half, 2 * hidden_cols), natural),
        ]
        + [pl.BlockSpec((half, width), whole)] * 5
        + [pl.BlockSpec((8, width), whole)],
        scratch_shapes=[
            pltpu.VMEM((width, 2 * hidden_cols), BF16),
            pltpu.VMEM((width, hidden_cols), BF16),
            pltpu.VMEM((width, 2 * cols), BF16),
            pltpu.VMEM((width, 2 * cols), BF16),
            pltpu.SemaphoreType.DMA((4, max(counts))),
        ],
    )
    flops = 2 * length * width * (4 * cols + 7 * hidden_cols)
    return pl.pallas_call(
        functools.partial(feed_kernel, hidden_cols, counts),
        grid_spec=spec,
        out_shape=[
            jax.ShapeDtypeStruct((length, width), BF16),
            jax.ShapeDtypeStruct((length, hidden_cols), BF16),
            jax.ShapeDtypeStruct((length, 2 * hidden_cols), BF16),
            jax.ShapeDtypeStruct((half, width), BF16),
            jax.ShapeDtypeStruct((half, width), BF16),
            jax.ShapeDtypeStruct((half, width), BF16),
            jax.ShapeDtypeStruct((half, width), BF16),
            jax.ShapeDtypeStruct((half, width), F32),
            jax.ShapeDtypeStruct((8, width), F32),
        ],
        compiler_params=params(),
        cost_estimate=pl.CostEstimate(
            flops=flops, bytes_accessed=12 << 20, transcendentals=length * hidden_cols
        ),
        name="feed",
    )(order, offs, *parts, x, cot, gains, *[piece for group in groups for piece in group])


def middle_kernel(order_ref, near, far, middle_ref, cot_ref, gains_ref, d_ref, low_ref):
    upstream = near[...].astype(F32) + far[...].astype(F32)
    middle = middle_ref[...]
    d_middle = cot_ref[...].astype(F32) + norm_back(
        middle, rms_scale(middle), gains_ref[1:2], upstream
    )
    d_ref[...] = d_middle
    low_ref[...] = d_middle.astype(BF16)


def input_kernel(order_ref, near, far, x_ref, d_ref, gains_ref, out_ref):
    upstream = near[...].astype(F32) + far[...].astype(F32)
    values = x_ref[...].astype(F32)
    out_ref[...] = (
        d_ref[...] + norm_back(values, rms_scale(values), gains_ref[0:1], upstream)
    ).astype(BF16)


def output_kernel(order_ref, near, far, middle_ref, out_ref):
    out_ref[...] = (
        middle_ref[...] + (near[...].astype(F32) + far[...].astype(F32)).astype(BF16).astype(F32)
    ).astype(BF16)


def half_call(kernel, name, buffer, order, arrays, placed, outs, gains=None):
    half, width = arrays[0].shape
    steps = 3
    block = half // steps
    mine = lambda i, *_: (i, 0)
    rows = lambda i, order, *_: ((2 * buffer + order[1]) * steps + i, 0)
    in_specs = [
        pl.BlockSpec((block, width), rows if at in placed else mine)
        for at in range(len(arrays))
    ]
    operands = list(arrays)
    if gains is not None:
        in_specs.append(pl.BlockSpec((8, width), lambda i, *_: (0, 0)))
        operands.append(gains)
    return pl.pallas_call(
        kernel,
        grid_spec=pltpu.PrefetchScalarGridSpec(
            num_scalar_prefetch=1,
            grid=(steps,),
            in_specs=in_specs,
            out_specs=[pl.BlockSpec((block, width), mine) for _ in outs],
        ),
        out_shape=[jax.ShapeDtypeStruct((half, width), kind) for kind in outs],
        compiler_params=params(),
        cost_estimate=pl.CostEstimate(
            flops=20 * half * width, bytes_accessed=12 * half * width, transcendentals=0
        ),
        name=name,
    )(order, *operands)


def back_kernel(buffer, slots, heads, counts, ends_ref, offs_ref, order_ref, *refs):
    near, far, qkv_ref, log_ref, strip_ref, x_ref = refs[:6]
    at = 6
    o_pieces = refs[at : at + counts[0]]
    at += counts[0]
    p_pieces = refs[at : at + counts[1]]
    at += counts[1]
    (
        low_ref,
        dqkv_ref,
        dn_send,
        dn_keep,
        gain_sum,
        dstrip,
        wbuf,
        obuf,
        qs,
        ks,
        vs,
        gs,
        qt,
        gt,
        dkt,
        dvt,
        dq,
        sems,
    ) = refs[at:]
    length = qkv_ref.shape[0]
    half = length // 2
    head_cols = heads * DH
    o_copies = start_rows(o_pieces, obuf, offs_ref, sems.at[0])
    p_copies = start_rows(p_pieces, wbuf, offs_ref, sems.at[1])
    mine = pl.ds(pl.multiple_of(order_ref[1] * half, LANES), half)
    other = pl.ds(pl.multiple_of(order_ref[0] * half, LANES), half)
    low_ref[mine] = near[...]
    low_ref[other] = far[...]
    for h in range(heads):
        qs[h] = qkv_ref[:, h * DH : (h + 1) * DH]
        ks[h] = qkv_ref[:, head_cols + h * DH : head_cols + (h + 1) * DH]
        vs[h] = qkv_ref[:, 2 * head_cols + h * DH : 2 * head_cols + (h + 1) * DH]
        qt[h] = qs[h].T
    dstrip[...] = jnp.zeros_like(dstrip)
    dkt[...] = jnp.zeros_like(dkt)
    dvt[...] = jnp.zeros_like(dvt)
    for copy in o_copies + p_copies:
        copy.wait()
    grads = mm(low_ref[...], obuf[:, :head_cols]).astype(BF16)
    for h in range(heads):
        gs[h] = grads[:, h * DH : (h + 1) * DH]
        gt[h] = gs[h].T
    blocks = length // LANES
    seg_keys = segments(
        lax.broadcasted_iota(jnp.int32, (1, length), 1), ends_ref, buffer, slots
    )

    @pl.loop(0, blocks)
    def _(block):
        begin = pl.multiple_of(block * LANES, LANES)
        rows = pl.ds(begin, LANES)
        window = pl.ds(pl.multiple_of((blocks - 1 - block) * LANES, LANES), length)
        seg_rows = segments(
            lax.broadcasted_iota(jnp.int32, (LANES, 1), 0) + begin, ends_ref, buffer, slots
        )
        same = seg_rows == seg_keys
        logs = log_ref[rows]
        for h in range(heads):
            scores = mm(qs[h, rows], ks[h], NT) + strip_ref[h, :, window]
            scores = jnp.where(same, scores, masked_score)
            probs = jnp.exp(scores - logs[:, h : h + 1])
            d_probs = mm(gs[h, rows], vs[h], NT)
            inner = jnp.sum(probs * d_probs, axis=1, keepdims=True)
            d_scores = (probs * (d_probs - inner)).astype(BF16)
            dstrip[h, :, window] = dstrip[h, :, window] + d_scores.astype(F32)
            dq[h, rows] = mm(d_scores, ks[h]).astype(BF16)
            dkt[h] = dkt[h] + mm(qt[h, :, rows], d_scores)
            dvt[h] = dvt[h] + mm(gt[h, :, rows], probs.astype(BF16))

    outs = [dq[h] for h in range(heads)]
    outs += [dkt[h].T.astype(BF16) for h in range(heads)]
    outs += [dvt[h].T.astype(BF16) for h in range(heads)]
    dqkv_ref[...] = jnp.concatenate(outs, axis=1)
    sums = []
    for target, which in ((dn_send, other), (dn_keep, mine)):
        dn = mm(dqkv_ref[which], wbuf[:, : 3 * head_cols], NT)
        values = x_ref[which].astype(F32)
        sums.append(fold_rows(dn * values * rms_scale(values)))
        target[...] = dn.astype(BF16)
    gain_sum[...] = sums[0] + sums[1]


def back(buffer, ends, offs, order, near, far, qkv, logs, strip, x, o_pieces, p_pieces, heads):
    length = qkv.shape[0]
    half = length // 2
    width = x.shape[1]
    head_cols = heads * DH
    counts = (len(o_pieces), len(p_pieces))
    whole = lambda i, *_: (0, 0)
    whole3 = lambda i, *_: (0, 0, 0)
    spec = pltpu.PrefetchScalarGridSpec(
        num_scalar_prefetch=3,
        grid=(1,),
        in_specs=[
            pl.BlockSpec((half, width), whole),
            pl.BlockSpec((half, width), whole),
            pl.BlockSpec(qkv.shape, whole),
            pl.BlockSpec(logs.shape, whole),
            pl.BlockSpec(strip.shape, whole3),
            pl.BlockSpec((length, width), lambda i, *_: (buffer, 0)),
        ]
        + [pl.BlockSpec(memory_space=ANY)] * sum(counts),
        out_specs=[
            pl.BlockSpec((length, width), whole),
            pl.BlockSpec((length, 3 * head_cols), whole),
            pl.BlockSpec((half, width), whole),
            pl.BlockSpec((half, width), whole),
            pl.BlockSpec((8, width), whole),
            pl.BlockSpec(strip.shape, whole3),
        ],
        scratch_shapes=[
            pltpu.VMEM((width, p_pieces[0].shape[1]), BF16),
            pltpu.VMEM((width, o_pieces[0].shape[1]), BF16),
            pltpu.VMEM((heads, length, DH), BF16),
            pltpu.VMEM((heads, length, DH), BF16),
            pltpu.VMEM((heads, length, DH), BF16),
            pltpu.VMEM((heads, length, DH), BF16),
            pltpu.VMEM((heads, DH, length), BF16),
            pltpu.VMEM((heads, DH, length), BF16),
            pltpu.VMEM((heads, DH, length), F32),
            pltpu.VMEM((heads, DH, length), F32),
            pltpu.VMEM((heads, length, DH), BF16),
            pltpu.SemaphoreType.DMA((2, max(counts))),
        ],
    )
    return pl.pallas_call(
        functools.partial(back_kernel, buffer, ends.shape[1], heads, counts),
        grid_spec=spec,
        out_shape=[
            jax.ShapeDtypeStruct((length, width), BF16),
            jax.ShapeDtypeStruct((length, 3 * head_cols), BF16),
            jax.ShapeDtypeStruct((half, width), BF16),
            jax.ShapeDtypeStruct((half, width), BF16),
            jax.ShapeDtypeStruct((8, width), F32),
            jax.ShapeDtypeStruct(strip.shape, F32),
        ],
        compiler_params=params(),
        cost_estimate=pl.CostEstimate(
            flops=40 * heads * DH * length * length,
            bytes_accessed=16 << 20,
            transcendentals=heads * length * length,
        ),
        name="back",
    )(ends, offs, order, near, far, qkv, logs, strip, x, *o_pieces, *p_pieces)


def scatter_rows(total, offs_ref, evens, odds):
    rows = evens[0].shape[0]
    for at in range(2 * len(evens)):
        begin = pl.multiple_of(offs_ref[at], 8)
        block = total[pl.ds(begin, rows)]
        if at % 2:
            odds[at // 2][...] = block.astype(BF16)
        else:
            evens[at // 2][...] = block


def feed_grad_kernel(count, hidden_cols, offs_ref, *refs):
    buffers = 2
    normed = refs[:buffers]
    gates = refs[buffers : 2 * buffers]
    hiddens = refs[2 * buffers : 3 * buffers]
    cot_ref = refs[3 * buffers]
    outs = refs[3 * buffers + 1 : -1]
    total = refs[-1]
    length = normed[0].shape[0]
    width = normed[0].shape[1]
    part = 256
    for begin in range(0, width, part):
        cols = slice(begin, begin + part)
        total[cols, : 2 * hidden_cols] = mm(normed[0][:, cols], gates[0][...], TN) + mm(
            normed[1][:, cols], gates[1][...], TN
        )
        total[cols, 2 * hidden_cols :] = mm(
            cot_ref[:length, cols], hiddens[0][...], TN
        ) + mm(cot_ref[length:, cols], hiddens[1][...], TN)
    if count > 1:
        scatter_rows(total, offs_ref, outs[: count // 2], outs[count // 2 :])
    else:
        outs[0][...] = total[...]


def attend_grad_kernel(count, heads, offs_ref, *refs):
    buffers = 2
    normed = refs[:buffers]
    dqkv = refs[buffers : 2 * buffers]
    lows = refs[2 * buffers : 3 * buffers]
    atts = refs[3 * buffers : 4 * buffers]
    sums_ref = refs[4 * buffers]
    outs = refs[4 * buffers + 1 : -1]
    total = refs[-1]
    width = normed[0].shape[1]
    head_cols = heads * DH
    qkv_cols = 3 * head_cols
    part = 256
    rows = lax.broadcasted_iota(jnp.int32, (LANES, width), 0)
    first = sums_ref[0] + sums_ref[1]
    second = sums_ref[2] + sums_ref[3]
    gain_rows = jnp.where(
        rows == DH,
        jnp.sum(first, axis=0, keepdims=True),
        jnp.where(rows == DH + 1, jnp.sum(second, axis=0, keepdims=True), 0.0),
    )
    gain_cols = gain_rows.T
    for begin in range(0, width, part):
        cols = slice(begin, begin + part)
        total[cols, :qkv_cols] = mm(normed[0][:, cols], dqkv[0][...], TN) + mm(
            normed[1][:, cols], dqkv[1][...], TN
        )
        total[cols, qkv_cols : qkv_cols + DH] = gain_cols[cols, DH:]
        total[cols, qkv_cols + DH : qkv_cols + DH + head_cols] = mm(
            lows[0][:, cols], atts[0][...], TN
        ) + mm(lows[1][:, cols], atts[1][...], TN)
    if count > 1:
        scatter_rows(total, offs_ref, outs[: count // 2], outs[count // 2 :])
    else:
        outs[0][...] = total[...]


def grad_call(kernel, name, offs, operands, width, cols, count, rows, flops):
    vmem = pl.BlockSpec(memory_space=pltpu.VMEM)
    if count > 1:
        shapes = [jax.ShapeDtypeStruct((rows, cols), F32)] * (count // 2)
        shapes += [jax.ShapeDtypeStruct((rows, cols), BF16)] * (count // 2)
    else:
        shapes = [jax.ShapeDtypeStruct((width, cols), F32)]
    return pl.pallas_call(
        kernel,
        in_specs=[pl.BlockSpec(memory_space=pltpu.SMEM)] + [vmem] * len(operands),
        out_specs=[vmem] * len(shapes),
        out_shape=shapes,
        scratch_shapes=[pltpu.VMEM((width, cols), F32)],
        compiler_params=params(),
        cost_estimate=pl.CostEstimate(flops=2 * flops, bytes_accessed=14 << 20, transcendentals=0),
        name=name,
    )(offs, *operands)


def bucket_kernel(heads, near_ref, far_ref, out_ref):
    lanes = near_ref.shape[2]
    blocks = (lanes // LANES + 1) // 2
    begin = (blocks - 2) * LANES
    end = begin + 3 * LANES
    rows = lax.broadcasted_iota(jnp.int32, (LANES, 3 * LANES), 0)
    ids = bucket_of(
        lax.broadcasted_iota(jnp.int32, (LANES, 3 * LANES), 1) - LANES - rows
    )
    lane = lax.broadcasted_iota(jnp.int32, (1, LANES), 1)
    out = jnp.zeros((1, LANES), F32)
    for h in range(heads):
        strip = near_ref[h] + far_ref[h]
        left = jnp.sum(jnp.sum(strip[:, :begin], axis=0, keepdims=True), axis=1, keepdims=True)
        right = jnp.sum(jnp.sum(strip[:, end:], axis=0, keepdims=True), axis=1, keepdims=True)
        out = out + jnp.where(lane == h * 32 + 15, left, 0.0)
        out = out + jnp.where(lane == h * 32 + 31, right, 0.0)
        middle = strip[:, begin:end]
        for b in range(32):
            if b == 16:
                continue
            part = jnp.sum(jnp.where(ids == b, middle, 0.0), axis=0, keepdims=True)
            part = jnp.sum(part, axis=1, keepdims=True)
            out = out + jnp.where(lane == h * 32 + b, part, 0.0)
    out_ref[...] = jnp.broadcast_to(out, (8, LANES))


def norm_kernel(wide, narrow, lists, gain_at, *refs):
    at = 0
    groups = []
    for count in lists:
        groups.append(refs[at : at + count])
        at += count
    bucket_ref = refs[at]
    outs = refs[at + 1 : at + 1 + len(lists)]
    stat_ref, gain_ref, table_ref, block, inbox, padded, send_sems, recv_sems = refs[
        at + 1 + len(lists) :
    ]
    total = wide * narrow
    w = lax.axis_index("wide")
    n = lax.axis_index("narrow")
    me = w * narrow + n
    barrier = pltpu.get_barrier_semaphore()

    @pl.loop(1, total)
    def _(k):
        peer = (me + k) % total
        pl.semaphore_signal(
            barrier, inc=1, device_id=(peer // narrow, peer % narrow), device_id_type=MESH
        )

    squares = jnp.zeros((8, LANES), F32)
    for which, (group, out) in enumerate(zip(groups, outs)):
        value = group[0][...].astype(F32)
        for more in group[1:]:
            value = value + more[...].astype(F32)
        out[...] = value
        squared = value * value
        if which == 0:
            lane = lax.broadcasted_iota(jnp.int32, value.shape, 1)
            inside = (lane >= gain_at) & (lane < gain_at + DH)
            squared = jnp.where(inside, 0.0, squared)
        squared = jnp.sum(squared, axis=1, keepdims=True)
        squares = squares + jnp.sum(squared, axis=0, keepdims=True)
    rows = outs[0].shape[0]
    low = gain_at // LANES * LANES
    padded[...] = jnp.zeros_like(padded)
    padded[0:rows] = outs[0][:, low : low + LANES]
    turned = padded[...].T
    row = lax.broadcasted_iota(jnp.int32, (8, LANES), 0)
    here = gain_at - low
    mine = jnp.where(row == 0, squares, 0.0)
    mine = jnp.where(row == 1, turned[here : here + 1], mine)
    mine = jnp.where(row == 2, turned[here + 1 : here + 2], mine)
    mine = jnp.where(row == 3, bucket_ref[...], mine)
    block[...] = mine
    inbox[me] = mine
    pl.semaphore_wait(barrier, total - 1)

    @pl.loop(1, total)
    def _(k):
        peer = (me + k) % total
        pltpu.make_async_remote_copy(
            src_ref=block,
            dst_ref=inbox.at[me],
            send_sem=send_sems.at[k],
            recv_sem=recv_sems.at[total - k],
            device_id=(peer // narrow, peer % narrow),
            device_id_type=MESH,
        ).start()

    @pl.loop(1, total)
    def _(k):
        peer = (me + k) % total
        copy = pltpu.make_async_remote_copy(
            src_ref=block,
            dst_ref=inbox.at[peer],
            send_sem=send_sems.at[k],
            recv_sem=recv_sems.at[k],
            device_id=(peer // narrow, peer % narrow),
            device_id_type=MESH,
        )
        copy.wait_send()
        copy.wait_recv()

    columns = [jnp.zeros((8, LANES), F32) for _ in range(narrow)]
    gain_square = jnp.zeros((8, LANES), F32)
    square_total = jnp.zeros((8, LANES), F32)
    for a in range(wide):
        gains = jnp.zeros((8, LANES), F32)
        for b in range(narrow):
            got = inbox[a * narrow + b]
            gains = gains + got
            columns[b] = columns[b] + got
        square_total = square_total + gains
        gain_square = gain_square + gains * gains
    own = inbox[w * narrow]
    for b in range(1, narrow):
        own = own + inbox[w * narrow + b]
    gain_ref[...] = own
    pick = (row == 1) | (row == 2)
    gain_square = jnp.where(pick, gain_square, 0.0)
    norm_square = square_total[0:1, 0:1] + jnp.sum(
        jnp.sum(gain_square, axis=0, keepdims=True), axis=1, keepdims=True
    )
    heads = LANES // 32 - 1
    lane = lax.broadcasted_iota(jnp.int32, (32, LANES), 1)
    depth = lax.broadcasted_iota(jnp.int32, (32, LANES), 0)
    table = jnp.zeros((32, LANES), F32)
    for b in range(narrow):
        line = columns[b][3:4]
        norm_square = norm_square + jnp.sum(line * line, axis=1, keepdims=True)
        for h in range(heads):
            column = jnp.sum(
                jnp.where(lane == depth + 32 * h, line, 0.0), axis=1, keepdims=True
            )
            table = jnp.where(lane == b * heads + h, column, table)
    table_ref[...] = table
    global_norm = jnp.sqrt(norm_square)
    factor = jnp.minimum(1.0, clip_limit / (global_norm + 1e-06))
    stat_ref[...] = jnp.where(row == 0, global_norm, factor)


def norm_call(wide, narrow, groups, bucket, gain_at):
    vmem = pl.BlockSpec(memory_space=pltpu.VMEM)
    lists = tuple(len(group) for group in groups)
    total = wide * narrow
    operands = [piece for group in groups for piece in group] + [bucket]
    return pl.pallas_call(
        functools.partial(norm_kernel, wide, narrow, lists, gain_at),
        in_specs=[vmem] * len(operands),
        out_specs=[vmem] * (len(lists) + 3),
        out_shape=[jax.ShapeDtypeStruct(group[0].shape, F32) for group in groups]
        + [
            jax.ShapeDtypeStruct((8, LANES), F32),
            jax.ShapeDtypeStruct((8, LANES), F32),
            jax.ShapeDtypeStruct((32, LANES), F32),
        ],
        scratch_shapes=[
            pltpu.VMEM((8, LANES), F32),
            pltpu.VMEM((total, 8, LANES), F32),
            pltpu.VMEM((LANES, LANES), F32),
            pltpu.SemaphoreType.DMA((total,)),
            pltpu.SemaphoreType.DMA((total,)),
        ],
        compiler_params=params(collective_id=0, has_side_effects=True),
        cost_estimate=pl.CostEstimate(flops=1 << 20, bytes_accessed=4 << 20, transcendentals=0),
        name="norm",
    )(*operands)


def adam_kernel(heads, hidden_cols, parts, att_ref, feed_ref, gain_ref, table_ref, stat_ref, *refs):
    weights, firsts, seconds = refs[:6], refs[6:12], refs[12:18]
    outs = refs[18:36]
    o_pad, s_pad = refs[36:]
    factor = stat_ref[1:2, 0:1]
    head_cols = heads * DH
    rows = att_ref.shape[0]
    gain_at = 3 * head_cols

    def update(which, index, gradient):
        results = adam_update(
            weights[which][index],
            firsts[which][index],
            seconds[which][index],
            factor * gradient,
            step_rates[which],
            decay_rates[which],
        )
        for at in range(3):
            outs[6 * at + which][index] = results[at]

    for i in range(3):
        update(0, i, att_ref[:, i * head_cols : (i + 1) * head_cols])
    part = hidden_cols // parts
    for j in range(parts):
        span = slice(j * part, (j + 1) * part)
        for i in range(2):
            begin = (3 * j + i) * part if parts > 1 else i * part
            update(2, (i, slice(None), span), feed_ref[:, begin : begin + part])
    o_pad[...] = jnp.zeros_like(o_pad)
    s_pad[...] = jnp.zeros_like(s_pad)
    o_pad[0:rows] = att_ref[:, gain_at + DH :]
    for j in range(parts):
        begin = (3 * j + 2) * part
        s_pad[0:rows, j * part : (j + 1) * part] = feed_ref[:, begin : begin + part]
    update(1, slice(None), o_pad[...].T[:head_cols, :rows])
    update(3, slice(None), s_pad[...].T[:, :rows])
    columns = weights[4].shape[1]
    update(4, slice(None), table_ref[:, :columns])
    update(5, slice(None), gain_ref[1:3, :rows])


def adam_call(
    att, feed_grad, gain, table, stat, params_in, firsts, seconds, heads, hidden_cols, direct=False
):
    vmem = pl.BlockSpec(memory_space=pltpu.VMEM)
    operands = [att, feed_grad, gain, table, stat, *params_in, *firsts, *seconds]
    pad_cols = att.shape[1] - (3 * heads * DH + DH)
    return pl.pallas_call(
        functools.partial(adam_kernel, heads, hidden_cols, 2 if direct else 1),
        in_specs=[vmem] * len(operands),
        out_specs=[vmem] * 18,
        out_shape=[jax.ShapeDtypeStruct(a.shape, F32) for a in params_in] * 3,
        scratch_shapes=[
            pltpu.VMEM((LANES, pad_cols), F32),
            pltpu.VMEM((LANES, hidden_cols), F32),
        ],
        compiler_params=params(),
        cost_estimate=pl.CostEstimate(flops=4 << 20, bytes_accessed=8 << 20, transcendentals=0),
        name="adam",
    )(*operands)


def place_kernel(offs_ref, *refs):
    step = pl.program_id(0)
    for at, piece in enumerate(refs[:-1]):

        @pl.when(step == at)
        def _(piece=piece):
            refs[-1][...] = piece[...]


def place(pieces, offs, rows):
    half, width = pieces[0].shape
    count = len(pieces)
    return pl.pallas_call(
        place_kernel,
        grid_spec=pltpu.PrefetchScalarGridSpec(
            num_scalar_prefetch=1,
            grid=(count,),
            in_specs=[pl.BlockSpec((half, width), lambda i, *_: (0, 0))] * count,
            out_specs=pl.BlockSpec((half, width), lambda i, offs: (offs[i] // half, 0)),
        ),
        out_shape=jax.ShapeDtypeStruct((rows, width), pieces[0].dtype),
        compiler_params=params(),
        cost_estimate=pl.CostEstimate(
            flops=0, bytes_accessed=4 * rows * width, transcendentals=0
        ),
        name="place",
    )(offs, *pieces)


def bias_strip(bucket_bias, n, heads, length):
    table = lax.dynamic_slice_in_dim(bucket_bias, n * heads, heads, 1).T
    blocks = length // LANES
    near_r = (
        jnp.arange(3 * LANES, dtype=jnp.int32)[None, :]
        - LANES
        - jnp.arange(LANES, dtype=jnp.int32)[:, None]
    )
    near_ids = bucket_of(near_r)
    near = sum(
        jnp.where(near_ids == b, table[:, b][:, None, None], 0.0) for b in range(32) if b != 16
    )
    far_shape = (heads, LANES, (blocks - 2) * LANES)
    return jnp.concatenate(
        [
            jnp.broadcast_to(table[:, 15][:, None, None], far_shape),
            near,
            jnp.broadcast_to(table[:, 31][:, None, None], far_shape),
        ],
        axis=2,
    )


def general_body(wide, narrow, *arguments):
    (
        block_input,
        cotangent,
        lengths,
        project_weight,
        output_weight,
        expand_weight,
        shrink_weight,
        bucket_bias,
        norm_gains,
    ) = arguments[:9]
    firsts = arguments[9:15]
    seconds = arguments[15:21]
    tokens, width = block_input.shape
    buffers = lengths.shape[0]
    length = tokens // buffers
    rows = norm_gains.shape[1]
    head_cols = project_weight.shape[2]
    heads = head_cols // DH
    hidden_cols = expand_weight.shape[2]
    w = lax.axis_index("wide")
    n = lax.axis_index("narrow")
    core = n % 2

    def swap(value, wide_mask, narrow_mask):
        pairs = [
            (a * narrow + b, (a ^ wide_mask) * narrow + (b ^ narrow_mask))
            for a in range(wide)
            for b in range(narrow)
        ]
        return lax.ppermute(value, ("wide", "narrow"), pairs)

    def gather(piece):
        return [lax.all_gather(piece, "wide", axis=0, tiled=True)]

    def reduce_wide(outs):
        return [lax.psum_scatter(outs[0], "wide", scatter_dimension=0, tiled=True)]

    offs = jnp.zeros((1,), jnp.int32)
    order = jnp.stack([1 - core, core, n // 2])

    p_piece = jnp.concatenate(
        [
            project_weight[0],
            project_weight[1],
            project_weight[2],
            norm_gains.T,
            jnp.zeros((rows, DH - 2), F32),
        ],
        axis=1,
    ).astype(BF16)
    p_pieces = gather(p_piece)
    o_piece = output_weight.astype(BF16).T
    o_pair = jnp.concatenate([o_piece, swap(o_piece, 0, 2)], axis=1)
    oa_pieces = gather(o_pair)
    ob_pieces = [swap(piece, 0, 1) for piece in oa_pieces]
    e_pieces = gather(
        jnp.concatenate([expand_weight[0], expand_weight[1]], axis=1).astype(BF16)
    )
    s_pieces = gather(shrink_weight.astype(BF16).T)

    ends = jnp.cumsum(lengths, axis=1)
    strip = bias_strip(bucket_bias, n, heads, length)

    normed_one, qkv, atts, logs, fours = [], [], [], [], []
    for b in range(buffers):
        normed, rows_b, att, log, gains = attend(
            b, ends, offs, block_input, strip, p_pieces, length, heads
        )
        normed_one.append(normed)
        qkv.append(rows_b)
        atts.append(att)
        logs.append(log)
        across = swap(att, 0, 2)
        fours.append((att, across, swap(att, 0, 1), swap(across, 0, 1)))

    def core_sum(kept, sent):
        return (kept.astype(F32) + swap(sent, 0, 1).astype(F32)).astype(BF16)

    normed_two, hiddens, gates, middles, ff_sums, dn_sums, sums_two = [], [], [], [], [], [], []
    for b in range(buffers):
        normed, hidden, gate, ff_send, ff_keep, dn_send, dn_keep, middle, sums = feed(
            b,
            order,
            offs,
            fours[b],
            block_input,
            cotangent,
            gains,
            (oa_pieces, ob_pieces, e_pieces, s_pieces),
            length,
            hidden_cols,
        )
        normed_two.append(normed)
        hiddens.append(hidden)
        gates.append(gate)
        middles.append(middle)
        sums_two.append(sums)
        dn_sums.append(core_sum(dn_keep, dn_send))
        ff_sums.append(core_sum(ff_keep, ff_send))

    d_middles, lows = [], []
    for b in range(buffers):
        d_middle, low = half_call(
            middle_kernel,
            "middle",
            b,
            order,
            [dn_sums[b], swap(dn_sums[b], 0, 2), middles[b], cotangent],
            (3,),
            (F32, BF16),
            gains,
        )
        d_middles.append(d_middle)
        lows.append((low, swap(low, 0, 1)))

    count = 1
    feed_outs = grad_call(
        functools.partial(feed_grad_kernel, count, hidden_cols),
        "feed_grad",
        offs,
        [*normed_two, *gates, *hiddens, cotangent],
        width,
        3 * hidden_cols,
        count,
        rows,
        2 * tokens * width * 3 * hidden_cols,
    )
    feed_group = reduce_wide(feed_outs)

    low_full, dqkv, dn_one, sums_one, strips = [], [], [], [], []
    for b in range(buffers):
        low, grads, dn_send, dn_keep, sums, dstrip = back(
            b,
            ends,
            offs,
            order,
            lows[b][0],
            lows[b][1],
            qkv[b],
            logs[b],
            strip,
            block_input,
            oa_pieces,
            p_pieces,
            heads,
        )
        low_full.append(low)
        dqkv.append(grads)
        sums_one.append(sums)
        strips.append(dstrip)
        dn_one.append(core_sum(dn_keep, dn_send))

    gain_at = 3 * head_cols
    att_outs = grad_call(
        functools.partial(attend_grad_kernel, count, heads),
        "attend_grad",
        offs,
        [*normed_one, *dqkv, *low_full, *atts, jnp.stack(sums_one + sums_two)],
        width,
        gain_at + DH + head_cols,
        count,
        rows,
        2 * tokens * width * 4 * head_cols,
    )
    att_group = reduce_wide(att_outs)
    vmem = pl.BlockSpec(memory_space=pltpu.VMEM)
    bucket = pl.pallas_call(
        functools.partial(bucket_kernel, heads),
        in_specs=[vmem, vmem],
        out_specs=vmem,
        out_shape=jax.ShapeDtypeStruct((8, LANES), F32),
        compiler_params=params(),
        cost_estimate=pl.CostEstimate(flops=8 << 20, bytes_accessed=4 << 20, transcendentals=0),
        name="bucket",
    )(*strips)

    half_offs = jnp.stack(
        [
            b * length + which * (length // 2)
            for b in range(buffers)
            for which in (core, 1 - core)
        ]
    )
    out_halves, in_halves = [], []
    for b in range(buffers):
        (half,) = half_call(
            output_kernel,
            "output",
            b,
            order,
            [ff_sums[b], swap(ff_sums[b], 0, 2), middles[b]],
            (),
            (BF16,),
        )
        out_halves += [half, swap(half, 0, 1)]
        (half,) = half_call(
            input_kernel,
            "input",
            b,
            order,
            [dn_one[b], swap(dn_one[b], 0, 2), block_input, d_middles[b]],
            (2,),
            (BF16,),
            gains,
        )
        in_halves += [half, swap(half, 0, 1)]
    block_output = place(out_halves, half_offs, tokens)
    input_gradient = place(in_halves, half_offs, tokens)

    att_grad, feed_grad, stat, gain, table_sum = norm_call(
        wide, narrow, [att_group, feed_group], bucket, gain_at
    )
    results = adam_call(
        att_grad,
        feed_grad,
        gain,
        table_sum,
        stat,
        arguments[3:9],
        firsts,
        seconds,
        heads,
        hidden_cols,
    )
    return (block_output, input_gradient, stat[0, 0], *results)


class Place:
    def __init__(self, wide, narrow):
        self.wide, self.narrow = wide, narrow
        self.w = lax.axis_index("wide")
        self.n = lax.axis_index("narrow")
        self.me = self.w * narrow + self.n
        self.z, self.x = self.w // 2, self.w % 2
        self.y, self.core = self.n // 2, self.n % 2
        self.n_far = (self.n + 2) % 4
        self.n_beside = self.n + 1 - 2 * self.core
        self.n_diag = (self.n_beside + 2) % 4
        self.across = (self.w, self.n_far)
        self.beside = (self.w, self.n_beside)
        self.flip = (self.z * 2 + 1 - self.x, self.n)

    def along(self, m):
        return (((self.z + m) % 4) * 2 + self.x, self.n)

    def near_owner(self, m):
        return ((self.z + m) % 4) * 2 + self.x

    def far_owner(self, m):
        return ((self.z + m) % 4) * 2 + 1 - self.x

    def peer(self, k):
        device = (self.me + k) % (self.wide * self.narrow)
        return device, (device // self.narrow, device % self.narrow)


def remote(source, target, send_sem, recv_sem, peer):
    return pltpu.make_async_remote_copy(
        src_ref=source,
        dst_ref=target,
        send_sem=send_sem,
        recv_sem=recv_sem,
        device_id=peer,
        device_id_type=MESH,
    )


class Gather:
    def __init__(self, spot, view, ssem, rsem, flip_first=False):
        self.spot, self.view, self.ssem, self.rsem = spot, view, ssem, rsem
        self.flip_first = flip_first

    def copy(self, owner, slot, peer):
        return remote(
            self.view(owner), self.view(owner), self.ssem.at[slot], self.rsem.at[owner], peer
        )

    def landed(self, owner):
        self.copy(owner, 0, self.spot.flip).wait_recv()

    def start(self, owner, slot, peer):
        self.copy(owner, slot, peer).start()

    def sent(self, owner, slot, peer):
        self.copy(owner, slot, peer).wait_send()

    def fan(self, owner, slot, act):
        z = self.spot.z
        act(owner, slot + 1, self.spot.along(2))
        pl.when(z != 3)(lambda: act(owner, slot, self.spot.along(1)))
        pl.when(z != 0)(lambda: act(owner, slot + 2, self.spot.along(3)))

    def pass_on(self, owner, slot, act):
        z = self.spot.z
        pl.when(z == 2)(lambda: act(owner, slot, self.spot.along(1)))
        pl.when(z == 1)(lambda: act(owner, slot, self.spot.along(3)))

    def begin(self):
        if self.flip_first:
            self.start(self.spot.w, 3, self.spot.flip)
        self.fan(self.spot.w, 0, self.start)
        if not self.flip_first:
            self.start(self.spot.w, 3, self.spot.flip)

    def forward(self):
        if self.flip_first:
            owner = self.spot.far_owner(0)
            self.landed(owner)
            self.fan(owner, 4, self.start)
            return
        owner = self.spot.near_owner(2)
        self.landed(owner)
        self.pass_on(owner, 7, self.start)
        self.start(owner, 5, self.spot.flip)
        early = 1 + 2 * ((3 - self.spot.z) // 3)
        for m in (early, 4 - early):
            owner = self.spot.near_owner(4 - m)
            self.landed(owner)
            self.start(owner, 3 + m, self.spot.flip)

    def middle(self):
        for owner, slot in ((self.spot.near_owner(2), 7), (self.spot.far_owner(2), 8)):
            self.landed(owner)
            self.pass_on(owner, slot, self.start)

    def finish(self):
        if self.flip_first:
            for m in (1, 3):
                self.landed(self.spot.near_owner(m))
                self.landed(self.spot.far_owner(m))
        else:
            for m in range(4):
                self.landed(self.spot.far_owner(m))

    def drain(self):
        self.sent(self.spot.w, 3, self.spot.flip)
        self.fan(self.spot.w, 0, self.sent)
        self.pass_on(self.spot.near_owner(2), 7, self.sent)
        if self.flip_first:
            self.fan(self.spot.far_owner(0), 4, self.sent)
            self.pass_on(self.spot.far_owner(2), 8, self.sent)
        else:
            for m in (1, 2, 3):
                self.sent(self.spot.near_owner(4 - m), 3 + m, self.spot.flip)


class Reduce:
    def __init__(self, spot, even, odd, flipped, mixed, landed, sems_s, sems_r):
        self.spot, self.even, self.odd = spot, even, odd
        self.flipped, self.mixed, self.landed = flipped, mixed, landed
        self.sems_s, self.sems_r = sems_s, sems_r

    def over(self, m):
        return remote(
            self.odd(m), self.flipped(m), self.sems_s.at[m], self.sems_r.at[m], self.spot.flip
        )

    def along(self, m):
        return remote(
            self.mixed(m - 1),
            self.landed(m - 1),
            self.sems_s.at[3 + m],
            self.sems_r.at[3 + m],
            self.spot.along(m),
        )

    def begin(self):
        for m in (2, 1, 3, 0):
            self.over(m).start()

    def relay(self, *ms):
        for m in ms:
            self.over(m).wait_recv()
            self.mixed(m - 1)[...] = (
                self.even(m).astype(F32) + self.flipped(m)[...].astype(F32)
            ).astype(BF16)
            self.along(m).start()

    def result(self):
        self.over(0).wait_recv()
        value = self.even(0).astype(F32) + self.flipped(0)[...].astype(F32)
        for m in (1, 2, 3):
            self.along(m).wait_recv()
            value = value + self.landed(m - 1)[...].astype(F32)
        return value

    def drain(self):
        for m in range(4):
            self.over(m).wait_send()
        for m in (1, 2, 3):
            self.along(m).wait_send()


def segments_of(index, lengths_ref, buffer, slots):
    end = lengths_ref[buffer, 0]
    total = (index >= end).astype(jnp.int32)
    for slot in range(1, slots):
        end = end + lengths_ref[buffer, slot]
        total = total + (index >= end).astype(jnp.int32)
    return total


def layer_kernel(dims, *refs):
    buffers, slots, heads, hidden_cols, wide, narrow = dims
    (
        lengths_ref,
        bias_ref,
        x_hbm,
        cot_hbm,
        pw_ref,
        ow_ref,
        ew_ref,
        sw_ref,
        gn_ref,
        out_ref,
        in_ref,
        p_grad,
        o_grad,
        feed_grad,
        stat_ref,
        gain_ref,
        table_ref,
        x_ref,
        cot_ref,
        strip,
        dstrip,
        pbuf,
        obuf,
        fbuf,
        att_ref,
        qkv_ref,
        log_ref,
        low_ref,
        middle_ref,
        hid,
        dg,
        total,
        opad,
        gpad,
        feed_flip,
        feed_mix,
        feed_land,
        o_even,
        o_odd,
        o_flip,
        o_mix,
        o_land,
        p_odd,
        p_flip,
        p_mix,
        p_land,
        ff_out,
        ff_in,
        ff_sum,
        dn_out,
        dn_in,
        dn_sum,
        dn_far,
        ws,
        kt,
        vt,
        qt,
        gt,
        dkt,
        dvt,
        gain_two_sum,
        block,
        inbox,
        gather_s,
        gather_r,
        lone_s,
        lone_r,
        red_s,
        red_r,
        norm_s,
        norm_r,
        credit,
        load,
    ) = refs
    spot = Place(wide, narrow)
    core = spot.core
    devices = wide * narrow
    tokens, width = x_ref.shape
    length = tokens // buffers
    half = length // 2
    head_cols = heads * DH
    qkv_cols = 3 * head_cols
    part = hidden_cols // 2
    chunk = 3 * part
    blocks = length // LANES
    owned = gn_ref.shape[1]
    normed_one, normed_two = in_ref, out_ref
    loads = [
        pltpu.make_async_copy(x_hbm, x_ref, load.at[0]),
        pltpu.make_async_copy(cot_hbm, cot_ref, load.at[1]),
    ]
    for copy in loads:
        copy.start()
    barrier = pltpu.get_barrier_semaphore()

    @pl.loop(1, devices)
    def _(k):
        pl.semaphore_signal(barrier, inc=1, device_id=spot.peer(k)[1], device_id_type=MESH)

    def at_rows(owner):
        return pl.ds(pl.multiple_of(owner * owned, 16), owned)

    def lone(view_from, view_to, slot, peer):
        return remote(view_from, view_to, lone_s.at[slot], lone_r.at[slot], peer)

    mine = at_rows(spot.w)
    gpad[...] = jnp.zeros_like(gpad)
    gpad[0:2, 0:owned] = gn_ref[...]
    pbuf[mine] = jnp.concatenate(
        [pw_ref[0], pw_ref[1], pw_ref[2], gpad[...].T[:owned, :DH]], axis=1
    ).astype(BF16)
    pl.semaphore_wait(barrier, devices - 1)
    split = 3 * LANES
    projections = [
        Gather(
            spot,
            lambda v, span=span: pbuf.at[at_rows(v), span],
            gather_s.at[at],
            gather_r.at[at],
        )
        for at, span in enumerate((slice(0, split), slice(split, qkv_cols + DH)))
    ]
    for group in projections:
        group.begin()
    opad[...] = jnp.zeros_like(opad)
    opad[0:head_cols, 0:owned] = ow_ref[...]
    obuf[spot.n, mine] = opad[...].T[:owned, :head_cols].astype(BF16)
    o_views = [
        lambda v: obuf.at[spot.n, at_rows(v)],
        lambda v: obuf.at[spot.n_far, at_rows(v)],
    ]
    outs_gather = [
        Gather(spot, view, gather_s.at[2 + at], gather_r.at[2 + at])
        for at, view in enumerate(o_views)
    ]
    lone(o_views[0](spot.w), o_views[0](spot.w), 0, spot.across).start()
    for j in range(2):
        span = slice(j * part, (j + 1) * part)
        fbuf[mine, j * chunk : j * chunk + part] = ew_ref[0, :, span].astype(BF16)
        fbuf[mine, j * chunk + part : j * chunk + 2 * part] = ew_ref[1, :, span].astype(BF16)
        fbuf[mine, j * chunk + 2 * part : (j + 1) * chunk] = sw_ref[:, span].astype(BF16)
    feed_cuts = (0, 256, 512, 768, 1024, 1280, 1536)
    feeds_gather = [
        Gather(
            spot,
            lambda v, at=at: fbuf.at[at_rows(v), feed_cuts[at] : feed_cuts[at + 1]],
            gather_s.at[4 + at],
            gather_r.at[4 + at],
            flip_first=at in (5,),
        )
        for at in range(len(feed_cuts) - 1)
    ]

    near_at = (blocks - 2) * LANES
    near_end = near_at + 3 * LANES
    near_ids = bucket_of(
        lax.broadcasted_iota(jnp.int32, (LANES, 3 * LANES), 1)
        - LANES
        - lax.broadcasted_iota(jnp.int32, (LANES, 3 * LANES), 0)
    )
    for h in range(heads):
        head = spot.n * heads + h
        near = jnp.zeros((LANES, 3 * LANES), F32)
        for b in range(32):
            if b != 16:
                near = jnp.where(near_ids == b, bias_ref[head, b], near)
        strip[h, :, near_at:near_end] = near
        strip[h, :, :near_at] = jnp.full((LANES, near_at), bias_ref[head, 15])
        strip[h, :, near_end:] = jnp.full((LANES, near_at), bias_ref[head, 31])
    lone(o_views[1](spot.w), o_views[1](spot.w), 0, spot.across).wait_recv()
    for group in outs_gather + feeds_gather:
        group.begin()
    dstrip[...] = jnp.zeros_like(dstrip)
    gain_two_sum[...] = jnp.zeros_like(gain_two_sum)

    projections[0].forward()
    projections[1].forward()
    for group in projections:
        group.finish()
    loads[0].wait()

    gains = pbuf[:, 4 * LANES :].astype(F32).T[qkv_cols - 4 * LANES : qkv_cols - 4 * LANES + 8]
    gain_one, gain_two = gains[0:1], gains[1:2]

    def relay_feeds(*ats):
        for at in ats:
            feeds_gather[at].forward()

    def relay_outs():
        for group in outs_gather:
            group.forward()

    def outs_beside():
        for group in outs_gather:
            group.finish()
        lone(obuf.at[spot.n], obuf.at[spot.n], 1, spot.beside).start()
        lone(obuf.at[spot.n_far], obuf.at[spot.n_far], 2, spot.beside).start()

    def att_view(which, b):
        return att_ref.at[which, b * length : (b + 1) * length]

    def att_copy(which, b, slot, peer):
        return lone(att_view(which, b), att_view(which, b), 3 + 3 * b + slot, peer)

    def att_send(b):
        att_copy(spot.n, b, 0, spot.across).start()
        att_copy(spot.n, b, 1, spot.beside).start()

    def att_relay(b):
        att_copy(spot.n_far, b, 0, spot.across).wait_recv()
        att_copy(spot.n_far, b, 2, spot.beside).start()

    step = 256
    qkv_events = ({}, {0: feeds_gather[0].forward})
    att_events = (
        {1: relay_outs, 2: lambda: relay_feeds(5)},
        {0: lambda: (outs_beside(), relay_feeds(1))[1], 1: feeds_gather[2].forward, 2: feeds_gather[3].forward},
    )

    def fire(events, at):
        for when, what in events.items():
            pl.when(at == when)(what)

    for b in range(buffers):
        base = b * length

        @pl.loop(0, length // step)
        def _(at, b=b, base=base):
            fire(qkv_events[b], at)
            begin = pl.multiple_of(at * step, step)
            here = pl.ds(begin, step)
            span = pl.ds(pl.multiple_of(base + begin, step), step)
            values = x_ref[span].astype(F32)
            normed = (values * rms_scale(values) * gain_one).astype(BF16)
            normed_one[span] = normed
            qkv = mm(normed, pbuf[...]).astype(BF16)
            qkv_ref[span] = qkv[:, :qkv_cols]
            for h in range(heads):
                k_at = head_cols + h * DH
                v_at = 2 * head_cols + h * DH
                kt[h, :, here] = qkv[:, k_at : k_at + DH].T
                ws[h, here] = qkv[:, v_at : v_at + DH]

        seg_keys = segments_of(
            lax.broadcasted_iota(jnp.int32, (1, length), 1), lengths_ref, b, slots
        )

        @pl.loop(0, blocks // 2)
        def _(at, b=b, base=base, seg_keys=seg_keys):
            fire(att_events[b], at)
            begin = pl.multiple_of(at * 2 * LANES, 2 * LANES)
            span = pl.ds(pl.multiple_of(base + begin, 2 * LANES), 2 * LANES)
            windows = [
                pl.ds(pl.multiple_of((blocks - 1 - r - 2 * at) * LANES, LANES), length)
                for r in range(2)
            ]
            seg_rows = segments_of(
                lax.broadcasted_iota(jnp.int32, (2 * LANES, 1), 0) + begin, lengths_ref, b, slots
            )
            same = seg_rows == seg_keys
            lane = lax.broadcasted_iota(jnp.int32, (2 * LANES, LANES), 1)
            logs = jnp.zeros((2 * LANES, LANES), F32)
            queries = qkv_ref[span, :head_cols]
            outs = []
            for h in range(heads):
                scores = mm(queries[:, h * DH : (h + 1) * DH], kt[h]) + jnp.concatenate(
                    [strip[h, :, window] for window in windows], axis=0
                )
                scores = jnp.where(same, scores, masked_score)
                row_max = jnp.max(scores, axis=1, keepdims=True)
                raised = jnp.exp(scores - row_max)
                sums = jnp.sum(raised, axis=1, keepdims=True)
                probs = (raised * (1.0 / sums)).astype(BF16)
                outs.append(mm(probs, ws[h]).astype(BF16))
                logs = jnp.where(lane == h, row_max + jnp.log(sums), logs)
            log_ref[span] = logs
            att_ref[spot.n, span] = jnp.concatenate(outs, axis=1)

        att_send(b)
        if b == 1:
            att_relay(0)

    k0 = 0.7978845608028654
    k1 = 0.044715

    def half_rows(b, which):
        return pl.ds(pl.multiple_of(b * length + which * half, LANES), half)

    def ff_core(b):
        return lone(ff_out.at[b], ff_in.at[b], 9 + b, spot.beside)

    def ff_across(b):
        return lone(ff_sum.at[b], ff_in.at[b], 11 + b, spot.across)

    def dn_core(b, turn):
        return lone(dn_out.at[b], dn_in.at[b], 13 + 2 * turn + b, spot.beside)

    def dn_across(b, turn):
        return lone(dn_sum.at[b], dn_far.at[b], 17 + 2 * turn + b, spot.across)

    def low_core(b, which):
        view = low_ref.at[half_rows(b, which)]
        return lone(view, view, 21 + b, spot.beside)

    def out_core(b, which):
        view = out_ref.at[half_rows(b, which)]
        return lone(view, view, 23 + b, spot.beside)

    def in_core(b, which):
        view = in_ref.at[half_rows(b, which)]
        return lone(view, view, 25 + b, spot.beside)

    def outs_ready():
        loads[1].wait()
        lone(obuf.at[spot.n_beside], obuf.at[spot.n_beside], 1, spot.beside).wait_recv()
        lone(obuf.at[spot.n_diag], obuf.at[spot.n_diag], 2, spot.beside).wait_recv()

    def first_feed():
        feeds_gather[4].forward()
        feeds_gather[5].middle()
        feeds_gather[0].finish()
        feeds_gather[1].finish()
        feeds_gather[2].finish()

    def last_feed():
        att_relay(1)
        feeds_gather[3].finish()
        feeds_gather[4].finish()
        feeds_gather[5].finish()

    def half_of(b, keep):
        return half_rows(b, (1 - core) * (1 - keep) + core * keep)

    def hidden_part(j, rows, normed_rows):
        at = j * chunk
        both = mm(normed_rows, fbuf[:, at : at + 2 * part])
        gate, up = both[:, :part], both[:, part:]
        square = gate * gate
        tanh = jnp.tanh(k0 * (gate + k1 * (square * gate)))
        lift = 0.5 * (1.0 + tanh)
        active = gate * lift
        slope = lift + (0.5 * gate) * (1.0 - tanh * tanh) * (k0 + (3.0 * k0 * k1) * square)
        d_hidden = mm(cot_ref[rows], fbuf[:, at + 2 * part : at + 3 * part])
        hid[rows, j * part : (j + 1) * part] = (active * up).astype(BF16)
        dg[rows, 2 * j * part : (2 * j + 1) * part] = (d_hidden * up * slope).astype(BF16)
        dg[rows, (2 * j + 1) * part : (2 * j + 2) * part] = (d_hidden * active).astype(BF16)

    @pl.loop(0, buffers)
    def _(b):
        def att_ready():
            span = pl.ds(pl.multiple_of(b * length, LANES), length)
            for slot, which in ((4, spot.n_beside), (5, spot.n_diag)):
                view = att_ref.at[which, span]
                lone(view, view, slot + 3 * b, spot.beside).wait_recv()

        att_ready()

        @pl.loop(0, 2)
        def _(keep):
            pl.when((b == 0) & (keep == 0))(outs_ready)
            rows = half_of(b, keep)
            attention = mm(att_ref[0, rows], obuf[0], NT)
            for a in range(1, 4):
                attention = attention + mm(att_ref[a, rows], obuf[a], NT)
            middle = x_ref[rows].astype(F32) + attention
            normed_rows = (middle * rms_scale(middle) * gain_two).astype(BF16)
            normed_two[rows] = normed_rows

            @pl.when(keep == 1)
            def _():
                middle_ref[b] = middle

            pl.when((b == 0) & (keep == 0))(first_feed)
            hidden_part(0, rows, normed_two[rows])

        pl.when(b == 0)(last_feed)

        @pl.loop(0, 2)
        def _(keep):
            rows = half_of(b, keep)
            normed_rows = normed_two[rows]
            hidden_part(1, rows, normed_rows)
            dn = mm(dg[rows, : 2 * part], fbuf[:, : 2 * part], NT) + mm(
                dg[rows, 2 * part :], fbuf[:, chunk : chunk + 2 * part], NT
            )
            gain_two_sum[...] = gain_two_sum[...] + fold_rows(dn * normed_rows.astype(F32))
            dn = dn.astype(BF16)

            @pl.when(keep == 0)
            def _():
                dn_out[b] = dn
                dn_core(b, 0).start()

            ff = (
                mm(hid[rows, :part], fbuf[:, 2 * part : chunk], NT)
                + mm(hid[rows, part:], fbuf[:, chunk + 2 * part :], NT)
            ).astype(BF16)

            @pl.when(keep == 0)
            def _():
                ff_out[b] = ff
                ff_core(b).start()

            @pl.when(keep == 1)
            def _():
                ff_core(b).wait_recv()
                ff_sum[b] = (ff.astype(F32) + ff_in[b].astype(F32)).astype(BF16)
                dn_core(b, 0).wait_recv()
                dn_sum[b] = (dn.astype(F32) + dn_in[b].astype(F32)).astype(BF16)
                dn_across(b, 0).start()

    def own_block(b, i):
        span = pl.ds(pl.multiple_of(i * LANES, LANES), LANES)
        here = pl.ds(pl.multiple_of(b * length + core * half + i * LANES, LANES), LANES)
        return span, here

    def finish_middle(b):
        dn_across(b, 0).wait_recv()

        @pl.loop(0, half // LANES)
        def _(i):
            span, here = own_block(b, i)
            upstream = dn_sum[b, span].astype(F32) + dn_far[b, span].astype(F32)
            middle = middle_ref[b, span]
            d_middle = cot_ref[here].astype(F32) + norm_back(
                middle, rms_scale(middle), gain_two, upstream
            )
            low_ref[here] = d_middle.astype(BF16)

        pl.semaphore_signal(credit.at[b], inc=1, device_id=spot.across, device_id_type=MESH)
        low_core(b, core).start()

    for group in feeds_gather:
        group.drain()
    for b in range(buffers):
        att_copy(spot.n_far, b, 2, spot.beside).wait_send()
    feed_reds = []
    for j in range(2):
        for begin in range(0, width, step):
            cols = slice(begin, begin + step)
            total[cols, : 2 * part] = mm(
                normed_two[:, cols], dg[:, 2 * j * part : (2 * j + 2) * part], TN
            )
            total[cols, 2 * part :] = mm(cot_ref[:, cols], hid[:, j * part : (j + 1) * part], TN)
        span = slice(j * chunk, (j + 1) * chunk)
        for m in range(4):
            even = total[pl.ds(pl.multiple_of(spot.near_owner(m) * owned, 8), owned)]
            odd = total[pl.ds(pl.multiple_of(spot.far_owner(m) * owned, 8), owned)]
            fbuf[m * owned : (m + 1) * owned, span] = even.astype(BF16)
            fbuf[(4 + m) * owned : (5 + m) * owned, span] = odd.astype(BF16)
        red = Reduce(
            spot,
            lambda m, span=span: fbuf[m * owned : (m + 1) * owned, span],
            lambda m, span=span: fbuf.at[(4 + m) * owned : (5 + m) * owned, span],
            lambda m, span=span: feed_flip.at[m, :, span],
            lambda m, span=span: feed_mix.at[m, :, span],
            lambda m, span=span: feed_land.at[m, :, span],
            red_s.at[j],
            red_r.at[j],
        )
        red.begin()
        feed_reds.append(red)
    finish_middle(0)
    feed_reds[0].relay(2, 1)

    out_red = Reduce(
        spot,
        lambda m: o_even[m],
        lambda m: o_odd.at[m],
        lambda m: o_flip.at[m],
        lambda m: o_mix.at[m],
        lambda m: o_land.at[m],
        red_s.at[2],
        red_r.at[2],
    )

    def out_weight_grad():
        for begin in range(0, width, step):
            cols = slice(begin, begin + step)
            total[cols, :head_cols] = mm(low_ref[:, cols], att_ref[spot.n], TN)
        for m in range(4):
            even = total[pl.ds(pl.multiple_of(spot.near_owner(m) * owned, 8), owned), :head_cols]
            odd = total[pl.ds(pl.multiple_of(spot.far_owner(m) * owned, 8), owned), :head_cols]
            o_even[m] = even
            o_odd[m] = odd.astype(BF16)
        out_red.begin()

    gain_sums = jnp.zeros((8, width), F32)
    def second_middle():
        finish_middle(1)
        ff_across(1).start()

    back_events = (
        {
            0: lambda: feed_reds[0].relay(3),
            2: lambda: ff_across(0).start(),
            3: lambda: feed_reds[1].relay(2),
            5: lambda: (feed_reds[1].relay(1), second_middle())[1],
        },
        {0: lambda: feed_reds[1].relay(3), 3: lambda: out_red.relay(2, 1), 4: lambda: out_red.relay(3)},
    )
    for b in range(buffers):
        base = b * length
        rows = slice(base, base + length)
        low_core(b, 1 - core).wait_recv()
        if b == 1:
            out_weight_grad()
        grads = mm(low_ref[rows], obuf[spot.n]).astype(BF16)
        att_ref[spot.n_far, :length] = grads
        for h in range(heads):
            keys = qkv_ref[rows, head_cols + h * DH : head_cols + (h + 1) * DH]
            values = qkv_ref[rows, 2 * head_cols + h * DH : 2 * head_cols + (h + 1) * DH]
            ws[h] = keys
            kt[h] = keys.T
            vt[h] = values.T
            qt[h] = qkv_ref[rows, h * DH : (h + 1) * DH].T
            gt[h] = grads[:, h * DH : (h + 1) * DH].T
        dkt[...] = jnp.zeros_like(dkt)
        dvt[...] = jnp.zeros_like(dvt)
        seg_keys = segments_of(
            lax.broadcasted_iota(jnp.int32, (1, length), 1), lengths_ref, b, slots
        )

        @pl.loop(0, blocks)
        def _(at, b=b, base=base, seg_keys=seg_keys):
            fire(back_events[b], at)
            begin = pl.multiple_of(at * LANES, LANES)
            here = pl.ds(begin, LANES)
            span = pl.ds(pl.multiple_of(base + begin, LANES), LANES)
            window = pl.ds(pl.multiple_of((blocks - 1 - at) * LANES, LANES), length)
            seg_rows = segments_of(
                lax.broadcasted_iota(jnp.int32, (LANES, 1), 0) + begin, lengths_ref, b, slots
            )
            same = seg_rows == seg_keys
            logs = log_ref[span]
            queries = qkv_ref[span, :head_cols]
            incoming = att_ref[spot.n_far, here]
            outs = []
            for h in range(heads):
                cols = slice(h * DH, (h + 1) * DH)
                scores = mm(queries[:, cols], kt[h]) + strip[h, :, window]
                scores = jnp.where(same, scores, masked_score)
                probs = jnp.exp(scores - logs[:, h : h + 1])
                d_probs = mm(incoming[:, cols], vt[h])
                inner = jnp.sum(probs * d_probs, axis=1, keepdims=True)
                d_scores = (probs * (d_probs - inner)).astype(BF16)
                dstrip[h, :, window] = dstrip[h, :, window] + d_scores.astype(F32)
                outs.append(mm(d_scores, ws[h]).astype(BF16))
                dkt[h] = dkt[h] + mm(qt[h, :, here], d_scores)
                dvt[h] = dvt[h] + mm(gt[h, :, here], probs.astype(BF16))
            dg[span, :head_cols] = jnp.concatenate(outs, axis=1)

        outs = [dkt[h].T.astype(BF16) for h in range(heads)]
        outs += [dvt[h].T.astype(BF16) for h in range(heads)]
        dg[rows, head_cols:qkv_cols] = jnp.concatenate(outs, axis=1)
        for keep in range(2):
            which = core if keep else 1 - core
            here = half_rows(b, which)
            if keep == 0:
                dn_core(b, 0).wait_send()
            else:
                dn_across(b, 0).wait_send()
            dn = mm(dg[here, :qkv_cols], pbuf[:, :qkv_cols], NT)
            values = x_ref[here].astype(F32)
            gain_sums = gain_sums + fold_rows(dn * values * rms_scale(values))
            dn = dn.astype(BF16)
            if keep == 0:
                dn_out[b] = dn
                dn_core(b, 1).start()
            else:
                dn_core(b, 1).wait_recv()
                dn_sum[b] = (dn.astype(F32) + dn_in[b].astype(F32)).astype(BF16)
                pl.semaphore_wait(credit.at[b], 1)
                dn_across(b, 1).start()

    row = lax.broadcasted_iota(jnp.int32, (LANES, width), 0)
    gain_rows = jnp.where(
        row == DH,
        jnp.sum(gain_sums, axis=0, keepdims=True),
        jnp.where(
            row == DH + 1, jnp.sum(gain_two_sum[...], axis=0, keepdims=True) / gain_two, 0.0
        ),
    )
    gain_cols = gain_rows.T
    p_cols = qkv_cols + DH
    p_reds = []
    for at, span in enumerate((slice(0, split), slice(split, p_cols))):
        stop = min(span.stop, qkv_cols)
        for begin in range(0, width, step):
            cols = slice(begin, begin + step)
            total[cols, span.start : stop] = mm(
                normed_one[:, cols], dg[:, span.start : stop], TN
            )
            if at:
                total[cols, qkv_cols:p_cols] = gain_cols[cols, DH:]
        for m in range(4):
            odd = total[pl.ds(pl.multiple_of(spot.far_owner(m) * owned, 8), owned), span]
            p_odd[m, :, span] = odd.astype(BF16)
        red = Reduce(
            spot,
            lambda m, span=span: total[
                pl.ds(pl.multiple_of(spot.near_owner(m) * owned, 8), owned), span
            ],
            lambda m, span=span: p_odd.at[m, :, span],
            lambda m, span=span: p_flip.at[m, :, span],
            lambda m, span=span: p_mix.at[m, :, span],
            lambda m, span=span: p_land.at[m, :, span],
            red_s.at[3 + at],
            red_r.at[3 + at],
        )
        red.begin()
        p_reds.append(red)

    def finish_out(b):
        ff_across(b).wait_recv()

        @pl.loop(0, half // LANES)
        def _(i):
            span, here = own_block(b, i)
            joined = (ff_sum[b, span].astype(F32) + ff_in[b, span].astype(F32)).astype(BF16)
            out_ref[here] = (middle_ref[b, span] + joined.astype(F32)).astype(BF16)

        out_core(b, core).start()

    def finish_in(b):
        dn_across(b, 1).wait_recv()

        @pl.loop(0, half // LANES)
        def _(i):
            span, here = own_block(b, i)
            upstream = dn_sum[b, span].astype(F32) + dn_far[b, span].astype(F32)
            values = x_ref[here].astype(F32)
            in_ref[here] = (
                low_ref[here].astype(F32)
                + norm_back(values, rms_scale(values), gain_one, upstream)
            ).astype(BF16)

        in_core(b, core).start()

    def square_of(value):
        return jnp.sum(jnp.sum(value * value, axis=1, keepdims=True), axis=0, keepdims=True)

    finish_out(0)
    p_reds[0].relay(2, 1, 3)
    finish_out(1)
    squares = jnp.zeros((1, 1), F32)
    for j in range(2):
        value = feed_reds[j].result()
        feed_grad[:, j * chunk : (j + 1) * chunk] = value
        squares = squares + square_of(value)
    p_reds[1].relay(2, 1, 3)
    value = out_red.result()
    o_grad[...] = value
    squares = squares + square_of(value)
    for b in range(buffers):
        out_core(b, 1 - core).wait_recv()
    finish_in(0)

    near_row = lax.broadcasted_iota(jnp.int32, (LANES, 4 * LANES), 0)
    diag = lax.broadcasted_iota(jnp.int32, (1, 4 * LANES), 1)
    ids = bucket_of(jnp.where(diag < 3 * LANES, diag - LANES, diag - 5 * LANES))
    lane = lax.broadcasted_iota(jnp.int32, (1, LANES), 1)
    onehot = jnp.where(near_row == ids, 1.0, 0.0)
    bucket_line = jnp.zeros((1, LANES), F32)
    for h in range(heads):
        left = jnp.sum(jnp.sum(dstrip[h, :, :near_at], axis=0, keepdims=True), axis=1, keepdims=True)
        right = jnp.sum(
            jnp.sum(dstrip[h, :, near_end:], axis=0, keepdims=True), axis=1, keepdims=True
        )
        near = jnp.concatenate(
            [dstrip[h, :, near_at:near_end], jnp.zeros((LANES, LANES), F32)], axis=1
        )
        for k in range(7):
            near = jnp.where(
                (near_row // (1 << k)) % 2 == 1, pltpu.roll(near, 4 * LANES - (1 << k), 1), near
            )
        binned = lax.dot_general(
            jnp.broadcast_to(jnp.sum(near, axis=0, keepdims=True), (8, 4 * LANES)),
            onehot,
            NT,
            precision=lax.Precision.HIGHEST,
            preferred_element_type=F32,
        )[0:1]
        binned = binned + jnp.where(lane == 15, left, 0.0) + jnp.where(lane == 31, right, 0.0)
        binned = jnp.where(lane < 32, binned, 0.0)
        bucket_line = bucket_line + (pltpu.roll(binned, 32 * h, 1) if h else binned)

    value = p_reds[0].result()
    p_grad[:, :split] = value
    squares = squares + square_of(value)
    value = p_reds[1].result()
    p_grad[:, split:] = value
    kept = lax.broadcasted_iota(jnp.int32, value.shape, 1) < qkv_cols - split
    squares = squares + square_of(jnp.where(kept, value, 0.0))
    low_lane = qkv_cols // LANES * LANES
    gpad[...] = jnp.zeros_like(gpad)
    gpad[0:owned, : p_cols - low_lane] = value[:, low_lane - split :]
    turned = gpad[...].T
    here = qkv_cols - low_lane
    row8 = lax.broadcasted_iota(jnp.int32, (8, LANES), 0)
    line = jnp.where(row8 == 0, squares, 0.0)
    line = jnp.where(row8 == 1, turned[here : here + 1], line)
    line = jnp.where(row8 == 2, turned[here + 1 : here + 2], line)
    line = jnp.where(row8 == 3, bucket_line, line)
    block[...] = line
    inbox[spot.me] = line

    @pl.loop(1, devices)
    def _(k):
        peer, where = spot.peer(k)
        remote(block, inbox.at[spot.me], norm_s.at[k], norm_r.at[devices - k], where).start()

    finish_in(1)

    @pl.loop(1, devices)
    def _(k):
        peer, where = spot.peer(k)
        copy = remote(block, inbox.at[peer], norm_s.at[k], norm_r.at[k], where)
        copy.wait_send()
        copy.wait_recv()

    columns = [jnp.zeros((8, LANES), F32) for _ in range(narrow)]
    gain_square = jnp.zeros((8, LANES), F32)
    square_total = jnp.zeros((8, LANES), F32)
    for a in range(wide):
        summed = jnp.zeros((8, LANES), F32)
        for c in range(narrow):
            got = inbox[a * narrow + c]
            summed = summed + got
            columns[c] = columns[c] + got
        square_total = square_total + summed
        gain_square = gain_square + summed * summed
    own = inbox[spot.w * narrow]
    for c in range(1, narrow):
        own = own + inbox[spot.w * narrow + c]
    gain_ref[...] = own
    gain_square = jnp.where((row8 == 1) | (row8 == 2), gain_square, 0.0)
    norm_square = square_total[0:1, 0:1] + jnp.sum(
        jnp.sum(gain_square, axis=1, keepdims=True), axis=0, keepdims=True
    )
    table_row = lax.broadcasted_iota(jnp.int32, (16, LANES), 0)
    table = jnp.zeros((16, LANES), F32)
    for c in range(narrow):
        got = columns[c][3:4]
        norm_square = norm_square + jnp.sum(got * got, axis=1, keepdims=True)
        for h in range(heads):
            moved = pltpu.roll(got, LANES - 32 * h, 1) if h else got
            table = jnp.where(table_row == c * heads + h, moved, table)
    table_ref[...] = table
    global_norm = jnp.sqrt(norm_square)
    factor = jnp.minimum(1.0, clip_limit / (global_norm + 1e-06))
    stat_ref[...] = jnp.where(row8 == 0, global_norm, factor)

    for b in range(buffers):
        in_core(b, 1 - core).wait_recv()
        for slot, which, peer in (
            (0, spot.n, spot.across),
            (1, spot.n, spot.beside),
        ):
            att_copy(which, b, slot, peer).wait_send()
        ff_core(b).wait_send()
        ff_across(b).wait_send()
        dn_core(b, 1).wait_send()
        dn_across(b, 1).wait_send()
        low_core(b, core).wait_send()
        out_core(b, core).wait_send()
        in_core(b, core).wait_send()
    lone(o_views[0](spot.w), o_views[0](spot.w), 0, spot.across).wait_send()
    lone(obuf.at[spot.n], obuf.at[spot.n], 1, spot.beside).wait_send()
    lone(obuf.at[spot.n_far], obuf.at[spot.n_far], 2, spot.beside).wait_send()
    for group in projections + outs_gather:
        group.drain()
    for group in feed_reds + p_reds + [out_red]:
        group.drain()


def layer(wide, narrow, lengths, bias, x, cot, pw, ow, ew, sw, gn):
    tokens, width = x.shape
    buffers, slots = lengths.shape
    length = tokens // buffers
    half = length // 2
    head_cols = pw.shape[2]
    heads = head_cols // DH
    hidden_cols = ew.shape[2]
    rows = gn.shape[1]
    devices = wide * narrow
    qkv_cols = 3 * head_cols
    p_cols = qkv_cols + DH
    feed_cols = 3 * hidden_cols
    strip_shape = (heads, LANES, (2 * (length // LANES) - 1) * LANES)
    vmem = pl.BlockSpec(memory_space=pltpu.VMEM)
    smem = pl.BlockSpec(memory_space=pltpu.SMEM)
    halves = pltpu.VMEM((buffers, half, width), BF16)
    tall = pltpu.VMEM((heads, DH, length), BF16)
    dma = pltpu.SemaphoreType.DMA

    def pieces(count, cols, kind=BF16):
        return pltpu.VMEM((count, rows, cols), kind)

    return pl.pallas_call(
        functools.partial(layer_kernel, (buffers, slots, heads, hidden_cols, wide, narrow)),
        in_specs=[smem, smem, pl.BlockSpec(memory_space=ANY), pl.BlockSpec(memory_space=ANY)]
        + [vmem] * 5,
        out_specs=[vmem] * 8,
        out_shape=[
            jax.ShapeDtypeStruct((tokens, width), BF16),
            jax.ShapeDtypeStruct((tokens, width), BF16),
            jax.ShapeDtypeStruct((rows, p_cols), F32),
            jax.ShapeDtypeStruct((rows, head_cols), F32),
            jax.ShapeDtypeStruct((rows, feed_cols), F32),
            jax.ShapeDtypeStruct((8, LANES), F32),
            jax.ShapeDtypeStruct((8, LANES), F32),
            jax.ShapeDtypeStruct((16, LANES), F32),
        ],
        scratch_shapes=[
            pltpu.VMEM((tokens, width), BF16),
            pltpu.VMEM((tokens, width), BF16),
            pltpu.VMEM(strip_shape, F32),
            pltpu.VMEM(strip_shape, F32),
            pltpu.VMEM((width, p_cols), BF16),
            pltpu.VMEM((narrow, width, head_cols), BF16),
            pltpu.VMEM((width, feed_cols), BF16),
            pltpu.VMEM((narrow, tokens, head_cols), BF16),
            pltpu.VMEM((tokens, qkv_cols), BF16),
            pltpu.VMEM((tokens, LANES), F32),
            pltpu.VMEM((tokens, width), BF16),
            pltpu.VMEM((buffers, half, width), F32),
            pltpu.VMEM((tokens, hidden_cols), BF16),
            pltpu.VMEM((tokens, 2 * hidden_cols), BF16),
            pltpu.VMEM((width, feed_cols // 2), F32),
            pltpu.VMEM((2 * LANES, LANES), F32),
            pltpu.VMEM((LANES, LANES), F32),
            pieces(4, feed_cols),
            pieces(3, feed_cols),
            pieces(3, feed_cols),
            pieces(4, head_cols, F32),
            pieces(4, head_cols),
            pieces(4, head_cols),
            pieces(3, head_cols),
            pieces(3, head_cols),
            pieces(4, p_cols),
            pieces(4, p_cols),
            pieces(3, p_cols),
            pieces(3, p_cols),
        ]
        + [halves] * 7
        + [
            pltpu.VMEM((heads, length, DH), BF16),
            tall,
            tall,
            tall,
            tall,
            pltpu.VMEM((heads, DH, length), F32),
            pltpu.VMEM((heads, DH, length), F32),
            pltpu.VMEM((8, width), F32),
            pltpu.VMEM((8, LANES), F32),
            pltpu.VMEM((devices, 8, LANES), F32),
            dma((12, 9)),
            dma((12, wide)),
            dma((27,)),
            dma((27,)),
            dma((5, 7)),
            dma((5, 7)),
            dma((devices,)),
            dma((devices,)),
            pltpu.SemaphoreType.REGULAR((buffers,)),
            dma((2,)),
        ],
        compiler_params=pltpu.CompilerParams(
            vmem_limit_bytes=64 << 20, collective_id=0, has_side_effects=True
        ),
        cost_estimate=pl.CostEstimate(
            flops=60 << 30, bytes_accessed=24 << 20, transcendentals=16 << 20
        ),
        name="layer",
    )(lengths, bias, x, cot, pw, ow, ew, sw, gn)


def update_kernel(
    heads, hidden_cols, from_out, from_in, p_ref, o_ref, feed_ref, stat_ref, gain_ref, table_ref, *refs
):
    weights, firsts, seconds = refs[:6], refs[6:12], refs[12:18]
    outs, norm_ref, to_out, to_in, o_pad, held, sems = refs[18:36], *refs[36:]
    pairs = ((from_out, to_out), (from_in, to_in))
    rows = from_out.shape[0] // 2
    ways = []
    for which, (source, target) in enumerate(pairs):
        for part in range(2):
            span = slice(part * rows, (part + 1) * rows)
            at = 2 * which + part
            ways.append(
                (
                    pltpu.make_async_copy(source.at[span], held.at[which, span], sems.at[0, at]),
                    pltpu.make_async_copy(held.at[which, span], target.at[span], sems.at[1, at]),
                )
            )
    for inward, _ in ways:
        inward.start()
    for inward, outward in ways:
        inward.wait()
        outward.start()
    factor = stat_ref[1:2, 0:1]
    norm_ref[0, 0] = jnp.sum(stat_ref[0:1, 0:1])
    head_cols = heads * DH
    rows = p_ref.shape[0]

    def update(which, index, gradient):
        results = adam_update(
            weights[which][index],
            firsts[which][index],
            seconds[which][index],
            factor * gradient,
            step_rates[which],
            decay_rates[which],
        )
        for at in range(3):
            outs[6 * at + which][index] = results[at]

    for i in range(3):
        update(0, i, p_ref[:, i * head_cols : (i + 1) * head_cols])
    part = hidden_cols // 2
    for j in range(2):
        span = slice(j * part, (j + 1) * part)
        for i in range(2):
            begin = (3 * j + i) * part
            update(2, (i, slice(None), span), feed_ref[:, begin : begin + part])
        begin = (3 * j + 2) * part
        update(3, (slice(None), span), feed_ref[:, begin : begin + part])
    o_pad[...] = jnp.zeros_like(o_pad)
    o_pad[0:rows, 0:head_cols] = o_ref[...]
    update(1, slice(None), o_pad[...].T[:head_cols, :rows])
    depth, columns = weights[4].shape
    update(4, slice(None), table_ref[:depth, :columns])
    update(5, slice(None), gain_ref[1:3, :rows])
    for _, outward in ways:
        outward.wait()


def update_call(activations, grads, params_in, firsts, seconds, heads, hidden_cols):
    vmem = pl.BlockSpec(memory_space=pltpu.VMEM)
    hbm = pl.BlockSpec(memory_space=ANY)
    operands = [*activations, *grads, *params_in, *firsts, *seconds]
    return pl.pallas_call(
        functools.partial(update_kernel, heads, hidden_cols),
        in_specs=[hbm] * 2 + [vmem] * (len(operands) - 2),
        out_specs=[vmem] * 18 + [pl.BlockSpec(memory_space=pltpu.SMEM)] + [hbm] * 2,
        out_shape=[jax.ShapeDtypeStruct(a.shape, F32) for a in params_in] * 3
        + [jax.ShapeDtypeStruct((1, 1), F32)]
        + [jax.ShapeDtypeStruct(a.shape, a.dtype) for a in activations],
        scratch_shapes=[
            pltpu.VMEM((LANES, 2 * LANES), F32),
            pltpu.VMEM((2, *activations[0].shape), BF16),
            pltpu.SemaphoreType.DMA((2, 4)),
        ],
        compiler_params=params(),
        cost_estimate=pl.CostEstimate(flops=4 << 20, bytes_accessed=16 << 20, transcendentals=0),
        name="update",
    )(*operands)


def direct_body(wide, narrow, *arguments):
    block_input, cotangent, lengths = arguments[:3]
    turned = (3, 4)
    flat = [
        value.T if at % 6 in turned else value for at, value in enumerate(arguments[3:21])
    ]
    weights, firsts, seconds = flat[:6], flat[6:12], flat[12:18]
    project, output, expand, shrink, bias, gains = weights
    block_output, input_gradient, *grads = layer(
        wide,
        narrow,
        lengths,
        bias,
        block_input,
        cotangent,
        project,
        output,
        expand,
        shrink,
        gains,
    )
    heads = project.shape[2] // DH
    *results, norm, block_output, input_gradient = update_call(
        (block_output, input_gradient), grads, weights, firsts, seconds, heads, expand.shape[2]
    )
    results = [value.T if at % 6 in turned else value for at, value in enumerate(results)]
    return (block_output, input_gradient, norm.reshape(()), *results)


def solution(mesh):
    wide, narrow = mesh.shape["wide"], mesh.shape["narrow"]
    body = direct_body if (wide, narrow) == (8, 4) else general_body
    state = (
        P(None, "wide", "narrow"),
        P("narrow", "wide"),
        P(None, "wide", "narrow"),
        P("narrow", "wide"),
        P(),
        P(None, "wide"),
    )
    rows = P("wide", None)
    return jax.shard_map(
        functools.partial(body, wide, narrow),
        mesh=mesh,
        in_specs=(rows, rows, rows, *state, *state, *state),
        out_specs=(rows, rows, P(), *state, *state, *state),
        check_vma=False,
    )
```

```python
import functools

import jax
import jax.numpy as jnp
from jax import lax
from jax.experimental import pallas as pl
from jax.experimental.pallas import tpu as pltpu
from jax.sharding import PartitionSpec as P

DH = 64
STEP = 10
LANES = 128
MESH = pl.DeviceIdType.MESH
F32 = jnp.float32
BF16 = jnp.bfloat16
ANY = pl.ANY

bucket_edges = (12, 16, 23, 32, 46, 64, 91)
norm_eps = 1e-06
clip_limit = 1.0
beta_one = 0.9
beta_two = 0.999
adam_eps = 1e-08
step_rates = (0.06, 0.3, 0.07, 0.06, 1.0, 0.3)
decay_rates = (0.01, 0.01, 0.01, 0.01, 0.0, 0.0)
masked_score = -1000000000.0
VMEM_LIMIT = 58 << 20

NN = (((1,), (0,)), ((), ()))
NT = (((1,), (1,)), ((), ()))
TN = (((0,), (0,)), ((), ()))


def mm(left, right, dims=NN):
    return lax.dot_general(left, right, dims, preferred_element_type=F32)


def bucket_of(offsets):
    distance = jnp.abs(offsets)
    far_bucket = 8 + sum(((distance >= threshold).astype(jnp.int32) for threshold in bucket_edges))
    return jnp.where(distance < 8, distance, far_bucket) + 16 * (offsets > 0).astype(jnp.int32)


def rms_scale(values):
    return lax.rsqrt(jnp.mean(values * values, axis=-1, keepdims=True) + norm_eps)


def norm_back(values, scale_vec, gain_vec, upstream):
    weighted = upstream * gain_vec
    inner_mean = jnp.mean(weighted * values, axis=-1, keepdims=True)
    return scale_vec * weighted - values * (scale_vec * scale_vec * scale_vec) * inner_mean


def adam_update(weight, moment_one, moment_two, gradient, step_rate, decay_rate):
    new_first = beta_one * moment_one + (1.0 - beta_one) * gradient
    new_second = beta_two * moment_two + (1.0 - beta_two) * gradient * gradient
    first_hat = new_first / (1.0 - beta_one**STEP)
    second_hat = new_second / (1.0 - beta_two**STEP)
    new_weight = weight - step_rate * (
        first_hat / (jnp.sqrt(second_hat) + adam_eps) + decay_rate * weight
    )
    return (new_weight, new_first, new_second)


def fold_rows(values):
    rows, cols = values.shape
    return jnp.sum(values.reshape(rows // 8, 8, cols), axis=0)


def start_rows(pieces, target, offs_ref, sems):
    copies = []
    for at, piece in enumerate(pieces):
        rows = piece.shape[0]
        begin = pl.multiple_of(offs_ref[at], 16)
        copies.append(
            pltpu.make_async_copy(piece, target.at[pl.ds(begin, rows)], sems.at[at])
        )
    for copy in copies:
        copy.start()
    return copies


def segments(index, ends_ref, buffer, slots):
    total = jnp.zeros(index.shape, jnp.int32)
    for slot in range(slots):
        total = total + (index >= ends_ref[buffer, slot]).astype(jnp.int32)
    return total


def params(**more):
    return pltpu.CompilerParams(vmem_limit_bytes=VMEM_LIMIT, **more)


def attend_kernel(
    buffer, slots, heads, count, ends_ref, offs_ref, x_ref, strip_ref, *refs
):
    pieces = refs[:count]
    normed_ref, qkv_ref, att_ref, log_ref, gains_ref, wbuf, qs, ks, vs, os, sems = refs[count:]
    length, width = x_ref.shape
    head_cols = heads * DH
    copies = start_rows(pieces, wbuf, offs_ref, sems)
    for copy in copies:
        copy.wait()
    gain_cols = wbuf[:, 4 * LANES :].astype(F32).T
    first = 3 * head_cols - 4 * LANES
    gains = gain_cols[first : first + 8]
    gains_ref[...] = gains
    gain_one = gains[0:1]
    step = 256

    @pl.loop(0, length // step)
    def _(block):
        rows = pl.ds(pl.multiple_of(block * step, step), step)
        values = x_ref[rows].astype(F32)
        normed = (values * rms_scale(values) * gain_one).astype(BF16)
        normed_ref[rows] = normed
        qkv = mm(normed, wbuf[...]).astype(BF16)
        qkv_ref[rows] = qkv[:, : 3 * head_cols]
        for h in range(heads):
            qs[h, rows] = qkv[:, h * DH : (h + 1) * DH]
            ks[h, rows] = qkv[:, head_cols + h * DH : head_cols + (h + 1) * DH]
            vs[h, rows] = qkv[:, 2 * head_cols + h * DH : 2 * head_cols + (h + 1) * DH]

    blocks = length // LANES
    seg_keys = segments(
        lax.broadcasted_iota(jnp.int32, (1, length), 1), ends_ref, buffer, slots
    )

    @pl.loop(0, blocks)
    def _(block):
        begin = pl.multiple_of(block * LANES, LANES)
        rows = pl.ds(begin, LANES)
        window = pl.ds(pl.multiple_of((blocks - 1 - block) * LANES, LANES), length)
        seg_rows = segments(
            lax.broadcasted_iota(jnp.int32, (LANES, 1), 0) + begin, ends_ref, buffer, slots
        )
        same = seg_rows == seg_keys
        lane = lax.broadcasted_iota(jnp.int32, (LANES, LANES), 1)
        logs = jnp.zeros((LANES, LANES), F32)
        for h in range(heads):
            scores = mm(qs[h, rows], ks[h], NT) + strip_ref[h, :, window]
            scores = jnp.where(same, scores, masked_score)
            row_max = jnp.max(scores, axis=1, keepdims=True)
            raised = jnp.exp(scores - row_max)
            total = jnp.sum(raised, axis=1, keepdims=True)
            probs = (raised * (1.0 / total)).astype(BF16)
            os[h, rows] = mm(probs, vs[h]).astype(BF16)
            logs = jnp.where(lane == h, row_max + jnp.log(total), logs)
        log_ref[rows] = logs

    att_ref[...] = jnp.concatenate([os[h] for h in range(heads)], axis=1)


def attend(buffer, ends, offs, x, strip, pieces, length, heads):
    width = x.shape[1]
    count = len(pieces)
    cols = pieces[0].shape[1]
    head_cols = heads * DH
    whole = lambda i, *_: (0, 0)
    spec = pltpu.PrefetchScalarGridSpec(
        num_scalar_prefetch=2,
        grid=(1,),
        in_specs=[
            pl.BlockSpec((length, width), lambda i, *_: (buffer, 0)),
            pl.BlockSpec(strip.shape, lambda i, *_: (0, 0, 0)),
        ]
        + [pl.BlockSpec(memory_space=ANY)] * count,
        out_specs=[
            pl.BlockSpec((length, width), whole),
            pl.BlockSpec((length, 3 * head_cols), whole),
            pl.BlockSpec((length, head_cols), whole),
            pl.BlockSpec((length, LANES), whole),
            pl.BlockSpec((8, width), whole),
        ],
        scratch_shapes=[
            pltpu.VMEM((width, cols), BF16),
            pltpu.VMEM((heads, length, DH), BF16),
            pltpu.VMEM((heads, length, DH), BF16),
            pltpu.VMEM((heads, length, DH), BF16),
            pltpu.VMEM((heads, length, DH), BF16),
            pltpu.SemaphoreType.DMA((count,)),
        ],
    )
    flops = 2 * length * (width * cols + 2 * heads * DH * length)
    return pl.pallas_call(
        functools.partial(attend_kernel, buffer, ends.shape[1], heads, count),
        grid_spec=spec,
        out_shape=[
            jax.ShapeDtypeStruct((length, width), BF16),
            jax.ShapeDtypeStruct((length, 3 * head_cols), BF16),
            jax.ShapeDtypeStruct((length, head_cols), BF16),
            jax.ShapeDtypeStruct((length, LANES), F32),
            jax.ShapeDtypeStruct((8, width), F32),
        ],
        compiler_params=params(),
        cost_estimate=pl.CostEstimate(
            flops=4 * flops, bytes_accessed=8 << 20, transcendentals=heads * length * length
        ),
        name="attend",
    )(ends, offs, x, strip, *pieces)


def feed_kernel(hidden_cols, counts, order_ref, offs_ref, *refs):
    own, across, beside, diagonal, x_ref, cot_ref, gains_ref = refs[:7]
    at = 7
    groups = []
    for count in counts:
        groups.append(refs[at : at + count])
        at += count
    (
        normed_ref,
        hidden_ref,
        gate_ref,
        ff_send,
        ff_keep,
        dn_send,
        dn_keep,
        middle_keep,
        gain_sum,
        ebuf,
        sbuf,
        oabuf,
        obbuf,
        sems,
    ) = refs[at:]
    step = pl.program_id(0)
    bufs = (oabuf, obbuf, ebuf, sbuf)

    @pl.when(step == 0)
    def _():
        copies = []
        for which, (group, target) in enumerate(zip(groups, bufs)):
            copies += start_rows(group, target, offs_ref, sems.at[which])
        for copy in copies:
            copy.wait()

    cols = own.shape[1]
    upper = order_ref[2] == 0
    pairs = []
    for near, far, weights in ((own, across, oabuf), (beside, diagonal, obbuf)):
        near_sum = mm(near[...], weights[:, :cols], NT)
        far_sum = mm(far[...], weights[:, cols:], NT)
        pairs.append(
            jnp.where(upper, near_sum, far_sum) + jnp.where(upper, far_sum, near_sum)
        )
    swap = order_ref[0] == 0
    attention = jnp.where(swap, pairs[0], pairs[1]) + jnp.where(swap, pairs[1], pairs[0])
    middle = x_ref[...].astype(F32) + attention
    scale_two = rms_scale(middle)
    gain_two = gains_ref[1:2]
    normed = (middle * scale_two * gain_two).astype(BF16)
    normed_ref[...] = normed
    cot = cot_ref[...]
    part = 256
    k0 = 0.7978845608028654
    k1 = 0.044715
    for begin in range(0, hidden_cols, part):
        gate = mm(normed, ebuf[:, begin : begin + part])
        up = mm(normed, ebuf[:, hidden_cols + begin : hidden_cols + begin + part])
        square = gate * gate
        tanh = jnp.tanh(k0 * (gate + k1 * (square * gate)))
        half = 0.5 * (1.0 + tanh)
        active = gate * half
        slope = half + (0.5 * gate) * (1.0 - tanh * tanh) * (k0 + (3.0 * k0 * k1) * square)
        d_hidden = mm(cot, sbuf[:, begin : begin + part])
        hidden_ref[:, begin : begin + part] = (active * up).astype(BF16)
        gate_ref[:, begin : begin + part] = (d_hidden * up * slope).astype(BF16)
        gate_ref[:, hidden_cols + begin : hidden_cols + begin + part] = (
            d_hidden * active
        ).astype(BF16)
    ff = mm(hidden_ref[...], sbuf[...], NT).astype(BF16)
    dn = mm(gate_ref[...], ebuf[...], NT)
    sums = fold_rows(dn * middle * scale_two)
    dn = dn.astype(BF16)

    @pl.when(step == 0)
    def _():
        ff_send[...] = ff
        dn_send[...] = dn
        gain_sum[...] = sums

    @pl.when(step == 1)
    def _():
        ff_keep[...] = ff
        dn_keep[...] = dn
        middle_keep[...] = middle
        gain_sum[...] = gain_sum[...] + sums


def feed(buffer, order, offs, parts, x, cot, gains, groups, length, hidden_cols):
    width = x.shape[1]
    half = length // 2
    cols = parts[0].shape[1]
    counts = [len(group) for group in groups]
    natural = lambda i, order, *_: (order[i], 0)
    rows = lambda i, order, *_: (2 * buffer + order[i], 0)
    whole = lambda i, *_: (0, 0)
    spec = pltpu.PrefetchScalarGridSpec(
        num_scalar_prefetch=2,
        grid=(2,),
        in_specs=[pl.BlockSpec((half, cols), natural)] * 4
        + [pl.BlockSpec((half, width), rows)] * 2
        + [pl.BlockSpec((8, width), whole)]
        + [pl.BlockSpec(memory_space=ANY)] * sum(counts),
        out_specs=[
            pl.BlockSpec((half, width), natural),
            pl.BlockSpec((half, hidden_cols), natural),
            pl.BlockSpec((half, 2 * hidden_cols), natural),
        ]
        + [pl.BlockSpec((half, width), whole)] * 5
        + [pl.BlockSpec((8, width), whole)],
        scratch_shapes=[
            pltpu.VMEM((width, 2 * hidden_cols), BF16),
            pltpu.VMEM((width, hidden_cols), BF16),
            pltpu.VMEM((width, 2 * cols), BF16),
            pltpu.VMEM((width, 2 * cols), BF16),
            pltpu.SemaphoreType.DMA((4, max(counts))),
        ],
    )
    flops = 2 * length * width * (4 * cols + 7 * hidden_cols)
    return pl.pallas_call(
        functools.partial(feed_kernel, hidden_cols, counts),
        grid_spec=spec,
        out_shape=[
            jax.ShapeDtypeStruct((length, width), BF16),
            jax.ShapeDtypeStruct((length, hidden_cols), BF16),
            jax.ShapeDtypeStruct((length, 2 * hidden_cols), BF16),
            jax.ShapeDtypeStruct((half, width), BF16),
            jax.ShapeDtypeStruct((half, width), BF16),
            jax.ShapeDtypeStruct((half, width), BF16),
            jax.ShapeDtypeStruct((half, width), BF16),
            jax.ShapeDtypeStruct((half, width), F32),
            jax.ShapeDtypeStruct((8, width), F32),
        ],
        compiler_params=params(),
        cost_estimate=pl.CostEstimate(
            flops=flops, bytes_accessed=12 << 20, transcendentals=length * hidden_cols
        ),
        name="feed",
    )(order, offs, *parts, x, cot, gains, *[piece for group in groups for piece in group])


def middle_kernel(order_ref, near, far, middle_ref, cot_ref, gains_ref, d_ref, low_ref):
    upstream = near[...].astype(F32) + far[...].astype(F32)
    middle = middle_ref[...]
    d_middle = cot_ref[...].astype(F32) + norm_back(
        middle, rms_scale(middle), gains_ref[1:2], upstream
    )
    d_ref[...] = d_middle
    low_ref[...] = d_middle.astype(BF16)


def input_kernel(order_ref, near, far, x_ref, d_ref, gains_ref, out_ref):
    upstream = near[...].astype(F32) + far[...].astype(F32)
    values = x_ref[...].astype(F32)
    out_ref[...] = (
        d_ref[...] + norm_back(values, rms_scale(values), gains_ref[0:1], upstream)
    ).astype(BF16)


def output_kernel(order_ref, near, far, middle_ref, out_ref):
    out_ref[...] = (
        middle_ref[...] + (near[...].astype(F32) + far[...].astype(F32)).astype(BF16).astype(F32)
    ).astype(BF16)


def half_call(kernel, name, buffer, order, arrays, placed, outs, gains=None):
    half, width = arrays[0].shape
    steps = 3
    block = half // steps
    mine = lambda i, *_: (i, 0)
    rows = lambda i, order, *_: ((2 * buffer + order[1]) * steps + i, 0)
    in_specs = [
        pl.BlockSpec((block, width), rows if at in placed else mine)
        for at in range(len(arrays))
    ]
    operands = list(arrays)
    if gains is not None:
        in_specs.append(pl.BlockSpec((8, width), lambda i, *_: (0, 0)))
        operands.append(gains)
    return pl.pallas_call(
        kernel,
        grid_spec=pltpu.PrefetchScalarGridSpec(
            num_scalar_prefetch=1,
            grid=(steps,),
            in_specs=in_specs,
            out_specs=[pl.BlockSpec((block, width), mine) for _ in outs],
        ),
        out_shape=[jax.ShapeDtypeStruct((half, width), kind) for kind in outs],
        compiler_params=params(),
        cost_estimate=pl.CostEstimate(
            flops=20 * half * width, bytes_accessed=12 * half * width, transcendentals=0
        ),
        name=name,
    )(order, *operands)


def back_kernel(buffer, slots, heads, counts, ends_ref, offs_ref, order_ref, *refs):
    near, far, qkv_ref, log_ref, strip_ref, x_ref = refs[:6]
    at = 6
    o_pieces = refs[at : at + counts[0]]
    at += counts[0]
    p_pieces = refs[at : at + counts[1]]
    at += counts[1]
    (
        low_ref,
        dqkv_ref,
        dn_send,
        dn_keep,
        gain_sum,
        dstrip,
        wbuf,
        obuf,
        qs,
        ks,
        vs,
        gs,
        qt,
        gt,
        dkt,
        dvt,
        dq,
        sems,
    ) = refs[at:]
    length = qkv_ref.shape[0]
    half = length // 2
    head_cols = heads * DH
    o_copies = start_rows(o_pieces, obuf, offs_ref, sems.at[0])
    p_copies = start_rows(p_pieces, wbuf, offs_ref, sems.at[1])
    mine = pl.ds(pl.multiple_of(order_ref[1] * half, LANES), half)
    other = pl.ds(pl.multiple_of(order_ref[0] * half, LANES), half)
    low_ref[mine] = near[...]
    low_ref[other] = far[...]
    for h in range(heads):
        qs[h] = qkv_ref[:, h * DH : (h + 1) * DH]
        ks[h] = qkv_ref[:, head_cols + h * DH : head_cols + (h + 1) * DH]
        vs[h] = qkv_ref[:, 2 * head_cols + h * DH : 2 * head_cols + (h + 1) * DH]
        qt[h] = qs[h].T
    dstrip[...] = jnp.zeros_like(dstrip)
    dkt[...] = jnp.zeros_like(dkt)
    dvt[...] = jnp.zeros_like(dvt)
    for copy in o_copies + p_copies:
        copy.wait()
    grads = mm(low_ref[...], obuf[:, :head_cols]).astype(BF16)
    for h in range(heads):
        gs[h] = grads[:, h * DH : (h + 1) * DH]
        gt[h] = gs[h].T
    blocks = length // LANES
    seg_keys = segments(
        lax.broadcasted_iota(jnp.int32, (1, length), 1), ends_ref, buffer, slots
    )

    @pl.loop(0, blocks)
    def _(block):
        begin = pl.multiple_of(block * LANES, LANES)
        rows = pl.ds(begin, LANES)
        window = pl.ds(pl.multiple_of((blocks - 1 - block) * LANES, LANES), length)
        seg_rows = segments(
            lax.broadcasted_iota(jnp.int32, (LANES, 1), 0) + begin, ends_ref, buffer, slots
        )
        same = seg_rows == seg_keys
        logs = log_ref[rows]
        for h in range(heads):
            scores = mm(qs[h, rows], ks[h], NT) + strip_ref[h, :, window]
            scores = jnp.where(same, scores, masked_score)
            probs = jnp.exp(scores - logs[:, h : h + 1])
            d_probs = mm(gs[h, rows], vs[h], NT)
            inner = jnp.sum(probs * d_probs, axis=1, keepdims=True)
            d_scores = (probs * (d_probs - inner)).astype(BF16)
            dstrip[h, :, window] = dstrip[h, :, window] + d_scores.astype(F32)
            dq[h, rows] = mm(d_scores, ks[h]).astype(BF16)
            dkt[h] = dkt[h] + mm(qt[h, :, rows], d_scores)
            dvt[h] = dvt[h] + mm(gt[h, :, rows], probs.astype(BF16))

    outs = [dq[h] for h in range(heads)]
    outs += [dkt[h].T.astype(BF16) for h in range(heads)]
    outs += [dvt[h].T.astype(BF16) for h in range(heads)]
    dqkv_ref[...] = jnp.concatenate(outs, axis=1)
    sums = []
    for target, which in ((dn_send, other), (dn_keep, mine)):
        dn = mm(dqkv_ref[which], wbuf[:, : 3 * head_cols], NT)
        values = x_ref[which].astype(F32)
        sums.append(fold_rows(dn * values * rms_scale(values)))
        target[...] = dn.astype(BF16)
    gain_sum[...] = sums[0] + sums[1]


def back(buffer, ends, offs, order, near, far, qkv, logs, strip, x, o_pieces, p_pieces, heads):
    length = qkv.shape[0]
    half = length // 2
    width = x.shape[1]
    head_cols = heads * DH
    counts = (len(o_pieces), len(p_pieces))
    whole = lambda i, *_: (0, 0)
    whole3 = lambda i, *_: (0, 0, 0)
    spec = pltpu.PrefetchScalarGridSpec(
        num_scalar_prefetch=3,
        grid=(1,),
        in_specs=[
            pl.BlockSpec((half, width), whole),
            pl.BlockSpec((half, width), whole),
            pl.BlockSpec(qkv.shape, whole),
            pl.BlockSpec(logs.shape, whole),
            pl.BlockSpec(strip.shape, whole3),
            pl.BlockSpec((length, width), lambda i, *_: (buffer, 0)),
        ]
        + [pl.BlockSpec(memory_space=ANY)] * sum(counts),
        out_specs=[
            pl.BlockSpec((length, width), whole),
            pl.BlockSpec((length, 3 * head_cols), whole),
            pl.BlockSpec((half, width), whole),
            pl.BlockSpec((half, width), whole),
            pl.BlockSpec((8, width), whole),
            pl.BlockSpec(strip.shape, whole3),
        ],
        scratch_shapes=[
            pltpu.VMEM((width, p_pieces[0].shape[1]), BF16),
            pltpu.VMEM((width, o_pieces[0].shape[1]), BF16),
            pltpu.VMEM((heads, length, DH), BF16),
            pltpu.VMEM((heads, length, DH), BF16),
            pltpu.VMEM((heads, length, DH), BF16),
            pltpu.VMEM((heads, length, DH), BF16),
            pltpu.VMEM((heads, DH, length), BF16),
            pltpu.VMEM((heads, DH, length), BF16),
            pltpu.VMEM((heads, DH, length), F32),
            pltpu.VMEM((heads, DH, length), F32),
            pltpu.VMEM((heads, length, DH), BF16),
            pltpu.SemaphoreType.DMA((2, max(counts))),
        ],
    )
    return pl.pallas_call(
        functools.partial(back_kernel, buffer, ends.shape[1], heads, counts),
        grid_spec=spec,
        out_shape=[
            jax.ShapeDtypeStruct((length, width), BF16),
            jax.ShapeDtypeStruct((length, 3 * head_cols), BF16),
            jax.ShapeDtypeStruct((half, width), BF16),
            jax.ShapeDtypeStruct((half, width), BF16),
            jax.ShapeDtypeStruct((8, width), F32),
            jax.ShapeDtypeStruct(strip.shape, F32),
        ],
        compiler_params=params(),
        cost_estimate=pl.CostEstimate(
            flops=40 * heads * DH * length * length,
            bytes_accessed=16 << 20,
            transcendentals=heads * length * length,
        ),
        name="back",
    )(ends, offs, order, near, far, qkv, logs, strip, x, *o_pieces, *p_pieces)


def scatter_rows(total, offs_ref, evens, odds):
    rows = evens[0].shape[0]
    for at in range(2 * len(evens)):
        begin = pl.multiple_of(offs_ref[at], 8)
        block = total[pl.ds(begin, rows)]
        if at % 2:
            odds[at // 2][...] = block.astype(BF16)
        else:
            evens[at // 2][...] = block


def feed_grad_kernel(count, hidden_cols, offs_ref, *refs):
    buffers = 2
    normed = refs[:buffers]
    gates = refs[buffers : 2 * buffers]
    hiddens = refs[2 * buffers : 3 * buffers]
    cot_ref = refs[3 * buffers]
    outs = refs[3 * buffers + 1 : -1]
    total = refs[-1]
    length = normed[0].shape[0]
    width = normed[0].shape[1]
    part = 256
    for begin in range(0, width, part):
        cols = slice(begin, begin + part)
        total[cols, : 2 * hidden_cols] = mm(normed[0][:, cols], gates[0][...], TN) + mm(
            normed[1][:, cols], gates[1][...], TN
        )
        total[cols, 2 * hidden_cols :] = mm(
            cot_ref[:length, cols], hiddens[0][...], TN
        ) + mm(cot_ref[length:, cols], hiddens[1][...], TN)
    if count > 1:
        scatter_rows(total, offs_ref, outs[: count // 2], outs[count // 2 :])
    else:
        outs[0][...] = total[...]


def attend_grad_kernel(count, heads, offs_ref, *refs):
    buffers = 2
    normed = refs[:buffers]
    dqkv = refs[buffers : 2 * buffers]
    lows = refs[2 * buffers : 3 * buffers]
    atts = refs[3 * buffers : 4 * buffers]
    sums_ref = refs[4 * buffers]
    outs = refs[4 * buffers + 1 : -1]
    total = refs[-1]
    width = normed[0].shape[1]
    head_cols = heads * DH
    qkv_cols = 3 * head_cols
    part = 256
    rows = lax.broadcasted_iota(jnp.int32, (LANES, width), 0)
    first = sums_ref[0] + sums_ref[1]
    second = sums_ref[2] + sums_ref[3]
    gain_rows = jnp.where(
        rows == DH,
        jnp.sum(first, axis=0, keepdims=True),
        jnp.where(rows == DH + 1, jnp.sum(second, axis=0, keepdims=True), 0.0),
    )
    gain_cols = gain_rows.T
    for begin in range(0, width, part):
        cols = slice(begin, begin + part)
        total[cols, :qkv_cols] = mm(normed[0][:, cols], dqkv[0][...], TN) + mm(
            normed[1][:, cols], dqkv[1][...], TN
        )
        total[cols, qkv_cols : qkv_cols + DH] = gain_cols[cols, DH:]
        total[cols, qkv_cols + DH : qkv_cols + DH + head_cols] = mm(
            lows[0][:, cols], atts[0][...], TN
        ) + mm(lows[1][:, cols], atts[1][...], TN)
    if count > 1:
        scatter_rows(total, offs_ref, outs[: count // 2], outs[count // 2 :])
    else:
        outs[0][...] = total[...]


def grad_call(kernel, name, offs, operands, width, cols, count, rows, flops):
    vmem = pl.BlockSpec(memory_space=pltpu.VMEM)
    if count > 1:
        shapes = [jax.ShapeDtypeStruct((rows, cols), F32)] * (count // 2)
        shapes += [jax.ShapeDtypeStruct((rows, cols), BF16)] * (count // 2)
    else:
        shapes = [jax.ShapeDtypeStruct((width, cols), F32)]
    return pl.pallas_call(
        kernel,
        in_specs=[pl.BlockSpec(memory_space=pltpu.SMEM)] + [vmem] * len(operands),
        out_specs=[vmem] * len(shapes),
        out_shape=shapes,
        scratch_shapes=[pltpu.VMEM((width, cols), F32)],
        compiler_params=params(),
        cost_estimate=pl.CostEstimate(flops=2 * flops, bytes_accessed=14 << 20, transcendentals=0),
        name=name,
    )(offs, *operands)


def bucket_kernel(heads, near_ref, far_ref, out_ref):
    lanes = near_ref.shape[2]
    blocks = (lanes // LANES + 1) // 2
    begin = (blocks - 2) * LANES
    end = begin + 3 * LANES
    rows = lax.broadcasted_iota(jnp.int32, (LANES, 3 * LANES), 0)
    ids = bucket_of(
        lax.broadcasted_iota(jnp.int32, (LANES, 3 * LANES), 1) - LANES - rows
    )
    lane = lax.broadcasted_iota(jnp.int32, (1, LANES), 1)
    out = jnp.zeros((1, LANES), F32)
    for h in range(heads):
        strip = near_ref[h] + far_ref[h]
        left = jnp.sum(jnp.sum(strip[:, :begin], axis=0, keepdims=True), axis=1, keepdims=True)
        right = jnp.sum(jnp.sum(strip[:, end:], axis=0, keepdims=True), axis=1, keepdims=True)
        out = out + jnp.where(lane == h * 32 + 15, left, 0.0)
        out = out + jnp.where(lane == h * 32 + 31, right, 0.0)
        middle = strip[:, begin:end]
        for b in range(32):
            if b == 16:
                continue
            part = jnp.sum(jnp.where(ids == b, middle, 0.0), axis=0, keepdims=True)
            part = jnp.sum(part, axis=1, keepdims=True)
            out = out + jnp.where(lane == h * 32 + b, part, 0.0)
    out_ref[...] = jnp.broadcast_to(out, (8, LANES))


def norm_kernel(wide, narrow, lists, gain_at, *refs):
    at = 0
    groups = []
    for count in lists:
        groups.append(refs[at : at + count])
        at += count
    bucket_ref = refs[at]
    outs = refs[at + 1 : at + 1 + len(lists)]
    stat_ref, gain_ref, table_ref, block, inbox, padded, send_sems, recv_sems = refs[
        at + 1 + len(lists) :
    ]
    total = wide * narrow
    w = lax.axis_index("wide")
    n = lax.axis_index("narrow")
    me = w * narrow + n
    barrier = pltpu.get_barrier_semaphore()

    @pl.loop(1, total)
    def _(k):
        peer = (me + k) % total
        pl.semaphore_signal(
            barrier, inc=1, device_id=(peer // narrow, peer % narrow), device_id_type=MESH
        )

    squares = jnp.zeros((8, LANES), F32)
    for which, (group, out) in enumerate(zip(groups, outs)):
        value = group[0][...].astype(F32)
        for more in group[1:]:
            value = value + more[...].astype(F32)
        out[...] = value
        squared = value * value
        if which == 0:
            lane = lax.broadcasted_iota(jnp.int32, value.shape, 1)
            inside = (lane >= gain_at) & (lane < gain_at + DH)
            squared = jnp.where(inside, 0.0, squared)
        squared = jnp.sum(squared, axis=1, keepdims=True)
        squares = squares + jnp.sum(squared, axis=0, keepdims=True)
    rows = outs[0].shape[0]
    low = gain_at // LANES * LANES
    padded[...] = jnp.zeros_like(padded)
    padded[0:rows] = outs[0][:, low : low + LANES]
    turned = padded[...].T
    row = lax.broadcasted_iota(jnp.int32, (8, LANES), 0)
    here = gain_at - low
    mine = jnp.where(row == 0, squares, 0.0)
    mine = jnp.where(row == 1, turned[here : here + 1], mine)
    mine = jnp.where(row == 2, turned[here + 1 : here + 2], mine)
    mine = jnp.where(row == 3, bucket_ref[...], mine)
    block[...] = mine
    inbox[me] = mine
    pl.semaphore_wait(barrier, total - 1)

    @pl.loop(1, total)
    def _(k):
        peer = (me + k) % total
        pltpu.make_async_remote_copy(
            src_ref=block,
            dst_ref=inbox.at[me],
            send_sem=send_sems.at[k],
            recv_sem=recv_sems.at[total - k],
            device_id=(peer // narrow, peer % narrow),
            device_id_type=MESH,
        ).start()

    @pl.loop(1, total)
    def _(k):
        peer = (me + k) % total
        copy = pltpu.make_async_remote_copy(
            src_ref=block,
            dst_ref=inbox.at[peer],
            send_sem=send_sems.at[k],
            recv_sem=recv_sems.at[k],
            device_id=(peer // narrow, peer % narrow),
            device_id_type=MESH,
        )
        copy.wait_send()
        copy.wait_recv()

    columns = [jnp.zeros((8, LANES), F32) for _ in range(narrow)]
    gain_square = jnp.zeros((8, LANES), F32)
    square_total = jnp.zeros((8, LANES), F32)
    for a in range(wide):
        gains = jnp.zeros((8, LANES), F32)
        for b in range(narrow):
            got = inbox[a * narrow + b]
            gains = gains + got
            columns[b] = columns[b] + got
        square_total = square_total + gains
        gain_square = gain_square + gains * gains
    own = inbox[w * narrow]
    for b in range(1, narrow):
        own = own + inbox[w * narrow + b]
    gain_ref[...] = own
    pick = (row == 1) | (row == 2)
    gain_square = jnp.where(pick, gain_square, 0.0)
    norm_square = square_total[0:1, 0:1] + jnp.sum(
        jnp.sum(gain_square, axis=0, keepdims=True), axis=1, keepdims=True
    )
    heads = LANES // 32 - 1
    lane = lax.broadcasted_iota(jnp.int32, (32, LANES), 1)
    depth = lax.broadcasted_iota(jnp.int32, (32, LANES), 0)
    table = jnp.zeros((32, LANES), F32)
    for b in range(narrow):
        line = columns[b][3:4]
        norm_square = norm_square + jnp.sum(line * line, axis=1, keepdims=True)
        for h in range(heads):
            column = jnp.sum(
                jnp.where(lane == depth + 32 * h, line, 0.0), axis=1, keepdims=True
            )
            table = jnp.where(lane == b * heads + h, column, table)
    table_ref[...] = table
    global_norm = jnp.sqrt(norm_square)
    factor = jnp.minimum(1.0, clip_limit / (global_norm + 1e-06))
    stat_ref[...] = jnp.where(row == 0, global_norm, factor)


def norm_call(wide, narrow, groups, bucket, gain_at):
    vmem = pl.BlockSpec(memory_space=pltpu.VMEM)
    lists = tuple(len(group) for group in groups)
    total = wide * narrow
    operands = [piece for group in groups for piece in group] + [bucket]
    return pl.pallas_call(
        functools.partial(norm_kernel, wide, narrow, lists, gain_at),
        in_specs=[vmem] * len(operands),
        out_specs=[vmem] * (len(lists) + 3),
        out_shape=[jax.ShapeDtypeStruct(group[0].shape, F32) for group in groups]
        + [
            jax.ShapeDtypeStruct((8, LANES), F32),
            jax.ShapeDtypeStruct((8, LANES), F32),
            jax.ShapeDtypeStruct((32, LANES), F32),
        ],
        scratch_shapes=[
            pltpu.VMEM((8, LANES), F32),
            pltpu.VMEM((total, 8, LANES), F32),
            pltpu.VMEM((LANES, LANES), F32),
            pltpu.SemaphoreType.DMA((total,)),
            pltpu.SemaphoreType.DMA((total,)),
        ],
        compiler_params=params(collective_id=0, has_side_effects=True),
        cost_estimate=pl.CostEstimate(flops=1 << 20, bytes_accessed=4 << 20, transcendentals=0),
        name="norm",
    )(*operands)


def adam_kernel(heads, hidden_cols, parts, att_ref, feed_ref, gain_ref, table_ref, stat_ref, *refs):
    weights, firsts, seconds = refs[:6], refs[6:12], refs[12:18]
    outs = refs[18:36]
    o_pad, s_pad = refs[36:]
    factor = stat_ref[1:2, 0:1]
    head_cols = heads * DH
    rows = att_ref.shape[0]
    gain_at = 3 * head_cols

    def update(which, index, gradient):
        results = adam_update(
            weights[which][index],
            firsts[which][index],
            seconds[which][index],
            factor * gradient,
            step_rates[which],
            decay_rates[which],
        )
        for at in range(3):
            outs[6 * at + which][index] = results[at]

    for i in range(3):
        update(0, i, att_ref[:, i * head_cols : (i + 1) * head_cols])
    part = hidden_cols // parts
    for j in range(parts):
        span = slice(j * part, (j + 1) * part)
        for i in range(2):
            begin = (3 * j + i) * part if parts > 1 else i * part
            update(2, (i, slice(None), span), feed_ref[:, begin : begin + part])
    o_pad[...] = jnp.zeros_like(o_pad)
    s_pad[...] = jnp.zeros_like(s_pad)
    o_pad[0:rows] = att_ref[:, gain_at + DH :]
    for j in range(parts):
        begin = (3 * j + 2) * part
        s_pad[0:rows, j * part : (j + 1) * part] = feed_ref[:, begin : begin + part]
    update(1, slice(None), o_pad[...].T[:head_cols, :rows])
    update(3, slice(None), s_pad[...].T[:, :rows])
    columns = weights[4].shape[1]
    update(4, slice(None), table_ref[:, :columns])
    update(5, slice(None), gain_ref[1:3, :rows])


def adam_call(
    att, feed_grad, gain, table, stat, params_in, firsts, seconds, heads, hidden_cols, direct=False
):
    vmem = pl.BlockSpec(memory_space=pltpu.VMEM)
    operands = [att, feed_grad, gain, table, stat, *params_in, *firsts, *seconds]
    pad_cols = att.shape[1] - (3 * heads * DH + DH)
    return pl.pallas_call(
        functools.partial(adam_kernel, heads, hidden_cols, 2 if direct else 1),
        in_specs=[vmem] * len(operands),
        out_specs=[vmem] * 18,
        out_shape=[jax.ShapeDtypeStruct(a.shape, F32) for a in params_in] * 3,
        scratch_shapes=[
            pltpu.VMEM((LANES, pad_cols), F32),
            pltpu.VMEM((LANES, hidden_cols), F32),
        ],
        compiler_params=params(),
        cost_estimate=pl.CostEstimate(flops=4 << 20, bytes_accessed=8 << 20, transcendentals=0),
        name="adam",
    )(*operands)


def place_kernel(offs_ref, *refs):
    step = pl.program_id(0)
    for at, piece in enumerate(refs[:-1]):

        @pl.when(step == at)
        def _(piece=piece):
            refs[-1][...] = piece[...]


def place(pieces, offs, rows):
    half, width = pieces[0].shape
    count = len(pieces)
    return pl.pallas_call(
        place_kernel,
        grid_spec=pltpu.PrefetchScalarGridSpec(
            num_scalar_prefetch=1,
            grid=(count,),
            in_specs=[pl.BlockSpec((half, width), lambda i, *_: (0, 0))] * count,
            out_specs=pl.BlockSpec((half, width), lambda i, offs: (offs[i] // half, 0)),
        ),
        out_shape=jax.ShapeDtypeStruct((rows, width), pieces[0].dtype),
        compiler_params=params(),
        cost_estimate=pl.CostEstimate(
            flops=0, bytes_accessed=4 * rows * width, transcendentals=0
        ),
        name="place",
    )(offs, *pieces)


def bias_strip(bucket_bias, n, heads, length):
    table = lax.dynamic_slice_in_dim(bucket_bias, n * heads, heads, 1).T
    blocks = length // LANES
    near_r = (
        jnp.arange(3 * LANES, dtype=jnp.int32)[None, :]
        - LANES
        - jnp.arange(LANES, dtype=jnp.int32)[:, None]
    )
    near_ids = bucket_of(near_r)
    near = sum(
        jnp.where(near_ids == b, table[:, b][:, None, None], 0.0) for b in range(32) if b != 16
    )
    far_shape = (heads, LANES, (blocks - 2) * LANES)
    return jnp.concatenate(
        [
            jnp.broadcast_to(table[:, 15][:, None, None], far_shape),
            near,
            jnp.broadcast_to(table[:, 31][:, None, None], far_shape),
        ],
        axis=2,
    )


def general_body(wide, narrow, *arguments):
    (
        block_input,
        cotangent,
        lengths,
        project_weight,
        output_weight,
        expand_weight,
        shrink_weight,
        bucket_bias,
        norm_gains,
    ) = arguments[:9]
    firsts = arguments[9:15]
    seconds = arguments[15:21]
    tokens, width = block_input.shape
    buffers = lengths.shape[0]
    length = tokens // buffers
    rows = norm_gains.shape[1]
    head_cols = project_weight.shape[2]
    heads = head_cols // DH
    hidden_cols = expand_weight.shape[2]
    w = lax.axis_index("wide")
    n = lax.axis_index("narrow")
    core = n % 2

    def swap(value, wide_mask, narrow_mask):
        pairs = [
            (a * narrow + b, (a ^ wide_mask) * narrow + (b ^ narrow_mask))
            for a in range(wide)
            for b in range(narrow)
        ]
        return lax.ppermute(value, ("wide", "narrow"), pairs)

    def gather(piece):
        return [lax.all_gather(piece, "wide", axis=0, tiled=True)]

    def reduce_wide(outs):
        return [lax.psum_scatter(outs[0], "wide", scatter_dimension=0, tiled=True)]

    offs = jnp.zeros((1,), jnp.int32)
    order = jnp.stack([1 - core, core, n // 2])

    p_piece = jnp.concatenate(
        [
            project_weight[0],
            project_weight[1],
            project_weight[2],
            norm_gains.T,
            jnp.zeros((rows, DH - 2), F32),
        ],
        axis=1,
    ).astype(BF16)
    p_pieces = gather(p_piece)
    o_piece = output_weight.astype(BF16).T
    o_pair = jnp.concatenate([o_piece, swap(o_piece, 0, 2)], axis=1)
    oa_pieces = gather(o_pair)
    ob_pieces = [swap(piece, 0, 1) for piece in oa_pieces]
    e_pieces = gather(
        jnp.concatenate([expand_weight[0], expand_weight[1]], axis=1).astype(BF16)
    )
    s_pieces = gather(shrink_weight.astype(BF16).T)

    ends = jnp.cumsum(lengths, axis=1)
    strip = bias_strip(bucket_bias, n, heads, length)

    normed_one, qkv, atts, logs, fours = [], [], [], [], []
    for b in range(buffers):
        normed, rows_b, att, log, gains = attend(
            b, ends, offs, block_input, strip, p_pieces, length, heads
        )
        normed_one.append(normed)
        qkv.append(rows_b)
        atts.append(att)
        logs.append(log)
        across = swap(att, 0, 2)
        fours.append((att, across, swap(att, 0, 1), swap(across, 0, 1)))

    def core_sum(kept, sent):
        return (kept.astype(F32) + swap(sent, 0, 1).astype(F32)).astype(BF16)

    normed_two, hiddens, gates, middles, ff_sums, dn_sums, sums_two = [], [], [], [], [], [], []
    for b in range(buffers):
        normed, hidden, gate, ff_send, ff_keep, dn_send, dn_keep, middle, sums = feed(
            b,
            order,
            offs,
            fours[b],
            block_input,
            cotangent,
            gains,
            (oa_pieces, ob_pieces, e_pieces, s_pieces),
            length,
            hidden_cols,
        )
        normed_two.append(normed)
        hiddens.append(hidden)
        gates.append(gate)
        middles.append(middle)
        sums_two.append(sums)
        dn_sums.append(core_sum(dn_keep, dn_send))
        ff_sums.append(core_sum(ff_keep, ff_send))

    d_middles, lows = [], []
    for b in range(buffers):
        d_middle, low = half_call(
            middle_kernel,
            "middle",
            b,
            order,
            [dn_sums[b], swap(dn_sums[b], 0, 2), middles[b], cotangent],
            (3,),
            (F32, BF16),
            gains,
        )
        d_middles.append(d_middle)
        lows.append((low, swap(low, 0, 1)))

    count = 1
    feed_outs = grad_call(
        functools.partial(feed_grad_kernel, count, hidden_cols),
        "feed_grad",
        offs,
        [*normed_two, *gates, *hiddens, cotangent],
        width,
        3 * hidden_cols,
        count,
        rows,
        2 * tokens * width * 3 * hidden_cols,
    )
    feed_group = reduce_wide(feed_outs)

    low_full, dqkv, dn_one, sums_one, strips = [], [], [], [], []
    for b in range(buffers):
        low, grads, dn_send, dn_keep, sums, dstrip = back(
            b,
            ends,
            offs,
            order,
            lows[b][0],
            lows[b][1],
            qkv[b],
            logs[b],
            strip,
            block_input,
            oa_pieces,
            p_pieces,
            heads,
        )
        low_full.append(low)
        dqkv.append(grads)
        sums_one.append(sums)
        strips.append(dstrip)
        dn_one.append(core_sum(dn_keep, dn_send))

    gain_at = 3 * head_cols
    att_outs = grad_call(
        functools.partial(attend_grad_kernel, count, heads),
        "attend_grad",
        offs,
        [*normed_one, *dqkv, *low_full, *atts, jnp.stack(sums_one + sums_two)],
        width,
        gain_at + DH + head_cols,
        count,
        rows,
        2 * tokens * width * 4 * head_cols,
    )
    att_group = reduce_wide(att_outs)
    vmem = pl.BlockSpec(memory_space=pltpu.VMEM)
    bucket = pl.pallas_call(
        functools.partial(bucket_kernel, heads),
        in_specs=[vmem, vmem],
        out_specs=vmem,
        out_shape=jax.ShapeDtypeStruct((8, LANES), F32),
        compiler_params=params(),
        cost_estimate=pl.CostEstimate(flops=8 << 20, bytes_accessed=4 << 20, transcendentals=0),
        name="bucket",
    )(*strips)

    half_offs = jnp.stack(
        [
            b * length + which * (length // 2)
            for b in range(buffers)
            for which in (core, 1 - core)
        ]
    )
    out_halves, in_halves = [], []
    for b in range(buffers):
        (half,) = half_call(
            output_kernel,
            "output",
            b,
            order,
            [ff_sums[b], swap(ff_sums[b], 0, 2), middles[b]],
            (),
            (BF16,),
        )
        out_halves += [half, swap(half, 0, 1)]
        (half,) = half_call(
            input_kernel,
            "input",
            b,
            order,
            [dn_one[b], swap(dn_one[b], 0, 2), block_input, d_middles[b]],
            (2,),
            (BF16,),
            gains,
        )
        in_halves += [half, swap(half, 0, 1)]
    block_output = place(out_halves, half_offs, tokens)
    input_gradient = place(in_halves, half_offs, tokens)

    att_grad, feed_grad, stat, gain, table_sum = norm_call(
        wide, narrow, [att_group, feed_group], bucket, gain_at
    )
    results = adam_call(
        att_grad,
        feed_grad,
        gain,
        table_sum,
        stat,
        arguments[3:9],
        firsts,
        seconds,
        heads,
        hidden_cols,
    )
    return (block_output, input_gradient, stat[0, 0], *results)


class Place:
    def __init__(self, wide, narrow):
        self.wide, self.narrow = wide, narrow
        self.w = lax.axis_index("wide")
        self.n = lax.axis_index("narrow")
        self.me = self.w * narrow + self.n
        self.z, self.x = self.w // 2, self.w % 2
        self.y, self.core = self.n // 2, self.n % 2
        self.n_far = (self.n + 2) % 4
        self.n_beside = self.n + 1 - 2 * self.core
        self.n_diag = (self.n_beside + 2) % 4
        self.across = (self.w, self.n_far)
        self.beside = (self.w, self.n_beside)
        self.flip = (self.z * 2 + 1 - self.x, self.n)

    def along(self, m):
        return (((self.z + m) % 4) * 2 + self.x, self.n)

    def near_owner(self, m):
        return ((self.z + m) % 4) * 2 + self.x

    def far_owner(self, m):
        return ((self.z + m) % 4) * 2 + 1 - self.x

    def peer(self, k):
        device = (self.me + k) % (self.wide * self.narrow)
        return device, (device // self.narrow, device % self.narrow)


def remote(source, target, send_sem, recv_sem, peer):
    return pltpu.make_async_remote_copy(
        src_ref=source,
        dst_ref=target,
        send_sem=send_sem,
        recv_sem=recv_sem,
        device_id=peer,
        device_id_type=MESH,
    )


class Gather:
    def __init__(self, spot, view, ssem, rsem, flip_first=False):
        self.spot, self.view, self.ssem, self.rsem = spot, view, ssem, rsem
        self.flip_first = flip_first

    def copy(self, owner, slot, peer):
        return remote(
            self.view(owner), self.view(owner), self.ssem.at[slot], self.rsem.at[owner], peer
        )

    def landed(self, owner):
        self.copy(owner, 0, self.spot.flip).wait_recv()

    def start(self, owner, slot, peer):
        self.copy(owner, slot, peer).start()

    def sent(self, owner, slot, peer):
        self.copy(owner, slot, peer).wait_send()

    def fan(self, owner, slot, act):
        z = self.spot.z
        act(owner, slot + 1, self.spot.along(2))
        pl.when(z != 3)(lambda: act(owner, slot, self.spot.along(1)))
        pl.when(z != 0)(lambda: act(owner, slot + 2, self.spot.along(3)))

    def pass_on(self, owner, slot, act):
        z = self.spot.z
        pl.when(z == 2)(lambda: act(owner, slot, self.spot.along(1)))
        pl.when(z == 1)(lambda: act(owner, slot, self.spot.along(3)))

    def begin(self):
        if self.flip_first:
            self.start(self.spot.w, 3, self.spot.flip)
        self.fan(self.spot.w, 0, self.start)
        if not self.flip_first:
            self.start(self.spot.w, 3, self.spot.flip)

    def forward(self):
        if self.flip_first:
            owner = self.spot.far_owner(0)
            self.landed(owner)
            self.fan(owner, 4, self.start)
            return
        owner = self.spot.near_owner(2)
        self.landed(owner)
        self.pass_on(owner, 7, self.start)
        self.start(owner, 5, self.spot.flip)
        early = 1 + 2 * ((3 - self.spot.z) // 3)
        for m in (early, 4 - early):
            owner = self.spot.near_owner(4 - m)
            self.landed(owner)
            self.start(owner, 3 + m, self.spot.flip)

    def middle(self):
        for owner, slot in ((self.spot.near_owner(2), 7), (self.spot.far_owner(2), 8)):
            self.landed(owner)
            self.pass_on(owner, slot, self.start)

    def finish(self):
        if self.flip_first:
            for m in (1, 3):
                self.landed(self.spot.near_owner(m))
                self.landed(self.spot.far_owner(m))
        else:
            for m in range(4):
                self.landed(self.spot.far_owner(m))

    def drain(self):
        self.sent(self.spot.w, 3, self.spot.flip)
        self.fan(self.spot.w, 0, self.sent)
        self.pass_on(self.spot.near_owner(2), 7, self.sent)
        if self.flip_first:
            self.fan(self.spot.far_owner(0), 4, self.sent)
            self.pass_on(self.spot.far_owner(2), 8, self.sent)
        else:
            for m in (1, 2, 3):
                self.sent(self.spot.near_owner(4 - m), 3 + m, self.spot.flip)


class Reduce:
    def __init__(self, spot, even, odd, flipped, mixed, landed, sems_s, sems_r):
        self.spot, self.even, self.odd = spot, even, odd
        self.flipped, self.mixed, self.landed = flipped, mixed, landed
        self.sems_s, self.sems_r = sems_s, sems_r

    def over(self, m):
        return remote(
            self.odd(m), self.flipped(m), self.sems_s.at[m], self.sems_r.at[m], self.spot.flip
        )

    def along(self, m):
        return remote(
            self.mixed(m - 1),
            self.landed(m - 1),
            self.sems_s.at[3 + m],
            self.sems_r.at[3 + m],
            self.spot.along(m),
        )

    def begin(self):
        for m in (2, 1, 3, 0):
            self.over(m).start()

    def relay(self, *ms):
        for m in ms:
            self.over(m).wait_recv()
            self.mixed(m - 1)[...] = (
                self.even(m).astype(F32) + self.flipped(m)[...].astype(F32)
            ).astype(BF16)
            self.along(m).start()

    def result(self):
        self.over(0).wait_recv()
        value = self.even(0).astype(F32) + self.flipped(0)[...].astype(F32)
        for m in (1, 2, 3):
            self.along(m).wait_recv()
            value = value + self.landed(m - 1)[...].astype(F32)
        return value

    def drain(self):
        for m in range(4):
            self.over(m).wait_send()
        for m in (1, 2, 3):
            self.along(m).wait_send()


def segments_of(index, lengths_ref, buffer, slots):
    end = lengths_ref[buffer, 0]
    total = (index >= end).astype(jnp.int32)
    for slot in range(1, slots):
        end = end + lengths_ref[buffer, slot]
        total = total + (index >= end).astype(jnp.int32)
    return total


def layer_kernel(dims, *refs):
    buffers, slots, heads, hidden_cols, wide, narrow = dims
    (
        lengths_ref,
        bias_ref,
        x_hbm,
        cot_hbm,
        pw_ref,
        ow_ref,
        ew_ref,
        sw_ref,
        gn_ref,
        out_ref,
        in_ref,
        p_grad,
        o_grad,
        feed_grad,
        stat_ref,
        gain_ref,
        table_ref,
        x_ref,
        cot_ref,
        strip,
        dstrip,
        pbuf,
        obuf,
        fbuf,
        att_ref,
        qkv_ref,
        log_ref,
        low_ref,
        middle_ref,
        hid,
        dg,
        total,
        opad,
        gpad,
        feed_flip,
        feed_mix,
        feed_land,
        o_even,
        o_odd,
        o_flip,
        o_mix,
        o_land,
        p_odd,
        p_flip,
        p_mix,
        p_land,
        ff_out,
        ff_in,
        ff_sum,
        dn_out,
        dn_in,
        dn_sum,
        dn_far,
        ws,
        kt,
        vt,
        qt,
        gt,
        dkt,
        dvt,
        gain_two_sum,
        block,
        inbox,
        gather_s,
        gather_r,
        lone_s,
        lone_r,
        red_s,
        red_r,
        norm_s,
        norm_r,
        credit,
        load,
        att_s,
        att_r,
    ) = refs
    spot = Place(wide, narrow)
    core = spot.core
    devices = wide * narrow
    tokens, width = x_ref.shape
    length = tokens // buffers
    half = length // 2
    head_cols = heads * DH
    qkv_cols = 3 * head_cols
    part = hidden_cols // 2
    chunk = 3 * part
    blocks = length // LANES
    owned = gn_ref.shape[1]
    normed_one, normed_two = in_ref, out_ref
    loads = [
        pltpu.make_async_copy(x_hbm, x_ref, load.at[0]),
        pltpu.make_async_copy(cot_hbm, cot_ref, load.at[1]),
    ]
    for copy in loads:
        copy.start()
    barrier = pltpu.get_barrier_semaphore()

    @pl.loop(1, devices)
    def _(k):
        pl.semaphore_signal(barrier, inc=1, device_id=spot.peer(k)[1], device_id_type=MESH)

    def at_rows(owner):
        return pl.ds(pl.multiple_of(owner * owned, 16), owned)

    def lone(view_from, view_to, slot, peer):
        return remote(view_from, view_to, lone_s.at[slot], lone_r.at[slot], peer)

    mine = at_rows(spot.w)
    gpad[...] = jnp.zeros_like(gpad)
    gpad[0:2, 0:owned] = gn_ref[...]
    pbuf[mine] = jnp.concatenate(
        [pw_ref[0], pw_ref[1], pw_ref[2], gpad[...].T[:owned, :DH]], axis=1
    ).astype(BF16)
    pl.semaphore_wait(barrier, devices - 1)
    split = 3 * LANES
    projections = [
        Gather(
            spot,
            lambda v, span=span: pbuf.at[at_rows(v), span],
            gather_s.at[at],
            gather_r.at[at],
        )
        for at, span in enumerate((slice(0, split), slice(split, qkv_cols + DH)))
    ]
    for group in projections:
        group.begin()
    opad[...] = jnp.zeros_like(opad)
    opad[0:head_cols, 0:owned] = ow_ref[...]
    obuf[spot.n, mine] = opad[...].T[:owned, :head_cols].astype(BF16)
    o_views = [
        lambda v: obuf.at[spot.n, at_rows(v)],
        lambda v: obuf.at[spot.n_far, at_rows(v)],
    ]
    outs_gather = [
        Gather(spot, view, gather_s.at[2 + at], gather_r.at[2 + at])
        for at, view in enumerate(o_views)
    ]
    lone(o_views[0](spot.w), o_views[0](spot.w), 0, spot.across).start()
    for j in range(2):
        span = slice(j * part, (j + 1) * part)
        fbuf[mine, j * chunk : j * chunk + part] = ew_ref[0, :, span].astype(BF16)
        fbuf[mine, j * chunk + part : j * chunk + 2 * part] = ew_ref[1, :, span].astype(BF16)
        fbuf[mine, j * chunk + 2 * part : (j + 1) * chunk] = sw_ref[:, span].astype(BF16)
    feed_cuts = (0, 256, 512, 768, 1024, 1280, 1536)
    feeds_gather = [
        Gather(
            spot,
            lambda v, at=at: fbuf.at[at_rows(v), feed_cuts[at] : feed_cuts[at + 1]],
            gather_s.at[4 + at],
            gather_r.at[4 + at],
            flip_first=at in (5,),
        )
        for at in range(len(feed_cuts) - 1)
    ]

    near_at = (blocks - 2) * LANES
    near_end = near_at + 3 * LANES
    near_ids = bucket_of(
        lax.broadcasted_iota(jnp.int32, (LANES, 3 * LANES), 1)
        - LANES
        - lax.broadcasted_iota(jnp.int32, (LANES, 3 * LANES), 0)
    )
    for h in range(heads):
        head = spot.n * heads + h
        near = jnp.zeros((LANES, 3 * LANES), F32)
        for b in range(32):
            if b != 16:
                near = jnp.where(near_ids == b, bias_ref[head, b], near)
        strip[h, :, near_at:near_end] = near
        strip[h, :, :near_at] = jnp.full((LANES, near_at), bias_ref[head, 15])
        strip[h, :, near_end:] = jnp.full((LANES, near_at), bias_ref[head, 31])
    lone(o_views[1](spot.w), o_views[1](spot.w), 0, spot.across).wait_recv()
    for group in outs_gather + feeds_gather:
        group.begin()
    dstrip[...] = jnp.zeros_like(dstrip)
    gain_two_sum[...] = jnp.zeros_like(gain_two_sum)

    projections[0].forward()
    projections[1].forward()
    for group in projections:
        group.finish()
    loads[0].wait()

    gains = pbuf[:, 4 * LANES :].astype(F32).T[qkv_cols - 4 * LANES : qkv_cols - 4 * LANES + 8]
    gain_one, gain_two = gains[0:1], gains[1:2]

    def relay_feeds(*ats):
        for at in ats:
            feeds_gather[at].forward()

    def relay_outs():
        for group in outs_gather:
            group.forward()

    def outs_beside():
        for group in outs_gather:
            group.finish()
        lone(obuf.at[spot.n], obuf.at[spot.n], 1, spot.beside).start()
        lone(obuf.at[spot.n_far], obuf.at[spot.n_far], 2, spot.beside).start()

    step = 256
    strides = length // step

    def att_piece(which, b, at, kind, peer):
        span = pl.ds(pl.multiple_of(b * length + at * step, step), step)
        view = att_ref.at[which, span]
        slot = (kind * buffers + b) * strides + at
        return remote(view, view, att_s.at[slot], att_r.at[slot], peer)

    def att_send(b, at):
        att_piece(spot.n, b, at, 0, spot.across).start()
        att_piece(spot.n, b, at, 1, spot.beside).start()

    def att_relay(b, pieces):
        for at in pieces:
            att_piece(spot.n_far, b, at, 0, spot.across).wait_recv()
            att_piece(spot.n_far, b, at, 2, spot.beside).start()

    qkv_events = ({}, {0: feeds_gather[1].forward})
    att_events = (
        {0: relay_outs, 1: lambda: relay_feeds(5), 2: feeds_gather[0].forward},
        {0: lambda: (outs_beside(), relay_feeds(2))[1], 1: feeds_gather[3].forward, 2: lambda: (relay_feeds(4), att_relay(0, range(1)))[1]},
    )

    def fire(events, at):
        for when, what in events.items():
            pl.when(at == when)(what)

    for b in range(buffers):
        base = b * length

        @pl.loop(0, length // step)
        def _(at, b=b, base=base):
            fire(qkv_events[b], at)
            begin = pl.multiple_of(at * step, step)
            here = pl.ds(begin, step)
            span = pl.ds(pl.multiple_of(base + begin, step), step)
            values = x_ref[span].astype(F32)
            normed = (values * rms_scale(values) * gain_one).astype(BF16)
            normed_one[span] = normed
            qkv = mm(normed, pbuf[...]).astype(BF16)
            qkv_ref[span] = qkv[:, :qkv_cols]
            for h in range(heads):
                k_at = head_cols + h * DH
                v_at = 2 * head_cols + h * DH
                kt[h, :, here] = qkv[:, k_at : k_at + DH].T
                ws[h, here] = qkv[:, v_at : v_at + DH]

        seg_keys = segments_of(
            lax.broadcasted_iota(jnp.int32, (1, length), 1), lengths_ref, b, slots
        )

        @pl.loop(0, blocks // 2)
        def _(at, b=b, base=base, seg_keys=seg_keys):
            fire(att_events[b], at)
            begin = pl.multiple_of(at * 2 * LANES, 2 * LANES)
            span = pl.ds(pl.multiple_of(base + begin, 2 * LANES), 2 * LANES)
            windows = [
                pl.ds(pl.multiple_of((blocks - 1 - r - 2 * at) * LANES, LANES), length)
                for r in range(2)
            ]
            seg_rows = segments_of(
                lax.broadcasted_iota(jnp.int32, (2 * LANES, 1), 0) + begin, lengths_ref, b, slots
            )
            same = seg_rows == seg_keys
            lane = lax.broadcasted_iota(jnp.int32, (2 * LANES, LANES), 1)
            logs = jnp.zeros((2 * LANES, LANES), F32)
            queries = qkv_ref[span, :head_cols]
            outs = []
            for h in range(heads):
                scores = mm(queries[:, h * DH : (h + 1) * DH], kt[h]) + jnp.concatenate(
                    [strip[h, :, window] for window in windows], axis=0
                )
                scores = jnp.where(same, scores, masked_score)
                row_max = jnp.max(scores, axis=1, keepdims=True)
                raised = jnp.exp(scores - row_max)
                sums = jnp.sum(raised, axis=1, keepdims=True)
                probs = (raised * (1.0 / sums)).astype(BF16)
                outs.append(mm(probs, ws[h]).astype(BF16))
                logs = jnp.where(lane == h, row_max + jnp.log(sums), logs)
            log_ref[span] = logs
            att_ref[spot.n, span] = jnp.concatenate(outs, axis=1)
            att_send(b, at)

        if b == 1:
            att_relay(0, range(1, strides))

    k0 = 0.7978845608028654
    k1 = 0.044715

    def half_rows(b, which):
        return pl.ds(pl.multiple_of(b * length + which * half, LANES), half)

    def ff_core(b):
        return lone(ff_out.at[b], ff_in.at[b], 9 + b, spot.beside)

    def ff_across(b):
        return lone(ff_sum.at[b], ff_in.at[b], 11 + b, spot.across)

    def dn_core(b, turn):
        return lone(dn_out.at[b], dn_in.at[b], 13 + 2 * turn + b, spot.beside)

    def dn_across(b, turn):
        return lone(dn_sum.at[b], dn_far.at[b], 17 + 2 * turn + b, spot.across)

    def low_core(b, which):
        view = low_ref.at[half_rows(b, which)]
        return lone(view, view, 21 + b, spot.beside)

    def out_core(b, which):
        view = out_ref.at[half_rows(b, which)]
        return lone(view, view, 23 + b, spot.beside)

    def in_core(b, which):
        view = in_ref.at[half_rows(b, which)]
        return lone(view, view, 25 + b, spot.beside)

    def outs_ready():
        loads[1].wait()
        lone(obuf.at[spot.n_beside], obuf.at[spot.n_beside], 1, spot.beside).wait_recv()
        lone(obuf.at[spot.n_diag], obuf.at[spot.n_diag], 2, spot.beside).wait_recv()

    def first_feed():
        feeds_gather[5].middle()
        feeds_gather[0].finish()
        feeds_gather[1].finish()
        feeds_gather[2].finish()

    def last_feed():
        att_relay(1, range(strides))
        feeds_gather[3].finish()
        feeds_gather[4].finish()
        feeds_gather[5].finish()

    def half_of(b, keep):
        return half_rows(b, (1 - core) * (1 - keep) + core * keep)

    def hidden_part(j, rows, normed_rows):
        at = j * chunk
        both = mm(normed_rows, fbuf[:, at : at + 2 * part])
        gate, up = both[:, :part], both[:, part:]
        square = gate * gate
        tanh = jnp.tanh(k0 * (gate + k1 * (square * gate)))
        lift = 0.5 * (1.0 + tanh)
        active = gate * lift
        slope = lift + (0.5 * gate) * (1.0 - tanh * tanh) * (k0 + (3.0 * k0 * k1) * square)
        d_hidden = mm(cot_ref[rows], fbuf[:, at + 2 * part : at + 3 * part])
        hid[rows, j * part : (j + 1) * part] = (active * up).astype(BF16)
        dg[rows, 2 * j * part : (2 * j + 1) * part] = (d_hidden * up * slope).astype(BF16)
        dg[rows, (2 * j + 1) * part : (2 * j + 2) * part] = (d_hidden * active).astype(BF16)

    @pl.loop(0, buffers)
    def _(b):
        def att_ready():
            for at in range(strides):
                att_piece(spot.n_beside, b, at, 1, spot.beside).wait_recv()
                att_piece(spot.n_diag, b, at, 2, spot.beside).wait_recv()

        att_ready()

        @pl.loop(0, 2)
        def _(keep):
            pl.when((b == 0) & (keep == 0))(outs_ready)
            rows = half_of(b, keep)
            attention = mm(att_ref[0, rows], obuf[0], NT)
            for a in range(1, 4):
                attention = attention + mm(att_ref[a, rows], obuf[a], NT)
            middle = x_ref[rows].astype(F32) + attention
            normed_rows = (middle * rms_scale(middle) * gain_two).astype(BF16)
            normed_two[rows] = normed_rows

            @pl.when(keep == 1)
            def _():
                middle_ref[b] = middle

            pl.when((b == 0) & (keep == 0))(first_feed)
            hidden_part(0, rows, normed_two[rows])

        pl.when(b == 0)(last_feed)

        @pl.loop(0, 2)
        def _(keep):
            rows = half_of(b, keep)
            normed_rows = normed_two[rows]
            hidden_part(1, rows, normed_rows)
            dn = mm(dg[rows, : 2 * part], fbuf[:, : 2 * part], NT) + mm(
                dg[rows, 2 * part :], fbuf[:, chunk : chunk + 2 * part], NT
            )
            gain_two_sum[...] = gain_two_sum[...] + fold_rows(dn * normed_rows.astype(F32))
            dn = dn.astype(BF16)

            @pl.when(keep == 0)
            def _():
                dn_out[b] = dn
                dn_core(b, 0).start()

            ff = (
                mm(hid[rows, :part], fbuf[:, 2 * part : chunk], NT)
                + mm(hid[rows, part:], fbuf[:, chunk + 2 * part :], NT)
            ).astype(BF16)

            @pl.when(keep == 0)
            def _():
                ff_out[b] = ff
                ff_core(b).start()

            @pl.when(keep == 1)
            def _():
                ff_core(b).wait_recv()
                ff_sum[b] = (ff.astype(F32) + ff_in[b].astype(F32)).astype(BF16)
                dn_core(b, 0).wait_recv()
                dn_sum[b] = (dn.astype(F32) + dn_in[b].astype(F32)).astype(BF16)
                dn_across(b, 0).start()

    def own_block(b, i):
        span = pl.ds(pl.multiple_of(i * LANES, LANES), LANES)
        here = pl.ds(pl.multiple_of(b * length + core * half + i * LANES, LANES), LANES)
        return span, here

    def finish_middle(b):
        dn_across(b, 0).wait_recv()

        @pl.loop(0, half // LANES)
        def _(i):
            span, here = own_block(b, i)
            upstream = dn_sum[b, span].astype(F32) + dn_far[b, span].astype(F32)
            middle = middle_ref[b, span]
            d_middle = cot_ref[here].astype(F32) + norm_back(
                middle, rms_scale(middle), gain_two, upstream
            )
            low_ref[here] = d_middle.astype(BF16)

        pl.semaphore_signal(credit.at[b], inc=1, device_id=spot.across, device_id_type=MESH)
        low_core(b, core).start()

    for group in feeds_gather:
        group.drain()
    for b in range(buffers):
        for at in range(strides):
            att_piece(spot.n_far, b, at, 2, spot.beside).wait_send()
    feed_reds = []
    for j in range(2):
        for begin in range(0, width, step):
            cols = slice(begin, begin + step)
            total[cols, : 2 * part] = mm(
                normed_two[:, cols], dg[:, 2 * j * part : (2 * j + 2) * part], TN
            )
            total[cols, 2 * part :] = mm(cot_ref[:, cols], hid[:, j * part : (j + 1) * part], TN)
        span = slice(j * chunk, (j + 1) * chunk)
        for m in range(4):
            even = total[pl.ds(pl.multiple_of(spot.near_owner(m) * owned, 8), owned)]
            odd = total[pl.ds(pl.multiple_of(spot.far_owner(m) * owned, 8), owned)]
            fbuf[m * owned : (m + 1) * owned, span] = even.astype(BF16)
            fbuf[(4 + m) * owned : (5 + m) * owned, span] = odd.astype(BF16)
        red = Reduce(
            spot,
            lambda m, span=span: fbuf[m * owned : (m + 1) * owned, span],
            lambda m, span=span: fbuf.at[(4 + m) * owned : (5 + m) * owned, span],
            lambda m, span=span: feed_flip.at[m, :, span],
            lambda m, span=span: feed_mix.at[m, :, span],
            lambda m, span=span: feed_land.at[m, :, span],
            red_s.at[j],
            red_r.at[j],
        )
        red.begin()
        feed_reds.append(red)
    finish_middle(0)
    feed_reds[0].relay(2, 1)

    out_red = Reduce(
        spot,
        lambda m: o_even[m],
        lambda m: o_odd.at[m],
        lambda m: o_flip.at[m],
        lambda m: o_mix.at[m],
        lambda m: o_land.at[m],
        red_s.at[2],
        red_r.at[2],
    )

    def out_weight_grad():
        for begin in range(0, width, step):
            cols = slice(begin, begin + step)
            total[cols, :head_cols] = mm(low_ref[:, cols], att_ref[spot.n], TN)
        for m in range(4):
            even = total[pl.ds(pl.multiple_of(spot.near_owner(m) * owned, 8), owned), :head_cols]
            odd = total[pl.ds(pl.multiple_of(spot.far_owner(m) * owned, 8), owned), :head_cols]
            o_even[m] = even
            o_odd[m] = odd.astype(BF16)
        out_red.begin()

    gain_sums = jnp.zeros((8, width), F32)
    def second_middle():
        finish_middle(1)
        ff_across(1).start()

    back_events = (
        {
            0: lambda: feed_reds[0].relay(3),
            2: lambda: ff_across(0).start(),
            3: lambda: feed_reds[1].relay(2),
            5: lambda: (feed_reds[1].relay(1), second_middle())[1],
        },
        {0: lambda: feed_reds[1].relay(3), 3: lambda: out_red.relay(2, 1), 4: lambda: out_red.relay(3)},
    )
    for b in range(buffers):
        base = b * length
        rows = slice(base, base + length)
        low_core(b, 1 - core).wait_recv()
        if b == 1:
            out_weight_grad()
        grads = mm(low_ref[rows], obuf[spot.n]).astype(BF16)
        att_ref[spot.n_far, :length] = grads
        for h in range(heads):
            keys = qkv_ref[rows, head_cols + h * DH : head_cols + (h + 1) * DH]
            values = qkv_ref[rows, 2 * head_cols + h * DH : 2 * head_cols + (h + 1) * DH]
            ws[h] = keys
            kt[h] = keys.T
            vt[h] = values.T
            qt[h] = qkv_ref[rows, h * DH : (h + 1) * DH].T
            gt[h] = grads[:, h * DH : (h + 1) * DH].T
        dkt[...] = jnp.zeros_like(dkt)
        dvt[...] = jnp.zeros_like(dvt)
        seg_keys = segments_of(
            lax.broadcasted_iota(jnp.int32, (1, length), 1), lengths_ref, b, slots
        )

        @pl.loop(0, blocks)
        def _(at, b=b, base=base, seg_keys=seg_keys):
            fire(back_events[b], at)
            begin = pl.multiple_of(at * LANES, LANES)
            here = pl.ds(begin, LANES)
            span = pl.ds(pl.multiple_of(base + begin, LANES), LANES)
            window = pl.ds(pl.multiple_of((blocks - 1 - at) * LANES, LANES), length)
            seg_rows = segments_of(
                lax.broadcasted_iota(jnp.int32, (LANES, 1), 0) + begin, lengths_ref, b, slots
            )
            same = seg_rows == seg_keys
            logs = log_ref[span]
            queries = qkv_ref[span, :head_cols]
            incoming = att_ref[spot.n_far, here]
            outs = []
            for h in range(heads):
                cols = slice(h * DH, (h + 1) * DH)
                scores = mm(queries[:, cols], kt[h]) + strip[h, :, window]
                scores = jnp.where(same, scores, masked_score)
                probs = jnp.exp(scores - logs[:, h : h + 1])
                d_probs = mm(incoming[:, cols], vt[h])
                inner = jnp.sum(probs * d_probs, axis=1, keepdims=True)
                d_scores = (probs * (d_probs - inner)).astype(BF16)
                dstrip[h, :, window] = dstrip[h, :, window] + d_scores.astype(F32)
                outs.append(mm(d_scores, ws[h]).astype(BF16))
                dkt[h] = dkt[h] + mm(qt[h, :, here], d_scores)
                dvt[h] = dvt[h] + mm(gt[h, :, here], probs.astype(BF16))
            dg[span, :head_cols] = jnp.concatenate(outs, axis=1)

        outs = [dkt[h].T.astype(BF16) for h in range(heads)]
        outs += [dvt[h].T.astype(BF16) for h in range(heads)]
        dg[rows, head_cols:qkv_cols] = jnp.concatenate(outs, axis=1)
        for keep in range(2):
            which = core if keep else 1 - core
            here = half_rows(b, which)
            if keep == 0:
                dn_core(b, 0).wait_send()
            else:
                dn_across(b, 0).wait_send()
            dn = mm(dg[here, :qkv_cols], pbuf[:, :qkv_cols], NT)
            values = x_ref[here].astype(F32)
            gain_sums = gain_sums + fold_rows(dn * values * rms_scale(values))
            dn = dn.astype(BF16)
            if keep == 0:
                dn_out[b] = dn
                dn_core(b, 1).start()
            else:
                dn_core(b, 1).wait_recv()
                dn_sum[b] = (dn.astype(F32) + dn_in[b].astype(F32)).astype(BF16)
                pl.semaphore_wait(credit.at[b], 1)
                dn_across(b, 1).start()

    row = lax.broadcasted_iota(jnp.int32, (LANES, width), 0)
    gain_rows = jnp.where(
        row == DH,
        jnp.sum(gain_sums, axis=0, keepdims=True),
        jnp.where(
            row == DH + 1, jnp.sum(gain_two_sum[...], axis=0, keepdims=True) / gain_two, 0.0
        ),
    )
    gain_cols = gain_rows.T
    p_cols = qkv_cols + DH
    p_reds = []
    for at, span in enumerate((slice(0, split), slice(split, p_cols))):
        stop = min(span.stop, qkv_cols)
        for begin in range(0, width, step):
            cols = slice(begin, begin + step)
            total[cols, span.start : stop] = mm(
                normed_one[:, cols], dg[:, span.start : stop], TN
            )
            if at:
                total[cols, qkv_cols:p_cols] = gain_cols[cols, DH:]
        for m in range(4):
            odd = total[pl.ds(pl.multiple_of(spot.far_owner(m) * owned, 8), owned), span]
            p_odd[m, :, span] = odd.astype(BF16)
        red = Reduce(
            spot,
            lambda m, span=span: total[
                pl.ds(pl.multiple_of(spot.near_owner(m) * owned, 8), owned), span
            ],
            lambda m, span=span: p_odd.at[m, :, span],
            lambda m, span=span: p_flip.at[m, :, span],
            lambda m, span=span: p_mix.at[m, :, span],
            lambda m, span=span: p_land.at[m, :, span],
            red_s.at[3 + at],
            red_r.at[3 + at],
        )
        red.begin()
        p_reds.append(red)

    def finish_out(b):
        ff_across(b).wait_recv()

        @pl.loop(0, half // LANES)
        def _(i):
            span, here = own_block(b, i)
            joined = (ff_sum[b, span].astype(F32) + ff_in[b, span].astype(F32)).astype(BF16)
            out_ref[here] = (middle_ref[b, span] + joined.astype(F32)).astype(BF16)

        out_core(b, core).start()

    def finish_in(b):
        dn_across(b, 1).wait_recv()

        @pl.loop(0, half // LANES)
        def _(i):
            span, here = own_block(b, i)
            upstream = dn_sum[b, span].astype(F32) + dn_far[b, span].astype(F32)
            values = x_ref[here].astype(F32)
            in_ref[here] = (
                low_ref[here].astype(F32)
                + norm_back(values, rms_scale(values), gain_one, upstream)
            ).astype(BF16)

        in_core(b, core).start()

    def square_of(value):
        return jnp.sum(jnp.sum(value * value, axis=1, keepdims=True), axis=0, keepdims=True)

    finish_out(0)
    p_reds[0].relay(2, 1, 3)
    finish_out(1)
    squares = jnp.zeros((1, 1), F32)
    for j in range(2):
        value = feed_reds[j].result()
        feed_grad[:, j * chunk : (j + 1) * chunk] = value
        squares = squares + square_of(value)
    p_reds[1].relay(2, 1, 3)
    value = out_red.result()
    o_grad[...] = value
    squares = squares + square_of(value)
    for b in range(buffers):
        out_core(b, 1 - core).wait_recv()
    finish_in(0)

    near_row = lax.broadcasted_iota(jnp.int32, (LANES, 4 * LANES), 0)
    diag = lax.broadcasted_iota(jnp.int32, (1, 4 * LANES), 1)
    ids = bucket_of(jnp.where(diag < 3 * LANES, diag - LANES, diag - 5 * LANES))
    lane = lax.broadcasted_iota(jnp.int32, (1, LANES), 1)
    onehot = jnp.where(near_row == ids, 1.0, 0.0)
    bucket_line = jnp.zeros((1, LANES), F32)
    for h in range(heads):
        left = jnp.sum(jnp.sum(dstrip[h, :, :near_at], axis=0, keepdims=True), axis=1, keepdims=True)
        right = jnp.sum(
            jnp.sum(dstrip[h, :, near_end:], axis=0, keepdims=True), axis=1, keepdims=True
        )
        near = jnp.concatenate(
            [dstrip[h, :, near_at:near_end], jnp.zeros((LANES, LANES), F32)], axis=1
        )
        for k in range(7):
            near = jnp.where(
                (near_row // (1 << k)) % 2 == 1, pltpu.roll(near, 4 * LANES - (1 << k), 1), near
            )
        binned = lax.dot_general(
            jnp.broadcast_to(jnp.sum(near, axis=0, keepdims=True), (8, 4 * LANES)),
            onehot,
            NT,
            precision=lax.Precision.HIGHEST,
            preferred_element_type=F32,
        )[0:1]
        binned = binned + jnp.where(lane == 15, left, 0.0) + jnp.where(lane == 31, right, 0.0)
        binned = jnp.where(lane < 32, binned, 0.0)
        bucket_line = bucket_line + (pltpu.roll(binned, 32 * h, 1) if h else binned)

    value = p_reds[0].result()
    p_grad[:, :split] = value
    squares = squares + square_of(value)
    value = p_reds[1].result()
    p_grad[:, split:] = value
    kept = lax.broadcasted_iota(jnp.int32, value.shape, 1) < qkv_cols - split
    squares = squares + square_of(jnp.where(kept, value, 0.0))
    low_lane = qkv_cols // LANES * LANES
    gpad[...] = jnp.zeros_like(gpad)
    gpad[0:owned, : p_cols - low_lane] = value[:, low_lane - split :]
    turned = gpad[...].T
    here = qkv_cols - low_lane
    row8 = lax.broadcasted_iota(jnp.int32, (8, LANES), 0)
    line = jnp.where(row8 == 0, squares, 0.0)
    line = jnp.where(row8 == 1, turned[here : here + 1], line)
    line = jnp.where(row8 == 2, turned[here + 1 : here + 2], line)
    line = jnp.where(row8 == 3, bucket_line, line)
    block[...] = line
    inbox[spot.me] = line

    @pl.loop(1, devices)
    def _(k):
        peer, where = spot.peer(k)
        remote(block, inbox.at[spot.me], norm_s.at[k], norm_r.at[devices - k], where).start()

    finish_in(1)

    @pl.loop(1, devices)
    def _(k):
        peer, where = spot.peer(k)
        copy = remote(block, inbox.at[peer], norm_s.at[k], norm_r.at[k], where)
        copy.wait_send()
        copy.wait_recv()

    columns = [jnp.zeros((8, LANES), F32) for _ in range(narrow)]
    gain_square = jnp.zeros((8, LANES), F32)
    square_total = jnp.zeros((8, LANES), F32)
    for a in range(wide):
        summed = jnp.zeros((8, LANES), F32)
        for c in range(narrow):
            got = inbox[a * narrow + c]
            summed = summed + got
            columns[c] = columns[c] + got
        square_total = square_total + summed
        gain_square = gain_square + summed * summed
    own = inbox[spot.w * narrow]
    for c in range(1, narrow):
        own = own + inbox[spot.w * narrow + c]
    gain_ref[...] = own
    gain_square = jnp.where((row8 == 1) | (row8 == 2), gain_square, 0.0)
    norm_square = square_total[0:1, 0:1] + jnp.sum(
        jnp.sum(gain_square, axis=1, keepdims=True), axis=0, keepdims=True
    )
    table_row = lax.broadcasted_iota(jnp.int32, (16, LANES), 0)
    table = jnp.zeros((16, LANES), F32)
    for c in range(narrow):
        got = columns[c][3:4]
        norm_square = norm_square + jnp.sum(got * got, axis=1, keepdims=True)
        for h in range(heads):
            moved = pltpu.roll(got, LANES - 32 * h, 1) if h else got
            table = jnp.where(table_row == c * heads + h, moved, table)
    table_ref[...] = table
    global_norm = jnp.sqrt(norm_square)
    factor = jnp.minimum(1.0, clip_limit / (global_norm + 1e-06))
    stat_ref[...] = jnp.where(row8 == 0, global_norm, factor)

    for b in range(buffers):
        in_core(b, 1 - core).wait_recv()
        for at in range(strides):
            att_piece(spot.n, b, at, 0, spot.across).wait_send()
            att_piece(spot.n, b, at, 1, spot.beside).wait_send()
        ff_core(b).wait_send()
        ff_across(b).wait_send()
        dn_core(b, 1).wait_send()
        dn_across(b, 1).wait_send()
        low_core(b, core).wait_send()
        out_core(b, core).wait_send()
        in_core(b, core).wait_send()
    lone(o_views[0](spot.w), o_views[0](spot.w), 0, spot.across).wait_send()
    lone(obuf.at[spot.n], obuf.at[spot.n], 1, spot.beside).wait_send()
    lone(obuf.at[spot.n_far], obuf.at[spot.n_far], 2, spot.beside).wait_send()
    for group in projections + outs_gather:
        group.drain()
    for group in feed_reds + p_reds + [out_red]:
        group.drain()


def layer(wide, narrow, lengths, bias, x, cot, pw, ow, ew, sw, gn):
    tokens, width = x.shape
    buffers, slots = lengths.shape
    length = tokens // buffers
    half = length // 2
    head_cols = pw.shape[2]
    heads = head_cols // DH
    hidden_cols = ew.shape[2]
    rows = gn.shape[1]
    devices = wide * narrow
    qkv_cols = 3 * head_cols
    p_cols = qkv_cols + DH
    feed_cols = 3 * hidden_cols
    strip_shape = (heads, LANES, (2 * (length // LANES) - 1) * LANES)
    vmem = pl.BlockSpec(memory_space=pltpu.VMEM)
    smem = pl.BlockSpec(memory_space=pltpu.SMEM)
    halves = pltpu.VMEM((buffers, half, width), BF16)
    tall = pltpu.VMEM((heads, DH, length), BF16)
    dma = pltpu.SemaphoreType.DMA

    def pieces(count, cols, kind=BF16):
        return pltpu.VMEM((count, rows, cols), kind)

    return pl.pallas_call(
        functools.partial(layer_kernel, (buffers, slots, heads, hidden_cols, wide, narrow)),
        in_specs=[smem, smem, pl.BlockSpec(memory_space=ANY), pl.BlockSpec(memory_space=ANY)]
        + [vmem] * 5,
        out_specs=[vmem] * 8,
        out_shape=[
            jax.ShapeDtypeStruct((tokens, width), BF16),
            jax.ShapeDtypeStruct((tokens, width), BF16),
            jax.ShapeDtypeStruct((rows, p_cols), F32),
            jax.ShapeDtypeStruct((rows, head_cols), F32),
            jax.ShapeDtypeStruct((rows, feed_cols), F32),
            jax.ShapeDtypeStruct((8, LANES), F32),
            jax.ShapeDtypeStruct((8, LANES), F32),
            jax.ShapeDtypeStruct((16, LANES), F32),
        ],
        scratch_shapes=[
            pltpu.VMEM((tokens, width), BF16),
            pltpu.VMEM((tokens, width), BF16),
            pltpu.VMEM(strip_shape, F32),
            pltpu.VMEM(strip_shape, F32),
            pltpu.VMEM((width, p_cols), BF16),
            pltpu.VMEM((narrow, width, head_cols), BF16),
            pltpu.VMEM((width, feed_cols), BF16),
            pltpu.VMEM((narrow, tokens, head_cols), BF16),
            pltpu.VMEM((tokens, qkv_cols), BF16),
            pltpu.VMEM((tokens, LANES), F32),
            pltpu.VMEM((tokens, width), BF16),
            pltpu.VMEM((buffers, half, width), F32),
            pltpu.VMEM((tokens, hidden_cols), BF16),
            pltpu.VMEM((tokens, 2 * hidden_cols), BF16),
            pltpu.VMEM((width, feed_cols // 2), F32),
            pltpu.VMEM((2 * LANES, LANES), F32),
            pltpu.VMEM((LANES, LANES), F32),
            pieces(4, feed_cols),
            pieces(3, feed_cols),
            pieces(3, feed_cols),
            pieces(4, head_cols, F32),
            pieces(4, head_cols),
            pieces(4, head_cols),
            pieces(3, head_cols),
            pieces(3, head_cols),
            pieces(4, p_cols),
            pieces(4, p_cols),
            pieces(3, p_cols),
            pieces(3, p_cols),
        ]
        + [halves] * 7
        + [
            pltpu.VMEM((heads, length, DH), BF16),
            tall,
            tall,
            tall,
            tall,
            pltpu.VMEM((heads, DH, length), F32),
            pltpu.VMEM((heads, DH, length), F32),
            pltpu.VMEM((8, width), F32),
            pltpu.VMEM((8, LANES), F32),
            pltpu.VMEM((devices, 8, LANES), F32),
            dma((12, 9)),
            dma((12, wide)),
            dma((27,)),
            dma((27,)),
            dma((5, 7)),
            dma((5, 7)),
            dma((devices,)),
            dma((devices,)),
            pltpu.SemaphoreType.REGULAR((buffers,)),
            dma((2,)),
            dma((3 * buffers * (length // 256),)),
            dma((3 * buffers * (length // 256),)),
        ],
        compiler_params=pltpu.CompilerParams(
            vmem_limit_bytes=64 << 20, collective_id=0, has_side_effects=True
        ),
        cost_estimate=pl.CostEstimate(
            flops=60 << 30, bytes_accessed=24 << 20, transcendentals=16 << 20
        ),
        name="layer",
    )(lengths, bias, x, cot, pw, ow, ew, sw, gn)


def update_kernel(
    heads, hidden_cols, from_out, from_in, p_ref, o_ref, feed_ref, stat_ref, gain_ref, table_ref, *refs
):
    weights, firsts, seconds = refs[:6], refs[6:12], refs[12:18]
    outs, norm_ref, to_out, to_in, o_pad, held, sems = refs[18:36], *refs[36:]
    pairs = ((from_out, to_out), (from_in, to_in))
    rows = from_out.shape[0] // 2
    ways = []
    for which, (source, target) in enumerate(pairs):
        for part in range(2):
            span = slice(part * rows, (part + 1) * rows)
            at = 2 * which + part
            ways.append(
                (
                    pltpu.make_async_copy(source.at[span], held.at[which, span], sems.at[0, at]),
                    pltpu.make_async_copy(held.at[which, span], target.at[span], sems.at[1, at]),
                )
            )
    for inward, _ in ways:
        inward.start()
    for inward, outward in ways:
        inward.wait()
        outward.start()
    factor = stat_ref[1:2, 0:1]
    norm_ref[0, 0] = jnp.sum(stat_ref[0:1, 0:1])
    head_cols = heads * DH
    rows = p_ref.shape[0]

    def update(which, index, gradient):
        results = adam_update(
            weights[which][index],
            firsts[which][index],
            seconds[which][index],
            factor * gradient,
            step_rates[which],
            decay_rates[which],
        )
        for at in range(3):
            outs[6 * at + which][index] = results[at]

    for i in range(3):
        update(0, i, p_ref[:, i * head_cols : (i + 1) * head_cols])
    part = hidden_cols // 2
    for j in range(2):
        span = slice(j * part, (j + 1) * part)
        for i in range(2):
            begin = (3 * j + i) * part
            update(2, (i, slice(None), span), feed_ref[:, begin : begin + part])
        begin = (3 * j + 2) * part
        update(3, (slice(None), span), feed_ref[:, begin : begin + part])
    o_pad[...] = jnp.zeros_like(o_pad)
    o_pad[0:rows, 0:head_cols] = o_ref[...]
    update(1, slice(None), o_pad[...].T[:head_cols, :rows])
    depth, columns = weights[4].shape
    update(4, slice(None), table_ref[:depth, :columns])
    update(5, slice(None), gain_ref[1:3, :rows])
    for _, outward in ways:
        outward.wait()


def update_call(activations, grads, params_in, firsts, seconds, heads, hidden_cols):
    vmem = pl.BlockSpec(memory_space=pltpu.VMEM)
    hbm = pl.BlockSpec(memory_space=ANY)
    operands = [*activations, *grads, *params_in, *firsts, *seconds]
    return pl.pallas_call(
        functools.partial(update_kernel, heads, hidden_cols),
        in_specs=[hbm] * 2 + [vmem] * (len(operands) - 2),
        out_specs=[vmem] * 18 + [pl.BlockSpec(memory_space=pltpu.SMEM)] + [hbm] * 2,
        out_shape=[jax.ShapeDtypeStruct(a.shape, F32) for a in params_in] * 3
        + [jax.ShapeDtypeStruct((1, 1), F32)]
        + [jax.ShapeDtypeStruct(a.shape, a.dtype) for a in activations],
        scratch_shapes=[
            pltpu.VMEM((LANES, 2 * LANES), F32),
            pltpu.VMEM((2, *activations[0].shape), BF16),
            pltpu.SemaphoreType.DMA((2, 4)),
        ],
        compiler_params=params(),
        cost_estimate=pl.CostEstimate(flops=4 << 20, bytes_accessed=16 << 20, transcendentals=0),
        name="update",
    )(*operands)


def direct_body(wide, narrow, *arguments):
    block_input, cotangent, lengths = arguments[:3]
    turned = (3, 4)
    flat = [
        value.T if at % 6 in turned else value for at, value in enumerate(arguments[3:21])
    ]
    weights, firsts, seconds = flat[:6], flat[6:12], flat[12:18]
    project, output, expand, shrink, bias, gains = weights
    block_output, input_gradient, *grads = layer(
        wide,
        narrow,
        lengths,
        bias,
        block_input,
        cotangent,
        project,
        output,
        expand,
        shrink,
        gains,
    )
    heads = project.shape[2] // DH
    *results, norm, block_output, input_gradient = update_call(
        (block_output, input_gradient), grads, weights, firsts, seconds, heads, expand.shape[2]
    )
    results = [value.T if at % 6 in turned else value for at, value in enumerate(results)]
    return (block_output, input_gradient, norm.reshape(()), *results)


def solution(mesh):
    wide, narrow = mesh.shape["wide"], mesh.shape["narrow"]
    body = direct_body if (wide, narrow) == (8, 4) else general_body
    state = (
        P(None, "wide", "narrow"),
        P("narrow", "wide"),
        P(None, "wide", "narrow"),
        P("narrow", "wide"),
        P(),
        P(None, "wide"),
    )
    rows = P("wide", None)
    return jax.shard_map(
        functools.partial(body, wide, narrow),
        mesh=mesh,
        in_specs=(rows, rows, rows, *state, *state, *state),
        out_specs=(rows, rows, P(), *state, *state, *state),
        check_vma=False,
    )
```

```python
import functools

import jax
import jax.numpy as jnp
from jax import lax
from jax.experimental import pallas as pl
from jax.experimental.pallas import tpu as pltpu
from jax.sharding import PartitionSpec as P

DH = 64
STEP = 10
LANES = 128
MESH = pl.DeviceIdType.MESH
F32 = jnp.float32
BF16 = jnp.bfloat16
ANY = pl.ANY

bucket_edges = (12, 16, 23, 32, 46, 64, 91)
norm_eps = 1e-06
clip_limit = 1.0
beta_one = 0.9
beta_two = 0.999
adam_eps = 1e-08
step_rates = (0.06, 0.3, 0.07, 0.06, 1.0, 0.3)
decay_rates = (0.01, 0.01, 0.01, 0.01, 0.0, 0.0)
masked_score = -1000000000.0
VMEM_LIMIT = 58 << 20

NN = (((1,), (0,)), ((), ()))
NT = (((1,), (1,)), ((), ()))
TN = (((0,), (0,)), ((), ()))


def mm(left, right, dims=NN):
    return lax.dot_general(left, right, dims, preferred_element_type=F32)


def bucket_of(offsets):
    distance = jnp.abs(offsets)
    far_bucket = 8 + sum(((distance >= threshold).astype(jnp.int32) for threshold in bucket_edges))
    return jnp.where(distance < 8, distance, far_bucket) + 16 * (offsets > 0).astype(jnp.int32)


def rms_scale(values):
    return lax.rsqrt(jnp.mean(values * values, axis=-1, keepdims=True) + norm_eps)


def norm_back(values, scale_vec, gain_vec, upstream):
    weighted = upstream * gain_vec
    inner_mean = jnp.mean(weighted * values, axis=-1, keepdims=True)
    return scale_vec * weighted - values * (scale_vec * scale_vec * scale_vec) * inner_mean


def adam_update(weight, moment_one, moment_two, gradient, step_rate, decay_rate):
    new_first = beta_one * moment_one + (1.0 - beta_one) * gradient
    new_second = beta_two * moment_two + (1.0 - beta_two) * gradient * gradient
    first_hat = new_first / (1.0 - beta_one**STEP)
    second_hat = new_second / (1.0 - beta_two**STEP)
    new_weight = weight - step_rate * (
        first_hat / (jnp.sqrt(second_hat) + adam_eps) + decay_rate * weight
    )
    return (new_weight, new_first, new_second)


def fold_rows(values):
    rows, cols = values.shape
    return jnp.sum(values.reshape(rows // 8, 8, cols), axis=0)


def start_rows(pieces, target, offs_ref, sems):
    copies = []
    for at, piece in enumerate(pieces):
        rows = piece.shape[0]
        begin = pl.multiple_of(offs_ref[at], 16)
        copies.append(
            pltpu.make_async_copy(piece, target.at[pl.ds(begin, rows)], sems.at[at])
        )
    for copy in copies:
        copy.start()
    return copies


def segments(index, ends_ref, buffer, slots):
    total = jnp.zeros(index.shape, jnp.int32)
    for slot in range(slots):
        total = total + (index >= ends_ref[buffer, slot]).astype(jnp.int32)
    return total


def params(**more):
    return pltpu.CompilerParams(vmem_limit_bytes=VMEM_LIMIT, **more)


def attend_kernel(
    buffer, slots, heads, count, ends_ref, offs_ref, x_ref, strip_ref, *refs
):
    pieces = refs[:count]
    normed_ref, qkv_ref, att_ref, log_ref, gains_ref, wbuf, qs, ks, vs, os, sems = refs[count:]
    length, width = x_ref.shape
    head_cols = heads * DH
    copies = start_rows(pieces, wbuf, offs_ref, sems)
    for copy in copies:
        copy.wait()
    gain_cols = wbuf[:, 4 * LANES :].astype(F32).T
    first = 3 * head_cols - 4 * LANES
    gains = gain_cols[first : first + 8]
    gains_ref[...] = gains
    gain_one = gains[0:1]
    step = 256

    @pl.loop(0, length // step)
    def _(block):
        rows = pl.ds(pl.multiple_of(block * step, step), step)
        values = x_ref[rows].astype(F32)
        normed = (values * rms_scale(values) * gain_one).astype(BF16)
        normed_ref[rows] = normed
        qkv = mm(normed, wbuf[...]).astype(BF16)
        qkv_ref[rows] = qkv[:, : 3 * head_cols]
        for h in range(heads):
            qs[h, rows] = qkv[:, h * DH : (h + 1) * DH]
            ks[h, rows] = qkv[:, head_cols + h * DH : head_cols + (h + 1) * DH]
            vs[h, rows] = qkv[:, 2 * head_cols + h * DH : 2 * head_cols + (h + 1) * DH]

    blocks = length // LANES
    seg_keys = segments(
        lax.broadcasted_iota(jnp.int32, (1, length), 1), ends_ref, buffer, slots
    )

    @pl.loop(0, blocks)
    def _(block):
        begin = pl.multiple_of(block * LANES, LANES)
        rows = pl.ds(begin, LANES)
        window = pl.ds(pl.multiple_of((blocks - 1 - block) * LANES, LANES), length)
        seg_rows = segments(
            lax.broadcasted_iota(jnp.int32, (LANES, 1), 0) + begin, ends_ref, buffer, slots
        )
        same = seg_rows == seg_keys
        lane = lax.broadcasted_iota(jnp.int32, (LANES, LANES), 1)
        logs = jnp.zeros((LANES, LANES), F32)
        for h in range(heads):
            scores = mm(qs[h, rows], ks[h], NT) + strip_ref[h, :, window]
            scores = jnp.where(same, scores, masked_score)
            row_max = jnp.max(scores, axis=1, keepdims=True)
            raised = jnp.exp(scores - row_max)
            total = jnp.sum(raised, axis=1, keepdims=True)
            probs = (raised * (1.0 / total)).astype(BF16)
            os[h, rows] = mm(probs, vs[h]).astype(BF16)
            logs = jnp.where(lane == h, row_max + jnp.log(total), logs)
        log_ref[rows] = logs

    att_ref[...] = jnp.concatenate([os[h] for h in range(heads)], axis=1)


def attend(buffer, ends, offs, x, strip, pieces, length, heads):
    width = x.shape[1]
    count = len(pieces)
    cols = pieces[0].shape[1]
    head_cols = heads * DH
    whole = lambda i, *_: (0, 0)
    spec = pltpu.PrefetchScalarGridSpec(
        num_scalar_prefetch=2,
        grid=(1,),
        in_specs=[
            pl.BlockSpec((length, width), lambda i, *_: (buffer, 0)),
            pl.BlockSpec(strip.shape, lambda i, *_: (0, 0, 0)),
        ]
        + [pl.BlockSpec(memory_space=ANY)] * count,
        out_specs=[
            pl.BlockSpec((length, width), whole),
            pl.BlockSpec((length, 3 * head_cols), whole),
            pl.BlockSpec((length, head_cols), whole),
            pl.BlockSpec((length, LANES), whole),
            pl.BlockSpec((8, width), whole),
        ],
        scratch_shapes=[
            pltpu.VMEM((width, cols), BF16),
            pltpu.VMEM((heads, length, DH), BF16),
            pltpu.VMEM((heads, length, DH), BF16),
            pltpu.VMEM((heads, length, DH), BF16),
            pltpu.VMEM((heads, length, DH), BF16),
            pltpu.SemaphoreType.DMA((count,)),
        ],
    )
    flops = 2 * length * (width * cols + 2 * heads * DH * length)
    return pl.pallas_call(
        functools.partial(attend_kernel, buffer, ends.shape[1], heads, count),
        grid_spec=spec,
        out_shape=[
            jax.ShapeDtypeStruct((length, width), BF16),
            jax.ShapeDtypeStruct((length, 3 * head_cols), BF16),
            jax.ShapeDtypeStruct((length, head_cols), BF16),
            jax.ShapeDtypeStruct((length, LANES), F32),
            jax.ShapeDtypeStruct((8, width), F32),
        ],
        compiler_params=params(),
        cost_estimate=pl.CostEstimate(
            flops=4 * flops, bytes_accessed=8 << 20, transcendentals=heads * length * length
        ),
        name="attend",
    )(ends, offs, x, strip, *pieces)


def feed_kernel(hidden_cols, counts, order_ref, offs_ref, *refs):
    own, across, beside, diagonal, x_ref, cot_ref, gains_ref = refs[:7]
    at = 7
    groups = []
    for count in counts:
        groups.append(refs[at : at + count])
        at += count
    (
        normed_ref,
        hidden_ref,
        gate_ref,
        ff_send,
        ff_keep,
        dn_send,
        dn_keep,
        middle_keep,
        gain_sum,
        ebuf,
        sbuf,
        oabuf,
        obbuf,
        sems,
    ) = refs[at:]
    step = pl.program_id(0)
    bufs = (oabuf, obbuf, ebuf, sbuf)

    @pl.when(step == 0)
    def _():
        copies = []
        for which, (group, target) in enumerate(zip(groups, bufs)):
            copies += start_rows(group, target, offs_ref, sems.at[which])
        for copy in copies:
            copy.wait()

    cols = own.shape[1]
    upper = order_ref[2] == 0
    pairs = []
    for near, far, weights in ((own, across, oabuf), (beside, diagonal, obbuf)):
        near_sum = mm(near[...], weights[:, :cols], NT)
        far_sum = mm(far[...], weights[:, cols:], NT)
        pairs.append(
            jnp.where(upper, near_sum, far_sum) + jnp.where(upper, far_sum, near_sum)
        )
    swap = order_ref[0] == 0
    attention = jnp.where(swap, pairs[0], pairs[1]) + jnp.where(swap, pairs[1], pairs[0])
    middle = x_ref[...].astype(F32) + attention
    scale_two = rms_scale(middle)
    gain_two = gains_ref[1:2]
    normed = (middle * scale_two * gain_two).astype(BF16)
    normed_ref[...] = normed
    cot = cot_ref[...]
    part = 256
    k0 = 0.7978845608028654
    k1 = 0.044715
    for begin in range(0, hidden_cols, part):
        gate = mm(normed, ebuf[:, begin : begin + part])
        up = mm(normed, ebuf[:, hidden_cols + begin : hidden_cols + begin + part])
        square = gate * gate
        tanh = jnp.tanh(k0 * (gate + k1 * (square * gate)))
        half = 0.5 * (1.0 + tanh)
        active = gate * half
        slope = half + (0.5 * gate) * (1.0 - tanh * tanh) * (k0 + (3.0 * k0 * k1) * square)
        d_hidden = mm(cot, sbuf[:, begin : begin + part])
        hidden_ref[:, begin : begin + part] = (active * up).astype(BF16)
        gate_ref[:, begin : begin + part] = (d_hidden * up * slope).astype(BF16)
        gate_ref[:, hidden_cols + begin : hidden_cols + begin + part] = (
            d_hidden * active
        ).astype(BF16)
    ff = mm(hidden_ref[...], sbuf[...], NT).astype(BF16)
    dn = mm(gate_ref[...], ebuf[...], NT)
    sums = fold_rows(dn * middle * scale_two)
    dn = dn.astype(BF16)

    @pl.when(step == 0)
    def _():
        ff_send[...] = ff
        dn_send[...] = dn
        gain_sum[...] = sums

    @pl.when(step == 1)
    def _():
        ff_keep[...] = ff
        dn_keep[...] = dn
        middle_keep[...] = middle
        gain_sum[...] = gain_sum[...] + sums


def feed(buffer, order, offs, parts, x, cot, gains, groups, length, hidden_cols):
    width = x.shape[1]
    half = length // 2
    cols = parts[0].shape[1]
    counts = [len(group) for group in groups]
    natural = lambda i, order, *_: (order[i], 0)
    rows = lambda i, order, *_: (2 * buffer + order[i], 0)
    whole = lambda i, *_: (0, 0)
    spec = pltpu.PrefetchScalarGridSpec(
        num_scalar_prefetch=2,
        grid=(2,),
        in_specs=[pl.BlockSpec((half, cols), natural)] * 4
        + [pl.BlockSpec((half, width), rows)] * 2
        + [pl.BlockSpec((8, width), whole)]
        + [pl.BlockSpec(memory_space=ANY)] * sum(counts),
        out_specs=[
            pl.BlockSpec((half, width), natural),
            pl.BlockSpec((half, hidden_cols), natural),
            pl.BlockSpec((half, 2 * hidden_cols), natural),
        ]
        + [pl.BlockSpec((half, width), whole)] * 5
        + [pl.BlockSpec((8, width), whole)],
        scratch_shapes=[
            pltpu.VMEM((width, 2 * hidden_cols), BF16),
            pltpu.VMEM((width, hidden_cols), BF16),
            pltpu.VMEM((width, 2 * cols), BF16),
            pltpu.VMEM((width, 2 * cols), BF16),
            pltpu.SemaphoreType.DMA((4, max(counts))),
        ],
    )
    flops = 2 * length * width * (4 * cols + 7 * hidden_cols)
    return pl.pallas_call(
        functools.partial(feed_kernel, hidden_cols, counts),
        grid_spec=spec,
        out_shape=[
            jax.ShapeDtypeStruct((length, width), BF16),
            jax.ShapeDtypeStruct((length, hidden_cols), BF16),
            jax.ShapeDtypeStruct((length, 2 * hidden_cols), BF16),
            jax.ShapeDtypeStruct((half, width), BF16),
            jax.ShapeDtypeStruct((half, width), BF16),
            jax.ShapeDtypeStruct((half, width), BF16),
            jax.ShapeDtypeStruct((half, width), BF16),
            jax.ShapeDtypeStruct((half, width), F32),
            jax.ShapeDtypeStruct((8, width), F32),
        ],
        compiler_params=params(),
        cost_estimate=pl.CostEstimate(
            flops=flops, bytes_accessed=12 << 20, transcendentals=length * hidden_cols
        ),
        name="feed",
    )(order, offs, *parts, x, cot, gains, *[piece for group in groups for piece in group])


def middle_kernel(order_ref, near, far, middle_ref, cot_ref, gains_ref, d_ref, low_ref):
    upstream = near[...].astype(F32) + far[...].astype(F32)
    middle = middle_ref[...]
    d_middle = cot_ref[...].astype(F32) + norm_back(
        middle, rms_scale(middle), gains_ref[1:2], upstream
    )
    d_ref[...] = d_middle
    low_ref[...] = d_middle.astype(BF16)


def input_kernel(order_ref, near, far, x_ref, d_ref, gains_ref, out_ref):
    upstream = near[...].astype(F32) + far[...].astype(F32)
    values = x_ref[...].astype(F32)
    out_ref[...] = (
        d_ref[...] + norm_back(values, rms_scale(values), gains_ref[0:1], upstream)
    ).astype(BF16)


def output_kernel(order_ref, near, far, middle_ref, out_ref):
    out_ref[...] = (
        middle_ref[...] + (near[...].astype(F32) + far[...].astype(F32)).astype(BF16).astype(F32)
    ).astype(BF16)


def half_call(kernel, name, buffer, order, arrays, placed, outs, gains=None):
    half, width = arrays[0].shape
    steps = 3
    block = half // steps
    mine = lambda i, *_: (i, 0)
    rows = lambda i, order, *_: ((2 * buffer + order[1]) * steps + i, 0)
    in_specs = [
        pl.BlockSpec((block, width), rows if at in placed else mine)
        for at in range(len(arrays))
    ]
    operands = list(arrays)
    if gains is not None:
        in_specs.append(pl.BlockSpec((8, width), lambda i, *_: (0, 0)))
        operands.append(gains)
    return pl.pallas_call(
        kernel,
        grid_spec=pltpu.PrefetchScalarGridSpec(
            num_scalar_prefetch=1,
            grid=(steps,),
            in_specs=in_specs,
            out_specs=[pl.BlockSpec((block, width), mine) for _ in outs],
        ),
        out_shape=[jax.ShapeDtypeStruct((half, width), kind) for kind in outs],
        compiler_params=params(),
        cost_estimate=pl.CostEstimate(
            flops=20 * half * width, bytes_accessed=12 * half * width, transcendentals=0
        ),
        name=name,
    )(order, *operands)


def back_kernel(buffer, slots, heads, counts, ends_ref, offs_ref, order_ref, *refs):
    near, far, qkv_ref, log_ref, strip_ref, x_ref = refs[:6]
    at = 6
    o_pieces = refs[at : at + counts[0]]
    at += counts[0]
    p_pieces = refs[at : at + counts[1]]
    at += counts[1]
    (
        low_ref,
        dqkv_ref,
        dn_send,
        dn_keep,
        gain_sum,
        dstrip,
        wbuf,
        obuf,
        qs,
        ks,
        vs,
        gs,
        qt,
        gt,
        dkt,
        dvt,
        dq,
        sems,
    ) = refs[at:]
    length = qkv_ref.shape[0]
    half = length // 2
    head_cols = heads * DH
    o_copies = start_rows(o_pieces, obuf, offs_ref, sems.at[0])
    p_copies = start_rows(p_pieces, wbuf, offs_ref, sems.at[1])
    mine = pl.ds(pl.multiple_of(order_ref[1] * half, LANES), half)
    other = pl.ds(pl.multiple_of(order_ref[0] * half, LANES), half)
    low_ref[mine] = near[...]
    low_ref[other] = far[...]
    for h in range(heads):
        qs[h] = qkv_ref[:, h * DH : (h + 1) * DH]
        ks[h] = qkv_ref[:, head_cols + h * DH : head_cols + (h + 1) * DH]
        vs[h] = qkv_ref[:, 2 * head_cols + h * DH : 2 * head_cols + (h + 1) * DH]
        qt[h] = qs[h].T
    dstrip[...] = jnp.zeros_like(dstrip)
    dkt[...] = jnp.zeros_like(dkt)
    dvt[...] = jnp.zeros_like(dvt)
    for copy in o_copies + p_copies:
        copy.wait()
    grads = mm(low_ref[...], obuf[:, :head_cols]).astype(BF16)
    for h in range(heads):
        gs[h] = grads[:, h * DH : (h + 1) * DH]
        gt[h] = gs[h].T
    blocks = length // LANES
    seg_keys = segments(
        lax.broadcasted_iota(jnp.int32, (1, length), 1), ends_ref, buffer, slots
    )

    @pl.loop(0, blocks)
    def _(block):
        begin = pl.multiple_of(block * LANES, LANES)
        rows = pl.ds(begin, LANES)
        window = pl.ds(pl.multiple_of((blocks - 1 - block) * LANES, LANES), length)
        seg_rows = segments(
            lax.broadcasted_iota(jnp.int32, (LANES, 1), 0) + begin, ends_ref, buffer, slots
        )
        same = seg_rows == seg_keys
        logs = log_ref[rows]
        for h in range(heads):
            scores = mm(qs[h, rows], ks[h], NT) + strip_ref[h, :, window]
            scores = jnp.where(same, scores, masked_score)
            probs = jnp.exp(scores - logs[:, h : h + 1])
            d_probs = mm(gs[h, rows], vs[h], NT)
            inner = jnp.sum(probs * d_probs, axis=1, keepdims=True)
            d_scores = (probs * (d_probs - inner)).astype(BF16)
            dstrip[h, :, window] = dstrip[h, :, window] + d_scores.astype(F32)
            dq[h, rows] = mm(d_scores, ks[h]).astype(BF16)
            dkt[h] = dkt[h] + mm(qt[h, :, rows], d_scores)
            dvt[h] = dvt[h] + mm(gt[h, :, rows], probs.astype(BF16))

    outs = [dq[h] for h in range(heads)]
    outs += [dkt[h].T.astype(BF16) for h in range(heads)]
    outs += [dvt[h].T.astype(BF16) for h in range(heads)]
    dqkv_ref[...] = jnp.concatenate(outs, axis=1)
    sums = []
    for target, which in ((dn_send, other), (dn_keep, mine)):
        dn = mm(dqkv_ref[which], wbuf[:, : 3 * head_cols], NT)
        values = x_ref[which].astype(F32)
        sums.append(fold_rows(dn * values * rms_scale(values)))
        target[...] = dn.astype(BF16)
    gain_sum[...] = sums[0] + sums[1]


def back(buffer, ends, offs, order, near, far, qkv, logs, strip, x, o_pieces, p_pieces, heads):
    length = qkv.shape[0]
    half = length // 2
    width = x.shape[1]
    head_cols = heads * DH
    counts = (len(o_pieces), len(p_pieces))
    whole = lambda i, *_: (0, 0)
    whole3 = lambda i, *_: (0, 0, 0)
    spec = pltpu.PrefetchScalarGridSpec(
        num_scalar_prefetch=3,
        grid=(1,),
        in_specs=[
            pl.BlockSpec((half, width), whole),
            pl.BlockSpec((half, width), whole),
            pl.BlockSpec(qkv.shape, whole),
            pl.BlockSpec(logs.shape, whole),
            pl.BlockSpec(strip.shape, whole3),
            pl.BlockSpec((length, width), lambda i, *_: (buffer, 0)),
        ]
        + [pl.BlockSpec(memory_space=ANY)] * sum(counts),
        out_specs=[
            pl.BlockSpec((length, width), whole),
            pl.BlockSpec((length, 3 * head_cols), whole),
            pl.BlockSpec((half, width), whole),
            pl.BlockSpec((half, width), whole),
            pl.BlockSpec((8, width), whole),
            pl.BlockSpec(strip.shape, whole3),
        ],
        scratch_shapes=[
            pltpu.VMEM((width, p_pieces[0].shape[1]), BF16),
            pltpu.VMEM((width, o_pieces[0].shape[1]), BF16),
            pltpu.VMEM((heads, length, DH), BF16),
            pltpu.VMEM((heads, length, DH), BF16),
            pltpu.VMEM((heads, length, DH), BF16),
            pltpu.VMEM((heads, length, DH), BF16),
            pltpu.VMEM((heads, DH, length), BF16),
            pltpu.VMEM((heads, DH, length), BF16),
            pltpu.VMEM((heads, DH, length), F32),
            pltpu.VMEM((heads, DH, length), F32),
            pltpu.VMEM((heads, length, DH), BF16),
            pltpu.SemaphoreType.DMA((2, max(counts))),
        ],
    )
    return pl.pallas_call(
        functools.partial(back_kernel, buffer, ends.shape[1], heads, counts),
        grid_spec=spec,
        out_shape=[
            jax.ShapeDtypeStruct((length, width), BF16),
            jax.ShapeDtypeStruct((length, 3 * head_cols), BF16),
            jax.ShapeDtypeStruct((half, width), BF16),
            jax.ShapeDtypeStruct((half, width), BF16),
            jax.ShapeDtypeStruct((8, width), F32),
            jax.ShapeDtypeStruct(strip.shape, F32),
        ],
        compiler_params=params(),
        cost_estimate=pl.CostEstimate(
            flops=40 * heads * DH * length * length,
            bytes_accessed=16 << 20,
            transcendentals=heads * length * length,
        ),
        name="back",
    )(ends, offs, order, near, far, qkv, logs, strip, x, *o_pieces, *p_pieces)


def scatter_rows(total, offs_ref, evens, odds):
    rows = evens[0].shape[0]
    for at in range(2 * len(evens)):
        begin = pl.multiple_of(offs_ref[at], 8)
        block = total[pl.ds(begin, rows)]
        if at % 2:
            odds[at // 2][...] = block.astype(BF16)
        else:
            evens[at // 2][...] = block


def feed_grad_kernel(count, hidden_cols, offs_ref, *refs):
    buffers = 2
    normed = refs[:buffers]
    gates = refs[buffers : 2 * buffers]
    hiddens = refs[2 * buffers : 3 * buffers]
    cot_ref = refs[3 * buffers]
    outs = refs[3 * buffers + 1 : -1]
    total = refs[-1]
    length = normed[0].shape[0]
    width = normed[0].shape[1]
    part = 256
    for begin in range(0, width, part):
        cols = slice(begin, begin + part)
        total[cols, : 2 * hidden_cols] = mm(normed[0][:, cols], gates[0][...], TN) + mm(
            normed[1][:, cols], gates[1][...], TN
        )
        total[cols, 2 * hidden_cols :] = mm(
            cot_ref[:length, cols], hiddens[0][...], TN
        ) + mm(cot_ref[length:, cols], hiddens[1][...], TN)
    if count > 1:
        scatter_rows(total, offs_ref, outs[: count // 2], outs[count // 2 :])
    else:
        outs[0][...] = total[...]


def attend_grad_kernel(count, heads, offs_ref, *refs):
    buffers = 2
    normed = refs[:buffers]
    dqkv = refs[buffers : 2 * buffers]
    lows = refs[2 * buffers : 3 * buffers]
    atts = refs[3 * buffers : 4 * buffers]
    sums_ref = refs[4 * buffers]
    outs = refs[4 * buffers + 1 : -1]
    total = refs[-1]
    width = normed[0].shape[1]
    head_cols = heads * DH
    qkv_cols = 3 * head_cols
    part = 256
    rows = lax.broadcasted_iota(jnp.int32, (LANES, width), 0)
    first = sums_ref[0] + sums_ref[1]
    second = sums_ref[2] + sums_ref[3]
    gain_rows = jnp.where(
        rows == DH,
        jnp.sum(first, axis=0, keepdims=True),
        jnp.where(rows == DH + 1, jnp.sum(second, axis=0, keepdims=True), 0.0),
    )
    gain_cols = gain_rows.T
    for begin in range(0, width, part):
        cols = slice(begin, begin + part)
        total[cols, :qkv_cols] = mm(normed[0][:, cols], dqkv[0][...], TN) + mm(
            normed[1][:, cols], dqkv[1][...], TN
        )
        total[cols, qkv_cols : qkv_cols + DH] = gain_cols[cols, DH:]
        total[cols, qkv_cols + DH : qkv_cols + DH + head_cols] = mm(
            lows[0][:, cols], atts[0][...], TN
        ) + mm(lows[1][:, cols], atts[1][...], TN)
    if count > 1:
        scatter_rows(total, offs_ref, outs[: count // 2], outs[count // 2 :])
    else:
        outs[0][...] = total[...]


def grad_call(kernel, name, offs, operands, width, cols, count, rows, flops):
    vmem = pl.BlockSpec(memory_space=pltpu.VMEM)
    if count > 1:
        shapes = [jax.ShapeDtypeStruct((rows, cols), F32)] * (count // 2)
        shapes += [jax.ShapeDtypeStruct((rows, cols), BF16)] * (count // 2)
    else:
        shapes = [jax.ShapeDtypeStruct((width, cols), F32)]
    return pl.pallas_call(
        kernel,
        in_specs=[pl.BlockSpec(memory_space=pltpu.SMEM)] + [vmem] * len(operands),
        out_specs=[vmem] * len(shapes),
        out_shape=shapes,
        scratch_shapes=[pltpu.VMEM((width, cols), F32)],
        compiler_params=params(),
        cost_estimate=pl.CostEstimate(flops=2 * flops, bytes_accessed=14 << 20, transcendentals=0),
        name=name,
    )(offs, *operands)


def bucket_kernel(heads, near_ref, far_ref, out_ref):
    lanes = near_ref.shape[2]
    blocks = (lanes // LANES + 1) // 2
    begin = (blocks - 2) * LANES
    end = begin + 3 * LANES
    rows = lax.broadcasted_iota(jnp.int32, (LANES, 3 * LANES), 0)
    ids = bucket_of(
        lax.broadcasted_iota(jnp.int32, (LANES, 3 * LANES), 1) - LANES - rows
    )
    lane = lax.broadcasted_iota(jnp.int32, (1, LANES), 1)
    out = jnp.zeros((1, LANES), F32)
    for h in range(heads):
        strip = near_ref[h] + far_ref[h]
        left = jnp.sum(jnp.sum(strip[:, :begin], axis=0, keepdims=True), axis=1, keepdims=True)
        right = jnp.sum(jnp.sum(strip[:, end:], axis=0, keepdims=True), axis=1, keepdims=True)
        out = out + jnp.where(lane == h * 32 + 15, left, 0.0)
        out = out + jnp.where(lane == h * 32 + 31, right, 0.0)
        middle = strip[:, begin:end]
        for b in range(32):
            if b == 16:
                continue
            part = jnp.sum(jnp.where(ids == b, middle, 0.0), axis=0, keepdims=True)
            part = jnp.sum(part, axis=1, keepdims=True)
            out = out + jnp.where(lane == h * 32 + b, part, 0.0)
    out_ref[...] = jnp.broadcast_to(out, (8, LANES))


def norm_kernel(wide, narrow, lists, gain_at, *refs):
    at = 0
    groups = []
    for count in lists:
        groups.append(refs[at : at + count])
        at += count
    bucket_ref = refs[at]
    outs = refs[at + 1 : at + 1 + len(lists)]
    stat_ref, gain_ref, table_ref, block, inbox, padded, send_sems, recv_sems = refs[
        at + 1 + len(lists) :
    ]
    total = wide * narrow
    w = lax.axis_index("wide")
    n = lax.axis_index("narrow")
    me = w * narrow + n
    barrier = pltpu.get_barrier_semaphore()

    @pl.loop(1, total)
    def _(k):
        peer = (me + k) % total
        pl.semaphore_signal(
            barrier, inc=1, device_id=(peer // narrow, peer % narrow), device_id_type=MESH
        )

    squares = jnp.zeros((8, LANES), F32)
    for which, (group, out) in enumerate(zip(groups, outs)):
        value = group[0][...].astype(F32)
        for more in group[1:]:
            value = value + more[...].astype(F32)
        out[...] = value
        squared = value * value
        if which == 0:
            lane = lax.broadcasted_iota(jnp.int32, value.shape, 1)
            inside = (lane >= gain_at) & (lane < gain_at + DH)
            squared = jnp.where(inside, 0.0, squared)
        squared = jnp.sum(squared, axis=1, keepdims=True)
        squares = squares + jnp.sum(squared, axis=0, keepdims=True)
    rows = outs[0].shape[0]
    low = gain_at // LANES * LANES
    padded[...] = jnp.zeros_like(padded)
    padded[0:rows] = outs[0][:, low : low + LANES]
    turned = padded[...].T
    row = lax.broadcasted_iota(jnp.int32, (8, LANES), 0)
    here = gain_at - low
    mine = jnp.where(row == 0, squares, 0.0)
    mine = jnp.where(row == 1, turned[here : here + 1], mine)
    mine = jnp.where(row == 2, turned[here + 1 : here + 2], mine)
    mine = jnp.where(row == 3, bucket_ref[...], mine)
    block[...] = mine
    inbox[me] = mine
    pl.semaphore_wait(barrier, total - 1)

    @pl.loop(1, total)
    def _(k):
        peer = (me + k) % total
        pltpu.make_async_remote_copy(
            src_ref=block,
            dst_ref=inbox.at[me],
            send_sem=send_sems.at[k],
            recv_sem=recv_sems.at[total - k],
            device_id=(peer // narrow, peer % narrow),
            device_id_type=MESH,
        ).start()

    @pl.loop(1, total)
    def _(k):
        peer = (me + k) % total
        copy = pltpu.make_async_remote_copy(
            src_ref=block,
            dst_ref=inbox.at[peer],
            send_sem=send_sems.at[k],
            recv_sem=recv_sems.at[k],
            device_id=(peer // narrow, peer % narrow),
            device_id_type=MESH,
        )
        copy.wait_send()
        copy.wait_recv()

    columns = [jnp.zeros((8, LANES), F32) for _ in range(narrow)]
    gain_square = jnp.zeros((8, LANES), F32)
    square_total = jnp.zeros((8, LANES), F32)
    for a in range(wide):
        gains = jnp.zeros((8, LANES), F32)
        for b in range(narrow):
            got = inbox[a * narrow + b]
            gains = gains + got
            columns[b] = columns[b] + got
        square_total = square_total + gains
        gain_square = gain_square + gains * gains
    own = inbox[w * narrow]
    for b in range(1, narrow):
        own = own + inbox[w * narrow + b]
    gain_ref[...] = own
    pick = (row == 1) | (row == 2)
    gain_square = jnp.where(pick, gain_square, 0.0)
    norm_square = square_total[0:1, 0:1] + jnp.sum(
        jnp.sum(gain_square, axis=0, keepdims=True), axis=1, keepdims=True
    )
    heads = LANES // 32 - 1
    lane = lax.broadcasted_iota(jnp.int32, (32, LANES), 1)
    depth = lax.broadcasted_iota(jnp.int32, (32, LANES), 0)
    table = jnp.zeros((32, LANES), F32)
    for b in range(narrow):
        line = columns[b][3:4]
        norm_square = norm_square + jnp.sum(line * line, axis=1, keepdims=True)
        for h in range(heads):
            column = jnp.sum(
                jnp.where(lane == depth + 32 * h, line, 0.0), axis=1, keepdims=True
            )
            table = jnp.where(lane == b * heads + h, column, table)
    table_ref[...] = table
    global_norm = jnp.sqrt(norm_square)
    factor = jnp.minimum(1.0, clip_limit / (global_norm + 1e-06))
    stat_ref[...] = jnp.where(row == 0, global_norm, factor)


def norm_call(wide, narrow, groups, bucket, gain_at):
    vmem = pl.BlockSpec(memory_space=pltpu.VMEM)
    lists = tuple(len(group) for group in groups)
    total = wide * narrow
    operands = [piece for group in groups for piece in group] + [bucket]
    return pl.pallas_call(
        functools.partial(norm_kernel, wide, narrow, lists, gain_at),
        in_specs=[vmem] * len(operands),
        out_specs=[vmem] * (len(lists) + 3),
        out_shape=[jax.ShapeDtypeStruct(group[0].shape, F32) for group in groups]
        + [
            jax.ShapeDtypeStruct((8, LANES), F32),
            jax.ShapeDtypeStruct((8, LANES), F32),
            jax.ShapeDtypeStruct((32, LANES), F32),
        ],
        scratch_shapes=[
            pltpu.VMEM((8, LANES), F32),
            pltpu.VMEM((total, 8, LANES), F32),
            pltpu.VMEM((LANES, LANES), F32),
            pltpu.SemaphoreType.DMA((total,)),
            pltpu.SemaphoreType.DMA((total,)),
        ],
        compiler_params=params(collective_id=0, has_side_effects=True),
        cost_estimate=pl.CostEstimate(flops=1 << 20, bytes_accessed=4 << 20, transcendentals=0),
        name="norm",
    )(*operands)


def adam_kernel(heads, hidden_cols, parts, att_ref, feed_ref, gain_ref, table_ref, stat_ref, *refs):
    weights, firsts, seconds = refs[:6], refs[6:12], refs[12:18]
    outs = refs[18:36]
    o_pad, s_pad = refs[36:]
    factor = stat_ref[1:2, 0:1]
    head_cols = heads * DH
    rows = att_ref.shape[0]
    gain_at = 3 * head_cols

    def update(which, index, gradient):
        results = adam_update(
            weights[which][index],
            firsts[which][index],
            seconds[which][index],
            factor * gradient,
            step_rates[which],
            decay_rates[which],
        )
        for at in range(3):
            outs[6 * at + which][index] = results[at]

    for i in range(3):
        update(0, i, att_ref[:, i * head_cols : (i + 1) * head_cols])
    part = hidden_cols // parts
    for j in range(parts):
        span = slice(j * part, (j + 1) * part)
        for i in range(2):
            begin = (3 * j + i) * part if parts > 1 else i * part
            update(2, (i, slice(None), span), feed_ref[:, begin : begin + part])
    o_pad[...] = jnp.zeros_like(o_pad)
    s_pad[...] = jnp.zeros_like(s_pad)
    o_pad[0:rows] = att_ref[:, gain_at + DH :]
    for j in range(parts):
        begin = (3 * j + 2) * part
        s_pad[0:rows, j * part : (j + 1) * part] = feed_ref[:, begin : begin + part]
    update(1, slice(None), o_pad[...].T[:head_cols, :rows])
    update(3, slice(None), s_pad[...].T[:, :rows])
    columns = weights[4].shape[1]
    update(4, slice(None), table_ref[:, :columns])
    update(5, slice(None), gain_ref[1:3, :rows])


def adam_call(
    att, feed_grad, gain, table, stat, params_in, firsts, seconds, heads, hidden_cols, direct=False
):
    vmem = pl.BlockSpec(memory_space=pltpu.VMEM)
    operands = [att, feed_grad, gain, table, stat, *params_in, *firsts, *seconds]
    pad_cols = att.shape[1] - (3 * heads * DH + DH)
    return pl.pallas_call(
        functools.partial(adam_kernel, heads, hidden_cols, 2 if direct else 1),
        in_specs=[vmem] * len(operands),
        out_specs=[vmem] * 18,
        out_shape=[jax.ShapeDtypeStruct(a.shape, F32) for a in params_in] * 3,
        scratch_shapes=[
            pltpu.VMEM((LANES, pad_cols), F32),
            pltpu.VMEM((LANES, hidden_cols), F32),
        ],
        compiler_params=params(),
        cost_estimate=pl.CostEstimate(flops=4 << 20, bytes_accessed=8 << 20, transcendentals=0),
        name="adam",
    )(*operands)


def place_kernel(offs_ref, *refs):
    step = pl.program_id(0)
    for at, piece in enumerate(refs[:-1]):

        @pl.when(step == at)
        def _(piece=piece):
            refs[-1][...] = piece[...]


def place(pieces, offs, rows):
    half, width = pieces[0].shape
    count = len(pieces)
    return pl.pallas_call(
        place_kernel,
        grid_spec=pltpu.PrefetchScalarGridSpec(
            num_scalar_prefetch=1,
            grid=(count,),
            in_specs=[pl.BlockSpec((half, width), lambda i, *_: (0, 0))] * count,
            out_specs=pl.BlockSpec((half, width), lambda i, offs: (offs[i] // half, 0)),
        ),
        out_shape=jax.ShapeDtypeStruct((rows, width), pieces[0].dtype),
        compiler_params=params(),
        cost_estimate=pl.CostEstimate(
            flops=0, bytes_accessed=4 * rows * width, transcendentals=0
        ),
        name="place",
    )(offs, *pieces)


def bias_strip(bucket_bias, n, heads, length):
    table = lax.dynamic_slice_in_dim(bucket_bias, n * heads, heads, 1).T
    blocks = length // LANES
    near_r = (
        jnp.arange(3 * LANES, dtype=jnp.int32)[None, :]
        - LANES
        - jnp.arange(LANES, dtype=jnp.int32)[:, None]
    )
    near_ids = bucket_of(near_r)
    near = sum(
        jnp.where(near_ids == b, table[:, b][:, None, None], 0.0) for b in range(32) if b != 16
    )
    far_shape = (heads, LANES, (blocks - 2) * LANES)
    return jnp.concatenate(
        [
            jnp.broadcast_to(table[:, 15][:, None, None], far_shape),
            near,
            jnp.broadcast_to(table[:, 31][:, None, None], far_shape),
        ],
        axis=2,
    )


def general_body(wide, narrow, *arguments):
    (
        block_input,
        cotangent,
        lengths,
        project_weight,
        output_weight,
        expand_weight,
        shrink_weight,
        bucket_bias,
        norm_gains,
    ) = arguments[:9]
    firsts = arguments[9:15]
    seconds = arguments[15:21]
    tokens, width = block_input.shape
    buffers = lengths.shape[0]
    length = tokens // buffers
    rows = norm_gains.shape[1]
    head_cols = project_weight.shape[2]
    heads = head_cols // DH
    hidden_cols = expand_weight.shape[2]
    w = lax.axis_index("wide")
    n = lax.axis_index("narrow")
    core = n % 2

    def swap(value, wide_mask, narrow_mask):
        pairs = [
            (a * narrow + b, (a ^ wide_mask) * narrow + (b ^ narrow_mask))
            for a in range(wide)
            for b in range(narrow)
        ]
        return lax.ppermute(value, ("wide", "narrow"), pairs)

    def gather(piece):
        return [lax.all_gather(piece, "wide", axis=0, tiled=True)]

    def reduce_wide(outs):
        return [lax.psum_scatter(outs[0], "wide", scatter_dimension=0, tiled=True)]

    offs = jnp.zeros((1,), jnp.int32)
    order = jnp.stack([1 - core, core, n // 2])

    p_piece = jnp.concatenate(
        [
            project_weight[0],
            project_weight[1],
            project_weight[2],
            norm_gains.T,
            jnp.zeros((rows, DH - 2), F32),
        ],
        axis=1,
    ).astype(BF16)
    p_pieces = gather(p_piece)
    o_piece = output_weight.astype(BF16).T
    o_pair = jnp.concatenate([o_piece, swap(o_piece, 0, 2)], axis=1)
    oa_pieces = gather(o_pair)
    ob_pieces = [swap(piece, 0, 1) for piece in oa_pieces]
    e_pieces = gather(
        jnp.concatenate([expand_weight[0], expand_weight[1]], axis=1).astype(BF16)
    )
    s_pieces = gather(shrink_weight.astype(BF16).T)

    ends = jnp.cumsum(lengths, axis=1)
    strip = bias_strip(bucket_bias, n, heads, length)

    normed_one, qkv, atts, logs, fours = [], [], [], [], []
    for b in range(buffers):
        normed, rows_b, att, log, gains = attend(
            b, ends, offs, block_input, strip, p_pieces, length, heads
        )
        normed_one.append(normed)
        qkv.append(rows_b)
        atts.append(att)
        logs.append(log)
        across = swap(att, 0, 2)
        fours.append((att, across, swap(att, 0, 1), swap(across, 0, 1)))

    def core_sum(kept, sent):
        return (kept.astype(F32) + swap(sent, 0, 1).astype(F32)).astype(BF16)

    normed_two, hiddens, gates, middles, ff_sums, dn_sums, sums_two = [], [], [], [], [], [], []
    for b in range(buffers):
        normed, hidden, gate, ff_send, ff_keep, dn_send, dn_keep, middle, sums = feed(
            b,
            order,
            offs,
            fours[b],
            block_input,
            cotangent,
            gains,
            (oa_pieces, ob_pieces, e_pieces, s_pieces),
            length,
            hidden_cols,
        )
        normed_two.append(normed)
        hiddens.append(hidden)
        gates.append(gate)
        middles.append(middle)
        sums_two.append(sums)
        dn_sums.append(core_sum(dn_keep, dn_send))
        ff_sums.append(core_sum(ff_keep, ff_send))

    d_middles, lows = [], []
    for b in range(buffers):
        d_middle, low = half_call(
            middle_kernel,
            "middle",
            b,
            order,
            [dn_sums[b], swap(dn_sums[b], 0, 2), middles[b], cotangent],
            (3,),
            (F32, BF16),
            gains,
        )
        d_middles.append(d_middle)
        lows.append((low, swap(low, 0, 1)))

    count = 1
    feed_outs = grad_call(
        functools.partial(feed_grad_kernel, count, hidden_cols),
        "feed_grad",
        offs,
        [*normed_two, *gates, *hiddens, cotangent],
        width,
        3 * hidden_cols,
        count,
        rows,
        2 * tokens * width * 3 * hidden_cols,
    )
    feed_group = reduce_wide(feed_outs)

    low_full, dqkv, dn_one, sums_one, strips = [], [], [], [], []
    for b in range(buffers):
        low, grads, dn_send, dn_keep, sums, dstrip = back(
            b,
            ends,
            offs,
            order,
            lows[b][0],
            lows[b][1],
            qkv[b],
            logs[b],
            strip,
            block_input,
            oa_pieces,
            p_pieces,
            heads,
        )
        low_full.append(low)
        dqkv.append(grads)
        sums_one.append(sums)
        strips.append(dstrip)
        dn_one.append(core_sum(dn_keep, dn_send))

    gain_at = 3 * head_cols
    att_outs = grad_call(
        functools.partial(attend_grad_kernel, count, heads),
        "attend_grad",
        offs,
        [*normed_one, *dqkv, *low_full, *atts, jnp.stack(sums_one + sums_two)],
        width,
        gain_at + DH + head_cols,
        count,
        rows,
        2 * tokens * width * 4 * head_cols,
    )
    att_group = reduce_wide(att_outs)
    vmem = pl.BlockSpec(memory_space=pltpu.VMEM)
    bucket = pl.pallas_call(
        functools.partial(bucket_kernel, heads),
        in_specs=[vmem, vmem],
        out_specs=vmem,
        out_shape=jax.ShapeDtypeStruct((8, LANES), F32),
        compiler_params=params(),
        cost_estimate=pl.CostEstimate(flops=8 << 20, bytes_accessed=4 << 20, transcendentals=0),
        name="bucket",
    )(*strips)

    half_offs = jnp.stack(
        [
            b * length + which * (length // 2)
            for b in range(buffers)
            for which in (core, 1 - core)
        ]
    )
    out_halves, in_halves = [], []
    for b in range(buffers):
        (half,) = half_call(
            output_kernel,
            "output",
            b,
            order,
            [ff_sums[b], swap(ff_sums[b], 0, 2), middles[b]],
            (),
            (BF16,),
        )
        out_halves += [half, swap(half, 0, 1)]
        (half,) = half_call(
            input_kernel,
            "input",
            b,
            order,
            [dn_one[b], swap(dn_one[b], 0, 2), block_input, d_middles[b]],
            (2,),
            (BF16,),
            gains,
        )
        in_halves += [half, swap(half, 0, 1)]
    block_output = place(out_halves, half_offs, tokens)
    input_gradient = place(in_halves, half_offs, tokens)

    att_grad, feed_grad, stat, gain, table_sum = norm_call(
        wide, narrow, [att_group, feed_group], bucket, gain_at
    )
    results = adam_call(
        att_grad,
        feed_grad,
        gain,
        table_sum,
        stat,
        arguments[3:9],
        firsts,
        seconds,
        heads,
        hidden_cols,
    )
    return (block_output, input_gradient, stat[0, 0], *results)


class Place:
    def __init__(self, wide, narrow):
        self.wide, self.narrow = wide, narrow
        self.w = lax.axis_index("wide")
        self.n = lax.axis_index("narrow")
        self.me = self.w * narrow + self.n
        self.z, self.x = self.w // 2, self.w % 2
        self.y, self.core = self.n // 2, self.n % 2
        self.n_far = (self.n + 2) % 4
        self.n_beside = self.n + 1 - 2 * self.core
        self.n_diag = (self.n_beside + 2) % 4
        self.across = (self.w, self.n_far)
        self.beside = (self.w, self.n_beside)
        self.flip = (self.z * 2 + 1 - self.x, self.n)

    def along(self, m):
        return (((self.z + m) % 4) * 2 + self.x, self.n)

    def near_owner(self, m):
        return ((self.z + m) % 4) * 2 + self.x

    def far_owner(self, m):
        return ((self.z + m) % 4) * 2 + 1 - self.x

    def peer(self, k):
        device = (self.me + k) % (self.wide * self.narrow)
        return device, (device // self.narrow, device % self.narrow)


def remote(source, target, send_sem, recv_sem, peer):
    return pltpu.make_async_remote_copy(
        src_ref=source,
        dst_ref=target,
        send_sem=send_sem,
        recv_sem=recv_sem,
        device_id=peer,
        device_id_type=MESH,
    )


class Gather:
    def __init__(self, spot, view, ssem, rsem, flip_first=False):
        self.spot, self.view, self.ssem, self.rsem = spot, view, ssem, rsem
        self.flip_first = flip_first

    def copy(self, owner, slot, peer):
        return remote(
            self.view(owner), self.view(owner), self.ssem.at[slot], self.rsem.at[owner], peer
        )

    def landed(self, owner):
        self.copy(owner, 0, self.spot.flip).wait_recv()

    def start(self, owner, slot, peer):
        self.copy(owner, slot, peer).start()

    def sent(self, owner, slot, peer):
        self.copy(owner, slot, peer).wait_send()

    def fan(self, owner, slot, act):
        z = self.spot.z
        act(owner, slot + 1, self.spot.along(2))
        pl.when(z != 3)(lambda: act(owner, slot, self.spot.along(1)))
        pl.when(z != 0)(lambda: act(owner, slot + 2, self.spot.along(3)))

    def pass_on(self, owner, slot, act):
        z = self.spot.z
        pl.when(z == 2)(lambda: act(owner, slot, self.spot.along(1)))
        pl.when(z == 1)(lambda: act(owner, slot, self.spot.along(3)))

    def begin(self):
        if self.flip_first:
            self.start(self.spot.w, 3, self.spot.flip)
        self.fan(self.spot.w, 0, self.start)
        if not self.flip_first:
            self.start(self.spot.w, 3, self.spot.flip)

    def forward(self):
        if self.flip_first:
            owner = self.spot.far_owner(0)
            self.landed(owner)
            self.fan(owner, 4, self.start)
            return
        owner = self.spot.near_owner(2)
        self.landed(owner)
        self.pass_on(owner, 7, self.start)
        self.start(owner, 5, self.spot.flip)
        early = 1 + 2 * ((3 - self.spot.z) // 3)
        for m in (early, 4 - early):
            owner = self.spot.near_owner(4 - m)
            self.landed(owner)
            self.start(owner, 3 + m, self.spot.flip)

    def middle(self):
        for owner, slot in ((self.spot.near_owner(2), 7), (self.spot.far_owner(2), 8)):
            self.landed(owner)
            self.pass_on(owner, slot, self.start)

    def finish(self):
        if self.flip_first:
            for m in (1, 3):
                self.landed(self.spot.near_owner(m))
                self.landed(self.spot.far_owner(m))
        else:
            for m in range(4):
                self.landed(self.spot.far_owner(m))

    def drain(self):
        self.sent(self.spot.w, 3, self.spot.flip)
        self.fan(self.spot.w, 0, self.sent)
        self.pass_on(self.spot.near_owner(2), 7, self.sent)
        if self.flip_first:
            self.fan(self.spot.far_owner(0), 4, self.sent)
            self.pass_on(self.spot.far_owner(2), 8, self.sent)
        else:
            for m in (1, 2, 3):
                self.sent(self.spot.near_owner(4 - m), 3 + m, self.spot.flip)


class Reduce:
    def __init__(self, spot, even, odd, flipped, mixed, landed, sems_s, sems_r):
        self.spot, self.even, self.odd = spot, even, odd
        self.flipped, self.mixed, self.landed = flipped, mixed, landed
        self.sems_s, self.sems_r = sems_s, sems_r

    def over(self, m):
        return remote(
            self.odd(m), self.flipped(m), self.sems_s.at[m], self.sems_r.at[m], self.spot.flip
        )

    def along(self, m):
        return remote(
            self.mixed(m - 1),
            self.landed(m - 1),
            self.sems_s.at[3 + m],
            self.sems_r.at[3 + m],
            self.spot.along(m),
        )

    def begin(self):
        for m in (2, 1, 3, 0):
            self.over(m).start()

    def relay(self, *ms):
        for m in ms:
            self.over(m).wait_recv()
            self.mixed(m - 1)[...] = (
                self.even(m).astype(F32) + self.flipped(m)[...].astype(F32)
            ).astype(BF16)
            self.along(m).start()

    def result(self):
        self.over(0).wait_recv()
        value = self.even(0).astype(F32) + self.flipped(0)[...].astype(F32)
        for m in (1, 2, 3):
            self.along(m).wait_recv()
            value = value + self.landed(m - 1)[...].astype(F32)
        return value

    def drain(self):
        for m in range(4):
            self.over(m).wait_send()
        for m in (1, 2, 3):
            self.along(m).wait_send()


def segments_of(index, lengths_ref, buffer, slots):
    end = lengths_ref[buffer, 0]
    total = (index >= end).astype(jnp.int32)
    for slot in range(1, slots):
        end = end + lengths_ref[buffer, slot]
        total = total + (index >= end).astype(jnp.int32)
    return total


def layer_kernel(dims, *refs):
    buffers, slots, heads, hidden_cols, wide, narrow = dims
    (
        lengths_ref,
        bias_ref,
        x_hbm,
        cot_hbm,
        pw_ref,
        ow_ref,
        ew_ref,
        sw_ref,
        gn_ref,
        out_ref,
        in_ref,
        p_grad,
        o_grad,
        feed_grad,
        stat_ref,
        gain_ref,
        table_ref,
        x_ref,
        cot_ref,
        strip,
        dstrip,
        pbuf,
        obuf,
        fbuf,
        att_ref,
        qkv_ref,
        log_ref,
        low_ref,
        middle_ref,
        hid,
        dg,
        total,
        opad,
        gpad,
        feed_flip,
        feed_mix,
        feed_land,
        o_even,
        o_odd,
        o_flip,
        o_mix,
        o_land,
        p_odd,
        p_flip,
        p_mix,
        p_land,
        ff_out,
        ff_in,
        ff_sum,
        dn_out,
        dn_in,
        dn_sum,
        dn_far,
        ws,
        kt,
        vt,
        qt,
        gt,
        dkt,
        dvt,
        gain_two_sum,
        block,
        inbox,
        gather_s,
        gather_r,
        lone_s,
        lone_r,
        red_s,
        red_r,
        norm_s,
        norm_r,
        credit,
        load,
        att_s,
        att_r,
        last_s,
        last_r,
    ) = refs
    spot = Place(wide, narrow)
    core = spot.core
    devices = wide * narrow
    tokens, width = x_ref.shape
    length = tokens // buffers
    half = length // 2
    head_cols = heads * DH
    qkv_cols = 3 * head_cols
    part = hidden_cols // 2
    chunk = 3 * part
    blocks = length // LANES
    owned = gn_ref.shape[1]
    normed_one, normed_two = in_ref, out_ref
    loads = [
        pltpu.make_async_copy(x_hbm, x_ref, load.at[0]),
        pltpu.make_async_copy(cot_hbm, cot_ref, load.at[1]),
    ]
    for copy in loads:
        copy.start()
    barrier = pltpu.get_barrier_semaphore()

    @pl.loop(1, devices)
    def _(k):
        pl.semaphore_signal(barrier, inc=1, device_id=spot.peer(k)[1], device_id_type=MESH)

    def at_rows(owner):
        return pl.ds(pl.multiple_of(owner * owned, 16), owned)

    def lone(view_from, view_to, slot, peer):
        return remote(view_from, view_to, lone_s.at[slot], lone_r.at[slot], peer)

    mine = at_rows(spot.w)
    gpad[...] = jnp.zeros_like(gpad)
    gpad[0:2, 0:owned] = gn_ref[...]
    pbuf[mine] = jnp.concatenate(
        [pw_ref[0], pw_ref[1], pw_ref[2], gpad[...].T[:owned, :DH]], axis=1
    ).astype(BF16)
    pl.semaphore_wait(barrier, devices - 1)
    split = 3 * LANES
    projections = [
        Gather(
            spot,
            lambda v, span=span: pbuf.at[at_rows(v), span],
            gather_s.at[at],
            gather_r.at[at],
        )
        for at, span in enumerate((slice(0, split), slice(split, qkv_cols + DH)))
    ]
    for group in projections:
        group.begin()
    opad[...] = jnp.zeros_like(opad)
    opad[0:head_cols, 0:owned] = ow_ref[...]
    obuf[spot.n, mine] = opad[...].T[:owned, :head_cols].astype(BF16)
    o_views = [
        lambda v: obuf.at[spot.n, at_rows(v)],
        lambda v: obuf.at[spot.n_far, at_rows(v)],
    ]
    outs_gather = [
        Gather(spot, view, gather_s.at[2 + at], gather_r.at[2 + at])
        for at, view in enumerate(o_views)
    ]
    lone(o_views[0](spot.w), o_views[0](spot.w), 0, spot.across).start()
    for j in range(2):
        span = slice(j * part, (j + 1) * part)
        fbuf[mine, j * chunk : j * chunk + part] = ew_ref[0, :, span].astype(BF16)
        fbuf[mine, j * chunk + part : j * chunk + 2 * part] = ew_ref[1, :, span].astype(BF16)
        fbuf[mine, j * chunk + 2 * part : (j + 1) * chunk] = sw_ref[:, span].astype(BF16)
    feed_cuts = (0, 256, 512, 768, 1024, 1280, 1536)
    feeds_gather = [
        Gather(
            spot,
            lambda v, at=at: fbuf.at[at_rows(v), feed_cuts[at] : feed_cuts[at + 1]],
            gather_s.at[4 + at],
            gather_r.at[4 + at],
            flip_first=at in (5,),
        )
        for at in range(len(feed_cuts) - 1)
    ]

    near_at = (blocks - 2) * LANES
    near_end = near_at + 3 * LANES
    near_ids = bucket_of(
        lax.broadcasted_iota(jnp.int32, (LANES, 3 * LANES), 1)
        - LANES
        - lax.broadcasted_iota(jnp.int32, (LANES, 3 * LANES), 0)
    )
    for h in range(heads):
        head = spot.n * heads + h
        near = jnp.zeros((LANES, 3 * LANES), F32)
        for b in range(32):
            if b != 16:
                near = jnp.where(near_ids == b, bias_ref[head, b], near)
        strip[h, :, near_at:near_end] = near
        strip[h, :, :near_at] = jnp.full((LANES, near_at), bias_ref[head, 15])
        strip[h, :, near_end:] = jnp.full((LANES, near_at), bias_ref[head, 31])
    lone(o_views[1](spot.w), o_views[1](spot.w), 0, spot.across).wait_recv()
    for group in outs_gather + feeds_gather:
        group.begin()
    dstrip[...] = jnp.zeros_like(dstrip)
    gain_two_sum[...] = jnp.zeros_like(gain_two_sum)

    projections[0].forward()
    projections[1].forward()
    for group in projections:
        group.finish()
    loads[0].wait()

    gains = pbuf[:, 4 * LANES :].astype(F32).T[qkv_cols - 4 * LANES : qkv_cols - 4 * LANES + 8]
    gain_one, gain_two = gains[0:1], gains[1:2]

    def relay_feeds(*ats):
        for at in ats:
            feeds_gather[at].forward()

    def relay_outs():
        for group in outs_gather:
            group.forward()

    def outs_beside():
        for group in outs_gather:
            group.finish()
        lone(obuf.at[spot.n], obuf.at[spot.n], 1, spot.beside).start()
        lone(obuf.at[spot.n_far], obuf.at[spot.n_far], 2, spot.beside).start()

    step = 256
    strides = length // step

    def att_piece(which, b, at, kind, peer):
        span = pl.ds(pl.multiple_of(b * length + at * step, step), step)
        view = att_ref.at[which, span]
        slot = (kind * buffers + b) * strides + at
        return remote(view, view, att_s.at[slot], att_r.at[slot], peer)

    def att_send(b, at):
        att_piece(spot.n, b, at, 0, spot.across).start()
        att_piece(spot.n, b, at, 1, spot.beside).start()

    def att_relay(b, pieces):
        for at in pieces:
            att_piece(spot.n_far, b, at, 0, spot.across).wait_recv()
            att_piece(spot.n_far, b, at, 2, spot.beside).start()

    qkv_events = ({}, {0: feeds_gather[1].forward})
    att_events = (
        {0: relay_outs, 1: lambda: relay_feeds(5), 2: feeds_gather[0].forward},
        {0: lambda: (outs_beside(), relay_feeds(2))[1], 1: feeds_gather[3].forward, 2: lambda: (relay_feeds(4), att_relay(0, range(1)))[1]},
    )

    def fire(events, at):
        for when, what in events.items():
            pl.when(at == when)(what)

    for b in range(buffers):
        base = b * length

        @pl.loop(0, length // step)
        def _(at, b=b, base=base):
            fire(qkv_events[b], at)
            begin = pl.multiple_of(at * step, step)
            here = pl.ds(begin, step)
            span = pl.ds(pl.multiple_of(base + begin, step), step)
            values = x_ref[span].astype(F32)
            normed = (values * rms_scale(values) * gain_one).astype(BF16)
            normed_one[span] = normed
            qkv = mm(normed, pbuf[...]).astype(BF16)
            qkv_ref[span] = qkv[:, :qkv_cols]
            for h in range(heads):
                k_at = head_cols + h * DH
                v_at = 2 * head_cols + h * DH
                kt[h, :, here] = qkv[:, k_at : k_at + DH].T
                ws[h, here] = qkv[:, v_at : v_at + DH]

        seg_keys = segments_of(
            lax.broadcasted_iota(jnp.int32, (1, length), 1), lengths_ref, b, slots
        )

        @pl.loop(0, blocks // 2)
        def _(at, b=b, base=base, seg_keys=seg_keys):
            fire(att_events[b], at)
            begin = pl.multiple_of(at * 2 * LANES, 2 * LANES)
            span = pl.ds(pl.multiple_of(base + begin, 2 * LANES), 2 * LANES)
            windows = [
                pl.ds(pl.multiple_of((blocks - 1 - r - 2 * at) * LANES, LANES), length)
                for r in range(2)
            ]
            seg_rows = segments_of(
                lax.broadcasted_iota(jnp.int32, (2 * LANES, 1), 0) + begin, lengths_ref, b, slots
            )
            same = seg_rows == seg_keys
            lane = lax.broadcasted_iota(jnp.int32, (2 * LANES, LANES), 1)
            logs = jnp.zeros((2 * LANES, LANES), F32)
            queries = qkv_ref[span, :head_cols]
            outs = []
            for h in range(heads):
                scores = mm(queries[:, h * DH : (h + 1) * DH], kt[h]) + jnp.concatenate(
                    [strip[h, :, window] for window in windows], axis=0
                )
                scores = jnp.where(same, scores, masked_score)
                row_max = jnp.max(scores, axis=1, keepdims=True)
                raised = jnp.exp(scores - row_max)
                sums = jnp.sum(raised, axis=1, keepdims=True)
                probs = (raised * (1.0 / sums)).astype(BF16)
                outs.append(mm(probs, ws[h]).astype(BF16))
                logs = jnp.where(lane == h, row_max + jnp.log(sums), logs)
            log_ref[span] = logs
            att_ref[spot.n, span] = jnp.concatenate(outs, axis=1)
            att_send(b, at)

        if b == 1:
            att_relay(0, range(1, strides))

    k0 = 0.7978845608028654
    k1 = 0.044715

    def half_rows(b, which):
        return pl.ds(pl.multiple_of(b * length + which * half, LANES), half)

    def ff_core(b):
        return lone(ff_out.at[b], ff_in.at[b], 9 + b, spot.beside)

    def ff_across(b):
        return lone(ff_sum.at[b], ff_in.at[b], 11 + b, spot.across)

    def dn_core(b, turn):
        return lone(dn_out.at[b], dn_in.at[b], 13 + 2 * turn + b, spot.beside)

    def dn_across(b, turn):
        return lone(dn_sum.at[b], dn_far.at[b], 17 + 2 * turn + b, spot.across)

    def low_core(b, which):
        view = low_ref.at[half_rows(b, which)]
        return lone(view, view, 21 + b, spot.beside)

    def out_core(b, which):
        view = out_ref.at[half_rows(b, which)]
        return lone(view, view, 23 + b, spot.beside)

    lasts = half // LANES

    def in_core(b, which, i):
        begin = pl.multiple_of(b * length + which * half + i * LANES, LANES)
        view = in_ref.at[pl.ds(begin, LANES)]
        at = lasts * (buffers + b) + i
        return remote(view, view, last_s.at[at], last_r.at[at], spot.beside)

    def dn_last(b, i):
        span = pl.ds(pl.multiple_of(i * LANES, LANES), LANES)
        at = lasts * b + i
        return remote(
            dn_sum.at[b, span], dn_far.at[b, span], last_s.at[at], last_r.at[at], spot.across
        )

    def outs_ready():
        loads[1].wait()
        lone(obuf.at[spot.n_beside], obuf.at[spot.n_beside], 1, spot.beside).wait_recv()
        lone(obuf.at[spot.n_diag], obuf.at[spot.n_diag], 2, spot.beside).wait_recv()

    def first_feed():
        feeds_gather[5].middle()
        feeds_gather[0].finish()
        feeds_gather[1].finish()
        feeds_gather[2].finish()

    def last_feed():
        att_relay(1, range(strides))
        feeds_gather[3].finish()
        feeds_gather[4].finish()
        feeds_gather[5].finish()

    def half_of(b, keep):
        return half_rows(b, (1 - core) * (1 - keep) + core * keep)

    def hidden_part(j, rows, normed_rows):
        at = j * chunk
        both = mm(normed_rows, fbuf[:, at : at + 2 * part])
        gate, up = both[:, :part], both[:, part:]
        square = gate * gate
        tanh = jnp.tanh(k0 * (gate + k1 * (square * gate)))
        lift = 0.5 * (1.0 + tanh)
        active = gate * lift
        slope = lift + (0.5 * gate) * (1.0 - tanh * tanh) * (k0 + (3.0 * k0 * k1) * square)
        d_hidden = mm(cot_ref[rows], fbuf[:, at + 2 * part : at + 3 * part])
        hid[rows, j * part : (j + 1) * part] = (active * up).astype(BF16)
        dg[rows, 2 * j * part : (2 * j + 1) * part] = (d_hidden * up * slope).astype(BF16)
        dg[rows, (2 * j + 1) * part : (2 * j + 2) * part] = (d_hidden * active).astype(BF16)

    @pl.loop(0, buffers)
    def _(b):
        def att_ready():
            for at in range(strides):
                att_piece(spot.n_beside, b, at, 1, spot.beside).wait_recv()
                att_piece(spot.n_diag, b, at, 2, spot.beside).wait_recv()

        att_ready()

        @pl.loop(0, 2)
        def _(keep):
            pl.when((b == 0) & (keep == 0))(outs_ready)
            rows = half_of(b, keep)
            attention = mm(att_ref[0, rows], obuf[0], NT)
            for a in range(1, 4):
                attention = attention + mm(att_ref[a, rows], obuf[a], NT)
            middle = x_ref[rows].astype(F32) + attention
            normed_rows = (middle * rms_scale(middle) * gain_two).astype(BF16)
            normed_two[rows] = normed_rows

            @pl.when(keep == 1)
            def _():
                middle_ref[b] = middle

            pl.when((b == 0) & (keep == 0))(first_feed)
            hidden_part(0, rows, normed_two[rows])

        pl.when(b == 0)(last_feed)

        @pl.loop(0, 2)
        def _(keep):
            rows = half_of(b, keep)
            normed_rows = normed_two[rows]
            hidden_part(1, rows, normed_rows)
            dn = mm(dg[rows, : 2 * part], fbuf[:, : 2 * part], NT) + mm(
                dg[rows, 2 * part :], fbuf[:, chunk : chunk + 2 * part], NT
            )
            gain_two_sum[...] = gain_two_sum[...] + fold_rows(dn * normed_rows.astype(F32))
            dn = dn.astype(BF16)

            @pl.when(keep == 0)
            def _():
                dn_out[b] = dn
                dn_core(b, 0).start()

            ff = (
                mm(hid[rows, :part], fbuf[:, 2 * part : chunk], NT)
                + mm(hid[rows, part:], fbuf[:, chunk + 2 * part :], NT)
            ).astype(BF16)

            @pl.when(keep == 0)
            def _():
                ff_out[b] = ff
                ff_core(b).start()

            @pl.when(keep == 1)
            def _():
                ff_core(b).wait_recv()
                ff_sum[b] = (ff.astype(F32) + ff_in[b].astype(F32)).astype(BF16)
                dn_core(b, 0).wait_recv()
                dn_sum[b] = (dn.astype(F32) + dn_in[b].astype(F32)).astype(BF16)
                dn_across(b, 0).start()

    def own_block(b, i):
        span = pl.ds(pl.multiple_of(i * LANES, LANES), LANES)
        here = pl.ds(pl.multiple_of(b * length + core * half + i * LANES, LANES), LANES)
        return span, here

    def finish_middle(b):
        dn_across(b, 0).wait_recv()

        @pl.loop(0, half // LANES)
        def _(i):
            span, here = own_block(b, i)
            upstream = dn_sum[b, span].astype(F32) + dn_far[b, span].astype(F32)
            middle = middle_ref[b, span]
            d_middle = cot_ref[here].astype(F32) + norm_back(
                middle, rms_scale(middle), gain_two, upstream
            )
            low_ref[here] = d_middle.astype(BF16)

        pl.semaphore_signal(credit.at[b], inc=1, device_id=spot.across, device_id_type=MESH)
        low_core(b, core).start()

    for group in feeds_gather:
        group.drain()
    for b in range(buffers):
        for at in range(strides):
            att_piece(spot.n_far, b, at, 2, spot.beside).wait_send()
    feed_reds = []
    for j in range(2):
        for begin in range(0, width, step):
            cols = slice(begin, begin + step)
            total[cols, : 2 * part] = mm(
                normed_two[:, cols], dg[:, 2 * j * part : (2 * j + 2) * part], TN
            )
            total[cols, 2 * part :] = mm(cot_ref[:, cols], hid[:, j * part : (j + 1) * part], TN)
        span = slice(j * chunk, (j + 1) * chunk)
        for m in range(4):
            even = total[pl.ds(pl.multiple_of(spot.near_owner(m) * owned, 8), owned)]
            odd = total[pl.ds(pl.multiple_of(spot.far_owner(m) * owned, 8), owned)]
            fbuf[m * owned : (m + 1) * owned, span] = even.astype(BF16)
            fbuf[(4 + m) * owned : (5 + m) * owned, span] = odd.astype(BF16)
        red = Reduce(
            spot,
            lambda m, span=span: fbuf[m * owned : (m + 1) * owned, span],
            lambda m, span=span: fbuf.at[(4 + m) * owned : (5 + m) * owned, span],
            lambda m, span=span: feed_flip.at[m, :, span],
            lambda m, span=span: feed_mix.at[m, :, span],
            lambda m, span=span: feed_land.at[m, :, span],
            red_s.at[j],
            red_r.at[j],
        )
        red.begin()
        feed_reds.append(red)
    finish_middle(0)
    feed_reds[0].relay(2, 1)

    out_red = Reduce(
        spot,
        lambda m: o_even[m],
        lambda m: o_odd.at[m],
        lambda m: o_flip.at[m],
        lambda m: o_mix.at[m],
        lambda m: o_land.at[m],
        red_s.at[2],
        red_r.at[2],
    )

    def out_weight_grad():
        for begin in range(0, width, step):
            cols = slice(begin, begin + step)
            total[cols, :head_cols] = mm(low_ref[:, cols], att_ref[spot.n], TN)
        for m in range(4):
            even = total[pl.ds(pl.multiple_of(spot.near_owner(m) * owned, 8), owned), :head_cols]
            odd = total[pl.ds(pl.multiple_of(spot.far_owner(m) * owned, 8), owned), :head_cols]
            o_even[m] = even
            o_odd[m] = odd.astype(BF16)
        out_red.begin()

    gain_sums = jnp.zeros((8, width), F32)
    def second_middle():
        finish_middle(1)
        ff_across(1).start()

    back_events = (
        {
            0: lambda: feed_reds[0].relay(3),
            2: lambda: ff_across(0).start(),
            3: lambda: feed_reds[1].relay(2),
            5: lambda: (feed_reds[1].relay(1), second_middle())[1],
        },
        {0: lambda: feed_reds[1].relay(3), 3: lambda: out_red.relay(2, 1), 4: lambda: out_red.relay(3)},
    )
    for b in range(buffers):
        base = b * length
        rows = slice(base, base + length)
        low_core(b, 1 - core).wait_recv()
        if b == 1:
            out_weight_grad()
        grads = mm(low_ref[rows], obuf[spot.n]).astype(BF16)
        att_ref[spot.n_far, :length] = grads
        for h in range(heads):
            keys = qkv_ref[rows, head_cols + h * DH : head_cols + (h + 1) * DH]
            values = qkv_ref[rows, 2 * head_cols + h * DH : 2 * head_cols + (h + 1) * DH]
            ws[h] = keys
            kt[h] = keys.T
            vt[h] = values.T
            qt[h] = qkv_ref[rows, h * DH : (h + 1) * DH].T
            gt[h] = grads[:, h * DH : (h + 1) * DH].T
        dkt[...] = jnp.zeros_like(dkt)
        dvt[...] = jnp.zeros_like(dvt)
        seg_keys = segments_of(
            lax.broadcasted_iota(jnp.int32, (1, length), 1), lengths_ref, b, slots
        )

        @pl.loop(0, blocks)
        def _(at, b=b, base=base, seg_keys=seg_keys):
            fire(back_events[b], at)
            begin = pl.multiple_of(at * LANES, LANES)
            here = pl.ds(begin, LANES)
            span = pl.ds(pl.multiple_of(base + begin, LANES), LANES)
            window = pl.ds(pl.multiple_of((blocks - 1 - at) * LANES, LANES), length)
            seg_rows = segments_of(
                lax.broadcasted_iota(jnp.int32, (LANES, 1), 0) + begin, lengths_ref, b, slots
            )
            same = seg_rows == seg_keys
            logs = log_ref[span]
            queries = qkv_ref[span, :head_cols]
            incoming = att_ref[spot.n_far, here]
            outs = []
            for h in range(heads):
                cols = slice(h * DH, (h + 1) * DH)
                scores = mm(queries[:, cols], kt[h]) + strip[h, :, window]
                scores = jnp.where(same, scores, masked_score)
                probs = jnp.exp(scores - logs[:, h : h + 1])
                d_probs = mm(incoming[:, cols], vt[h])
                inner = jnp.sum(probs * d_probs, axis=1, keepdims=True)
                d_scores = (probs * (d_probs - inner)).astype(BF16)
                dstrip[h, :, window] = dstrip[h, :, window] + d_scores.astype(F32)
                outs.append(mm(d_scores, ws[h]).astype(BF16))
                dkt[h] = dkt[h] + mm(qt[h, :, here], d_scores)
                dvt[h] = dvt[h] + mm(gt[h, :, here], probs.astype(BF16))
            dg[span, :head_cols] = jnp.concatenate(outs, axis=1)

        outs = [dkt[h].T.astype(BF16) for h in range(heads)]
        outs += [dvt[h].T.astype(BF16) for h in range(heads)]
        dg[rows, head_cols:qkv_cols] = jnp.concatenate(outs, axis=1)
        for keep in range(2):
            which = core if keep else 1 - core
            here = half_rows(b, which)
            if keep == 0:
                dn_core(b, 0).wait_send()
            else:
                dn_across(b, 0).wait_send()
            dn = mm(dg[here, :qkv_cols], pbuf[:, :qkv_cols], NT)
            values = x_ref[here].astype(F32)
            gain_sums = gain_sums + fold_rows(dn * values * rms_scale(values))
            dn = dn.astype(BF16)
            if keep == 0:
                dn_out[b] = dn
                dn_core(b, 1).start()
            else:
                dn_core(b, 1).wait_recv()
                dn_sum[b] = (dn.astype(F32) + dn_in[b].astype(F32)).astype(BF16)
                pl.semaphore_wait(credit.at[b], 1)
                for i in range(lasts):
                    dn_last(b, i).start()

    row = lax.broadcasted_iota(jnp.int32, (LANES, width), 0)
    gain_rows = jnp.where(
        row == DH,
        jnp.sum(gain_sums, axis=0, keepdims=True),
        jnp.where(
            row == DH + 1, jnp.sum(gain_two_sum[...], axis=0, keepdims=True) / gain_two, 0.0
        ),
    )
    gain_cols = gain_rows.T
    p_cols = qkv_cols + DH
    p_reds = []
    for at, span in enumerate((slice(0, split), slice(split, p_cols))):
        stop = min(span.stop, qkv_cols)
        for begin in range(0, width, step):
            cols = slice(begin, begin + step)
            total[cols, span.start : stop] = mm(
                normed_one[:, cols], dg[:, span.start : stop], TN
            )
            if at:
                total[cols, qkv_cols:p_cols] = gain_cols[cols, DH:]
        for m in range(4):
            odd = total[pl.ds(pl.multiple_of(spot.far_owner(m) * owned, 8), owned), span]
            p_odd[m, :, span] = odd.astype(BF16)
        red = Reduce(
            spot,
            lambda m, span=span: total[
                pl.ds(pl.multiple_of(spot.near_owner(m) * owned, 8), owned), span
            ],
            lambda m, span=span: p_odd.at[m, :, span],
            lambda m, span=span: p_flip.at[m, :, span],
            lambda m, span=span: p_mix.at[m, :, span],
            lambda m, span=span: p_land.at[m, :, span],
            red_s.at[3 + at],
            red_r.at[3 + at],
        )
        red.begin()
        p_reds.append(red)

    def finish_out(b):
        ff_across(b).wait_recv()

        @pl.loop(0, half // LANES)
        def _(i):
            span, here = own_block(b, i)
            joined = (ff_sum[b, span].astype(F32) + ff_in[b, span].astype(F32)).astype(BF16)
            out_ref[here] = (middle_ref[b, span] + joined.astype(F32)).astype(BF16)

        out_core(b, core).start()

    def finish_in(b):
        @pl.loop(0, half // LANES)
        def _(i):
            dn_last(b, i).wait_recv()
            span, here = own_block(b, i)
            upstream = dn_sum[b, span].astype(F32) + dn_far[b, span].astype(F32)
            values = x_ref[here].astype(F32)
            in_ref[here] = (
                low_ref[here].astype(F32)
                + norm_back(values, rms_scale(values), gain_one, upstream)
            ).astype(BF16)
            in_core(b, core, i).start()

    def square_of(value):
        return jnp.sum(jnp.sum(value * value, axis=1, keepdims=True), axis=0, keepdims=True)

    finish_out(0)
    p_reds[0].relay(2, 1, 3)
    finish_out(1)
    squares = jnp.zeros((1, 1), F32)
    for j in range(2):
        value = feed_reds[j].result()
        feed_grad[:, j * chunk : (j + 1) * chunk] = value
        squares = squares + square_of(value)
    p_reds[1].relay(2, 1, 3)
    value = out_red.result()
    o_grad[...] = value
    squares = squares + square_of(value)
    for b in range(buffers):
        out_core(b, 1 - core).wait_recv()
    finish_in(0)

    near_row = lax.broadcasted_iota(jnp.int32, (LANES, 4 * LANES), 0)
    diag = lax.broadcasted_iota(jnp.int32, (1, 4 * LANES), 1)
    ids = bucket_of(jnp.where(diag < 3 * LANES, diag - LANES, diag - 5 * LANES))
    lane = lax.broadcasted_iota(jnp.int32, (1, LANES), 1)
    onehot = jnp.where(near_row == ids, 1.0, 0.0)
    bucket_line = jnp.zeros((1, LANES), F32)
    for h in range(heads):
        left = jnp.sum(jnp.sum(dstrip[h, :, :near_at], axis=0, keepdims=True), axis=1, keepdims=True)
        right = jnp.sum(
            jnp.sum(dstrip[h, :, near_end:], axis=0, keepdims=True), axis=1, keepdims=True
        )
        near = jnp.concatenate(
            [dstrip[h, :, near_at:near_end], jnp.zeros((LANES, LANES), F32)], axis=1
        )
        for k in range(7):
            near = jnp.where(
                (near_row // (1 << k)) % 2 == 1, pltpu.roll(near, 4 * LANES - (1 << k), 1), near
            )
        binned = lax.dot_general(
            jnp.broadcast_to(jnp.sum(near, axis=0, keepdims=True), (8, 4 * LANES)),
            onehot,
            NT,
            precision=lax.Precision.HIGHEST,
            preferred_element_type=F32,
        )[0:1]
        binned = binned + jnp.where(lane == 15, left, 0.0) + jnp.where(lane == 31, right, 0.0)
        binned = jnp.where(lane < 32, binned, 0.0)
        bucket_line = bucket_line + (pltpu.roll(binned, 32 * h, 1) if h else binned)

    value = p_reds[0].result()
    p_grad[:, :split] = value
    squares = squares + square_of(value)
    value = p_reds[1].result()
    p_grad[:, split:] = value
    kept = lax.broadcasted_iota(jnp.int32, value.shape, 1) < qkv_cols - split
    squares = squares + square_of(jnp.where(kept, value, 0.0))
    low_lane = qkv_cols // LANES * LANES
    gpad[...] = jnp.zeros_like(gpad)
    gpad[0:owned, : p_cols - low_lane] = value[:, low_lane - split :]
    turned = gpad[...].T
    here = qkv_cols - low_lane
    row8 = lax.broadcasted_iota(jnp.int32, (8, LANES), 0)
    line = jnp.where(row8 == 0, squares, 0.0)
    line = jnp.where(row8 == 1, turned[here : here + 1], line)
    line = jnp.where(row8 == 2, turned[here + 1 : here + 2], line)
    line = jnp.where(row8 == 3, bucket_line, line)
    block[...] = line
    inbox[spot.me] = line

    @pl.loop(1, devices)
    def _(k):
        peer, where = spot.peer(k)
        remote(block, inbox.at[spot.me], norm_s.at[k], norm_r.at[devices - k], where).start()

    finish_in(1)

    @pl.loop(1, devices)
    def _(k):
        peer, where = spot.peer(k)
        copy = remote(block, inbox.at[peer], norm_s.at[k], norm_r.at[k], where)
        copy.wait_send()
        copy.wait_recv()

    columns = [jnp.zeros((8, LANES), F32) for _ in range(narrow)]
    gain_square = jnp.zeros((8, LANES), F32)
    square_total = jnp.zeros((8, LANES), F32)
    for a in range(wide):
        summed = jnp.zeros((8, LANES), F32)
        for c in range(narrow):
            got = inbox[a * narrow + c]
            summed = summed + got
            columns[c] = columns[c] + got
        square_total = square_total + summed
        gain_square = gain_square + summed * summed
    own = inbox[spot.w * narrow]
    for c in range(1, narrow):
        own = own + inbox[spot.w * narrow + c]
    gain_ref[...] = own
    gain_square = jnp.where((row8 == 1) | (row8 == 2), gain_square, 0.0)
    norm_square = square_total[0:1, 0:1] + jnp.sum(
        jnp.sum(gain_square, axis=1, keepdims=True), axis=0, keepdims=True
    )
    table_row = lax.broadcasted_iota(jnp.int32, (16, LANES), 0)
    table = jnp.zeros((16, LANES), F32)
    for c in range(narrow):
        got = columns[c][3:4]
        norm_square = norm_square + jnp.sum(got * got, axis=1, keepdims=True)
        for h in range(heads):
            moved = pltpu.roll(got, LANES - 32 * h, 1) if h else got
            table = jnp.where(table_row == c * heads + h, moved, table)
    table_ref[...] = table
    global_norm = jnp.sqrt(norm_square)
    factor = jnp.minimum(1.0, clip_limit / (global_norm + 1e-06))
    stat_ref[...] = jnp.where(row8 == 0, global_norm, factor)

    for b in range(buffers):
        for i in range(lasts):
            in_core(b, 1 - core, i).wait_recv()
        for at in range(strides):
            att_piece(spot.n, b, at, 0, spot.across).wait_send()
            att_piece(spot.n, b, at, 1, spot.beside).wait_send()
        ff_core(b).wait_send()
        ff_across(b).wait_send()
        dn_core(b, 1).wait_send()
        for i in range(lasts):
            dn_last(b, i).wait_send()
            in_core(b, core, i).wait_send()
        low_core(b, core).wait_send()
        out_core(b, core).wait_send()
    lone(o_views[0](spot.w), o_views[0](spot.w), 0, spot.across).wait_send()
    lone(obuf.at[spot.n], obuf.at[spot.n], 1, spot.beside).wait_send()
    lone(obuf.at[spot.n_far], obuf.at[spot.n_far], 2, spot.beside).wait_send()
    for group in projections + outs_gather:
        group.drain()
    for group in feed_reds + p_reds + [out_red]:
        group.drain()


def layer(wide, narrow, lengths, bias, x, cot, pw, ow, ew, sw, gn):
    tokens, width = x.shape
    buffers, slots = lengths.shape
    length = tokens // buffers
    half = length // 2
    head_cols = pw.shape[2]
    heads = head_cols // DH
    hidden_cols = ew.shape[2]
    rows = gn.shape[1]
    devices = wide * narrow
    qkv_cols = 3 * head_cols
    p_cols = qkv_cols + DH
    feed_cols = 3 * hidden_cols
    strip_shape = (heads, LANES, (2 * (length // LANES) - 1) * LANES)
    vmem = pl.BlockSpec(memory_space=pltpu.VMEM)
    smem = pl.BlockSpec(memory_space=pltpu.SMEM)
    halves = pltpu.VMEM((buffers, half, width), BF16)
    tall = pltpu.VMEM((heads, DH, length), BF16)
    dma = pltpu.SemaphoreType.DMA

    def pieces(count, cols, kind=BF16):
        return pltpu.VMEM((count, rows, cols), kind)

    return pl.pallas_call(
        functools.partial(layer_kernel, (buffers, slots, heads, hidden_cols, wide, narrow)),
        in_specs=[smem, smem, pl.BlockSpec(memory_space=ANY), pl.BlockSpec(memory_space=ANY)]
        + [vmem] * 5,
        out_specs=[vmem] * 8,
        out_shape=[
            jax.ShapeDtypeStruct((tokens, width), BF16),
            jax.ShapeDtypeStruct((tokens, width), BF16),
            jax.ShapeDtypeStruct((rows, p_cols), F32),
            jax.ShapeDtypeStruct((rows, head_cols), F32),
            jax.ShapeDtypeStruct((rows, feed_cols), F32),
            jax.ShapeDtypeStruct((8, LANES), F32),
            jax.ShapeDtypeStruct((8, LANES), F32),
            jax.ShapeDtypeStruct((16, LANES), F32),
        ],
        scratch_shapes=[
            pltpu.VMEM((tokens, width), BF16),
            pltpu.VMEM((tokens, width), BF16),
            pltpu.VMEM(strip_shape, F32),
            pltpu.VMEM(strip_shape, F32),
            pltpu.VMEM((width, p_cols), BF16),
            pltpu.VMEM((narrow, width, head_cols), BF16),
            pltpu.VMEM((width, feed_cols), BF16),
            pltpu.VMEM((narrow, tokens, head_cols), BF16),
            pltpu.VMEM((tokens, qkv_cols), BF16),
            pltpu.VMEM((tokens, LANES), F32),
            pltpu.VMEM((tokens, width), BF16),
            pltpu.VMEM((buffers, half, width), F32),
            pltpu.VMEM((tokens, hidden_cols), BF16),
            pltpu.VMEM((tokens, 2 * hidden_cols), BF16),
            pltpu.VMEM((width, feed_cols // 2), F32),
            pltpu.VMEM((2 * LANES, LANES), F32),
            pltpu.VMEM((LANES, LANES), F32),
            pieces(4, feed_cols),
            pieces(3, feed_cols),
            pieces(3, feed_cols),
            pieces(4, head_cols, F32),
            pieces(4, head_cols),
            pieces(4, head_cols),
            pieces(3, head_cols),
            pieces(3, head_cols),
            pieces(4, p_cols),
            pieces(4, p_cols),
            pieces(3, p_cols),
            pieces(3, p_cols),
        ]
        + [halves] * 7
        + [
            pltpu.VMEM((heads, length, DH), BF16),
            tall,
            tall,
            tall,
            tall,
            pltpu.VMEM((heads, DH, length), F32),
            pltpu.VMEM((heads, DH, length), F32),
            pltpu.VMEM((8, width), F32),
            pltpu.VMEM((8, LANES), F32),
            pltpu.VMEM((devices, 8, LANES), F32),
            dma((12, 9)),
            dma((12, wide)),
            dma((27,)),
            dma((27,)),
            dma((5, 7)),
            dma((5, 7)),
            dma((devices,)),
            dma((devices,)),
            pltpu.SemaphoreType.REGULAR((buffers,)),
            dma((2,)),
            dma((3 * buffers * (length // 256),)),
            dma((3 * buffers * (length // 256),)),
            dma((2 * buffers * (half // LANES),)),
            dma((2 * buffers * (half // LANES),)),
        ],
        compiler_params=pltpu.CompilerParams(
            vmem_limit_bytes=64 << 20, collective_id=0, has_side_effects=True
        ),
        cost_estimate=pl.CostEstimate(
            flops=60 << 30, bytes_accessed=24 << 20, transcendentals=16 << 20
        ),
        name="layer",
    )(lengths, bias, x, cot, pw, ow, ew, sw, gn)


def update_kernel(
    heads, hidden_cols, from_out, from_in, p_ref, o_ref, feed_ref, stat_ref, gain_ref, table_ref, *refs
):
    weights, firsts, seconds = refs[:6], refs[6:12], refs[12:18]
    outs, norm_ref, to_out, to_in, o_pad, held, sems = refs[18:36], *refs[36:]
    pairs = ((from_out, to_out), (from_in, to_in))
    rows = from_out.shape[0] // 2
    ways = []
    for which, (source, target) in enumerate(pairs):
        for part in range(2):
            span = slice(part * rows, (part + 1) * rows)
            at = 2 * which + part
            ways.append(
                (
                    pltpu.make_async_copy(source.at[span], held.at[which, span], sems.at[0, at]),
                    pltpu.make_async_copy(held.at[which, span], target.at[span], sems.at[1, at]),
                )
            )
    for inward, _ in ways:
        inward.start()
    for inward, outward in ways:
        inward.wait()
        outward.start()
    factor = stat_ref[1:2, 0:1]
    norm_ref[0, 0] = jnp.sum(stat_ref[0:1, 0:1])
    head_cols = heads * DH
    rows = p_ref.shape[0]

    def update(which, index, gradient):
        results = adam_update(
            weights[which][index],
            firsts[which][index],
            seconds[which][index],
            factor * gradient,
            step_rates[which],
            decay_rates[which],
        )
        for at in range(3):
            outs[6 * at + which][index] = results[at]

    for i in range(3):
        update(0, i, p_ref[:, i * head_cols : (i + 1) * head_cols])
    part = hidden_cols // 2
    for j in range(2):
        span = slice(j * part, (j + 1) * part)
        for i in range(2):
            begin = (3 * j + i) * part
            update(2, (i, slice(None), span), feed_ref[:, begin : begin + part])
        begin = (3 * j + 2) * part
        update(3, (slice(None), span), feed_ref[:, begin : begin + part])
    o_pad[...] = jnp.zeros_like(o_pad)
    o_pad[0:rows, 0:head_cols] = o_ref[...]
    update(1, slice(None), o_pad[...].T[:head_cols, :rows])
    depth, columns = weights[4].shape
    update(4, slice(None), table_ref[:depth, :columns])
    update(5, slice(None), gain_ref[1:3, :rows])
    for _, outward in ways:
        outward.wait()


def update_call(activations, grads, params_in, firsts, seconds, heads, hidden_cols):
    vmem = pl.BlockSpec(memory_space=pltpu.VMEM)
    hbm = pl.BlockSpec(memory_space=ANY)
    operands = [*activations, *grads, *params_in, *firsts, *seconds]
    return pl.pallas_call(
        functools.partial(update_kernel, heads, hidden_cols),
        in_specs=[hbm] * 2 + [vmem] * (len(operands) - 2),
        out_specs=[vmem] * 18 + [pl.BlockSpec(memory_space=pltpu.SMEM)] + [hbm] * 2,
        out_shape=[jax.ShapeDtypeStruct(a.shape, F32) for a in params_in] * 3
        + [jax.ShapeDtypeStruct((1, 1), F32)]
        + [jax.ShapeDtypeStruct(a.shape, a.dtype) for a in activations],
        scratch_shapes=[
            pltpu.VMEM((LANES, 2 * LANES), F32),
            pltpu.VMEM((2, *activations[0].shape), BF16),
            pltpu.SemaphoreType.DMA((2, 4)),
        ],
        compiler_params=params(),
        cost_estimate=pl.CostEstimate(flops=4 << 20, bytes_accessed=16 << 20, transcendentals=0),
        name="update",
    )(*operands)


def direct_body(wide, narrow, *arguments):
    block_input, cotangent, lengths = arguments[:3]
    turned = (3, 4)
    flat = [
        value.T if at % 6 in turned else value for at, value in enumerate(arguments[3:21])
    ]
    weights, firsts, seconds = flat[:6], flat[6:12], flat[12:18]
    project, output, expand, shrink, bias, gains = weights
    block_output, input_gradient, *grads = layer(
        wide,
        narrow,
        lengths,
        bias,
        block_input,
        cotangent,
        project,
        output,
        expand,
        shrink,
        gains,
    )
    heads = project.shape[2] // DH
    *results, norm, block_output, input_gradient = update_call(
        (block_output, input_gradient), grads, weights, firsts, seconds, heads, expand.shape[2]
    )
    results = [value.T if at % 6 in turned else value for at, value in enumerate(results)]
    return (block_output, input_gradient, norm.reshape(()), *results)


def solution(mesh):
    wide, narrow = mesh.shape["wide"], mesh.shape["narrow"]
    body = direct_body if (wide, narrow) == (8, 4) else general_body
    state = (
        P(None, "wide", "narrow"),
        P("narrow", "wide"),
        P(None, "wide", "narrow"),
        P("narrow", "wide"),
        P(),
        P(None, "wide"),
    )
    rows = P("wide", None)
    return jax.shard_map(
        functools.partial(body, wide, narrow),
        mesh=mesh,
        in_specs=(rows, rows, rows, *state, *state, *state),
        out_specs=(rows, rows, P(), *state, *state, *state),
        check_vma=False,
    )
```
